32 devices in a mesh: seq: 4 (over y, x), fsdp: 8 (over z, core).
Axes of the slice: x: 2, y: 2, z: 4, core: 2. Of those that a mesh axis runs over, the one named last changes fastest.
Arguments:
- tokens: bfloat16 [8, 1024, 768], P('fsdp', 'seq'), may hold values from -6 to 6
- encoded: bfloat16 [8, 512, 768], P('fsdp', 'seq'), may hold values from -6 to 6
- lengths: int32 [8], P('fsdp'), may hold values from 512 to 1024, as said below
- cotangent: bfloat16 [8, 1024, 768], P('fsdp', 'seq'), may hold values from -6 to 6
- gain_self: bfloat16 [768], replicated, may hold values from 0.5 to 1.5
- gain_cross: bfloat16 [768], replicated, may hold values from 0.5 to 1.5
- gain_ff: bfloat16 [768], replicated, may hold values from 0.5 to 1.5
- bucket_table: bfloat16 [32, 12], replicated, may hold values from -4 to 4
- self_query: bfloat16 [768, 768], P('fsdp'), may hold values from -0.0390625 to 0.0390625
- self_key: bfloat16 [768, 768], P('fsdp'), may hold values from -0.21875 to 0.21875
- self_value: bfloat16 [768, 768], P('fsdp'), may hold values from -0.21875 to 0.21875
- self_out: bfloat16 [768, 768], P('fsdp'), may hold values from -3.5 to 3.5
- cross_query: bfloat16 [768, 768], P('fsdp'), may hold values from -0.0390625 to 0.0390625
- cross_key: bfloat16 [768, 768], P('fsdp'), may hold values from -0.21875 to 0.21875
- cross_value: bfloat16 [768, 768], P('fsdp'), may hold values from -0.21875 to 0.21875
- cross_out: bfloat16 [768, 768], P('fsdp'), may hold values from -1.5 to 1.5
- ff_gate: bfloat16 [768, 2048], P('fsdp'), may hold values from -0.21875 to 0.21875
- ff_up: bfloat16 [768, 2048], P('fsdp'), may hold values from -0.21875 to 0.21875
- ff_down: bfloat16 [2048, 768], P('fsdp'), may hold values from -0.125 to 0.125
Outputs:
- layer_out: bfloat16 [8, 1024, 768], P('fsdp', 'seq')
- grad_tokens: float32 [8, 1024, 768], P('fsdp', 'seq')
- grad_encoded: float32 [8, 512, 768], P('fsdp', 'seq')
- grad_gain_self: float32 [768], replicated
- grad_gain_cross: float32 [768], replicated
- grad_gain_ff: float32 [768], replicated
- grad_bucket_table: float32 [32, 12], replicated
- grad_self_query: float32 [768, 768], P('fsdp')
- grad_self_key: float32 [768, 768], P('fsdp')
- grad_self_value: float32 [768, 768], P('fsdp')
- grad_self_out: float32 [768, 768], P('fsdp')
- grad_cross_query: float32 [768, 768], P('fsdp')
- grad_cross_key: float32 [768, 768], P('fsdp')
- grad_cross_value: float32 [768, 768], P('fsdp')
- grad_cross_out: float32 [768, 768], P('fsdp')
- grad_ff_gate: float32 [768, 2048], P('fsdp')
- grad_ff_up: float32 [768, 2048], P('fsdp')
- grad_ff_down: float32 [2048, 768], P('fsdp')
The draws below stay inside these ranges and needn't reach their ends.
Inputs may be any that keep to these rules, and one draw needn't show every extreme that they name: Slots from lengths[s] on are unused; some sequence uses all 1024 slots and some uses exactly half of them.
All inputs are finite; a program needn't handle non-finite values.
Results may differ from the reference program's by a relative error of at most 0.02.
The reference program's roundings to bfloat16 on the way count: a program that leaves them out, or rounds other values in their place, can miss the bound.
Values may be sent and summed in bfloat16 or wider, within the bound.
A program may use at most 192 MiB of HBM per device.

```python
import math
import jax
import jax.numpy as jnp
from jax import lax

D = 768
FF = 2048
HEADS = 12
HEAD = 64
BUCKETS = 32
MAX_DISTANCE = 128
SEQS = 8
SEQ_SLOTS = 1024
ENC = 512


def draw_lengths(key, part):
    slot_total = SEQ_SLOTS
    lowest = slot_total // 2
    key_values = jax.random.fold_in(key, 11)
    key_long = jax.random.fold_in(key, 12)
    key_short = jax.random.fold_in(key, 13)
    drawn = jax.random.randint(key_values, (SEQS,), lowest, slot_total + 1, dtype=jnp.int32)
    longest = jax.random.randint(key_long, (), 0, SEQS, dtype=jnp.int32)
    jump = jax.random.randint(key_short, (), 1, max(SEQS, 2), dtype=jnp.int32)
    shortest = (longest + jump) % SEQS
    places = jnp.arange(SEQS, dtype=jnp.int32)
    drawn = jnp.where(places == shortest, lowest, drawn)
    return jnp.where(places == longest, slot_total, drawn).astype(jnp.int32)


def block_scale(key, dims, split, smallest, top_value):
    level, own = 1.0, jax.random.fold_in(key, 6)
    for position, blocks in split:
        heights = jnp.exp(jax.random.uniform(jax.random.fold_in(own, position), (blocks,), jnp.float32, smallest / len(split), top_value / len(split)))
        level = level * jnp.repeat(heights, dims[position] // blocks).reshape([-1 if axis == position else 1 for axis in range(len(dims))])
    return level


def scatter_about(rng, extent, spread, reach, shards=(), kind=jnp.bfloat16):
    entries = spread * jax.random.normal(rng, extent, jnp.float32)
    if shards:
        entries = entries * block_scale(rng, extent, shards, -0.22, 0.18)
    return jnp.clip(entries, -reach, reach).astype(kind)


def setup_inputs(seed: int = 0) -> dict:
    streams_of = jax.random.split(jax.random.key(seed), 20)
    tokens = scatter_about(streams_of[0], (SEQS, SEQ_SLOTS, D), 1.0, 6.0, ((0, 8), (1, 4)))
    encoded = scatter_about(streams_of[1], (SEQS, ENC, D), 1.0, 6.0, ((0, 8), (1, 4)))
    lengths = draw_lengths(jax.random.fold_in(streams_of[19], 71), 0)
    cotangent = scatter_about(streams_of[3], (SEQS, SEQ_SLOTS, D), 1.0, 6.0, ((0, 8), (1, 4)))
    gain_self = jnp.clip(1.0 + 0.1 * jax.random.normal(streams_of[4], (D,), jnp.float32), 0.5, 1.5).astype(jnp.bfloat16)
    gain_cross = jnp.clip(1.0 + 0.1 * jax.random.normal(streams_of[5], (D,), jnp.float32), 0.5, 1.5).astype(jnp.bfloat16)
    gain_ff = jnp.clip(1.0 + 0.1 * jax.random.normal(streams_of[6], (D,), jnp.float32), 0.5, 1.5).astype(jnp.bfloat16)
    bucket_table = scatter_about(streams_of[7], (BUCKETS, HEADS), 1.0, 4.0)
    self_query = scatter_about(streams_of[8], (D, HEADS * HEAD), (D * 28) ** -0.5, 0.0390625, ((0, 8),))
    self_key = scatter_about(streams_of[9], (D, HEADS * HEAD), D ** -0.5, 0.21875, ((0, 8),))
    self_value = scatter_about(streams_of[10], (D, HEADS * HEAD), D ** -0.5, 0.21875, ((0, 8),))
    self_out = scatter_about(streams_of[11], (HEADS * HEAD, D), (max(HEADS * HEAD // 256, 1)) ** -0.5, 3.5, ((0, 8),))
    cross_query = scatter_about(streams_of[12], (D, HEADS * HEAD), (D * 28) ** -0.5, 0.0390625, ((0, 8),))
    cross_key = scatter_about(streams_of[13], (D, HEADS * HEAD), D ** -0.5, 0.21875, ((0, 8),))
    cross_value = scatter_about(streams_of[14], (D, HEADS * HEAD), D ** -0.5, 0.21875, ((0, 8),))
    cross_out = scatter_about(streams_of[15], (HEADS * HEAD, D), (max(HEADS * HEAD // 48, 1)) ** -0.5, 1.5, ((0, 8),))
    ff_gate = scatter_about(streams_of[16], (D, FF), D ** -0.5, 0.21875, ((0, 8),))
    ff_up = scatter_about(streams_of[17], (D, FF), D ** -0.5, 0.21875, ((0, 8),))
    ff_down = scatter_about(streams_of[18], (FF, D), FF ** -0.5, 0.125, ((0, 8),))
    return {"tokens": tokens, "encoded": encoded, "lengths": lengths, "cotangent": cotangent, "gain_self": gain_self, "gain_cross": gain_cross, "gain_ff": gain_ff, "bucket_table": bucket_table, "self_query": self_query, "self_key": self_key, "self_value": self_value, "self_out": self_out, "cross_query": cross_query, "cross_key": cross_key, "cross_value": cross_value, "cross_out": cross_out, "ff_gate": ff_gate, "ff_up": ff_up, "ff_down": ff_down}


EPSILON = 1e-06
HIGHEST = lax.Precision.HIGHEST

@jax.custom_vjp
def low(v):
    return lax.optimization_barrier(v.astype(jnp.bfloat16)).astype(jnp.float32)

@jax.custom_vjp
def low_back(v):
    return v

def low_keep(v):
    return (low(v), None)

def low_pass(kept, grad):
    return (grad,)

def back_keep(v):
    return (v, None)

def back_low(kept, grad):
    return (low(grad),)
low.defvjp(low_keep, low_pass)
low_back.defvjp(back_keep, back_low)

def thresholds():
    exact_limit = BUCKETS // 2
    return [int(math.ceil(exact_limit * (MAX_DISTANCE / exact_limit) ** (number / exact_limit))) for number in range(1, exact_limit)]

def bucket_ids(key_count):
    exact_limit = BUCKETS // 2
    offsets = jnp.arange(key_count, dtype=jnp.int32)
    passed = jnp.zeros((key_count,), jnp.int32)
    for border in thresholds():
        passed = passed + (offsets >= border).astype(jnp.int32)
    return jnp.where(offsets < exact_limit, offsets, exact_limit + passed)

def diagonal_fill(profile, first_row, block_rows):
    head_count, key_count = profile.shape
    flipped = profile[:, ::-1]
    padded = jnp.concatenate([jnp.zeros((head_count, 1), profile.dtype), flipped, jnp.zeros((head_count, key_count + block_rows), profile.dtype)], axis=1)
    offset = (key_count - block_rows - first_row).astype(jnp.int32)
    span = key_count + block_rows + 1
    window = lax.dynamic_slice_in_dim(padded, offset, span, 1)
    repeated = jnp.broadcast_to(window[:, None, :], (head_count, block_rows, span))
    flattened = repeated.reshape(head_count, block_rows * span)[:, :block_rows * (span - 1)]
    return flattened.reshape(head_count, block_rows, span - 1)[:, :, block_rows:block_rows + key_count]

def rms_scale(values, gain):
    return values * lax.rsqrt(lax.optimization_barrier(jnp.mean(values * values, axis=-1, keepdims=True)) + EPSILON) * gain

def multiply(left, right):
    return jnp.dot(left, right, precision=HIGHEST, preferred_element_type=jnp.float32)

def softmax_rows(scores):
    row_max = lax.optimization_barrier(jnp.max(scores, axis=-1, keepdims=True))
    raised = jnp.exp(scores - row_max)
    return raised / lax.optimization_barrier(jnp.sum(raised, axis=-1, keepdims=True))

def sequence_layer(source, encoded, length, params):
    gain_self, gain_cross, gain_ff, table, self_query, self_key, self_value, self_out, cross_query, cross_key, cross_value, cross_out, ff_gate, ff_up, ff_down = params
    slot_count = source.shape[0]
    enc_count = encoded.shape[0]
    block_rows = min(512, slot_count)
    width = HEADS * HEAD
    first_normed_input = low(rms_scale(source, gain_self))
    queries = low_back(low(multiply(first_normed_input, self_query))).reshape(slot_count, HEADS, HEAD)
    keys_three = low_back(low(multiply(first_normed_input, self_key))).reshape(slot_count, HEADS, HEAD)
    values_three = low_back(low(multiply(first_normed_input, self_value))).reshape(slot_count, HEADS, HEAD)
    profile = table[bucket_ids(slot_count)].T

    def self_block(block_index):
        first_row = (block_index * block_rows).astype(jnp.int32)
        block_query = lax.dynamic_slice_in_dim(queries, first_row, block_rows, 0)
        raw_scores = jnp.einsum('qhd,khd->hqk', block_query, keys_three, precision=HIGHEST, preferred_element_type=jnp.float32)
        scores = low_back(raw_scores + diagonal_fill(profile, first_row, block_rows))
        row_ids = first_row + jnp.arange(block_rows, dtype=jnp.int32)
        col_ids = jnp.arange(slot_count, dtype=jnp.int32)
        allowed = (col_ids[None, :] <= row_ids[:, None]) & (col_ids[None, :] < length)
        soft_low = low(softmax_rows(jnp.where(allowed[None], scores, -1e+30)))
        mixed_rows = jnp.einsum('hqk,khd->qhd', soft_low, values_three, precision=HIGHEST, preferred_element_type=jnp.float32)
        return mixed_rows.reshape(block_rows, width)
    block_ids = jnp.arange(slot_count // block_rows, dtype=jnp.int32)
    mixed_self = low_back(low(lax.map(jax.checkpoint(self_block), block_ids).reshape(slot_count, width)))
    hidden_one = source + low_back(multiply(mixed_self, self_out))
    normed_two = low(rms_scale(hidden_one, gain_cross))
    cross_q = low_back(low(multiply(normed_two, cross_query))).reshape(slot_count, HEADS, HEAD)
    cross_k = low_back(low(multiply(encoded, cross_key))).reshape(enc_count, HEADS, HEAD)
    cross_v = low_back(low(multiply(encoded, cross_value))).reshape(enc_count, HEADS, HEAD)

    def cross_block(block_index):
        first_row = (block_index * block_rows).astype(jnp.int32)
        block_query = lax.dynamic_slice_in_dim(cross_q, first_row, block_rows, 0)
        scores = low_back(jnp.einsum('qhd,khd->hqk', block_query, cross_k, precision=HIGHEST, preferred_element_type=jnp.float32))
        soft_low = low(softmax_rows(scores))
        mixed_rows = jnp.einsum('hqk,khd->qhd', soft_low, cross_v, precision=HIGHEST, preferred_element_type=jnp.float32)
        return mixed_rows.reshape(block_rows, width)
    mixed_cross = low_back(low(lax.map(jax.checkpoint(cross_block), block_ids).reshape(slot_count, width)))
    hidden_two = hidden_one + low_back(multiply(mixed_cross, cross_out))
    normed_three = low(rms_scale(hidden_two, gain_ff))
    gate_proj = low_back(multiply(normed_three, ff_gate))
    up_part = low_back(multiply(normed_three, ff_up))
    activated = low(jax.nn.gelu(gate_proj, approximate=True) * up_part)
    branch_ff = low_back(multiply(activated, ff_down))
    valid = (jnp.arange(slot_count, dtype=jnp.int32) < length).astype(jnp.float32)
    return valid[:, None] * (hidden_two + branch_ff)

def reference(tokens, encoded, lengths, cotangent, gain_self, gain_cross, gain_ff, bucket_table, self_query, self_key, self_value, self_out, cross_query, cross_key, cross_value, cross_out, ff_gate, ff_up, ff_down):
    params = tuple((weight.astype(jnp.float32) for weight in (gain_self, gain_cross, gain_ff, bucket_table, self_query, self_key, self_value, self_out, cross_query, cross_key, cross_value, cross_out, ff_gate, ff_up, ff_down)))

    def whole(source_all, encoded_all, weights):

        def one_sequence(sequence_item):
            return sequence_layer(sequence_item[0], sequence_item[1], sequence_item[2], weights)
        return lax.map(one_sequence, (source_all, encoded_all, lengths))
    result, pullback = jax.vjp(whole, tokens.astype(jnp.float32), encoded.astype(jnp.float32), params)
    grad_tokens, grad_encoded, grad_params = pullback(cotangent.astype(jnp.float32))
    return (result.astype(jnp.bfloat16), grad_tokens, grad_encoded, grad_params[0], grad_params[1], grad_params[2], grad_params[3], grad_params[4], grad_params[5], grad_params[6], grad_params[7], grad_params[8], grad_params[9], grad_params[10], grad_params[11], grad_params[12], grad_params[13], grad_params[14])
```

```python
import functools
import math

import jax
import jax.numpy as jnp
from jax import lax
from jax.experimental import pallas as pl
from jax.experimental.pallas import tpu as pltpu
from jax.sharding import PartitionSpec as P

HEADS = 12
HEAD = 64
BUCKETS = 32
MAX_DISTANCE = 128
EPSILON = 1e-06
NEGATIVE = -1e30
BLOCK = 256
PAIR = 2 * HEAD
MESH = pl.DeviceIdType.MESH


def thresholds():
    exact_limit = BUCKETS // 2
    return [
        int(math.ceil(exact_limit * (MAX_DISTANCE / exact_limit) ** (number / exact_limit)))
        for number in range(1, exact_limit)
    ]


def bucket_ids(key_count):
    exact_limit = BUCKETS // 2
    offsets = jnp.arange(key_count, dtype=jnp.int32)
    passed = jnp.zeros((key_count,), jnp.int32)
    for border in thresholds():
        passed = passed + (offsets >= border).astype(jnp.int32)
    return jnp.where(offsets < exact_limit, offsets, exact_limit + passed)


def rms_scale(values, gain):
    return values * lax.rsqrt(jnp.mean(values * values, axis=-1, keepdims=True) + EPSILON) * gain


def norm_back(values, gain, grad_normed):
    _, pullback = jax.vjp(rms_scale, values, gain)
    return pullback(grad_normed)


def product(left, right):
    return jnp.dot(left, right, preferred_element_type=jnp.float32)


def inner_rows(left, right):
    return lax.dot_general(
        left, right, (((0,), (0,)), ((), ())), preferred_element_type=jnp.float32
    )


def outer_rows(left, right):
    return lax.dot_general(
        left, right, (((1,), (1,)), ((), ())), preferred_element_type=jnp.float32
    )


def iota(shape, axis):
    return lax.broadcasted_iota(jnp.int32, shape, axis)


def head_rows(value, head):
    place = iota(value.shape, 0) // HEAD
    return jnp.where(place == head, value, jnp.zeros_like(value))


def head_cols(value, head):
    place = iota(value.shape, 1) // HEAD
    return jnp.where(place == head, value, jnp.zeros_like(value))


def skew(profile_row):
    wide = jnp.broadcast_to(profile_row, (BLOCK, BLOCK))
    return pltpu.roll(wide, 0, 1, stride=1, stride_axis=0)


def unskew(tile):
    rows = iota(tile.shape, 0)
    bit = 1
    while bit < BLOCK:
        tile = jnp.where((rows // bit) % 2 == 1, pltpu.roll(tile, BLOCK - bit, 1), tile)
        bit *= 2
    return tile


def self_forward_kernel(place_ref, profile_ref, q_ref, k_ref, v_ref, o_ref, ot_ref, log_ref, s_buf, vt_buf):
    place = place_ref[0]
    length = place_ref[1]
    qt = q_ref[...].T
    vt_buf[...] = v_ref[...].T
    later = iota((BLOCK, BLOCK), 1) >= iota((BLOCK, BLOCK), 0)
    key_rows = iota((BLOCK, BLOCK), 0)
    for head in range(2):
        qm = head_rows(qt, head)
        profile = profile_ref[0, head : head + 1, :]
        far = profile[:, BLOCK - 1 :]

        def tile_scores(block, bias):
            start = pl.multiple_of(block * BLOCK, BLOCK)
            scores = product(k_ref[pl.ds(start, BLOCK), :], qm) + bias
            scores = jnp.where(key_rows < length - start, scores, NEGATIVE)
            return start, scores

        def far_step(block, top):
            start, scores = tile_scores(block, far)
            s_buf[pl.ds(start, BLOCK), :] = scores
            return jnp.maximum(top, jnp.max(scores, axis=0, keepdims=True))

        top = lax.fori_loop(0, place - 1, far_step, jnp.full((1, BLOCK), NEGATIVE, jnp.float32))
        near = skew(profile)

        def near_step(block, top):
            start, scores = tile_scores(block, jnp.where(later, far, near))
            s_buf[pl.ds(start, BLOCK), :] = scores
            return jnp.maximum(top, jnp.max(scores, axis=0, keepdims=True))

        top = lax.fori_loop(jnp.maximum(place - 1, 0), place, near_step, top)
        start, scores = tile_scores(place, near)
        scores = jnp.where(later, scores, NEGATIVE)
        s_buf[pl.ds(start, BLOCK), :] = scores
        top = jnp.maximum(top, jnp.max(scores, axis=0, keepdims=True))

        def raise_step(block, total):
            start = pl.multiple_of(block * BLOCK, BLOCK)
            raised = jnp.exp(s_buf[pl.ds(start, BLOCK), :] - top)
            s_buf[pl.ds(start, BLOCK), :] = raised
            return total + jnp.sum(raised, axis=0, keepdims=True)

        total = lax.fori_loop(0, place + 1, raise_step, jnp.zeros((1, BLOCK), jnp.float32))
        share = 1.0 / total

        def mix_step(block, mixed):
            start = pl.multiple_of(block * BLOCK, BLOCK)
            soft = (s_buf[pl.ds(start, BLOCK), :] * share).astype(jnp.bfloat16)
            return mixed + product(
                vt_buf[head * HEAD : (head + 1) * HEAD, pl.ds(start, BLOCK)], soft
            )

        mixed = lax.fori_loop(0, place + 1, mix_step, jnp.zeros((HEAD, BLOCK), jnp.float32))
        ot_ref[head * HEAD : (head + 1) * HEAD, :] = mixed
        log_ref[0, head : head + 1, :] = top + jnp.log(total)
    o_ref[...] = ot_ref[...].T.astype(jnp.bfloat16)


def cross_forward_kernel(q_ref, k_ref, v_ref, o_ref, ot_ref, log_ref):
    qt = q_ref[...].T
    vt = v_ref[...].T
    for head in range(2):
        scores = product(k_ref[...], head_rows(qt, head))
        top = jnp.max(scores, axis=0, keepdims=True)
        raised = jnp.exp(scores - top)
        total = jnp.sum(raised, axis=0, keepdims=True)
        soft = (raised * (1.0 / total)).astype(jnp.bfloat16)
        ot_ref[head * HEAD : (head + 1) * HEAD, :] = product(
            vt[head * HEAD : (head + 1) * HEAD, :], soft
        )
        log_ref[0, head : head + 1, :] = top + jnp.log(total)
    o_ref[...] = ot_ref[...].T.astype(jnp.bfloat16)


def self_backward_kernel(
    place_ref, profile_ref, q_ref, k_ref, v_ref, g_ref, ot_ref, log_ref,
    dq_ref, dk_ref, dv_ref, near_ref, far_ref, tile_buf, kt_buf, dqt_buf, far_buf,
):
    place = place_ref[0]
    length = place_ref[1]
    q_value = q_ref[...]
    g_value = g_ref[...]
    qt = q_value.T
    gt = g_value.T
    kt_buf[...] = k_ref[...].T
    later = iota((BLOCK, BLOCK), 1) >= iota((BLOCK, BLOCK), 0)
    key_rows = iota((BLOCK, BLOCK), 0)
    both_q = jnp.concatenate([head_cols(q_value, 0), head_cols(q_value, 1)], axis=0)
    both_g = jnp.concatenate([head_cols(g_value, 0), head_cols(g_value, 1)], axis=0)
    weighted = gt.astype(jnp.float32) * ot_ref[...]
    sides = []
    for head in range(2):
        rows = slice(head * HEAD, (head + 1) * HEAD)
        profile = profile_ref[0, head : head + 1, :]
        delta = jnp.sum(weighted[rows, :], axis=0, keepdims=True)
        sides.append(
            (head_rows(qt, head), head_rows(gt, head), profile[:, BLOCK - 1 :], delta,
             log_ref[0, head : head + 1, :], rows)
        )
        tile_buf[head] = skew(profile)
    dqt_buf[...] = jnp.zeros_like(dqt_buf)
    far_buf[...] = jnp.zeros_like(far_buf)

    def one_block(block, kind):
        start = pl.multiple_of(block * BLOCK, BLOCK)
        k_block = k_ref[pl.ds(start, BLOCK), :]
        v_block = v_ref[pl.ds(start, BLOCK), :]
        softs, grads = [], []
        for head, (qm, gm, far, delta, log, rows) in enumerate(sides):
            if kind == 0:
                bias = tile_buf[head]
            elif kind == 1:
                bias = jnp.where(later, far, tile_buf[head])
            else:
                bias = far
            scores = product(k_block, qm) + bias
            allowed = key_rows < length - start
            if kind == 0:
                allowed = allowed & later
            soft = jnp.exp(jnp.where(allowed, scores, NEGATIVE) - log)
            grad_soft = product(v_block, gm)
            grad = (soft * (grad_soft - delta)).astype(jnp.bfloat16)
            softs.append(soft.astype(jnp.bfloat16))
            grads.append(grad)
            dqt_buf[rows, :] += product(kt_buf[rows, pl.ds(start, BLOCK)], grad)
            wide = grad.astype(jnp.float32)
            if kind == 2:
                far_buf[head : head + 1, :] += jnp.sum(wide, axis=0, keepdims=True)
            elif kind == 1:
                far_buf[head : head + 1, :] += jnp.sum(
                    jnp.where(later, wide, 0.0), axis=0, keepdims=True
                )
                near_ref[0, head : head + 1, :] += jnp.sum(
                    unskew(jnp.where(later, 0.0, wide)), axis=0, keepdims=True
                )
            else:
                near_ref[0, head : head + 1, :] = jnp.sum(unskew(wide), axis=0, keepdims=True)
        dv_ref[pl.ds(start, BLOCK), :] = product(jnp.concatenate(softs, axis=1), both_g).astype(
            jnp.bfloat16
        )
        dk_ref[pl.ds(start, BLOCK), :] = product(jnp.concatenate(grads, axis=1), both_q).astype(
            jnp.bfloat16
        )

    one_block(place, 0)

    @pl.when(place >= 1)
    def _():
        one_block(place - 1, 1)

    @pl.loop(0, place - 1)
    def _(block):
        one_block(block, 2)

    @pl.loop(place + 1, k_ref.shape[0] // BLOCK)
    def _(block):
        start = pl.multiple_of(block * BLOCK, BLOCK)
        dk_ref[pl.ds(start, BLOCK), :] = jnp.zeros((BLOCK, PAIR), jnp.bfloat16)
        dv_ref[pl.ds(start, BLOCK), :] = jnp.zeros((BLOCK, PAIR), jnp.bfloat16)

    dq_ref[...] = dqt_buf[...].T.astype(jnp.bfloat16)
    far_ref[0] = far_buf[...]


def cross_backward_kernel(q_ref, k_ref, v_ref, g_ref, ot_ref, log_ref, dq_ref, dk_ref, dv_ref, dqt_buf):
    q_value = q_ref[...]
    g_value = g_ref[...]
    qt = q_value.T
    gt = g_value.T
    kt = k_ref[...].T
    both_q = jnp.concatenate([head_cols(q_value, 0), head_cols(q_value, 1)], axis=0)
    both_g = jnp.concatenate([head_cols(g_value, 0), head_cols(g_value, 1)], axis=0)
    weighted = gt.astype(jnp.float32) * ot_ref[...]
    keys = k_ref.shape[0]
    sides = []
    for head in range(2):
        rows = slice(head * HEAD, (head + 1) * HEAD)
        delta = jnp.sum(weighted[rows, :], axis=0, keepdims=True)
        sides.append(
            (head_rows(qt, head), head_rows(gt, head), delta, log_ref[0, head : head + 1, :], rows)
        )
    dqt_buf[...] = jnp.zeros_like(dqt_buf)
    step = min(BLOCK, keys)
    for start in range(0, keys, step):
        k_block = k_ref[start : start + step, :]
        v_block = v_ref[start : start + step, :]
        softs, grads = [], []
        for qm, gm, delta, log, rows in sides:
            soft = jnp.exp(product(k_block, qm) - log)
            grad = (soft * (product(v_block, gm) - delta)).astype(jnp.bfloat16)
            softs.append(soft.astype(jnp.bfloat16))
            grads.append(grad)
            dqt_buf[rows, :] += product(kt[rows, start : start + step], grad)
        dv_ref[start : start + step, :] = product(jnp.concatenate(softs, axis=1), both_g).astype(
            jnp.bfloat16
        )
        dk_ref[start : start + step, :] = product(jnp.concatenate(grads, axis=1), both_q).astype(
            jnp.bfloat16
        )
    dq_ref[...] = dqt_buf[...].T.astype(jnp.bfloat16)


def pair_block(rows):
    return pl.BlockSpec((rows, PAIR), lambda pair: (0, pair))


def turned_block(rows):
    return pl.BlockSpec((PAIR, rows), lambda pair: (pair, 0))


def head_block(width):
    return pl.BlockSpec((1, 2, width), lambda pair: (pair, 0, 0))


SCALARS = pl.BlockSpec(memory_space=pltpu.SMEM)
PAIRS = HEADS // 2


def shaped(shape, dtype):
    return jax.ShapeDtypeStruct(shape, dtype)


def self_forward(place, profile, queries, keys, values):
    rows, width = queries.shape
    count = keys.shape[0]
    return pl.pallas_call(
        self_forward_kernel,
        grid=(PAIRS,),
        in_specs=[SCALARS, head_block(BLOCK), pair_block(rows), pair_block(count), pair_block(count)],
        out_specs=[pair_block(rows), turned_block(rows), head_block(rows)],
        out_shape=[
            shaped((rows, width), jnp.bfloat16),
            shaped((width, rows), jnp.float32),
            shaped((PAIRS, 2, rows), jnp.float32),
        ],
        scratch_shapes=[pltpu.VMEM((count, rows), jnp.float32), pltpu.VMEM((PAIR, count), jnp.bfloat16)],
        name="self_forward",
    )(place, profile, queries, keys, values)


def cross_forward(queries, keys, values):
    rows, width = queries.shape
    count = keys.shape[0]
    return pl.pallas_call(
        cross_forward_kernel,
        grid=(PAIRS,),
        in_specs=[pair_block(rows), pair_block(count), pair_block(count)],
        out_specs=[pair_block(rows), turned_block(rows), head_block(rows)],
        out_shape=[
            shaped((rows, width), jnp.bfloat16),
            shaped((width, rows), jnp.float32),
            shaped((PAIRS, 2, rows), jnp.float32),
        ],
        name="cross_forward",
    )(queries, keys, values)


def self_backward(place, profile, queries, keys, values, grad_mixed, mixed_turned, log_totals):
    rows, width = queries.shape
    count = keys.shape[0]
    return pl.pallas_call(
        self_backward_kernel,
        grid=(PAIRS,),
        in_specs=[
            SCALARS, head_block(BLOCK), pair_block(rows), pair_block(count), pair_block(count),
            pair_block(rows), turned_block(rows), head_block(rows),
        ],
        out_specs=[
            pair_block(rows), pair_block(count), pair_block(count), head_block(BLOCK), head_block(rows),
        ],
        out_shape=[
            shaped((rows, width), jnp.bfloat16),
            shaped((count, width), jnp.bfloat16),
            shaped((count, width), jnp.bfloat16),
            shaped((PAIRS, 2, BLOCK), jnp.float32),
            shaped((PAIRS, 2, rows), jnp.float32),
        ],
        scratch_shapes=[
            pltpu.VMEM((2, BLOCK, BLOCK), jnp.float32),
            pltpu.VMEM((PAIR, count), jnp.bfloat16),
            pltpu.VMEM((PAIR, rows), jnp.float32),
            pltpu.VMEM((2, rows), jnp.float32),
        ],
        name="self_backward",
    )(place, profile, queries, keys, values, grad_mixed, mixed_turned, log_totals)


def cross_backward(queries, keys, values, grad_mixed, mixed_turned, log_totals):
    rows, width = queries.shape
    count = keys.shape[0]
    return pl.pallas_call(
        cross_backward_kernel,
        grid=(PAIRS,),
        in_specs=[
            pair_block(rows), pair_block(count), pair_block(count),
            pair_block(rows), turned_block(rows), head_block(rows),
        ],
        out_specs=[pair_block(rows), pair_block(count), pair_block(count)],
        out_shape=[
            shaped((rows, width), jnp.bfloat16),
            shaped((count, width), jnp.bfloat16),
            shaped((count, width), jnp.bfloat16),
        ],
        scratch_shapes=[pltpu.VMEM((PAIR, rows), jnp.float32)],
        name="cross_backward",
    )(queries, keys, values, grad_mixed, mixed_turned, log_totals)


class Peers:
    def __init__(self, planes):
        self.seq = lax.axis_index("seq")
        fsdp = lax.axis_index("fsdp")
        self.planes = planes
        self.plane = fsdp // 2
        self.core = fsdp % 2
        self.fsdp = fsdp
        self.along_x = self.seq + 1 - 2 * (self.seq % 2)
        self.along_y = (self.seq + 2) % 4
        self.corner = (self.along_x + 2) % 4
        self.partner = (self.seq, fsdp + 1 - 2 * self.core)
        self.to_x = (self.along_x, fsdp)
        self.to_y = (self.along_y, fsdp)
        self.to_corner = (self.corner, fsdp)

    def ahead(self, steps):
        return (self.plane + steps) % self.planes

    def at_plane(self, plane):
        return (self.seq, 2 * plane + self.core)

    def everyone(self):
        return [self.partner, self.to_x, self.to_y, self.to_corner] + [
            self.at_plane(self.ahead(k)) for k in range(1, self.planes)
        ]

    def meet(self):
        barrier = pltpu.get_barrier_semaphore()
        others = self.everyone()
        for other in others:
            pl.semaphore_signal(barrier, inc=1, device_id=other, device_id_type=MESH)
        pl.semaphore_wait(barrier, len(others))


def remote(source, target, send_sem, recv_sem, device):
    return pltpu.make_async_remote_copy(
        src_ref=source, dst_ref=target, send_sem=send_sem, recv_sem=recv_sem,
        device_id=device, device_id_type=MESH,
    )


class Stack:
    def __init__(self, rows, cols):
        self.rows, self.cols = rows, cols

    def own(self, ref, quarter, first=0, count=None):
        return ref.at[quarter, pl.ds(first, count or self.rows), :]

    def part(self, ref, quarter, plane, core, first=0, count=None):
        return ref.at[quarter, plane, core, pl.ds(first, count or self.rows), :]

    def planes(self, ref, quarter, core):
        return ref.at[quarter, :, core]

    def whole(self, ref, plane, core):
        return ref.at[:, plane, core]


class Wide:
    def __init__(self, rows, cols):
        self.rows, self.cols = rows, cols

    def own(self, ref, quarter, first=0, count=None):
        return ref.at[pl.ds(first, count or self.rows), pl.ds(quarter * self.cols, self.cols)]

    def part(self, ref, quarter, plane, core, first=0, count=None):
        return ref.at[
            plane, core, pl.ds(first, count or self.rows), pl.ds(quarter * self.cols, self.cols)
        ]

    def planes(self, ref, quarter, core):
        return ref.at[:, core, :, pl.ds(quarter * self.cols, self.cols)]

    def whole(self, ref, plane, core):
        return ref.at[plane, core]


class Tall:
    def __init__(self, rows, cols):
        self.rows, self.cols = rows, cols

    def own(self, ref, quarter, first=0, count=None):
        return ref.at[pl.ds(quarter * self.rows + first, count or self.rows), :]

    def part(self, ref, quarter, plane, core, first=0, count=None):
        return ref.at[plane, core, pl.ds(quarter * self.rows + first, count or self.rows), :]

    def planes(self, ref, quarter, core):
        return ref.at[:, core, pl.ds(quarter * self.rows, self.rows), :]

    def whole(self, ref, plane, core):
        return ref.at[plane, core]


def gather_kernel(kinds, planes, *refs):
    groups = len(kinds)
    ins, refs = refs[:groups], refs[groups:]
    rows_in, refs = refs[:2], refs[2:]
    outs, refs = refs[:groups], refs[groups:]
    rows_out, refs = refs[:2], refs[2:]
    own_sem, z_send, z_recv, x_send, x_recv, y_send, y_recv, dx_send, dx_recv, dy_send, dy_recv = refs[:11]
    c_send, c_recv, r_own, r_send, r_recv = refs[11:]
    here = Peers(planes)
    me, plane, core = here.seq, here.plane, here.core
    here.meet()
    started, local = [], []

    def send(source, target, send_sem, recv_sem, device):
        copy = remote(source, target, send_sem, recv_sem, device)
        copy.start()
        started.append(copy)
        return copy

    for item in range(2):
        to = rows_out[item].at[me]
        send(rows_in[item], to, r_send.at[item, 0], r_recv.at[item, 0], here.to_x)
        send(rows_in[item], to, r_send.at[item, 1], r_recv.at[item, 1], here.to_y)
    for g, kind in enumerate(kinds):
        for k in range(1, planes):
            send(
                kind.own(ins[g], me), kind.part(outs[g], me, plane, core),
                z_send.at[g, k - 1], z_recv.at[g, k - 1], here.at_plane(here.ahead(k)),
            )
    for g, kind in enumerate(kinds):
        send(ins[g], kind.whole(outs[g], plane, core), c_send.at[g, 0], c_recv.at[g, 0], here.partner)
    for item in range(2):
        copy = pltpu.make_async_copy(rows_in[item], rows_out[item].at[me], r_own.at[item])
        copy.start()
        local.append(copy)
    for g, kind in enumerate(kinds):
        copy = pltpu.make_async_copy(ins[g], kind.whole(outs[g], plane, core), own_sem.at[g])
        copy.start()
        local.append(copy)

    def arrived(target, recv_sem):
        pltpu.make_async_copy(target, target, recv_sem).wait()

    half_rows = [ref.shape[0] // 2 for ref in rows_in]
    for item in range(2):
        half = half_rows[item]
        first = rows_out[item].at[here.along_x, pl.ds(0, half), :]
        second = rows_out[item].at[here.along_y, pl.ds(half, half), :]
        arrived(rows_out[item].at[here.along_x], r_recv.at[item, 0])
        send(first, first, r_send.at[item, 2], r_recv.at[item, 2], here.to_y)
        arrived(rows_out[item].at[here.along_y], r_recv.at[item, 1])
        send(second, second, r_send.at[item, 3], r_recv.at[item, 3], here.to_x)

    def from_plane(g, k):
        kind = kinds[g]
        behind = here.ahead(planes - k)
        chunk = kind.part(outs[g], me, behind, core)
        arrived(chunk, z_recv.at[g, k - 1])
        send(chunk, chunk, x_send.at[g, k - 1], x_recv.at[g, k - 1], here.to_x)
        send(chunk, chunk, y_send.at[g, k - 1], y_recv.at[g, k - 1], here.to_y)

    def from_sides(g, k):
        kind = kinds[g]
        behind = here.ahead(planes - k)
        half = kind.rows // 2
        arrived(kind.part(outs[g], here.along_x, behind, core), x_recv.at[g, k - 1])
        first = kind.part(outs[g], here.along_x, behind, core, 0, half)
        send(first, first, dy_send.at[g, k - 1], dy_recv.at[g, k - 1], here.to_y)
        arrived(kind.part(outs[g], here.along_y, behind, core), y_recv.at[g, k - 1])
        second = kind.part(outs[g], here.along_y, behind, core, half, half)
        send(second, second, dx_send.at[g, k - 1], dx_recv.at[g, k - 1], here.to_x)

    def from_corner(g, k):
        kind = kinds[g]
        behind = here.ahead(planes - k)
        half = kind.rows // 2
        arrived(kind.part(outs[g], here.corner, behind, core, 0, half), dy_recv.at[g, k - 1])
        arrived(kind.part(outs[g], here.corner, behind, core, half, half), dx_recv.at[g, k - 1])
        whole = kind.whole(outs[g], behind, core)
        send(whole, whole, c_send.at[g, k], c_recv.at[g, k], here.partner)

    for step in range(groups + 2):
        for k in range(1, planes):
            if step < groups:
                from_plane(step, k)
            if 0 <= step - 1 < groups:
                from_sides(step - 1, k)
            if 0 <= step - 2 < groups:
                from_corner(step - 2, k)
    for item in range(2):
        half = half_rows[item]
        arrived(rows_out[item].at[here.corner, pl.ds(0, half), :], r_recv.at[item, 2])
        arrived(rows_out[item].at[here.corner, pl.ds(half, half), :], r_recv.at[item, 3])
    for g, kind in enumerate(kinds):
        arrived(kind.whole(outs[g], plane, 1 - core), c_recv.at[g, 0])
        for k in range(1, planes):
            arrived(kind.whole(outs[g], here.ahead(planes - k), 1 - core), c_recv.at[g, k])
    for copy in started:
        copy.wait_send()
    for copy in local:
        copy.wait()


def full_shapes(kinds, planes, cores=2):
    shapes = []
    for kind in kinds:
        if isinstance(kind, Stack):
            shapes.append((4, planes, cores, kind.rows, kind.cols))
        elif isinstance(kind, Wide):
            shapes.append((planes, cores, kind.rows, 4 * kind.cols))
        else:
            shapes.append((planes, cores, 4 * kind.rows, kind.cols))
    return shapes


ANYWHERE = pl.BlockSpec(memory_space=pl.ANY)
DMA = pltpu.SemaphoreType.DMA


def make_kinds(shards):
    square, wide, down = shards[0], shards[8], shards[10]
    stack = Stack(*square.shape)
    band = Wide(wide.shape[0], wide.shape[1] // 4)
    tall = Tall(down.shape[0] // 4, down.shape[1])
    return [stack, stack, band, band, tall]


def kernels_fit(shards):
    kinds = make_kinds(shards)
    return (
        lax.axis_size("seq") == 4
        and lax.axis_size("fsdp") == 8
        and all(kind.rows % 32 == 0 and kind.cols % 128 == 0 for kind in kinds)
    )


def gather_plain(shards, tokens, encoded):
    full = [lax.all_gather(shard, "fsdp", axis=0, tiled=True) for shard in shards]
    return (
        full,
        lax.all_gather(tokens, "seq", axis=0, tiled=True),
        lax.all_gather(encoded, "seq", axis=0, tiled=True),
    )


def gather_all(shards, tokens, encoded):
    if not kernels_fit(shards):
        return gather_plain(shards, tokens, encoded)
    kinds = make_kinds(shards)
    planes = lax.axis_size("fsdp") // 2
    groups = len(kinds)
    ins = [jnp.stack(shards[:4]), jnp.stack(shards[4:8]), *shards[8:], tokens, encoded]
    shapes = full_shapes(kinds, planes) + [(4,) + tokens.shape, (4,) + encoded.shape]
    steps = planes - 1
    outs = pl.pallas_call(
        functools.partial(gather_kernel, kinds, planes),
        in_specs=[ANYWHERE] * len(ins),
        out_specs=[ANYWHERE] * len(shapes),
        out_shape=[shaped(shape, jnp.bfloat16) for shape in shapes],
        scratch_shapes=[DMA((groups,))]
        + [DMA((groups, steps))] * 10
        + [DMA((groups, steps + 1))] * 2
        + [DMA((2,)), DMA((2, 4)), DMA((2, 4))],
        compiler_params=pltpu.CompilerParams(collective_id=0, has_side_effects=True),
        name="gather_all",
    )(*ins)
    one, two, gate, up, down, tokens_all, encoded_all = outs
    width = shards[0].shape[1]
    one = one.reshape(4, -1, width)
    two = two.reshape(4, -1, width)
    full = [one[m] for m in range(4)] + [two[m] for m in range(4)]
    full += [gate.reshape(-1, gate.shape[-1]), up.reshape(-1, up.shape[-1]), down.reshape(-1, width)]
    return full, tokens_all.reshape(-1, width), encoded_all.reshape(-1, width)


def add_low(target, *terms):
    total = target[...].astype(jnp.float32)
    for term in terms:
        total = total + term[...].astype(jnp.float32)
    target[...] = total.astype(jnp.bfloat16)


def reduce_kernel(kinds, planes, *refs):
    groups = len(kinds)
    parts, refs = refs[:groups], refs[groups:]
    row_parts, refs = refs[:2], refs[2:]
    small_ref, refs = refs[0], refs[1:]
    outs, refs = refs[:groups], refs[groups:]
    row_outs, refs = refs[:2], refs[2:]
    small_out, refs = refs[0], refs[1:]
    mine, refs = refs[:groups], refs[groups:]
    other, refs = refs[:groups], refs[groups:]
    side_x, refs = refs[:groups], refs[groups:]
    side_y, refs = refs[:groups], refs[groups:]
    last, refs = refs[:groups], refs[groups:]
    from_z, refs = refs[:groups], refs[groups:]
    final, refs = refs[:groups], refs[groups:]
    row_got, refs = refs[:2], refs[2:]
    small_core, small_seq, small_plane = refs[:3]
    (l_sem, c_send, c_recv, a_send, a_recv, b_send, b_recv, z_send, z_recv, g_send, g_recv,
     rl_sem, r_send, r_recv, s_send, s_recv) = refs[3:]
    here = Peers(planes)
    me, plane, core = here.seq, here.plane, here.core
    lower = planes // 2
    here.meet()
    started = []

    def send(source, target, send_sem, recv_sem, device):
        copy = remote(source, target, send_sem, recv_sem, device)
        copy.start()
        started.append(copy)

    def arrived(target, recv_sem):
        pltpu.make_async_copy(target, target, recv_sem).wait()

    for g, kind in enumerate(kinds):
        for q in range(4):
            send(
                kind.planes(parts[g], q, 1 - core), other[g].at[q],
                c_send.at[g, q], c_recv.at[g, q], here.partner,
            )
            pltpu.make_async_copy(
                kind.planes(parts[g], q, core), mine[g].at[q], l_sem.at[g, q]
            ).start()
    send(small_ref, small_core.at[1], s_send.at[0], s_recv.at[0], here.partner)
    for item in range(2):
        for k, (quarter, device) in enumerate(
            ((here.along_x, here.to_x), (here.along_y, here.to_y), (here.corner, here.to_corner))
        ):
            send(
                row_parts[item].at[quarter], row_got[item].at[k],
                r_send.at[item, k], r_recv.at[item, k], device,
            )
        pltpu.make_async_copy(row_parts[item].at[me], row_got[item].at[3], rl_sem.at[item]).start()

    def pair_sum(g):
        for q in range(4):
            arrived(other[g].at[q], c_recv.at[g, q])
            pltpu.make_async_copy(
                kinds[g].planes(parts[g], q, core), mine[g].at[q], l_sem.at[g, q]
            ).wait()

        @pl.loop(0, 4)
        def _(q):
            @pl.loop(0, planes)
            def _(z):
                add_low(mine[g].at[q, z], other[g].at[q, z])

        low, high = pl.ds(0, lower), pl.ds(lower, planes - lower)
        for n, quarter in enumerate((here.along_x, here.corner)):
            send(mine[g].at[quarter, low], side_x[g].at[n], a_send.at[g, n], a_recv.at[g, n], here.to_x)
        for n, quarter in enumerate((here.along_y, here.corner)):
            send(
                mine[g].at[quarter, high], side_y[g].at[n],
                a_send.at[g, 2 + n], a_recv.at[g, 2 + n], here.to_y,
            )

    def first_side(g):
        for n in range(2):
            arrived(side_x[g].at[n], a_recv.at[g, n])
            arrived(side_y[g].at[n], a_recv.at[g, 2 + n])

        @pl.loop(0, lower)
        def _(z):
            add_low(mine[g].at[here.along_y, z], side_x[g].at[1, z])
            add_low(mine[g].at[here.along_x, lower + z], side_y[g].at[1, z])

        send(
            mine[g].at[here.along_y, pl.ds(0, lower)], last[g].at[0],
            b_send.at[g, 0], b_recv.at[g, 0], here.to_y,
        )
        send(
            mine[g].at[here.along_x, pl.ds(lower, lower)], last[g].at[1],
            b_send.at[g, 1], b_recv.at[g, 1], here.to_x,
        )

    def second_side(g):
        arrived(last[g].at[0], b_recv.at[g, 0])
        arrived(last[g].at[1], b_recv.at[g, 1])

        @pl.loop(0, lower)
        def _(z):
            add_low(mine[g].at[me, z], side_x[g].at[0, z], last[g].at[0, z])
            add_low(mine[g].at[me, lower + z], side_y[g].at[0, z], last[g].at[1, z])

        for k in range(1, planes):
            to = here.ahead(k)
            send(
                mine[g].at[me, to], from_z[g].at[k - 1],
                z_send.at[g, k - 1], z_recv.at[g, k - 1], here.at_plane(to),
            )

    def along_planes(g):
        for k in range(1, planes):
            arrived(from_z[g].at[k - 1], z_recv.at[g, k - 1])
        total = mine[g][me, plane].astype(jnp.float32)
        for k in range(1, planes):
            total = total + from_z[g][k - 1].astype(jnp.float32)
        final[g][me] = total.astype(jnp.bfloat16)
        chunk = final[g].at[me]
        send(chunk, chunk, g_send.at[g, 0], g_recv.at[g, 0], here.to_x)
        send(chunk, chunk, g_send.at[g, 1], g_recv.at[g, 1], here.to_y)

    def spread(g):
        half = kinds[g].rows // 2
        arrived(final[g].at[here.along_x], g_recv.at[g, 0])
        first = final[g].at[here.along_x, pl.ds(0, half), :]
        send(first, first, g_send.at[g, 2], g_recv.at[g, 2], here.to_y)
        arrived(final[g].at[here.along_y], g_recv.at[g, 1])
        second = final[g].at[here.along_y, pl.ds(half, half), :]
        send(second, second, g_send.at[g, 3], g_recv.at[g, 3], here.to_x)

    def finish(g):
        kind = kinds[g]
        half = kind.rows // 2
        arrived(final[g].at[here.corner, pl.ds(0, half), :], g_recv.at[g, 2])
        arrived(final[g].at[here.corner, pl.ds(half, half), :], g_recv.at[g, 3])
        for q in range(4):
            if isinstance(kind, Stack):
                outs[g][q] = final[g][q]
            elif isinstance(kind, Wide):
                outs[g][:, q * kind.cols : (q + 1) * kind.cols] = final[g][q]
            else:
                outs[g][q * kind.rows : (q + 1) * kind.rows, :] = final[g][q]

    def rows_sum(item):
        for k in range(3):
            arrived(row_got[item].at[k], r_recv.at[item, k])
        pltpu.make_async_copy(row_parts[item].at[me], row_got[item].at[3], rl_sem.at[item]).wait()
        step = 64

        @pl.loop(0, row_got[item].shape[1] // step)
        def _(n):
            rows = pl.ds(pl.multiple_of(n * step, step), step)
            total = row_got[item][3, rows, :].astype(jnp.float32)
            for k in range(3):
                total = total + row_got[item][k, rows, :].astype(jnp.float32)
            row_outs[item][rows, :] = total

    def small_pair():
        arrived(small_core.at[1], s_recv.at[0])
        small_seq[me] = small_ref[...] + small_core[1]
        for k, device in enumerate((here.to_x, here.to_y, here.to_corner)):
            send(small_seq.at[me], small_seq.at[me], s_send.at[1 + k], s_recv.at[1 + k], device)

    def small_square():
        for k, quarter in enumerate((here.along_x, here.along_y, here.corner)):
            arrived(small_seq.at[quarter], s_recv.at[1 + k])
        small_plane[plane] = (small_seq[0] + small_seq[1]) + (small_seq[2] + small_seq[3])
        for k in range(1, planes):
            send(
                small_plane.at[plane], small_plane.at[plane],
                s_send.at[3 + k], s_recv.at[3 + k], here.at_plane(here.ahead(k)),
            )

    def small_end():
        for k in range(1, planes):
            arrived(small_plane.at[here.ahead(planes - k)], s_recv.at[3 + k])
        total = small_plane[0]
        for k in range(1, planes):
            total = total + small_plane[k]
        small_out[...] = total

    small_stages = [small_pair, small_square, small_end]
    stages = [pair_sum, first_side, second_side, along_planes, spread, finish]
    for step in range(groups + len(stages) - 1):
        for depth, stage in enumerate(stages):
            if 0 <= step - depth < groups:
                stage(step - depth)
        if step < 3:
            small_stages[step]()
        if 1 <= step < 3:
            rows_sum(step - 1)
    for copy in started:
        copy.wait_send()


def reduce_plain(grads, token_part, enc_part, small):
    def sums(value):
        return lax.psum_scatter(value.astype(jnp.float32), "seq", scatter_dimension=0, tiled=True)

    reduced = [
        lax.psum(
            lax.psum_scatter(grad.astype(jnp.float32), "fsdp", scatter_dimension=0, tiled=True), "seq"
        )
        for grad in grads
    ]
    return reduced, sums(token_part), sums(enc_part), lax.psum(small, ("seq", "fsdp"))


def reduce_all(shards, grads, token_part, enc_part, small):
    if not kernels_fit(shards):
        return reduce_plain(grads, token_part, enc_part, small)
    kinds = make_kinds(shards)
    planes = lax.axis_size("fsdp") // 2
    lower = planes // 2
    groups = len(kinds)
    width = token_part.shape[1]
    order = [2, 3, 4, 1, 0]
    kinds = [kinds[n] for n in order]
    shapes = full_shapes(kinds, planes)
    whole = [jnp.stack(grads[:4]), jnp.stack(grads[4:8]), *grads[8:]]
    parts = [whole[n].reshape(shape) for n, shape in zip(order, shapes)]
    rows = [token_part.reshape(4, -1, width), enc_part.reshape(4, -1, width)]
    own = [stack if stack.ndim == 2 else stack for stack in (jnp.stack(shards[:4]), jnp.stack(shards[4:8]), *shards[8:])]
    low = jnp.bfloat16
    in_vmem = pl.BlockSpec(memory_space=pltpu.VMEM)

    def chunks(*lead):
        return [pltpu.VMEM(lead + (kind.rows, kind.cols), low) for kind in kinds]

    outs = pl.pallas_call(
        functools.partial(reduce_kernel, kinds, planes),
        in_specs=[ANYWHERE] * (groups + 2) + [in_vmem],
        out_specs=[in_vmem] * (groups + 3),
        out_shape=[shaped(own[n].shape, low) for n in order]
        + [shaped(row.shape[1:], jnp.float32) for row in rows]
        + [shaped(small.shape, jnp.float32)],
        scratch_shapes=chunks(4, planes)
        + chunks(4, planes)
        + chunks(2, lower)
        + chunks(2, lower)
        + chunks(2, lower)
        + chunks(planes - 1)
        + chunks(4)
        + [pltpu.VMEM((4,) + row.shape[1:], low) for row in rows]
        + [
            pltpu.VMEM((2,) + small.shape, jnp.float32),
            pltpu.VMEM((4,) + small.shape, jnp.float32),
            pltpu.VMEM((planes,) + small.shape, jnp.float32),
        ]
        + [DMA((groups, 4))] * 5
        + [DMA((groups, 2))] * 2
        + [DMA((groups, planes - 1))] * 2
        + [DMA((groups, 4))] * 2
        + [DMA((2,))]
        + [DMA((2, 3))] * 2
        + [DMA((3 + planes,))] * 2,
        compiler_params=pltpu.CompilerParams(
            collective_id=1, has_side_effects=True, vmem_limit_bytes=62 * 1024 * 1024
        ),
        name="reduce_all",
    )(*parts, *rows, small)
    got = dict(zip(order, outs[:groups]))
    reduced = [got[0][m] for m in range(4)] + [got[1][m] for m in range(4)] + [got[2], got[3], got[4]]
    return [value.astype(jnp.float32) for value in reduced], outs[groups], outs[groups + 1], outs[groups + 2]


def local(
    tokens, encoded, lengths, cotangent, gain_self, gain_cross, gain_ff, bucket_table,
    self_query, self_key, self_value, self_out, cross_query, cross_key, cross_value, cross_out,
    ff_gate, ff_up, ff_down,
):
    rows_here = tokens.shape[1]
    seq_place = lax.axis_index("seq")
    length = lengths[0]
    bf16, f32 = jnp.bfloat16, jnp.float32
    gain_one = gain_self.astype(f32)
    gain_two = gain_cross.astype(f32)
    gain_three = gain_ff.astype(f32)
    shards = (
        self_query, self_key, self_value, self_out, cross_query, cross_key, cross_value, cross_out,
        ff_gate, ff_up, ff_down,
    )
    weights, tokens_all, enc_all = gather_all(shards, tokens[0], encoded[0])
    (w_query, w_key, w_value, w_sout, w_cquery, w_ckey, w_cvalue, w_cout, w_gate, w_up, w_down) = weights
    one_hot = (
        bucket_ids(BLOCK)[:, None] == jnp.arange(BUCKETS, dtype=jnp.int32)[None, :]
    ).astype(bf16)
    profile = inner_rows(bucket_table, one_hot.T).reshape(PAIRS, 2, BLOCK)
    place = jnp.stack([seq_place.astype(jnp.int32), length])

    source = tokens[0].astype(f32)
    normed_all = rms_scale(tokens_all.astype(f32), gain_one).astype(bf16)
    normed_one = rms_scale(source, gain_one).astype(bf16)
    queries = product(normed_one, w_query).astype(bf16)
    keys = product(normed_all, w_key).astype(bf16)
    values = product(normed_all, w_value).astype(bf16)
    mixed_self, mixed_self_turned, log_self = self_forward(place, profile, queries, keys, values)
    hidden_one = source + product(mixed_self, w_sout)
    normed_two = rms_scale(hidden_one, gain_two).astype(bf16)
    cqueries = product(normed_two, w_cquery).astype(bf16)
    ckeys = product(enc_all, w_ckey).astype(bf16)
    cvalues = product(enc_all, w_cvalue).astype(bf16)
    mixed_cross, mixed_cross_turned, log_cross = cross_forward(cqueries, ckeys, cvalues)
    hidden_two = hidden_one + product(mixed_cross, w_cout)
    normed_three = rms_scale(hidden_two, gain_three).astype(bf16)
    gate = product(normed_three, w_gate)
    up = product(normed_three, w_up)

    def gated(gate_rows, up_rows):
        return jax.nn.gelu(gate_rows, approximate=True) * up_rows

    activated_f, pull_gate = jax.vjp(gated, gate, up)
    activated = activated_f.astype(bf16)
    slot_ids = seq_place * rows_here + jnp.arange(rows_here, dtype=jnp.int32)
    valid = (slot_ids < length).astype(f32)[:, None]
    result = (valid * (hidden_two + product(activated, w_down))).astype(bf16)

    grad_result = valid * cotangent[0].astype(f32)
    branch_ff = grad_result.astype(bf16)
    grad_gate_f, grad_up_f = pull_gate(outer_rows(branch_ff, w_down))
    grad_gate = grad_gate_f.astype(bf16)
    grad_up = grad_up_f.astype(bf16)
    g_down = inner_rows(activated, branch_ff).astype(bf16)
    g_gate = inner_rows(normed_three, grad_gate).astype(bf16)
    g_up = inner_rows(normed_three, grad_up).astype(bf16)
    grad_three, grad_gain_three = norm_back(
        hidden_two, gain_three, outer_rows(grad_gate, w_gate) + outer_rows(grad_up, w_up)
    )
    grad_two = grad_result + grad_three
    branch_cross = grad_two.astype(bf16)
    g_cout = inner_rows(mixed_cross, branch_cross).astype(bf16)
    grad_mixed_cross = outer_rows(branch_cross, w_cout).astype(bf16)
    grad_cq, grad_ck, grad_cv = cross_backward(
        cqueries, ckeys, cvalues, grad_mixed_cross, mixed_cross_turned, log_cross
    )
    g_cquery = inner_rows(normed_two, grad_cq).astype(bf16)
    g_ckey = inner_rows(enc_all, grad_ck).astype(bf16)
    g_cvalue = inner_rows(enc_all, grad_cv).astype(bf16)
    enc_part = (outer_rows(grad_ck, w_ckey) + outer_rows(grad_cv, w_cvalue)).astype(bf16)
    grad_two_back, grad_gain_two = norm_back(hidden_one, gain_two, outer_rows(grad_cq, w_cquery))
    grad_one = grad_two + grad_two_back
    branch_self = grad_one.astype(bf16)
    g_sout = inner_rows(mixed_self, branch_self).astype(bf16)
    grad_mixed_self = outer_rows(branch_self, w_sout).astype(bf16)
    grad_q, grad_k, grad_v, near_part, far_part = self_backward(
        place, profile, queries, keys, values, grad_mixed_self, mixed_self_turned, log_self
    )
    g_query = inner_rows(normed_one, grad_q).astype(bf16)
    g_key = inner_rows(normed_all, grad_k).astype(bf16)
    g_value = inner_rows(normed_all, grad_v).astype(bf16)
    token_part = (outer_rows(grad_k, w_key) + outer_rows(grad_v, w_value)).astype(bf16)
    query_part = outer_rows(grad_q, w_query)

    near_rows = near_part.reshape(HEADS, BLOCK)
    far_rows = jnp.sum(far_part, axis=-1).reshape(HEADS)
    table_part = lax.dot_general(
        one_hot.astype(f32), near_rows, (((0,), (1,)), ((), ())),
        precision=lax.Precision.HIGHEST, preferred_element_type=f32,
    )
    table_part = table_part.at[BUCKETS - 1].add(far_rows)

    hat_all = rms_scale(tokens_all.astype(f32), jnp.ones_like(gain_one))
    hat_one = rms_scale(source, jnp.ones_like(gain_one))
    grad_gain_one = jnp.sum(token_part.astype(f32) * hat_all, axis=0) + jnp.sum(
        query_part * hat_one, axis=0
    )
    table_row = jnp.zeros((gain_one.shape[0],), f32).at[: BUCKETS * HEADS].set(table_part.reshape(-1))
    small = jnp.stack([grad_gain_one, grad_gain_two, grad_gain_three, table_row] + [jnp.zeros_like(gain_one)] * 4)
    reduced, token_sum, enc_sum, small = reduce_all(
        shards,
        (g_query, g_key, g_value, g_sout, g_cquery, g_ckey, g_cvalue, g_cout, g_gate, g_up, g_down),
        token_part, enc_part, small,
    )
    grad_zero, _ = norm_back(source, gain_one, query_part + token_sum)
    grad_tokens = grad_one + grad_zero
    table_sum = small[3, : BUCKETS * HEADS].reshape(BUCKETS, HEADS)
    small = (small[0], small[1], small[2], table_sum)
    return (result[None], grad_tokens[None], enc_sum[None], *small, *reduced)


def solution(mesh):
    rows3 = P("fsdp", "seq", None)
    rows2 = P("fsdp", None)
    return jax.shard_map(
        local,
        mesh=mesh,
        in_specs=(rows3, rows3, P("fsdp"), rows3, P(), P(), P(), P(), *([rows2] * 11)),
        out_specs=(rows3, rows3, rows3, P(), P(), P(), P(), *([rows2] * 11)),
        check_vma=False,
    )
```

```python
import functools
import math

import jax
import jax.numpy as jnp
from jax import lax
from jax.experimental import pallas as pl
from jax.experimental.pallas import tpu as pltpu
from jax.sharding import PartitionSpec as P

HEADS = 12
HEAD = 64
BUCKETS = 32
MAX_DISTANCE = 128
EPSILON = 1e-06
NEGATIVE = -1e30
BLOCK = 256
PAIR = 2 * HEAD
MESH = pl.DeviceIdType.MESH


def thresholds():
    exact_limit = BUCKETS // 2
    return [
        int(math.ceil(exact_limit * (MAX_DISTANCE / exact_limit) ** (number / exact_limit)))
        for number in range(1, exact_limit)
    ]


def bucket_ids(key_count):
    exact_limit = BUCKETS // 2
    offsets = jnp.arange(key_count, dtype=jnp.int32)
    passed = jnp.zeros((key_count,), jnp.int32)
    for border in thresholds():
        passed = passed + (offsets >= border).astype(jnp.int32)
    return jnp.where(offsets < exact_limit, offsets, exact_limit + passed)


def rms_scale(values, gain):
    return values * lax.rsqrt(jnp.mean(values * values, axis=-1, keepdims=True) + EPSILON) * gain


def norm_back(values, gain, grad_normed):
    _, pullback = jax.vjp(rms_scale, values, gain)
    return pullback(grad_normed)


def product(left, right):
    return jnp.dot(left, right, preferred_element_type=jnp.float32)


def inner_rows(left, right):
    return lax.dot_general(
        left, right, (((0,), (0,)), ((), ())), preferred_element_type=jnp.float32
    )


def outer_rows(left, right):
    return lax.dot_general(
        left, right, (((1,), (1,)), ((), ())), preferred_element_type=jnp.float32
    )


def iota(shape, axis):
    return lax.broadcasted_iota(jnp.int32, shape, axis)


def head_rows(value, head):
    place = iota(value.shape, 0) // HEAD
    return jnp.where(place == head, value, jnp.zeros_like(value))


def head_cols(value, head):
    place = iota(value.shape, 1) // HEAD
    return jnp.where(place == head, value, jnp.zeros_like(value))


def skew(profile_row):
    wide = jnp.broadcast_to(profile_row, (BLOCK, BLOCK))
    return pltpu.roll(wide, 0, 1, stride=1, stride_axis=0)


def unskew(tile):
    rows = iota(tile.shape, 0)
    bit = 1
    while bit < BLOCK:
        tile = jnp.where((rows // bit) % 2 == 1, pltpu.roll(tile, BLOCK - bit, 1), tile)
        bit *= 2
    return tile


def fill_pads(pads, length):
    rows = pads.shape[1]
    lanes = iota((BLOCK, PAIR), 1)

    @pl.loop(0, rows // BLOCK)
    def _(n):
        start = pl.multiple_of(n * BLOCK, BLOCK)
        beyond = iota((BLOCK, PAIR), 0) >= length - start
        for head in range(2):
            first = (1 - head) * HEAD
            ones = jnp.where((lanes > first) & (lanes <= first + 3), 1.0, 0.0)
            pads[head, pl.ds(start, BLOCK), :] = jnp.where(
                (lanes == first) & beyond, NEGATIVE, ones
            ).astype(jnp.bfloat16)


def padded(value, pads, head, start):
    own = iota(value.shape, 1) // HEAD == head
    return jnp.where(own, value, pads[head, start : start + value.shape[0], :])


def split_low(value):
    first = value.astype(jnp.bfloat16).astype(jnp.float32)
    rest = value - first
    second = rest.astype(jnp.bfloat16).astype(jnp.float32)
    return first, second, rest - second


def with_terms(turned, head, mask_term, terms):
    place = iota(turned.shape, 0)
    first = (1 - head) * HEAD
    value = jnp.where(place // HEAD == head, turned.astype(jnp.float32), 0.0)
    value = jnp.where(place == first, mask_term, value)
    for n, term in enumerate(terms):
        value = jnp.where(place == first + 1 + n, term, value)
    return value.astype(jnp.bfloat16)


HIDDEN, DIAGONAL, NEAR, FAR = range(4)


def fill_fixed_bias(bias):
    for head in range(2):
        bias[head, HIDDEN] = jnp.full((BLOCK, BLOCK), NEGATIVE, jnp.float32)
        bias[head, FAR] = jnp.zeros((BLOCK, BLOCK), jnp.float32)


def fill_near_bias(bias, profile_ref):
    later = iota((BLOCK, BLOCK), 1) >= iota((BLOCK, BLOCK), 0)
    for head in range(2):
        profile = profile_ref[head : head + 1, :]
        near = skew(profile - profile[:, BLOCK - 1 :])
        bias[head, DIAGONAL] = jnp.where(later, near, NEGATIVE)
        bias[head, NEAR] = jnp.where(later, 0.0, near)


def bias_kind(place, block):
    return jnp.clip(place - block, -1, 2) + 1


def self_forward_pair(place, profile_ref, q_ref, k_ref, v_ref, o_ref, ot_ref, log_ref, pads, bias, s_buf, vt_buf):
    qt = q_ref[...].T
    vt_buf[...] = v_ref[...].T
    fill_near_bias(bias, profile_ref)
    blocks = k_ref.shape[0] // BLOCK
    tops = []
    for head in range(2):
        far = profile_ref[head : head + 1, BLOCK - 1 :]
        queries = with_terms(qt, head, 1.0, (far,))
        top = None
        for block in range(blocks):
            start = block * BLOCK
            keys = padded(k_ref[start : start + BLOCK, :], pads, head, start)
            scores = product(keys, queries) + bias[head, bias_kind(place, block)]
            s_buf[head, start : start + BLOCK, :] = scores
            most = jnp.max(scores, axis=0, keepdims=True)
            top = most if top is None else jnp.maximum(top, most)
        tops.append(top)
    totals = []
    for head in range(2):
        total = None
        for block in range(blocks):
            part = slice(block * BLOCK, (block + 1) * BLOCK)
            raised = jnp.exp(s_buf[head, part, :] - tops[head])
            s_buf[head, part, :] = raised
            amount = jnp.sum(raised, axis=0, keepdims=True)
            total = amount if total is None else total + amount
        totals.append(total)
    for head in range(2):
        rows = slice(head * HEAD, (head + 1) * HEAD)
        scale, mixed = 1.0 / totals[head], None
        for block in range(blocks):
            part = slice(block * BLOCK, (block + 1) * BLOCK)
            soft = (s_buf[head, part, :] * scale).astype(jnp.bfloat16)
            share = product(vt_buf[rows, part], soft)
            mixed = share if mixed is None else mixed + share
        ot_ref[rows, :] = mixed
        log_ref[head : head + 1, :] = tops[head] + jnp.log(totals[head])
    o_ref[...] = ot_ref[...].T.astype(jnp.bfloat16)


def self_forward_kernel(place_ref, profile_ref, q_ref, k_ref, v_ref, o_ref, ot_ref, log_ref, pads, bias, s_buf, vt_buf):
    @pl.when(pl.program_id(0) == 0)
    def _():
        fill_pads(pads, place_ref[1])
        fill_fixed_bias(bias)

    self_forward_pair(
        place_ref[0], profile_ref.at[0], q_ref, k_ref, v_ref, o_ref, ot_ref, log_ref.at[0],
        pads, bias, s_buf, vt_buf,
    )


def cross_forward_pair(q_ref, k_ref, v_ref, o_ref, ot_ref, log_ref):
    qt = q_ref[...].T
    vt = v_ref[...].T
    all_scores = [product(k_ref[...], head_rows(qt, head)) for head in range(2)]
    for head, scores in enumerate(all_scores):
        top = jnp.max(scores, axis=0, keepdims=True)
        raised = jnp.exp(scores - top)
        total = jnp.sum(raised, axis=0, keepdims=True)
        soft = (raised * (1.0 / total)).astype(jnp.bfloat16)
        ot_ref[head * HEAD : (head + 1) * HEAD, :] = product(vt[head * HEAD : (head + 1) * HEAD, :], soft)
        log_ref[head : head + 1, :] = top + jnp.log(total)
    o_ref[...] = ot_ref[...].T.astype(jnp.bfloat16)


def cross_forward_kernel(q_ref, k_ref, v_ref, o_ref, ot_ref, log_ref):
    cross_forward_pair(q_ref, k_ref, v_ref, o_ref, ot_ref, log_ref.at[0])


EXTRA = 16


def backward_pair(
    place, profile_ref, q_ref, k_ref, v_ref, g_ref, ot_ref, log_ref, dq_ref, dk_ref, dv_ref,
    near_ref, far_ref, pads, bias, kt_buf, grad_buf,
):
    q_value = q_ref[...]
    g_value = g_ref[...]
    qt = q_value.T
    gt = g_value.T
    kt = k_ref[...].T
    keys_count = k_ref.shape[0]
    ones = jnp.ones((EXTRA, keys_count), jnp.bfloat16)
    for head in range(2):
        kt_buf[head, 0:HEAD, 0:keys_count] = kt[head * HEAD : (head + 1) * HEAD, :]
        kt_buf[head, HEAD : HEAD + EXTRA, 0:keys_count] = ones
    both_q = jnp.concatenate([head_cols(q_value, 0), head_cols(q_value, 1)], axis=0)
    both_g = jnp.concatenate([head_cols(g_value, 0), head_cols(g_value, 1)], axis=0)
    weighted = gt.astype(jnp.float32) * ot_ref[...]
    if profile_ref is not None:
        fill_near_bias(bias, profile_ref)
    queries, grads_out = [], []
    for head in range(2):
        rows = slice(head * HEAD, (head + 1) * HEAD)
        delta = jnp.sum(weighted[rows, :], axis=0, keepdims=True)
        constant = -log_ref[head : head + 1, :]
        if profile_ref is not None:
            constant = constant + profile_ref[head : head + 1, BLOCK - 1 :]
        queries.append(with_terms(qt, head, 1.0, split_low(constant)))
        grads_out.append(with_terms(gt, head, 0.0, split_low(-delta)))
    sums = [None, None]
    for start in range(0, keys_count, BLOCK):
        k_block = k_ref[start : start + BLOCK, :]
        v_block = v_ref[start : start + BLOCK, :]
        softs, grads = [], []
        for head in range(2):
            scores = product(padded(k_block, pads, head, start), queries[head])
            if profile_ref is not None:
                scores = scores + bias[head, bias_kind(place, start // BLOCK)]
            soft = jnp.exp(scores)
            change = product(padded(v_block, pads, head, start), grads_out[head])
            grad = (soft * change).astype(jnp.bfloat16)
            softs.append(soft.astype(jnp.bfloat16))
            grads.append(grad)
            if profile_ref is not None:
                grad_buf[head, start // BLOCK] = grad
            share = product(kt_buf[head, :, start : start + BLOCK], grad)
            sums[head] = share if sums[head] is None else sums[head] + share
        dv_ref[start : start + BLOCK, :] = product(jnp.concatenate(softs, axis=1), both_g).astype(
            jnp.bfloat16
        )
        dk_ref[start : start + BLOCK, :] = product(jnp.concatenate(grads, axis=1), both_q).astype(
            jnp.bfloat16
        )
    turned = jnp.concatenate([sums[0][0:HEAD, :], sums[1][0:HEAD, :]], axis=0)
    dq_ref[...] = turned.T.astype(jnp.bfloat16)
    if profile_ref is not None:
        later = iota((BLOCK, BLOCK), 1) >= iota((BLOCK, BLOCK), 0)
        for head in range(2):
            diagonal = grad_buf[head, place].astype(jnp.float32)
            before = grad_buf[head, jnp.maximum(place - 1, 0)].astype(jnp.float32)
            before = jnp.where(place >= 1, before, 0.0)
            near = jnp.sum(unskew(jnp.where(later, diagonal, before)), axis=0, keepdims=True)
            near_ref[head : head + 1, :] = near
            far_ref[head : head + 1, :] = sums[head][HEAD : HEAD + 1, :] - near


def self_backward_kernel(
    place_ref, profile_ref, q_ref, k_ref, v_ref, g_ref, ot_ref, log_ref,
    dq_ref, dk_ref, dv_ref, near_ref, far_ref, pads, bias, kt_buf, grad_buf,
):
    @pl.when(pl.program_id(0) == 0)
    def _():
        fill_pads(pads, place_ref[1])
        fill_fixed_bias(bias)

    backward_pair(
        place_ref[0], profile_ref.at[0], q_ref, k_ref, v_ref, g_ref, ot_ref, log_ref.at[0],
        dq_ref, dk_ref, dv_ref, near_ref.at[0], far_ref.at[0], pads, bias, kt_buf, grad_buf,
    )


def cross_backward_kernel(q_ref, k_ref, v_ref, g_ref, ot_ref, log_ref, dq_ref, dk_ref, dv_ref, pads, kt_buf):
    @pl.when(pl.program_id(0) == 0)
    def _():
        fill_pads(pads, pads.shape[1])

    backward_pair(
        None, None, q_ref, k_ref, v_ref, g_ref, ot_ref, log_ref.at[0], dq_ref, dk_ref, dv_ref,
        None, None, pads, None, kt_buf, None,
    )


def forward_scratch(count, rows):
    return [
        pltpu.VMEM((2, count, PAIR), jnp.bfloat16),
        pltpu.VMEM((2, 4, BLOCK, BLOCK), jnp.float32),
        pltpu.VMEM((2, count, rows), jnp.float32),
        pltpu.VMEM((PAIR, count), jnp.bfloat16),
    ]


def backward_scratch(count):
    return [
        pltpu.VMEM((2, count, PAIR), jnp.bfloat16),
        pltpu.VMEM((2, 4, BLOCK, BLOCK), jnp.float32),
        pltpu.VMEM((2, HEAD + EXTRA, count), jnp.bfloat16),
        pltpu.VMEM((2, count // BLOCK, BLOCK, BLOCK), jnp.bfloat16),
    ]


def pair_block(rows):
    return pl.BlockSpec((rows, PAIR), lambda pair: (0, pair))


def turned_block(rows):
    return pl.BlockSpec((PAIR, rows), lambda pair: (pair, 0))


def head_block(width):
    return pl.BlockSpec((1, 2, width), lambda pair: (pair, 0, 0))


SCALARS = pl.BlockSpec(memory_space=pltpu.SMEM)
PAIRS = HEADS // 2


def shaped(shape, dtype):
    return jax.ShapeDtypeStruct(shape, dtype)


def self_forward(place, profile, queries, keys, values):
    rows, width = queries.shape
    count = keys.shape[0]
    return pl.pallas_call(
        self_forward_kernel,
        grid=(PAIRS,),
        in_specs=[SCALARS, head_block(BLOCK), pair_block(rows), pair_block(count), pair_block(count)],
        out_specs=[pair_block(rows), turned_block(rows), head_block(rows)],
        out_shape=[
            shaped((rows, width), jnp.bfloat16),
            shaped((width, rows), jnp.float32),
            shaped((PAIRS, 2, rows), jnp.float32),
        ],
        scratch_shapes=forward_scratch(count, rows),
        name="self_forward",
    )(place, profile, queries, keys, values)


def cross_forward(queries, keys, values):
    rows, width = queries.shape
    count = keys.shape[0]
    return pl.pallas_call(
        cross_forward_kernel,
        grid=(PAIRS,),
        in_specs=[pair_block(rows), pair_block(count), pair_block(count)],
        out_specs=[pair_block(rows), turned_block(rows), head_block(rows)],
        out_shape=[
            shaped((rows, width), jnp.bfloat16),
            shaped((width, rows), jnp.float32),
            shaped((PAIRS, 2, rows), jnp.float32),
        ],
        name="cross_forward",
    )(queries, keys, values)


def self_backward(place, profile, queries, keys, values, grad_mixed, mixed_turned, log_totals):
    rows, width = queries.shape
    count = keys.shape[0]
    return pl.pallas_call(
        self_backward_kernel,
        grid=(PAIRS,),
        in_specs=[
            SCALARS, head_block(BLOCK), pair_block(rows), pair_block(count), pair_block(count),
            pair_block(rows), turned_block(rows), head_block(rows),
        ],
        out_specs=[
            pair_block(rows), pair_block(count), pair_block(count), head_block(BLOCK), head_block(rows),
        ],
        out_shape=[
            shaped((rows, width), jnp.bfloat16),
            shaped((count, width), jnp.bfloat16),
            shaped((count, width), jnp.bfloat16),
            shaped((PAIRS, 2, BLOCK), jnp.float32),
            shaped((PAIRS, 2, rows), jnp.float32),
        ],
        scratch_shapes=backward_scratch(count),
        name="self_backward",
    )(place, profile, queries, keys, values, grad_mixed, mixed_turned, log_totals)


def cross_backward(queries, keys, values, grad_mixed, mixed_turned, log_totals):
    rows, width = queries.shape
    count = keys.shape[0]
    return pl.pallas_call(
        cross_backward_kernel,
        grid=(PAIRS,),
        in_specs=[
            pair_block(rows), pair_block(count), pair_block(count),
            pair_block(rows), turned_block(rows), head_block(rows),
        ],
        out_specs=[pair_block(rows), pair_block(count), pair_block(count)],
        out_shape=[
            shaped((rows, width), jnp.bfloat16),
            shaped((count, width), jnp.bfloat16),
            shaped((count, width), jnp.bfloat16),
        ],
        scratch_shapes=[
            pltpu.VMEM((2, count, PAIR), jnp.bfloat16),
            pltpu.VMEM((2, HEAD + EXTRA, count), jnp.bfloat16),
        ],
        name="cross_backward",
    )(queries, keys, values, grad_mixed, mixed_turned, log_totals)


class Peers:
    def __init__(self, planes):
        self.seq = lax.axis_index("seq")
        fsdp = lax.axis_index("fsdp")
        self.planes = planes
        self.plane = fsdp // 2
        self.core = fsdp % 2
        self.fsdp = fsdp
        self.along_x = self.seq + 1 - 2 * (self.seq % 2)
        self.along_y = (self.seq + 2) % 4
        self.corner = (self.along_x + 2) % 4
        self.partner = (self.seq, fsdp + 1 - 2 * self.core)
        self.to_x = (self.along_x, fsdp)
        self.to_y = (self.along_y, fsdp)
        self.to_corner = (self.corner, fsdp)

    def ahead(self, steps):
        return (self.plane + steps) % self.planes

    def at_plane(self, plane):
        return (self.seq, 2 * plane + self.core)

    def everyone(self):
        return [self.partner, self.to_x, self.to_y, self.to_corner] + [
            self.at_plane(self.ahead(k)) for k in range(1, self.planes)
        ]

    def meet(self):
        barrier = pltpu.get_barrier_semaphore()
        others = self.everyone()
        for other in others:
            pl.semaphore_signal(barrier, inc=1, device_id=other, device_id_type=MESH)
        pl.semaphore_wait(barrier, len(others))


def remote(source, target, send_sem, recv_sem, device):
    return pltpu.make_async_remote_copy(
        src_ref=source, dst_ref=target, send_sem=send_sem, recv_sem=recv_sem,
        device_id=device, device_id_type=MESH,
    )


class Stack:
    def __init__(self, rows, cols):
        self.rows, self.cols = rows, cols

    def own(self, ref, quarter, first=0, count=None):
        return ref.at[quarter, pl.ds(first, count or self.rows), :]

    def part(self, ref, quarter, plane, core, first=0, count=None):
        return ref.at[quarter, plane, core, pl.ds(first, count or self.rows), :]

    def planes(self, ref, quarter, core):
        return ref.at[quarter, :, core]

    def whole(self, ref, plane, core):
        return ref.at[:, plane, core]


class Wide:
    def __init__(self, rows, cols):
        self.rows, self.cols = rows, cols

    def own(self, ref, quarter, first=0, count=None):
        return ref.at[pl.ds(first, count or self.rows), pl.ds(quarter * self.cols, self.cols)]

    def part(self, ref, quarter, plane, core, first=0, count=None):
        return ref.at[
            plane, core, pl.ds(first, count or self.rows), pl.ds(quarter * self.cols, self.cols)
        ]

    def planes(self, ref, quarter, core):
        return ref.at[:, core, :, pl.ds(quarter * self.cols, self.cols)]

    def whole(self, ref, plane, core):
        return ref.at[plane, core]


class Tall:
    def __init__(self, rows, cols):
        self.rows, self.cols = rows, cols

    def own(self, ref, quarter, first=0, count=None):
        return ref.at[pl.ds(quarter * self.rows + first, count or self.rows), :]

    def part(self, ref, quarter, plane, core, first=0, count=None):
        return ref.at[plane, core, pl.ds(quarter * self.rows + first, count or self.rows), :]

    def planes(self, ref, quarter, core):
        return ref.at[:, core, pl.ds(quarter * self.rows, self.rows), :]

    def whole(self, ref, plane, core):
        return ref.at[plane, core]


def full_shapes(kinds, planes, cores=2):
    shapes = []
    for kind in kinds:
        if isinstance(kind, Stack):
            shapes.append((4, planes, cores, kind.rows, kind.cols))
        elif isinstance(kind, Wide):
            shapes.append((planes, cores, kind.rows, 4 * kind.cols))
        else:
            shapes.append((planes, cores, 4 * kind.rows, kind.cols))
    return shapes


ANYWHERE = pl.BlockSpec(memory_space=pl.ANY)
DMA = pltpu.SemaphoreType.DMA


def make_kinds(shards):
    square, wide, down = shards[0], shards[8], shards[10]
    stack = Stack(*square.shape)
    band = Wide(wide.shape[0], wide.shape[1] // 4)
    tall = Tall(down.shape[0] // 4, down.shape[1])
    return [stack, stack, band, band, tall]


def kernels_fit(shards):
    kinds = make_kinds(shards)
    return (
        lax.axis_size("seq") == 4
        and lax.axis_size("fsdp") == 8
        and all(kind.rows % 32 == 0 and kind.cols % 128 == 0 for kind in kinds)
    )


def gather_plain(shards, tokens, encoded):
    full = [lax.all_gather(shard, "fsdp", axis=0, tiled=True) for shard in shards]
    return (
        full,
        lax.all_gather(tokens, "seq", axis=0, tiled=True),
        lax.all_gather(encoded, "seq", axis=0, tiled=True),
    )


def add_low(target, *terms):
    total = target[...].astype(jnp.float32)
    for term in terms:
        total = total + term[...].astype(jnp.float32)
    target[...] = total.astype(jnp.bfloat16)


def reduce_plain(grads, token_part, enc_part, small):
    def sums(value):
        return lax.psum_scatter(value.astype(jnp.float32), "seq", scatter_dimension=0, tiled=True)

    reduced = [
        lax.psum(
            lax.psum_scatter(grad.astype(jnp.float32), "fsdp", scatter_dimension=0, tiled=True), "seq"
        )
        for grad in grads
    ]
    return reduced, sums(token_part), sums(enc_part), lax.psum(small, ("seq", "fsdp"))


def columns(pair):
    return pl.ds(pl.multiple_of(pair * PAIR, PAIR), PAIR)


def tiles(count):
    def run(body):
        @pl.loop(0, count // BLOCK)
        def _(n):
            body(pl.ds(pl.multiple_of(n * BLOCK, BLOCK), BLOCK))

    return run


def times_turned(store, left, weight):
    value = left[...]

    @tiles(weight.shape[0])
    def _(part):
        store(part, outer_rows(value, weight[part, :]))


def times(store, left, weight):
    value = left[...]

    @tiles(weight.shape[1])
    def _(part):
        store(part, product(value, weight[:, part]))


def weight_grad(out, turned, right):
    across = right.shape[1] // BLOCK

    @pl.loop(0, (turned.shape[0] // BLOCK) * across)
    def _(n):
        first = pl.ds(pl.multiple_of((n // across) * BLOCK, BLOCK), BLOCK)
        second = pl.ds(pl.multiple_of((n % across) * BLOCK, BLOCK), BLOCK)
        out[first, second] = product(turned[first, :], right[:, second]).astype(jnp.bfloat16)


def turn(out, source):
    @tiles(source.shape[0])
    def _(part):
        out[:, part] = source[part, :].T


ROW_STEP = 32


def row_steps(count):
    def run(body):
        @pl.loop(0, count // ROW_STEP)
        def _(n):
            body(pl.ds(pl.multiple_of(n * ROW_STEP, ROW_STEP), ROW_STEP))

    return run


def norm_back_rows(values, gain, grad_normed):
    scale = lax.rsqrt(jnp.mean(values * values, axis=-1, keepdims=True) + EPSILON)
    scaled = grad_normed * gain
    along = jnp.mean(values * scaled, axis=-1, keepdims=True)
    grad_values = scale * scaled - values * (scale * scale * scale) * along
    return grad_values, jnp.sum(grad_normed * values * scale, axis=0, keepdims=True)


GATE, UP, DOWN, CROSS, SELF = range(5)


class Space:
    def __init__(self, layout, refs):
        refs = list(refs)
        for name, count in layout.items():
            value = refs.pop(0) if count is None else [refs.pop(0) for _ in range(count)]
            setattr(self, name, value)


def flatten(*tables):
    layout, flat = {}, []
    for table in tables:
        for name, value in table.items():
            many = isinstance(value, list)
            layout[name] = len(value) if many else None
            flat += value if many else [value]
    return layout, flat


class Reduction:
    def __init__(self, kinds, here, r):
        self.kinds, self.here, self.r = kinds, here, r
        self.planes = here.planes
        self.lower = here.planes // 2
        self.started = []
        shape = (4, here.planes, 2, kinds[CROSS].rows, kinds[CROSS].cols)
        self.parts = [
            *r.ffn_parts,
            r.grad_cross.reshape(*shape), r.grad_self.reshape(*shape),
        ]
        self.sums = r.sums

    def send(self, make):
        remote(*make()).start()
        self.started.append(make)

    def arrived(self, target, recv_sem):
        pltpu.make_async_copy(target, target, recv_sem).wait()

    def own_copy(self, g, q):
        stage = (self.r.stage_tall if g == DOWN else self.r.stage_band)
        return pltpu.make_async_copy(
            self.kinds[g].planes(self.parts[g], q, self.here.core), stage.at[q], self.r.own_sem.at[g, q]
        )

    def load_own(self, g):
        for q in range(4):
            self.own_copy(g, q).start()

    def start_pair(self, g):
        r = self.r
        for q in range(4):
            self.send(lambda g=g, q=q: (self.kinds[g].planes(self.parts[g], q, 1 - self.here.core), self.sums[g].at[q],
                r.c_send.at[g, q], r.c_recv.at[g, q], self.here.partner))

    def pair_sum(self, g):
        r, here, sums, planes = self.r, self.here, self.sums[g], self.planes
        for q in range(4):
            self.arrived(sums.at[q], r.c_recv.at[g, q])
            if g <= DOWN:
                self.own_copy(g, q).wait()
        if g <= DOWN:
            stage = r.stage_tall if g == DOWN else r.stage_band

        @pl.loop(0, 4 * planes)
        def _(n):
            q, z = n // planes, n % planes
            own = stage.at[q, z] if g <= DOWN else self.parts[g].at[q, z, here.core]
            add_low(sums.at[q, z], own)

        if g == GATE:
            self.load_own(UP)
        low, high = pl.ds(0, self.lower), pl.ds(self.lower, planes - self.lower)
        for n, quarter in enumerate((here.along_x, here.corner)):
            self.send(lambda g=g, n=n, quarter=quarter: (sums.at[quarter, low], r.side_x[g].at[n],
                r.a_send.at[g, n], r.a_recv.at[g, n], here.to_x))
        for n, quarter in enumerate((here.along_y, here.corner)):
            self.send(lambda g=g, n=n, quarter=quarter: (sums.at[quarter, high], r.side_y[g].at[n],
                r.a_send.at[g, 2 + n], r.a_recv.at[g, 2 + n], here.to_y))

    def first_side(self, g):
        r, here, sums, lower = self.r, self.here, self.sums[g], self.lower
        side_x, side_y, last = r.side_x[g], r.side_y[g], r.last[g]
        for n in range(2):
            self.arrived(side_x.at[n], r.a_recv.at[g, n])
            self.arrived(side_y.at[n], r.a_recv.at[g, 2 + n])

        @pl.loop(0, lower)
        def _(z):
            add_low(sums.at[here.along_y, z], side_x.at[1, z])
            add_low(sums.at[here.along_x, lower + z], side_y.at[1, z])

        self.send(lambda g=g: (sums.at[here.along_y, pl.ds(0, lower)], last.at[0],
            r.b_send.at[g, 0], r.b_recv.at[g, 0], here.to_y))
        self.send(lambda g=g: (sums.at[here.along_x, pl.ds(lower, lower)], last.at[1],
            r.b_send.at[g, 1], r.b_recv.at[g, 1], here.to_x))

    def second_side(self, g):
        r, here, sums, lower = self.r, self.here, self.sums[g], self.lower
        side_x, side_y, last = r.side_x[g], r.side_y[g], r.last[g]
        self.arrived(last.at[0], r.b_recv.at[g, 0])
        self.arrived(last.at[1], r.b_recv.at[g, 1])

        @pl.loop(0, lower)
        def _(z):
            add_low(sums.at[here.seq, z], side_x.at[0, z], last.at[0, z])
            add_low(sums.at[here.seq, lower + z], side_y.at[0, z], last.at[1, z])

        for k in range(1, self.planes):
            self.send(
                lambda k=k: (
                    sums.at[here.seq, here.ahead(k)], r.from_z[g].at[k - 1],
                    r.z_send.at[g, k - 1], r.z_recv.at[g, k - 1], here.at_plane(here.ahead(k)),
                )
            )

    def along_planes(self, g):
        r, here, sums = self.r, self.here, self.sums[g]
        from_z, final = r.from_z[g], r.final[g]
        for k in range(1, self.planes):
            self.arrived(from_z.at[k - 1], r.z_recv.at[g, k - 1])
        step = 32

        @pl.loop(0, self.kinds[g].rows // step)
        def _(n):
            rows = pl.ds(pl.multiple_of(n * step, step), step)
            total = sums[here.seq, here.plane, rows, :].astype(jnp.float32)
            for k in range(1, self.planes):
                total = total + from_z[k - 1, rows, :].astype(jnp.float32)
            final[here.seq, rows, :] = total.astype(jnp.bfloat16)

        for n, device in enumerate((here.to_x, here.to_y)):
            self.send(
                lambda n=n, device=device: (
                    final.at[here.seq], final.at[here.seq], r.g_send.at[g, n], r.g_recv.at[g, n], device
                )
            )

    def spread(self, g):
        r, here, final = self.r, self.here, self.r.final[g]
        half = self.kinds[g].rows // 2
        turns = ((here.along_x, 0, here.to_y), (here.along_y, half, here.to_x))
        for n, (quarter, first, device) in enumerate(turns):
            self.arrived(final.at[quarter], r.g_recv.at[g, n])

            def make(n=n, quarter=quarter, first=first, device=device):
                chunk = final.at[quarter, pl.ds(first, half), :]
                return chunk, chunk, r.g_send.at[g, 2 + n], r.g_recv.at[g, 2 + n], device

            self.send(make)

    def out_copies(self, g):
        r, kind, final = self.r, self.kinds[g], self.r.final[g]
        out = r.out[g]
        if not isinstance(kind, Wide):
            return [pltpu.make_async_copy(final, out, r.out_sem.at[g, 0])]
        return [
            pltpu.make_async_copy(
                final.at[q], out.at[:, pl.ds(q * kind.cols, kind.cols)], r.out_sem.at[g, q]
            )
            for q in range(4)
        ]

    def finish(self, g):
        r, here, final = self.r, self.here, self.r.final[g]
        half = self.kinds[g].rows // 2
        self.arrived(final.at[here.corner, pl.ds(0, half), :], r.g_recv.at[g, 2])
        self.arrived(final.at[here.corner, pl.ds(half, half), :], r.g_recv.at[g, 3])
        for copy in self.out_copies(g):
            copy.start()

    def end(self):
        for g in range(5):
            for copy in self.out_copies(g):
                copy.wait()
        for make in self.started:
            remote(*make()).wait_send()


def backward_kernel(kinds, planes, layout, *refs):
    r = Space(layout, refs)
    bf16, f32 = jnp.bfloat16, jnp.float32
    here = Peers(planes)
    place, length = here.seq, r.length[0]
    red = Reduction(kinds, here, r)
    rows = r.grad_two.shape[0]
    count = r.keys.shape[0]
    enc_count = r.ckeys_in.shape[0]

    ckeys, cvalues = r.dk.at[pl.ds(0, enc_count), :], r.dk.at[pl.ds(enc_count, enc_count), :]
    dck, dcv = r.dv.at[pl.ds(0, enc_count), :], r.dv.at[pl.ds(enc_count, enc_count), :]
    enc_all = r.token_part.at[pl.ds(0, enc_count), :]
    enc_part = r.token_part.at[pl.ds(enc_count, enc_count), :]
    enc_turned = r.rows_turned.at[:, pl.ds(0, enc_count)]

    def load(n, source, target):
        copy = pltpu.make_async_copy(source, target, r.load_sem.at[n])
        copy.start()
        return copy

    here.meet()
    red.start_pair(GATE)
    grad_two_load = load(0, r.grad_two_in, r.grad_two)
    w_cout_load = load(1, r.w_two.at[3], r.weights.at[3])
    mixed_load = load(2, r.mixed_cross_in, r.mixed)
    cqueries_load = load(3, r.cqueries_in, r.queries)
    ckeys_load = load(4, r.ckeys_in, ckeys)
    cvalues_load = load(5, r.cvalues_in, cvalues)
    red.start_pair(UP)
    red.start_pair(DOWN)
    red.load_own(GATE)
    red.load_own(DOWN)
    normed_two_load = load(6, r.normed_two_in, r.normed)
    encoded_load = load(7, r.enc_in, enc_all)
    w_two_loads = [load(8 + m, r.w_two.at[m], r.weights.at[m]) for m in range(3)]
    hidden_load = load(11, r.hidden_one_in, r.hidden)
    w_sout_load = load(12, r.w_one.at[3], r.weights.at[4])
    keys_load = load(13, r.keys_in, r.keys)
    values_load = load(14, r.values_in, r.values)

    fill_pads(r.pads, count)
    fill_fixed_bias(r.bias)

    def to_branch():
        @row_steps(rows)
        def _(part):
            r.branch[part, :] = r.grad_two[part, :].astype(bf16)

    def store_grad_mixed(part, value):
        r.grad_mixed[:, part] = value.astype(bf16)

    def mixed_low():
        @pl.loop(0, r.mixed.shape[0] // PAIR)
        def _(n):
            part = columns(n)
            r.mixed_low[part, :] = r.mixed[part, :].astype(bf16)

    grad_two_load.wait()
    to_branch()
    w_cout_load.wait()
    times_turned(store_grad_mixed, r.branch, r.weights.at[3])
    mixed_load.wait()
    mixed_low()
    weight_grad(r.grad_cross.at[3], r.mixed_low, r.branch)
    for copy in (cqueries_load, ckeys_load, cvalues_load):
        copy.wait()
    cross_steps = {
        1: [lambda: red.pair_sum(GATE)],
        2: [lambda: red.pair_sum(UP)],
        3: [lambda: red.pair_sum(DOWN)],
    }

    @pl.loop(0, PAIRS)
    def _(pair):
        part = columns(pair)
        backward_pair(
            None, None, r.queries.at[:, part], ckeys.at[:, part], cvalues.at[:, part],
            r.grad_mixed.at[:, part], r.mixed.at[part, :], r.log_cross.at[pair],
            r.dq.at[:, part], dck.at[:, part], dcv.at[:, part], None, None, r.pads, None, r.kt_buf, None,
        )
        for when, steps in cross_steps.items():

            @pl.when(pair == when)
            def _(steps=steps):
                for step in steps:
                    step()

    fill_pads(r.pads, length)
    mixed_self_load = load(15, r.mixed_self_in, r.mixed)
    queries_load = load(16, r.queries_in, r.queries)
    w_two_loads[0].wait()

    def store_gy(part, value):
        r.gy[:, part] = value

    times_turned(store_gy, r.dq, r.weights.at[0])
    red.first_side(GATE)
    normed_two_load.wait()
    r.normed_turned[...] = r.normed[...].T
    weight_grad(r.grad_cross.at[0], r.normed_turned, r.dq)
    encoded_load.wait()
    turn(enc_turned, enc_all)
    weight_grad(r.grad_cross.at[1], enc_turned, dck)
    weight_grad(r.grad_cross.at[2], enc_turned, dcv)
    red.start_pair(CROSS)
    w_two_loads[1].wait()
    w_two_loads[2].wait()

    @pl.loop(0, (enc_count // BLOCK) * (enc_all.shape[1] // BLOCK))
    def _(n):
        across = enc_all.shape[1] // BLOCK
        first = pl.ds(pl.multiple_of((n // across) * BLOCK, BLOCK), BLOCK)
        second = pl.ds(pl.multiple_of((n % across) * BLOCK, BLOCK), BLOCK)
        total = outer_rows(dck[first, :], r.weights[1, second, :])
        total = total + outer_rows(dcv[first, :], r.weights[2, second, :])
        enc_part[first, second] = total.astype(bf16)

    quarters = ((here.along_x, here.to_x), (here.along_y, here.to_y), (here.corner, here.to_corner))

    def send_rows(item, source, size):
        makes = []
        for k, (quarter, device) in enumerate(quarters):

            def make(k=k, quarter=quarter, device=device):
                return (
                    source.at[pl.ds(quarter * size, size), :], r.rows_got[item].at[k],
                    r.r_send.at[item, k], r.r_recv.at[item, k], device,
                )

            remote(*make()).start()
            makes.append(make)
        return makes

    def sum_rows(item, source, size, store):
        got = r.rows_got[item]
        for k in range(3):
            red.arrived(got.at[k], r.r_recv.at[item, k])

        @row_steps(size)
        def _(part):
            start = pl.multiple_of(place * size + part.start, ROW_STEP)
            total = source[pl.ds(start, ROW_STEP), :].astype(f32)
            for k in range(3):
                total = total + got[k, part, :].astype(f32)
            store(part, total)

    enc_rows = enc_count // 4
    enc_sends = send_rows(1, enc_part, enc_rows)
    hidden_load.wait()
    r.small[...] = jnp.zeros_like(r.small)
    r.small[2:3, :] = r.grad_gain_three[...]

    @row_steps(rows)
    def _(part):
        grad, gain = norm_back_rows(r.hidden[part, :], r.gain_two[...], r.gy[part, :])
        total = r.grad_two[part, :] + grad
        r.grad_two[part, :] = total
        r.branch[part, :] = total.astype(bf16)
        r.small[1:2, :] += gain

    w_sout_load.wait()
    times_turned(store_grad_mixed, r.branch, r.weights.at[4])
    mixed_self_load.wait()
    mixed_low()
    weight_grad(r.grad_self.at[3], r.mixed_low, r.branch)
    w_one_loads = [load(17 + m, r.w_one.at[m], r.weights.at[m]) for m in range(3)]
    for copy in (queries_load, keys_load, values_load):
        copy.wait()

    def keep_enc(part, total):
        r.enc_total[part, :] = total

    def enc_done():
        sum_rows(1, enc_part, enc_rows, keep_enc)
        for make in enc_sends:
            remote(*make()).wait_send()
        pltpu.make_async_copy(r.enc_total, r.enc_sum, r.load_sem.at[20]).start()

    def load_normed():
        pltpu.make_async_copy(r.normed_all_in, r.token_part, r.load_sem.at[21]).start()

    def turn_normed():
        pltpu.make_async_copy(r.normed_all_in, r.token_part, r.load_sem.at[21]).wait()
        turn(r.rows_turned, r.token_part)

    self_steps = {
        0: [lambda: red.first_side(UP), lambda: red.pair_sum(CROSS)],
        1: [lambda: red.first_side(DOWN), enc_done, load_normed],
        2: [lambda: red.second_side(GATE), turn_normed],
        3: [lambda: red.second_side(UP)],
        4: [lambda: red.second_side(DOWN), lambda: red.along_planes(GATE)],
        5: [lambda: red.first_side(CROSS), lambda: red.along_planes(UP)],
    }

    @pl.loop(0, PAIRS)
    def _(pair):
        part = columns(pair)
        backward_pair(
            place, r.profile.at[pair], r.queries.at[:, part], r.keys.at[:, part],
            r.values.at[:, part], r.grad_mixed.at[:, part], r.mixed.at[part, :],
            r.log_self.at[pair], r.dq.at[:, part], r.dk.at[:, part], r.dv.at[:, part],
            r.near.at[pair], r.far.at[pair], r.pads, r.bias, r.kt_buf, r.grad_buf,
        )
        for when, steps in self_steps.items():

            @pl.when(pair == when)
            def _(steps=steps):
                for step in steps:
                    step()

    tokens_load = load(22, r.tokens_all_in, r.keys)
    own = pl.ds(pl.multiple_of(place * rows, BLOCK), rows)
    weight_grad(r.grad_self.at[0], r.rows_turned.at[:, own], r.dq)
    weight_grad(r.grad_self.at[1], r.rows_turned, r.dk)
    weight_grad(r.grad_self.at[2], r.rows_turned, r.dv)
    red.start_pair(SELF)
    red.spread(GATE)
    for copy in w_one_loads:
        copy.wait()

    @pl.loop(0, (count // BLOCK) * (r.dk.shape[1] // BLOCK))
    def _(n):
        across = r.dk.shape[1] // BLOCK
        first = pl.ds(pl.multiple_of((n // across) * BLOCK, BLOCK), BLOCK)
        second = pl.ds(pl.multiple_of((n % across) * BLOCK, BLOCK), BLOCK)
        total = outer_rows(r.dk[first, :], r.weights[1, second, :])
        total = total + outer_rows(r.dv[first, :], r.weights[2, second, :])
        r.token_part[first, second] = total.astype(bf16)

    times_turned(store_gy, r.dq, r.weights.at[0])
    red.pair_sum(SELF)
    red.started += send_rows(0, r.token_part, rows)
    red.second_side(CROSS)
    red.along_planes(DOWN)
    red.spread(UP)
    tokens_load.wait()

    @row_steps(count)
    def _(part):
        values = r.keys[part, :].astype(f32)
        scale = lax.rsqrt(jnp.mean(values * values, axis=-1, keepdims=True) + EPSILON)
        grad = r.token_part[part, :].astype(f32)
        r.small[0:1, :] += jnp.sum(grad * values * scale, axis=0, keepdims=True)

    @row_steps(rows)
    def _(part):
        values = r.keys[pl.ds(pl.multiple_of(place * rows + part.start, ROW_STEP), ROW_STEP), :].astype(f32)
        scale = lax.rsqrt(jnp.mean(values * values, axis=-1, keepdims=True) + EPSILON)
        r.small[0:1, :] += jnp.sum(r.gy[part, :] * values * scale, axis=0, keepdims=True)

    for pair in range(PAIRS):
        table = jnp.dot(
            r.near[pair], r.one_hot[...], precision=lax.Precision.HIGHEST, preferred_element_type=f32
        )
        last_bucket = iota(table.shape, 1) == BUCKETS - 1
        table = table + jnp.where(last_bucket, jnp.sum(r.far[pair], axis=1, keepdims=True), 0.0)
        r.small[8 + 2 * pair : 10 + 2 * pair, 0 : table.shape[1]] = table

    small, small_core, small_seq, small_plane = r.small, r.small_core, r.small_seq, r.small_plane
    s_send, s_recv = r.s_send, r.s_recv
    red.send(lambda : (small, small_core, s_send.at[0], s_recv.at[0], here.partner))
    red.finish(GATE)
    red.first_side(SELF)
    red.arrived(small_core, s_recv.at[0])
    small_seq[place] = small[...] + small_core[...]
    for k, (_, device) in enumerate(quarters):
        red.send(lambda k=k, device=device: (small_seq.at[place], small_seq.at[place], s_send.at[1 + k], s_recv.at[1 + k], device))
    red.along_planes(CROSS)
    red.spread(DOWN)
    red.finish(UP)
    red.second_side(SELF)
    for k, (quarter, _) in enumerate(quarters):
        red.arrived(small_seq.at[quarter], s_recv.at[1 + k])
    small_plane[here.plane] = (small_seq[0] + small_seq[1]) + (small_seq[2] + small_seq[3])
    for k in range(1, planes):
        red.send(lambda k=k: (small_plane.at[here.plane], small_plane.at[here.plane],
            s_send.at[3 + k], s_recv.at[3 + k], here.at_plane(here.ahead(k))))

    def keep_tokens(part, total):
        values = r.keys[pl.ds(pl.multiple_of(place * rows + part.start, ROW_STEP), ROW_STEP), :].astype(f32)
        grad, _ = norm_back_rows(values, r.gain_one[...], r.gy[part, :] + total)
        r.hidden[part, :] = r.grad_two[part, :] + grad

    sum_rows(0, r.token_part, rows, keep_tokens)
    token_copy = pltpu.make_async_copy(r.hidden, r.grad_tokens, r.load_sem.at[23])
    token_copy.start()
    red.spread(CROSS)
    red.finish(DOWN)
    for k in range(1, planes):
        red.arrived(small_plane.at[here.ahead(planes - k)], s_recv.at[3 + k])
    total = small_plane[0]
    for k in range(1, planes):
        total = total + small_plane[k]
    r.small_out[...] = total
    red.along_planes(SELF)
    red.finish(CROSS)
    red.spread(SELF)
    red.finish(SELF)
    token_copy.wait()
    pltpu.make_async_copy(r.enc_total, r.enc_sum, r.load_sem.at[20]).wait()
    red.end()


def backward_fused(shards, length, small, large):
    kinds = make_kinds(shards)
    planes = lax.axis_size("fsdp") // 2
    lower = planes // 2
    kinds = [kinds[n] for n in (2, 3, 4, 1, 0)]
    shapes = full_shapes(kinds, planes)
    f32, low = jnp.float32, jnp.bfloat16
    rows, width = large["grad_two_in"].shape
    count, enc_count = large["keys_in"].shape[0], large["ckeys_in"].shape[0]
    in_vmem = pl.BlockSpec(memory_space=pltpu.VMEM)
    large["ffn_parts"] = [part.reshape(shape) for part, shape in zip(large["ffn_parts"], shapes)]
    in_layout, operands = flatten(dict(length=length), small, large)
    in_specs = [SCALARS] + [in_vmem] * len(small)
    in_specs += [ANYWHERE] * (len(operands) - len(in_specs))
    small_shape = (24, width)

    def chunks(*lead):
        return [pltpu.VMEM(lead + (kind.rows, kind.cols), low) for kind in kinds]

    results = dict(
        out=[
            shaped((kind.rows, 4 * kind.cols) if isinstance(kind, Wide) else (4, kind.rows, kind.cols), low)
            for kind in kinds
        ],
        grad_tokens=shaped((rows, width), f32),
        enc_sum=shaped((enc_count // 4, width), f32),
        small_out=shaped(small_shape, f32),
    )
    out_layout, out_shapes = flatten(results)
    square = (width, width)
    all_rows = pltpu.VMEM((count, width), low)
    some_rows = pltpu.VMEM((rows, width), low)
    turned_rows = pltpu.VMEM((width, rows), low)
    wide_rows = pltpu.VMEM((rows, width), f32)
    backward_buffers = backward_scratch(count)
    scratch = dict(
        sums=chunks(4, planes),
        side_x=chunks(2, lower),
        side_y=chunks(2, lower),
        last=chunks(2, lower),
        from_z=chunks(planes - 1),
        final=chunks(4),
        stage_band=pltpu.VMEM((4, planes, kinds[GATE].rows, kinds[GATE].cols), low),
        stage_tall=pltpu.VMEM((4, planes, kinds[DOWN].rows, kinds[DOWN].cols), low),
        grad_cross=pltpu.VMEM((4,) + square, low),
        grad_self=pltpu.VMEM((4,) + square, low),
        weights=pltpu.VMEM((5,) + square, low),
        keys=all_rows, values=all_rows, dk=all_rows, dv=all_rows, token_part=all_rows,
        rows_turned=pltpu.VMEM((width, count), low),
        queries=some_rows, normed=some_rows, branch=some_rows, grad_mixed=some_rows, dq=some_rows,
        mixed_low=turned_rows, normed_turned=turned_rows,
        grad_two=wide_rows, hidden=wide_rows, gy=wide_rows,
        mixed=pltpu.VMEM((width, rows), f32),
        enc_total=pltpu.VMEM((enc_count // 4, width), f32),
        rows_got=[pltpu.VMEM((3, rows, width), low), pltpu.VMEM((3, enc_count // 4, width), low)],
        pads=backward_buffers[0], bias=backward_buffers[1], kt_buf=backward_buffers[2],
        grad_buf=backward_buffers[3],
        near=pltpu.VMEM((PAIRS, 2, BLOCK), f32),
        far=pltpu.VMEM((PAIRS, 2, rows), f32),
        small=pltpu.VMEM(small_shape, f32),
        small_core=pltpu.VMEM(small_shape, f32),
        small_seq=pltpu.VMEM((4,) + small_shape, f32),
        small_plane=pltpu.VMEM((planes,) + small_shape, f32),
        own_sem=DMA((3, 4)),
        c_send=DMA((5, 4)), c_recv=DMA((5, 4)),
        a_send=DMA((5, 4)), a_recv=DMA((5, 4)),
        b_send=DMA((5, 2)), b_recv=DMA((5, 2)),
        z_send=DMA((5, planes - 1)), z_recv=DMA((5, planes - 1)),
        g_send=DMA((5, 4)), g_recv=DMA((5, 4)),
        r_send=DMA((2, 3)), r_recv=DMA((2, 3)),
        s_send=DMA((3 + planes,)), s_recv=DMA((3 + planes,)),
        out_sem=DMA((5, 4)), load_sem=DMA((24,)),
    )
    scratch_layout, scratch_shapes = flatten(scratch)
    outs = pl.pallas_call(
        functools.partial(backward_kernel, kinds, planes, in_layout | out_layout | scratch_layout),
        in_specs=in_specs,
        out_specs=[ANYWHERE] * (len(out_shapes) - 1) + [in_vmem],
        out_shape=out_shapes,
        scratch_shapes=scratch_shapes,
        compiler_params=pltpu.CompilerParams(
            collective_id=1, has_side_effects=True, vmem_limit_bytes=66_000_000
        ),
        name="backward_fused",
    )(*operands)
    got = Space(out_layout, outs)
    grads = [got.out[SELF][m] for m in range(4)] + [got.out[CROSS][m] for m in range(4)]
    grads += [got.out[GATE], got.out[UP], got.out[DOWN].reshape(-1, width)]
    return [grad.astype(f32) for grad in grads], got.grad_tokens, got.enc_sum, got.small_out


ONE, TWO, GATE_IN, UP_IN, DOWN_IN = range(5)


class Gathering:
    def __init__(self, kinds, here, r):
        self.kinds, self.here, self.r = kinds, here, r
        self.planes = here.planes
        shape = (4, here.planes, 2, kinds[ONE].rows, kinds[ONE].cols)
        self.full = [r.weights_one.reshape(*shape), r.weights_two.reshape(*shape), *r.ffn_full]
        self.shards = [r.shards[0:4], r.shards[4:8], r.shards[8], r.shards[9], r.shards[10]]
        self.started = []

    def send(self, make):
        remote(*make()).start()
        self.started.append(make)

    def arrived(self, target, recv_sem):
        pltpu.make_async_copy(target, target, recv_sem).wait()

    def plane_copy(self, g, k, source):
        here, r = self.here, self.r
        return remote(
            source, self.kinds[g].part(self.full[g], here.seq, here.plane, here.core),
            r.z_send.at[g, k - 1], r.z_recv.at[g, k - 1], here.at_plane(here.ahead(k)),
        )

    def start_planes(self, g):
        for k in range(1, self.planes):
            if g <= TWO:
                for m in range(4):

                    @pl.when(self.here.seq == m)
                    def _(m=m, k=k):
                        self.plane_copy(g, k, self.shards[g][m]).start()

            else:
                self.plane_copy(g, k, self.kinds[g].own(self.shards[g], self.here.seq)).start()

    def own_copies(self, g):
        here, r, full = self.here, self.r, self.full[g]
        if g <= TWO:
            return [
                pltpu.make_async_copy(
                    self.shards[g][m], full.at[m, here.plane, here.core], r.own_sem.at[g, m]
                )
                for m in range(4)
            ]
        return [
            pltpu.make_async_copy(
                self.shards[g], self.kinds[g].whole(full, here.plane, here.core), r.own_sem.at[g, 0]
            )
        ]

    def start_own(self, g):
        here, r, full = self.here, self.r, self.full[g]
        for copy in self.own_copies(g):
            copy.start()
        if g <= TWO:
            for m in range(4):
                self.send(
                    lambda m=m: (
                        self.shards[g][m], full.at[m, here.plane, here.core],
                        r.p_send.at[g, m], r.p_recv.at[g, m], here.partner,
                    )
                )
        else:
            self.send(
                lambda: (
                    self.shards[g], self.kinds[g].whole(full, here.plane, here.core),
                    r.p_send.at[g, 0], r.p_recv.at[g, 0], here.partner,
                )
            )

    def chunk(self, g, quarter, k, first=0, count=None):
        here = self.here
        return self.kinds[g].part(self.full[g], quarter, here.ahead(self.planes - k), here.core, first, count)

    def from_plane(self, g):
        here, r = self.here, self.r
        for k in range(1, self.planes):
            self.arrived(self.chunk(g, here.seq, k), r.z_recv.at[g, k - 1])
            for n, device in enumerate((here.to_x, here.to_y)):

                def make(k=k, n=n, device=device):
                    chunk = self.chunk(g, here.seq, k)
                    return chunk, chunk, r.x_send.at[n, g, k - 1], r.x_recv.at[n, g, k - 1], device

                self.send(make)

    def from_sides(self, g):
        here, r = self.here, self.r
        half = self.kinds[g].rows // 2
        turns = ((here.along_x, 0, here.to_y), (here.along_y, half, here.to_x))
        for k in range(1, self.planes):
            for n, (quarter, first, device) in enumerate(turns):
                self.arrived(self.chunk(g, quarter, k), r.x_recv.at[n, g, k - 1])

                def make(k=k, n=n, quarter=quarter, first=first, device=device):
                    chunk = self.chunk(g, quarter, k, first, half)
                    return chunk, chunk, r.d_send.at[n, g, k - 1], r.d_recv.at[n, g, k - 1], device

                self.send(make)

    def from_corner(self, g):
        here, r = self.here, self.r
        half = self.kinds[g].rows // 2
        for k in range(1, self.planes):
            self.arrived(self.chunk(g, here.corner, k, 0, half), r.d_recv.at[0, g, k - 1])
            self.arrived(self.chunk(g, here.corner, k, half, half), r.d_recv.at[1, g, k - 1])

            def make(k=k):
                whole = self.kinds[g].whole(self.full[g], here.ahead(self.planes - k), here.core)
                return whole, whole, r.c_send.at[g, k - 1], r.c_recv.at[g, k - 1], here.partner

            self.send(make)

    def complete(self, g):
        here, r, full = self.here, self.r, self.full[g]
        for copy in self.own_copies(g):
            copy.wait()
        if g <= TWO:
            for m in range(4):
                self.arrived(full.at[m, here.plane, 1 - here.core], r.p_recv.at[g, m])
        else:
            self.arrived(self.kinds[g].whole(full, here.plane, 1 - here.core), r.p_recv.at[g, 0])
        for k in range(1, self.planes):
            behind = here.ahead(self.planes - k)
            self.arrived(self.kinds[g].whole(full, behind, 1 - here.core), r.c_recv.at[g, k - 1])

    def end(self):
        for g in range(5):
            for k in range(1, self.planes):
                source = self.shards[g][0] if g <= TWO else self.kinds[g].own(self.shards[g], self.here.seq)
                self.plane_copy(g, k, source).wait_send()
        for make in self.started:
            remote(*make()).wait_send()


def forward_kernel(kinds, planes, layout, *refs):
    r = Space(layout, refs)
    bf16, f32 = jnp.bfloat16, jnp.float32
    here = Peers(planes)
    place, length = here.seq, r.length[0]
    gather = Gathering(kinds, here, r)
    rows, width = r.tokens.shape
    count, enc_count = r.normed.shape[0], r.encoded_rows.shape[0]
    row_ins = (r.tokens, r.encoded)
    row_alls = (r.source_rows, r.encoded_rows)
    stores = []

    def store(n, source, target):
        stores.append((n, source, target))
        pltpu.make_async_copy(source, target, r.store_sem.at[n]).start()

    def block_of(item, quarter, first=0, size=None):
        size_here = row_ins[item].shape[0]
        return row_alls[item].at[pl.ds(quarter * size_here + first, size or size_here), :]

    def rows_start(item):
        for n, device in enumerate((here.to_x, here.to_y)):
            gather.send(
                lambda n=n, device=device: (
                    row_ins[item], block_of(item, place), r.r_send.at[item, n], r.r_recv.at[item, n], device
                )
            )
        pltpu.make_async_copy(row_ins[item], block_of(item, place), r.r_own.at[item]).start()

    def rows_turn(item):
        half = row_ins[item].shape[0] // 2
        turns = ((here.along_x, 0, here.to_y), (here.along_y, half, here.to_x))
        for n, (quarter, first, device) in enumerate(turns):
            gather.arrived(block_of(item, quarter), r.r_recv.at[item, n])

            def make(n=n, quarter=quarter, first=first, device=device):
                chunk = block_of(item, quarter, first, half)
                return chunk, chunk, r.r_send.at[item, 2 + n], r.r_recv.at[item, 2 + n], device

            gather.send(make)

    def rows_done(item):
        half = row_ins[item].shape[0] // 2
        gather.arrived(block_of(item, here.corner, 0, half), r.r_recv.at[item, 2])
        gather.arrived(block_of(item, here.corner, half, half), r.r_recv.at[item, 3])
        pltpu.make_async_copy(row_ins[item], block_of(item, place), r.r_own.at[item]).wait()

    def norm_rows(values, gain):
        scale = lax.rsqrt(jnp.mean(values * values, axis=-1, keepdims=True) + EPSILON)
        return (values * scale * gain[...]).astype(bf16)

    def project(out, left, weight):
        across = weight.shape[1] // BLOCK

        @pl.loop(0, (left.shape[0] // BLOCK) * across)
        def _(n):
            first = pl.ds(pl.multiple_of((n // across) * BLOCK, BLOCK), BLOCK)
            second = pl.ds(pl.multiple_of((n % across) * BLOCK, BLOCK), BLOCK)
            out[first, second] = product(left[first, :], weight[:, second]).astype(out.dtype)

    here.meet()
    rows_start(0)
    gather.start_planes(ONE)
    rows_start(1)
    for g in (TWO, GATE_IN, UP_IN, DOWN_IN):
        gather.start_planes(g)
    for g in range(5):
        gather.start_own(g)
    fill_pads(r.pads, length)
    fill_fixed_bias(r.bias)
    rows_turn(0)
    gather.from_plane(ONE)
    rows_turn(1)
    rows_done(0)

    @row_steps(count)
    def _(part):
        r.normed[part, :] = norm_rows(r.source_rows[part, :].astype(f32), r.gain_one)

    store(0, r.source_rows, r.tokens_all)
    store(1, r.normed, r.normed_all)
    gather.from_sides(ONE)
    gather.from_plane(TWO)
    gather.from_corner(ONE)
    rows_done(1)
    store(2, r.encoded_rows, r.enc_all)
    gather.complete(ONE)
    store(3, r.weights_one, r.w_one)
    own = pl.ds(pl.multiple_of(place * rows, BLOCK), rows)
    project(r.query_rows, r.normed.at[own, :], r.weights_one.at[0])
    project(r.key_rows, r.normed, r.weights_one.at[1])
    project(r.value_rows, r.normed, r.weights_one.at[2])
    store(4, r.query_rows, r.queries)
    store(5, r.key_rows, r.keys)
    store(6, r.value_rows, r.values)
    gather.from_plane(GATE_IN)
    gather.from_sides(TWO)
    self_steps = {2: [lambda: gather.from_plane(UP_IN)], 4: [lambda: gather.from_corner(TWO)]}

    def stepped(table, pair):
        for when, steps in table.items():

            @pl.when(pair == when)
            def _(steps=steps):
                for step in steps:
                    step()

    @pl.loop(0, PAIRS)
    def _(pair):
        part = columns(pair)
        self_forward_pair(
            place, r.profile.at[pair], r.query_rows.at[:, part], r.key_rows.at[:, part],
            r.value_rows.at[:, part], r.mixed.at[:, part], r.turned_one.at[part, :], r.log_self.at[pair],
            r.pads, r.bias, r.s_buf, r.vt_buf,
        )
        stepped(self_steps, pair)

    store(7, r.turned_one, r.mixed_self_turned)
    project(r.hidden, r.mixed, r.weights_one.at[3])

    @row_steps(rows)
    def _(part):
        start = pl.multiple_of(place * rows + part.start, ROW_STEP)
        total = r.hidden[part, :] + r.source_rows[pl.ds(start, ROW_STEP), :].astype(f32)
        r.hidden[part, :] = total
        r.normed_rows[part, :] = norm_rows(total, r.gain_two)

    store(8, r.hidden, r.hidden_one)
    store(9, r.normed_rows, r.normed_two)
    gather.from_plane(DOWN_IN)
    gather.from_sides(GATE_IN)
    gather.complete(TWO)
    store(10, r.weights_two, r.w_two)
    project(r.cquery_rows, r.normed_rows, r.weights_two.at[0])
    project(r.ckey_rows, r.encoded_rows, r.weights_two.at[1])
    project(r.cvalue_rows, r.encoded_rows, r.weights_two.at[2])
    store(11, r.cquery_rows, r.cqueries)
    store(12, r.ckey_rows, r.ckeys)
    store(13, r.cvalue_rows, r.cvalues)
    cross_steps = {
        1: [lambda: gather.from_corner(GATE_IN)],
        3: [lambda: gather.from_sides(UP_IN)],
    }

    @pl.loop(0, PAIRS)
    def _(pair):
        part = columns(pair)
        cross_forward_pair(
            r.cquery_rows.at[:, part], r.ckey_rows.at[:, part], r.cvalue_rows.at[:, part],
            r.cmixed.at[:, part], r.turned_two.at[part, :], r.log_cross.at[pair],
        )
        stepped(cross_steps, pair)

    store(14, r.turned_two, r.mixed_cross_turned)
    gather.from_sides(DOWN_IN)
    project(r.hidden_last, r.cmixed, r.weights_two.at[3])

    @row_steps(rows)
    def _(part):
        total = r.hidden_last[part, :] + r.hidden[part, :]
        r.hidden_last[part, :] = total
        r.normed_last[part, :] = norm_rows(total, r.gain_three)

    store(15, r.hidden_last, r.hidden_two)
    store(16, r.normed_last, r.normed_three)
    gather.from_corner(UP_IN)
    gather.from_corner(DOWN_IN)
    for g in (GATE_IN, UP_IN, DOWN_IN):
        gather.complete(g)
    gather.end()
    for n, source, target in stores:
        pltpu.make_async_copy(source, target, r.store_sem.at[n]).wait()


def forward_fused(shards, length, tokens, encoded, small):
    kinds = make_kinds(shards)
    planes = lax.axis_size("fsdp") // 2
    f32, low = jnp.float32, jnp.bfloat16
    rows, width = tokens.shape
    enc_rows = encoded.shape[0]
    count, enc_count = 4 * rows, 4 * enc_rows
    square = (4, width, width)
    in_vmem = pl.BlockSpec(memory_space=pltpu.VMEM)
    in_layout, operands = flatten(
        dict(length=length), small, dict(tokens=tokens, encoded=encoded, shards=list(shards))
    )
    in_specs = [SCALARS] + [in_vmem] * len(small)
    in_specs += [ANYWHERE] * (len(operands) - len(in_specs))
    shapes = full_shapes(kinds, planes)
    large_outs = dict(
        w_one=shaped(square, low), w_two=shaped(square, low),
        ffn_full=[shaped(shape, low) for shape in shapes[2:]],
        tokens_all=shaped((count, width), low), normed_all=shaped((count, width), low),
        enc_all=shaped((enc_count, width), low),
        queries=shaped((rows, width), low), keys=shaped((count, width), low),
        values=shaped((count, width), low), mixed_self_turned=shaped((width, rows), f32),
        hidden_one=shaped((rows, width), f32), normed_two=shaped((rows, width), low),
        cqueries=shaped((rows, width), low), ckeys=shaped((enc_count, width), low),
        cvalues=shaped((enc_count, width), low), mixed_cross_turned=shaped((width, rows), f32),
        hidden_two=shaped((rows, width), f32), normed_three=shaped((rows, width), low),
    )
    small_outs = dict(
        log_self=shaped((PAIRS, 2, rows), f32), log_cross=shaped((PAIRS, 2, rows), f32)
    )
    out_layout, out_shapes = flatten(large_outs, small_outs)
    all_rows = pltpu.VMEM((count, width), low)
    enc_all = pltpu.VMEM((enc_count, width), low)
    some_rows = pltpu.VMEM((rows, width), low)
    wide_rows = pltpu.VMEM((rows, width), f32)
    turned = pltpu.VMEM((width, rows), f32)
    buffers = forward_scratch(count, rows)
    steps = planes - 1
    scratch = dict(
        weights_one=pltpu.VMEM(square, low), weights_two=pltpu.VMEM(square, low),
        source_rows=all_rows, normed=all_rows, key_rows=all_rows, value_rows=all_rows,
        encoded_rows=enc_all, ckey_rows=enc_all, cvalue_rows=enc_all,
        query_rows=some_rows, cquery_rows=some_rows, mixed=some_rows, cmixed=some_rows,
        normed_rows=some_rows, normed_last=some_rows,
        hidden=wide_rows, hidden_last=wide_rows, turned_one=turned, turned_two=turned,
        pads=buffers[0], bias=buffers[1], s_buf=buffers[2], vt_buf=buffers[3],
        z_send=DMA((5, steps)), z_recv=DMA((5, steps)),
        own_sem=DMA((5, 4)), p_send=DMA((5, 4)), p_recv=DMA((5, 4)),
        x_send=DMA((2, 5, steps)), x_recv=DMA((2, 5, steps)),
        d_send=DMA((2, 5, steps)), d_recv=DMA((2, 5, steps)),
        c_send=DMA((5, steps)), c_recv=DMA((5, steps)),
        r_send=DMA((2, 4)), r_recv=DMA((2, 4)), r_own=DMA((2,)), store_sem=DMA((17,)),
    )
    scratch_layout, scratch_shapes = flatten(scratch)
    outs = pl.pallas_call(
        functools.partial(forward_kernel, kinds, planes, in_layout | out_layout | scratch_layout),
        in_specs=in_specs,
        out_specs=[ANYWHERE] * (len(out_shapes) - 2) + [in_vmem] * 2,
        out_shape=out_shapes,
        scratch_shapes=scratch_shapes,
        compiler_params=pltpu.CompilerParams(
            collective_id=0, has_side_effects=True, vmem_limit_bytes=66_000_000
        ),
        name="forward_fused",
    )(*operands)
    return Space(out_layout, outs)


def local(
    tokens, encoded, lengths, cotangent, gain_self, gain_cross, gain_ff, bucket_table,
    self_query, self_key, self_value, self_out, cross_query, cross_key, cross_value, cross_out,
    ff_gate, ff_up, ff_down,
):
    rows_here = tokens.shape[1]
    seq_place = lax.axis_index("seq")
    length = lengths[0]
    bf16, f32 = jnp.bfloat16, jnp.float32
    gain_one = gain_self.astype(f32)
    gain_two = gain_cross.astype(f32)
    gain_three = gain_ff.astype(f32)
    shards = (
        self_query, self_key, self_value, self_out, cross_query, cross_key, cross_value, cross_out,
        ff_gate, ff_up, ff_down,
    )
    one_hot = (
        bucket_ids(BLOCK)[:, None] == jnp.arange(BUCKETS, dtype=jnp.int32)[None, :]
    ).astype(bf16)
    profile = inner_rows(bucket_table, one_hot.T).reshape(PAIRS, 2, BLOCK)
    place = jnp.stack([seq_place.astype(jnp.int32), length])

    source = tokens[0].astype(f32)
    fit = kernels_fit(shards)
    if fit:
        forward = forward_fused(
            shards, lengths, tokens[0], encoded[0],
            dict(
                profile=profile, gain_one=gain_one[None], gain_two=gain_two[None], gain_three=gain_three[None]
            ),
        )
        width = source.shape[1]
        hidden_two, normed_three = forward.hidden_two, forward.normed_three
        w_gate, w_up, w_down = (full.reshape(-1, full.shape[-1]) for full in forward.ffn_full)
    else:
        weights, tokens_all, enc_all = gather_plain(shards, tokens[0], encoded[0])
        (w_query, w_key, w_value, w_sout, w_cquery, w_ckey, w_cvalue, w_cout, w_gate, w_up, w_down) = weights
        normed_all = rms_scale(tokens_all.astype(f32), gain_one).astype(bf16)
        normed_one = rms_scale(source, gain_one).astype(bf16)
        queries = product(normed_one, w_query).astype(bf16)
        keys = product(normed_all, w_key).astype(bf16)
        values = product(normed_all, w_value).astype(bf16)
        mixed_self, mixed_self_turned, log_self = self_forward(place, profile, queries, keys, values)
        hidden_one = source + product(mixed_self, w_sout)
        normed_two = rms_scale(hidden_one, gain_two).astype(bf16)
        cqueries = product(normed_two, w_cquery).astype(bf16)
        ckeys = product(enc_all, w_ckey).astype(bf16)
        cvalues = product(enc_all, w_cvalue).astype(bf16)
        mixed_cross, mixed_cross_turned, log_cross = cross_forward(cqueries, ckeys, cvalues)
        hidden_two = hidden_one + product(mixed_cross, w_cout)
        normed_three = rms_scale(hidden_two, gain_three).astype(bf16)
    gate = product(normed_three, w_gate)
    up = product(normed_three, w_up)

    def gated(gate_rows, up_rows):
        return jax.nn.gelu(gate_rows, approximate=True) * up_rows

    activated_f, pull_gate = jax.vjp(gated, gate, up)
    activated = activated_f.astype(bf16)
    slot_ids = seq_place * rows_here + jnp.arange(rows_here, dtype=jnp.int32)
    valid = (slot_ids < length).astype(f32)[:, None]
    result = (valid * (hidden_two + product(activated, w_down))).astype(bf16)

    grad_result = valid * cotangent[0].astype(f32)
    branch_ff = grad_result.astype(bf16)
    grad_gate_f, grad_up_f = pull_gate(outer_rows(branch_ff, w_down))
    grad_gate = grad_gate_f.astype(bf16)
    grad_up = grad_up_f.astype(bf16)
    g_down = inner_rows(activated, branch_ff).astype(bf16)
    g_gate = inner_rows(normed_three, grad_gate).astype(bf16)
    g_up = inner_rows(normed_three, grad_up).astype(bf16)
    grad_three, grad_gain_three = norm_back(
        hidden_two, gain_three, outer_rows(grad_gate, w_gate) + outer_rows(grad_up, w_up)
    )
    grad_two = grad_result + grad_three
    if fit:
        one_hot_wide = jnp.pad(one_hot.astype(f32), ((0, 0), (0, PAIR - BUCKETS)))
        grads, grad_tokens, enc_sum, small = backward_fused(
            shards, lengths,
            dict(
                profile=profile, log_cross=forward.log_cross, log_self=forward.log_self,
                gain_one=gain_one[None], gain_two=gain_two[None], grad_gain_three=grad_gain_three[None],
                one_hot=one_hot_wide,
            ),
            dict(
                ffn_parts=[g_gate, g_up, g_down], w_one=forward.w_one, w_two=forward.w_two,
                grad_two_in=grad_two, mixed_cross_in=forward.mixed_cross_turned,
                cqueries_in=forward.cqueries, ckeys_in=forward.ckeys, cvalues_in=forward.cvalues,
                normed_two_in=forward.normed_two, enc_in=forward.enc_all, hidden_one_in=forward.hidden_one,
                mixed_self_in=forward.mixed_self_turned, queries_in=forward.queries, keys_in=forward.keys,
                values_in=forward.values, normed_all_in=forward.normed_all,
                tokens_all_in=forward.tokens_all,
            ),
        )
        table_sum = small[8 : 8 + HEADS, :BUCKETS].T
        return (
            result[None], grad_tokens[None], enc_sum[None], small[0], small[1], small[2], table_sum, *grads
        )
    branch_cross = grad_two.astype(bf16)
    g_cout = inner_rows(mixed_cross, branch_cross).astype(bf16)
    grad_mixed_cross = outer_rows(branch_cross, w_cout).astype(bf16)
    grad_cq, grad_ck, grad_cv = cross_backward(
        cqueries, ckeys, cvalues, grad_mixed_cross, mixed_cross_turned, log_cross
    )
    g_cquery = inner_rows(normed_two, grad_cq).astype(bf16)
    g_ckey = inner_rows(enc_all, grad_ck).astype(bf16)
    g_cvalue = inner_rows(enc_all, grad_cv).astype(bf16)
    enc_part = (outer_rows(grad_ck, w_ckey) + outer_rows(grad_cv, w_cvalue)).astype(bf16)
    grad_two_back, grad_gain_two = norm_back(hidden_one, gain_two, outer_rows(grad_cq, w_cquery))
    grad_one = grad_two + grad_two_back
    branch_self = grad_one.astype(bf16)
    g_sout = inner_rows(mixed_self, branch_self).astype(bf16)
    grad_mixed_self = outer_rows(branch_self, w_sout).astype(bf16)
    grad_q, grad_k, grad_v, near_part, far_part = self_backward(
        place, profile, queries, keys, values, grad_mixed_self, mixed_self_turned, log_self
    )
    g_query = inner_rows(normed_one, grad_q).astype(bf16)
    g_key = inner_rows(normed_all, grad_k).astype(bf16)
    g_value = inner_rows(normed_all, grad_v).astype(bf16)
    token_part = (outer_rows(grad_k, w_key) + outer_rows(grad_v, w_value)).astype(bf16)
    query_part = outer_rows(grad_q, w_query)

    near_rows = near_part.reshape(HEADS, BLOCK)
    far_rows = jnp.sum(far_part, axis=-1).reshape(HEADS)
    table_part = lax.dot_general(
        one_hot.astype(f32), near_rows, (((0,), (1,)), ((), ())),
        precision=lax.Precision.HIGHEST, preferred_element_type=f32,
    )
    table_part = table_part.at[BUCKETS - 1].add(far_rows)

    hat_all = rms_scale(tokens_all.astype(f32), jnp.ones_like(gain_one))
    hat_one = rms_scale(source, jnp.ones_like(gain_one))
    grad_gain_one = jnp.sum(token_part.astype(f32) * hat_all, axis=0) + jnp.sum(
        query_part * hat_one, axis=0
    )
    table_row = jnp.zeros((gain_one.shape[0],), f32).at[: BUCKETS * HEADS].set(table_part.reshape(-1))
    small = jnp.stack([grad_gain_one, grad_gain_two, grad_gain_three, table_row] + [jnp.zeros_like(gain_one)] * 4)
    reduced, token_sum, enc_sum, small = reduce_plain(
        (g_query, g_key, g_value, g_sout, g_cquery, g_ckey, g_cvalue, g_cout, g_gate, g_up, g_down),
        token_part, enc_part, small,
    )
    grad_zero, _ = norm_back(source, gain_one, query_part + token_sum)
    grad_tokens = grad_one + grad_zero
    table_sum = small[3, : BUCKETS * HEADS].reshape(BUCKETS, HEADS)
    small = (small[0], small[1], small[2], table_sum)
    return (result[None], grad_tokens[None], enc_sum[None], *small, *reduced)


def solution(mesh):
    rows3 = P("fsdp", "seq", None)
    rows2 = P("fsdp", None)
    return jax.shard_map(
        local,
        mesh=mesh,
        in_specs=(rows3, rows3, P("fsdp"), rows3, P(), P(), P(), P(), *([rows2] * 11)),
        out_specs=(rows3, rows3, rows3, P(), P(), P(), P(), *([rows2] * 11)),
        check_vma=False,
    )
```

```python
import functools
import math

import jax
import jax.numpy as jnp
from jax import lax
from jax.experimental import pallas as pl
from jax.experimental.pallas import tpu as pltpu
from jax.sharding import PartitionSpec as P

HEADS = 12
HEAD = 64
BUCKETS = 32
MAX_DISTANCE = 128
EPSILON = 1e-06
NEGATIVE = -1e30
BLOCK = 256
PAIR = 2 * HEAD
MESH = pl.DeviceIdType.MESH


def thresholds():
    exact_limit = BUCKETS // 2
    return [
        int(math.ceil(exact_limit * (MAX_DISTANCE / exact_limit) ** (number / exact_limit)))
        for number in range(1, exact_limit)
    ]


def bucket_ids(key_count):
    exact_limit = BUCKETS // 2
    offsets = jnp.arange(key_count, dtype=jnp.int32)
    passed = jnp.zeros((key_count,), jnp.int32)
    for border in thresholds():
        passed = passed + (offsets >= border).astype(jnp.int32)
    return jnp.where(offsets < exact_limit, offsets, exact_limit + passed)


def rms_scale(values, gain):
    return values * lax.rsqrt(jnp.mean(values * values, axis=-1, keepdims=True) + EPSILON) * gain


def norm_back(values, gain, grad_normed):
    _, pullback = jax.vjp(rms_scale, values, gain)
    return pullback(grad_normed)


def product(left, right):
    return jnp.dot(left, right, preferred_element_type=jnp.float32)


def inner_rows(left, right):
    return lax.dot_general(
        left, right, (((0,), (0,)), ((), ())), preferred_element_type=jnp.float32
    )


def outer_rows(left, right):
    return lax.dot_general(
        left, right, (((1,), (1,)), ((), ())), preferred_element_type=jnp.float32
    )


def iota(shape, axis):
    return lax.broadcasted_iota(jnp.int32, shape, axis)


def head_rows(value, head):
    place = iota(value.shape, 0) // HEAD
    return jnp.where(place == head, value, jnp.zeros_like(value))


def head_cols(value, head):
    place = iota(value.shape, 1) // HEAD
    return jnp.where(place == head, value, jnp.zeros_like(value))


def skew(profile_row):
    wide = jnp.broadcast_to(profile_row, (BLOCK, BLOCK))
    return pltpu.roll(wide, 0, 1, stride=1, stride_axis=0)


def unskew(tile):
    rows = iota(tile.shape, 0)
    bit = 1
    while bit < BLOCK:
        tile = jnp.where((rows // bit) % 2 == 1, pltpu.roll(tile, BLOCK - bit, 1), tile)
        bit *= 2
    return tile


def fill_pads(pads, length):
    rows = pads.shape[1]
    lanes = iota((BLOCK, PAIR), 1)

    @pl.loop(0, rows // BLOCK)
    def _(n):
        start = pl.multiple_of(n * BLOCK, BLOCK)
        beyond = iota((BLOCK, PAIR), 0) >= length - start
        for head in range(2):
            first = (1 - head) * HEAD
            ones = jnp.where((lanes > first) & (lanes <= first + 3), 1.0, 0.0)
            pads[head, pl.ds(start, BLOCK), :] = jnp.where(
                (lanes == first) & beyond, NEGATIVE, ones
            ).astype(jnp.bfloat16)


def padded(value, pads, head, start):
    own = iota(value.shape, 1) // HEAD == head
    return jnp.where(own, value, pads[head, start : start + value.shape[0], :])


def split_low(value):
    first = value.astype(jnp.bfloat16).astype(jnp.float32)
    rest = value - first
    second = rest.astype(jnp.bfloat16).astype(jnp.float32)
    return first, second, rest - second


def with_terms(turned, head, mask_term, terms):
    place = iota(turned.shape, 0)
    first = (1 - head) * HEAD
    value = jnp.where(place // HEAD == head, turned.astype(jnp.float32), 0.0)
    value = jnp.where(place == first, mask_term, value)
    for n, term in enumerate(terms):
        value = jnp.where(place == first + 1 + n, term, value)
    return value.astype(jnp.bfloat16)


HIDDEN, DIAGONAL, NEAR, FAR = range(4)


def fill_fixed_bias(bias):
    for head in range(2):
        bias[head, HIDDEN] = jnp.full((BLOCK, BLOCK), NEGATIVE, jnp.float32)
        bias[head, FAR] = jnp.zeros((BLOCK, BLOCK), jnp.float32)


def fill_near_bias(bias, profile_ref):
    later = iota((BLOCK, BLOCK), 1) >= iota((BLOCK, BLOCK), 0)
    for head in range(2):
        profile = profile_ref[head : head + 1, :]
        near = skew(profile - profile[:, BLOCK - 1 :])
        bias[head, DIAGONAL] = jnp.where(later, near, NEGATIVE)
        bias[head, NEAR] = jnp.where(later, 0.0, near)


def bias_kind(place, block):
    return jnp.clip(place - block, -1, 2) + 1


def self_forward_pair(place, profile_ref, q_ref, k_ref, v_ref, o_ref, ot_ref, log_ref, pads, bias, s_buf, vt_buf):
    qt = q_ref[...].T
    vt_buf[...] = v_ref[...].T
    fill_near_bias(bias, profile_ref)
    blocks = k_ref.shape[0] // BLOCK
    tops = []
    for head in range(2):
        far = profile_ref[head : head + 1, BLOCK - 1 :]
        queries = with_terms(qt, head, 1.0, (far,))
        top = None
        for block in range(blocks):
            start = block * BLOCK
            keys = padded(k_ref[start : start + BLOCK, :], pads, head, start)
            scores = product(keys, queries) + bias[head, bias_kind(place, block)]
            s_buf[head, start : start + BLOCK, :] = scores
            most = jnp.max(scores, axis=0, keepdims=True)
            top = most if top is None else jnp.maximum(top, most)
        tops.append(top)
    totals = []
    for head in range(2):
        total = None
        for block in range(blocks):
            part = slice(block * BLOCK, (block + 1) * BLOCK)
            raised = jnp.exp(s_buf[head, part, :] - tops[head])
            s_buf[head, part, :] = raised
            amount = jnp.sum(raised, axis=0, keepdims=True)
            total = amount if total is None else total + amount
        totals.append(total)
    for head in range(2):
        rows = slice(head * HEAD, (head + 1) * HEAD)
        scale, mixed = 1.0 / totals[head], None
        for block in range(blocks):
            part = slice(block * BLOCK, (block + 1) * BLOCK)
            soft = (s_buf[head, part, :] * scale).astype(jnp.bfloat16)
            share = product(vt_buf[rows, part], soft)
            mixed = share if mixed is None else mixed + share
        ot_ref[rows, :] = mixed
        log_ref[head : head + 1, :] = tops[head] + jnp.log(totals[head])
    o_ref[...] = ot_ref[...].T.astype(jnp.bfloat16)


def self_forward_kernel(place_ref, profile_ref, q_ref, k_ref, v_ref, o_ref, ot_ref, log_ref, pads, bias, s_buf, vt_buf):
    @pl.when(pl.program_id(0) == 0)
    def _():
        fill_pads(pads, place_ref[1])
        fill_fixed_bias(bias)

    self_forward_pair(
        place_ref[0], profile_ref.at[0], q_ref, k_ref, v_ref, o_ref, ot_ref, log_ref.at[0],
        pads, bias, s_buf, vt_buf,
    )


def cross_forward_pair(q_ref, k_ref, v_ref, o_ref, ot_ref, log_ref):
    qt = q_ref[...].T
    vt = v_ref[...].T
    all_scores = [product(k_ref[...], head_rows(qt, head)) for head in range(2)]
    for head, scores in enumerate(all_scores):
        top = jnp.max(scores, axis=0, keepdims=True)
        raised = jnp.exp(scores - top)
        total = jnp.sum(raised, axis=0, keepdims=True)
        soft = (raised * (1.0 / total)).astype(jnp.bfloat16)
        ot_ref[head * HEAD : (head + 1) * HEAD, :] = product(vt[head * HEAD : (head + 1) * HEAD, :], soft)
        log_ref[head : head + 1, :] = top + jnp.log(total)
    o_ref[...] = ot_ref[...].T.astype(jnp.bfloat16)


def cross_forward_kernel(q_ref, k_ref, v_ref, o_ref, ot_ref, log_ref):
    cross_forward_pair(q_ref, k_ref, v_ref, o_ref, ot_ref, log_ref.at[0])


EXTRA = 16


def backward_pair(
    place, profile_ref, q_ref, k_ref, v_ref, g_ref, ot_ref, log_ref, dq_ref, dk_ref, dv_ref,
    near_ref, far_ref, pads, bias, kt_buf, grad_buf,
):
    q_value = q_ref[...]
    g_value = g_ref[...]
    qt = q_value.T
    gt = g_value.T
    kt = k_ref[...].T
    keys_count = k_ref.shape[0]
    ones = jnp.ones((EXTRA, keys_count), jnp.bfloat16)
    for head in range(2):
        kt_buf[head, 0:HEAD, 0:keys_count] = kt[head * HEAD : (head + 1) * HEAD, :]
        kt_buf[head, HEAD : HEAD + EXTRA, 0:keys_count] = ones
    both_q = jnp.concatenate([head_cols(q_value, 0), head_cols(q_value, 1)], axis=0)
    both_g = jnp.concatenate([head_cols(g_value, 0), head_cols(g_value, 1)], axis=0)
    weighted = gt.astype(jnp.float32) * ot_ref[...]
    if profile_ref is not None:
        fill_near_bias(bias, profile_ref)
    queries, grads_out = [], []
    for head in range(2):
        rows = slice(head * HEAD, (head + 1) * HEAD)
        delta = jnp.sum(weighted[rows, :], axis=0, keepdims=True)
        constant = -log_ref[head : head + 1, :]
        if profile_ref is not None:
            constant = constant + profile_ref[head : head + 1, BLOCK - 1 :]
        queries.append(with_terms(qt, head, 1.0, split_low(constant)))
        grads_out.append(with_terms(gt, head, 0.0, split_low(-delta)))
    sums = [None, None]
    for start in range(0, keys_count, BLOCK):
        k_block = k_ref[start : start + BLOCK, :]
        v_block = v_ref[start : start + BLOCK, :]
        softs, grads = [], []
        for head in range(2):
            scores = product(padded(k_block, pads, head, start), queries[head])
            if profile_ref is not None:
                scores = scores + bias[head, bias_kind(place, start // BLOCK)]
            soft = jnp.exp(scores)
            change = product(padded(v_block, pads, head, start), grads_out[head])
            grad = (soft * change).astype(jnp.bfloat16)
            softs.append(soft.astype(jnp.bfloat16))
            grads.append(grad)
            if profile_ref is not None:
                grad_buf[head, start // BLOCK] = grad
            share = product(kt_buf[head, :, start : start + BLOCK], grad)
            sums[head] = share if sums[head] is None else sums[head] + share
        dv_ref[start : start + BLOCK, :] = product(jnp.concatenate(softs, axis=1), both_g).astype(
            jnp.bfloat16
        )
        dk_ref[start : start + BLOCK, :] = product(jnp.concatenate(grads, axis=1), both_q).astype(
            jnp.bfloat16
        )
    turned = jnp.concatenate([sums[0][0:HEAD, :], sums[1][0:HEAD, :]], axis=0)
    dq_ref[...] = turned.T.astype(jnp.bfloat16)
    if profile_ref is not None:
        later = iota((BLOCK, BLOCK), 1) >= iota((BLOCK, BLOCK), 0)
        for head in range(2):
            diagonal = grad_buf[head, place].astype(jnp.float32)
            before = grad_buf[head, jnp.maximum(place - 1, 0)].astype(jnp.float32)
            before = jnp.where(place >= 1, before, 0.0)
            near = jnp.sum(unskew(jnp.where(later, diagonal, before)), axis=0, keepdims=True)
            near_ref[head : head + 1, :] = near
            far_ref[head : head + 1, :] = sums[head][HEAD : HEAD + 1, :] - near


def self_backward_kernel(
    place_ref, profile_ref, q_ref, k_ref, v_ref, g_ref, ot_ref, log_ref,
    dq_ref, dk_ref, dv_ref, near_ref, far_ref, pads, bias, kt_buf, grad_buf,
):
    @pl.when(pl.program_id(0) == 0)
    def _():
        fill_pads(pads, place_ref[1])
        fill_fixed_bias(bias)

    backward_pair(
        place_ref[0], profile_ref.at[0], q_ref, k_ref, v_ref, g_ref, ot_ref, log_ref.at[0],
        dq_ref, dk_ref, dv_ref, near_ref.at[0], far_ref.at[0], pads, bias, kt_buf, grad_buf,
    )


def cross_backward_kernel(q_ref, k_ref, v_ref, g_ref, ot_ref, log_ref, dq_ref, dk_ref, dv_ref, pads, kt_buf):
    @pl.when(pl.program_id(0) == 0)
    def _():
        fill_pads(pads, pads.shape[1])

    backward_pair(
        None, None, q_ref, k_ref, v_ref, g_ref, ot_ref, log_ref.at[0], dq_ref, dk_ref, dv_ref,
        None, None, pads, None, kt_buf, None,
    )


def forward_scratch(count, rows):
    return [
        pltpu.VMEM((2, count, PAIR), jnp.bfloat16),
        pltpu.VMEM((2, 4, BLOCK, BLOCK), jnp.float32),
        pltpu.VMEM((2, count, rows), jnp.float32),
        pltpu.VMEM((PAIR, count), jnp.bfloat16),
    ]


def backward_scratch(count):
    return [
        pltpu.VMEM((2, count, PAIR), jnp.bfloat16),
        pltpu.VMEM((2, 4, BLOCK, BLOCK), jnp.float32),
        pltpu.VMEM((2, HEAD + EXTRA, count), jnp.bfloat16),
        pltpu.VMEM((2, count // BLOCK, BLOCK, BLOCK), jnp.bfloat16),
    ]


def pair_block(rows):
    return pl.BlockSpec((rows, PAIR), lambda pair: (0, pair))


def turned_block(rows):
    return pl.BlockSpec((PAIR, rows), lambda pair: (pair, 0))


def head_block(width):
    return pl.BlockSpec((1, 2, width), lambda pair: (pair, 0, 0))


SCALARS = pl.BlockSpec(memory_space=pltpu.SMEM)
PAIRS = HEADS // 2


def shaped(shape, dtype):
    return jax.ShapeDtypeStruct(shape, dtype)


def self_forward(place, profile, queries, keys, values):
    rows, width = queries.shape
    count = keys.shape[0]
    return pl.pallas_call(
        self_forward_kernel,
        grid=(PAIRS,),
        in_specs=[SCALARS, head_block(BLOCK), pair_block(rows), pair_block(count), pair_block(count)],
        out_specs=[pair_block(rows), turned_block(rows), head_block(rows)],
        out_shape=[
            shaped((rows, width), jnp.bfloat16),
            shaped((width, rows), jnp.float32),
            shaped((PAIRS, 2, rows), jnp.float32),
        ],
        scratch_shapes=forward_scratch(count, rows),
        name="self_forward",
    )(place, profile, queries, keys, values)


def cross_forward(queries, keys, values):
    rows, width = queries.shape
    count = keys.shape[0]
    return pl.pallas_call(
        cross_forward_kernel,
        grid=(PAIRS,),
        in_specs=[pair_block(rows), pair_block(count), pair_block(count)],
        out_specs=[pair_block(rows), turned_block(rows), head_block(rows)],
        out_shape=[
            shaped((rows, width), jnp.bfloat16),
            shaped((width, rows), jnp.float32),
            shaped((PAIRS, 2, rows), jnp.float32),
        ],
        name="cross_forward",
    )(queries, keys, values)


def self_backward(place, profile, queries, keys, values, grad_mixed, mixed_turned, log_totals):
    rows, width = queries.shape
    count = keys.shape[0]
    return pl.pallas_call(
        self_backward_kernel,
        grid=(PAIRS,),
        in_specs=[
            SCALARS, head_block(BLOCK), pair_block(rows), pair_block(count), pair_block(count),
            pair_block(rows), turned_block(rows), head_block(rows),
        ],
        out_specs=[
            pair_block(rows), pair_block(count), pair_block(count), head_block(BLOCK), head_block(rows),
        ],
        out_shape=[
            shaped((rows, width), jnp.bfloat16),
            shaped((count, width), jnp.bfloat16),
            shaped((count, width), jnp.bfloat16),
            shaped((PAIRS, 2, BLOCK), jnp.float32),
            shaped((PAIRS, 2, rows), jnp.float32),
        ],
        scratch_shapes=backward_scratch(count),
        name="self_backward",
    )(place, profile, queries, keys, values, grad_mixed, mixed_turned, log_totals)


def cross_backward(queries, keys, values, grad_mixed, mixed_turned, log_totals):
    rows, width = queries.shape
    count = keys.shape[0]
    return pl.pallas_call(
        cross_backward_kernel,
        grid=(PAIRS,),
        in_specs=[
            pair_block(rows), pair_block(count), pair_block(count),
            pair_block(rows), turned_block(rows), head_block(rows),
        ],
        out_specs=[pair_block(rows), pair_block(count), pair_block(count)],
        out_shape=[
            shaped((rows, width), jnp.bfloat16),
            shaped((count, width), jnp.bfloat16),
            shaped((count, width), jnp.bfloat16),
        ],
        scratch_shapes=[
            pltpu.VMEM((2, count, PAIR), jnp.bfloat16),
            pltpu.VMEM((2, HEAD + EXTRA, count), jnp.bfloat16),
        ],
        name="cross_backward",
    )(queries, keys, values, grad_mixed, mixed_turned, log_totals)


class Peers:
    def __init__(self, planes):
        self.seq = lax.axis_index("seq")
        fsdp = lax.axis_index("fsdp")
        self.planes = planes
        self.plane = fsdp // 2
        self.core = fsdp % 2
        self.fsdp = fsdp
        self.along_x = self.seq + 1 - 2 * (self.seq % 2)
        self.along_y = (self.seq + 2) % 4
        self.corner = (self.along_x + 2) % 4
        self.partner = (self.seq, fsdp + 1 - 2 * self.core)
        self.to_x = (self.along_x, fsdp)
        self.to_y = (self.along_y, fsdp)
        self.to_corner = (self.corner, fsdp)

    def ahead(self, steps):
        return (self.plane + steps) % self.planes

    def at_plane(self, plane):
        return (self.seq, 2 * plane + self.core)

    def everyone(self):
        return [self.partner, self.to_x, self.to_y, self.to_corner] + [
            self.at_plane(self.ahead(k)) for k in range(1, self.planes)
        ]

    def meet(self):
        barrier = pltpu.get_barrier_semaphore()
        others = self.everyone()
        for other in others:
            pl.semaphore_signal(barrier, inc=1, device_id=other, device_id_type=MESH)
        pl.semaphore_wait(barrier, len(others))


def remote(source, target, send_sem, recv_sem, device):
    return pltpu.make_async_remote_copy(
        src_ref=source, dst_ref=target, send_sem=send_sem, recv_sem=recv_sem,
        device_id=device, device_id_type=MESH,
    )


class Stack:
    def __init__(self, rows, cols):
        self.rows, self.cols = rows, cols

    def own(self, ref, quarter, first=0, count=None):
        return ref.at[quarter, pl.ds(first, count or self.rows), :]

    def part(self, ref, quarter, plane, core, first=0, count=None):
        return ref.at[quarter, plane, core, pl.ds(first, count or self.rows), :]

    def planes(self, ref, quarter, core):
        return ref.at[quarter, :, core]

    def whole(self, ref, plane, core):
        return ref.at[:, plane, core]


class Wide:
    def __init__(self, rows, cols):
        self.rows, self.cols = rows, cols

    def own(self, ref, quarter, first=0, count=None):
        return ref.at[pl.ds(first, count or self.rows), pl.ds(quarter * self.cols, self.cols)]

    def part(self, ref, quarter, plane, core, first=0, count=None):
        return ref.at[
            plane, core, pl.ds(first, count or self.rows), pl.ds(quarter * self.cols, self.cols)
        ]

    def planes(self, ref, quarter, core):
        return ref.at[:, core, :, pl.ds(quarter * self.cols, self.cols)]

    def whole(self, ref, plane, core):
        return ref.at[plane, core]


class Tall:
    def __init__(self, rows, cols):
        self.rows, self.cols = rows, cols

    def own(self, ref, quarter, first=0, count=None):
        return ref.at[pl.ds(quarter * self.rows + first, count or self.rows), :]

    def part(self, ref, quarter, plane, core, first=0, count=None):
        return ref.at[plane, core, pl.ds(quarter * self.rows + first, count or self.rows), :]

    def planes(self, ref, quarter, core):
        return ref.at[:, core, pl.ds(quarter * self.rows, self.rows), :]

    def whole(self, ref, plane, core):
        return ref.at[plane, core]


def full_shapes(kinds, planes, cores=2):
    shapes = []
    for kind in kinds:
        if isinstance(kind, Stack):
            shapes.append((4, planes, cores, kind.rows, kind.cols))
        elif isinstance(kind, Wide):
            shapes.append((planes, cores, kind.rows, 4 * kind.cols))
        else:
            shapes.append((planes, cores, 4 * kind.rows, kind.cols))
    return shapes


ANYWHERE = pl.BlockSpec(memory_space=pl.ANY)
DMA = pltpu.SemaphoreType.DMA


def make_kinds(shards):
    square, wide, down = shards[0], shards[8], shards[10]
    stack = Stack(*square.shape)
    band = Wide(wide.shape[0], wide.shape[1] // 4)
    tall = Tall(down.shape[0] // 4, down.shape[1])
    return [stack, stack, band, band, tall]


def kernels_fit(shards):
    kinds = make_kinds(shards)
    return (
        lax.axis_size("seq") == 4
        and lax.axis_size("fsdp") == 8
        and all(kind.rows % 32 == 0 and kind.cols % 128 == 0 for kind in kinds)
    )


def gather_plain(shards, tokens, encoded):
    full = [lax.all_gather(shard, "fsdp", axis=0, tiled=True) for shard in shards]
    return (
        full,
        lax.all_gather(tokens, "seq", axis=0, tiled=True),
        lax.all_gather(encoded, "seq", axis=0, tiled=True),
    )


def add_low(target, *terms):
    total = target[...].astype(jnp.float32)
    for term in terms:
        total = total + term[...].astype(jnp.float32)
    target[...] = total.astype(jnp.bfloat16)


def reduce_plain(grads, token_part, enc_part, small):
    def sums(value):
        return lax.psum_scatter(value.astype(jnp.float32), "seq", scatter_dimension=0, tiled=True)

    reduced = [
        lax.psum(
            lax.psum_scatter(grad.astype(jnp.float32), "fsdp", scatter_dimension=0, tiled=True), "seq"
        )
        for grad in grads
    ]
    return reduced, sums(token_part), sums(enc_part), lax.psum(small, ("seq", "fsdp"))


def columns(pair):
    return pl.ds(pl.multiple_of(pair * PAIR, PAIR), PAIR)


def row_steps(count, step):
    def run(body):
        @pl.loop(0, count // step)
        def _(n):
            body(pl.ds(pl.multiple_of(n * step, step), step))

    return run


def weight_grad(out, left, right):
    @row_steps(out.shape[0], 384)
    def _(part):
        out[part, :] = inner_rows(left[:, part], right[...]).astype(jnp.bfloat16)


def weight_grad_turned(out, turned, right):
    @row_steps(out.shape[0], 384)
    def _(part):
        out[part, :] = product(turned[part, :].astype(jnp.bfloat16), right[...]).astype(jnp.bfloat16)


def norm_back_rows(values, gain, grad_normed):
    scale = lax.rsqrt(jnp.mean(values * values, axis=-1, keepdims=True) + EPSILON)
    scaled = grad_normed * gain
    along = jnp.mean(values * scaled, axis=-1, keepdims=True)
    grad_values = scale * scaled - values * (scale * scale * scale) * along
    return grad_values, jnp.sum(grad_normed * values * scale, axis=0, keepdims=True)


class Space:
    def __init__(self, layout, refs):
        refs = list(refs)
        for name, count in layout.items():
            value = refs.pop(0) if count is None else [refs.pop(0) for _ in range(count)]
            setattr(self, name, value)


def flatten(*tables):
    layout, flat = {}, []
    for table in tables:
        for name, value in table.items():
            many = isinstance(value, list)
            layout[name] = len(value) if many else None
            flat += value if many else [value]
    return layout, flat


class StackRows(Stack):
    def __init__(self, first, rows, cols):
        super().__init__(rows, cols)
        self.first = first

    def planes(self, ref, quarter, core):
        return ref.at[quarter, :, core, pl.ds(self.first, self.rows), :]


DOWN, GATE, UP, CROSS, SELF, SELF_REST = range(6)
GROUPS = 6


class Sum:
    planes_first = False

    def __init__(self, g, kind, here, r, part):
        self.g, self.kind, self.here, self.r = g, kind, here, r
        self.part = part
        self.planes = here.planes
        self.sums, self.final = r.sums[g], r.final[g]
        self.side_x, self.side_y, self.last, self.from_z = r.side_x[g], r.side_y[g], r.last[g], r.from_z[g]
        self.started = []

    def send(self, make):
        remote(*make()).start()
        self.started.append(make)

    def arrived(self, target, recv_sem):
        pltpu.make_async_copy(target, target, recv_sem).wait()

    def pair_source(self, n, core):
        return self.kind.planes(self.part, n, core), self.sums.at[n]

    def start_pair(self, n):
        r, g = self.r, self.g
        source, target = self.pair_source(n, 1 - self.here.core)
        remote(source, target, r.c_send.at[g, n], r.c_recv.at[g, n], self.here.partner).start()

    def pair_sum(self):
        for n in range(4):
            source, target = self.pair_source(n, self.here.core)
            self.arrived(target, self.r.c_recv.at[self.g, n])

            @pl.loop(0, 4)
            def _(m, n=n, source=source, target=target):
                add_low(target.at[m], source.at[m])

    def pair_sent(self):
        for n in range(4):
            source, target = self.pair_source(n, 1 - self.here.core)
            remote(
                source, target, self.r.c_send.at[self.g, n], self.r.c_recv.at[self.g, n], self.here.partner
            ).wait_send()

    def half(self, quarter, second):
        size = self.planes // 2
        return self.sums.at[quarter, pl.ds(second * size, size)]

    def sides(self):
        r, g, here = self.r, self.g, self.here
        for n, quarter in enumerate((here.along_x, here.corner)):
            self.send(
                lambda n=n, quarter=quarter: (
                    self.half(quarter, 0), self.side_x.at[n], r.a_send.at[g, n], r.a_recv.at[g, n], here.to_x
                )
            )
        for n, quarter in enumerate((here.along_y, here.corner)):
            self.send(
                lambda n=n, quarter=quarter: (
                    self.half(quarter, 1), self.side_y.at[n],
                    r.a_send.at[g, 2 + n], r.a_recv.at[g, 2 + n], here.to_y,
                )
            )

    def add_half(self, quarter, second, terms, out=None):
        size = self.planes // 2

        @pl.loop(0, size)
        def _(z):
            add_low(self.sums.at[quarter, second * size + z], *[term.at[z] for term in terms])

    def first_side(self):
        r, g, here = self.r, self.g, self.here
        for n in range(2):
            self.arrived(self.side_x.at[n], r.a_recv.at[g, n])
            self.arrived(self.side_y.at[n], r.a_recv.at[g, 2 + n])
        self.add_half(here.along_y, 0, [self.side_x.at[1]])
        self.add_half(here.along_x, 1, [self.side_y.at[1]])
        for n, (quarter, device) in enumerate(((here.along_y, here.to_y), (here.along_x, here.to_x))):
            self.send(
                lambda n=n, quarter=quarter, device=device: (
                    self.half(quarter, n), self.last.at[n], r.b_send.at[g, n], r.b_recv.at[g, n], device
                )
            )

    def second_side(self):
        r, g, here = self.r, self.g, self.here
        for n in range(2):
            self.arrived(self.last.at[n], r.b_recv.at[g, n])
        self.add_half(here.seq, 0, [self.side_x.at[0], self.last.at[0]])
        self.add_half(here.seq, 1, [self.side_y.at[0], self.last.at[1]])
        self.after_square()

    def after_square(self):
        self.start_planes()

    def plane_share(self, plane):
        return self.sums.at[self.here.seq, plane]

    def start_planes(self):
        r, g, here = self.r, self.g, self.here
        for k in range(1, self.planes):
            self.send(
                lambda k=k: (
                    self.plane_share(here.ahead(k)), self.from_z.at[k - 1],
                    r.z_send.at[g, k - 1], r.z_recv.at[g, k - 1], here.at_plane(here.ahead(k)),
                )
            )

    def along_planes(self):
        r, g, here = self.r, self.g, self.here
        for k in range(1, self.planes):
            self.arrived(self.from_z.at[k - 1], r.z_recv.at[g, k - 1])
        step = 16

        @pl.loop(0, self.kind.rows // step)
        def _(n):
            rows = pl.ds(pl.multiple_of(n * step, step), step)
            total = self.sums[here.seq, here.plane, rows, :].astype(jnp.float32)
            for k in range(1, self.planes):
                total = total + self.from_z[k - 1, rows, :].astype(jnp.float32)
            self.final[here.seq, rows, :] = total.astype(jnp.bfloat16)

        self.start_spread()

    def start_spread(self):
        r, g, here = self.r, self.g, self.here
        for n, device in enumerate((here.to_x, here.to_y)):
            self.send(
                lambda n=n, device=device: (
                    self.final.at[here.seq], self.final.at[here.seq], r.g_send.at[g, n], r.g_recv.at[g, n], device
                )
            )

    def across(self, quarter, second):
        size = self.kind.cols // 2
        return self.final.at[quarter, :, pl.ds(second * size, size)]

    def spread(self):
        r, g, here = self.r, self.g, self.here
        for n, (quarter, device) in enumerate(((here.along_x, here.to_y), (here.along_y, here.to_x))):
            self.arrived(self.final.at[quarter], r.g_recv.at[g, n])
            self.send(
                lambda n=n, quarter=quarter, device=device: (
                    self.across(quarter, n), self.across(quarter, n),
                    r.g_send.at[g, 2 + n], r.g_recv.at[g, 2 + n], device,
                )
            )

    def out_copies(self):
        r, g, kind = self.r, self.g, self.kind
        if isinstance(kind, Wide):
            return [
                pltpu.make_async_copy(
                    self.final.at[q], r.out[g].at[:, pl.ds(q * kind.cols, kind.cols)], r.out_sem.at[g, q]
                )
                for q in range(4)
            ]
        out = r.out[min(g, SELF)]
        if isinstance(kind, StackRows):
            out = out.at[:, pl.ds(kind.first, kind.rows), :]
        return [pltpu.make_async_copy(self.final, out, r.out_sem.at[g, 0])]

    def finish(self):
        r, g, here = self.r, self.g, self.here
        for n in range(2):
            self.arrived(self.across(here.corner, n), r.g_recv.at[g, 2 + n])
        for copy in self.out_copies():
            copy.start()

    def end(self):
        for copy in self.out_copies():
            copy.wait()
        if self.g not in (DOWN, CROSS):
            self.pair_sent()
        for make in self.started:
            remote(*make()).wait_send()


class PlanesFirst(Sum):
    planes_first = True

    def pair_source(self, n, core):
        return self.part.at[n, core], self.sums.at[:, n]

    def half(self, quarter, second):
        size = self.kind.cols // 2
        return self.sums.at[quarter, self.here.plane, :, pl.ds(second * size, size)]

    def plane_share(self, plane):
        return self.sums.at[:, plane]

    def along_planes(self):
        r, g, here = self.r, self.g, self.here
        for k in range(1, self.planes):
            self.arrived(self.from_z.at[k - 1], r.z_recv.at[g, k - 1])

        @pl.loop(0, 4)
        def _(q):
            add_low(self.sums.at[q, here.plane], *[self.from_z.at[k - 1, q] for k in range(1, self.planes)])

        self.sides()

    def add_half(self, quarter, second, terms, out=None):
        size = self.kind.cols // 2
        add_low(self.half(quarter, second), *terms)

    def after_square(self):
        self.final[self.here.seq] = self.sums[self.here.seq, self.here.plane]
        self.start_spread()


class BandSum(Sum):
    def pair_source(self, n, core):
        return self.part.at[n, :, core], self.sums.at[n]


class RowSum(Sum):
    def __init__(self, g, here, r, source, n):
        self.g, self.here, self.r, self.source = g, here, r, source
        self.size, self.cols = source.shape[0] // 4, source.shape[1] // 2
        self.side_x, self.side_y, self.last = r.row_x[n], r.row_y[n], r.row_last[n]
        self.started = []

    def half(self, quarter, second):
        return self.source.at[pl.ds(quarter * self.size, self.size), pl.ds(second * self.cols, self.cols)]

    def add_half(self, quarter, second, terms):
        @row_steps(self.size, 64)
        def _(part):
            add_low(self.half(quarter, second).at[part, :], *[term.at[part, :] for term in terms])

    def total(self, keep):
        r, g, here = self.r, self.g, self.here
        for n in range(2):
            self.arrived(self.last.at[n], r.b_recv.at[g, n])
        step = 64

        @row_steps(self.size, step)
        def _(part):
            halves = []
            for second, side in enumerate((self.side_x, self.side_y)):
                value = self.half(here.seq, second)[part, :].astype(jnp.float32)
                halves.append(
                    value + side[0, part, :].astype(jnp.float32) + self.last[second, part, :].astype(jnp.float32)
                )
            keep(part, jnp.concatenate(halves, axis=1))

    def sent(self):
        for make in self.started:
            remote(*make()).wait_send()


GELU_SCALE = math.sqrt(2.0 / math.pi)
GELU_CUBE = 0.044715
TOKENS, ENCODED = GROUPS, GROUPS + 1


def backward_kernel(kinds, planes, layout, *refs):
    r = Space(layout, refs)
    bf16, f32 = jnp.bfloat16, jnp.float32
    here = Peers(planes)
    place, length = here.seq, r.length[0]
    rows, width = r.grad_two.shape
    count, enc_count = r.rows_both.shape[0] // 2, r.ckeys_in.shape[0]
    owner_rows = width // (2 * planes)
    shape = (4, planes, 2, owner_rows, width)
    band = kinds[GATE].cols
    band_shape = (4, planes, 2, owner_rows, band)
    tall_shape = (planes, 2, 4, kinds[DOWN].rows, width)
    keys, values = r.rows_both.at[pl.ds(0, count), :], r.rows_both.at[pl.ds(count, count), :]
    down = PlanesFirst(DOWN, kinds[DOWN], here, r, r.rows_both.reshape(*tall_shape))
    gate = BandSum(GATE, kinds[GATE], here, r, r.grad_gate.reshape(*band_shape))
    up = BandSum(UP, kinds[UP], here, r, r.grad_up.reshape(*band_shape))
    cross = Sum(CROSS, kinds[CROSS], here, r, r.grad_cross.reshape(*shape))
    self_one = Sum(SELF, kinds[SELF], here, r, r.grad_self.reshape(*shape))
    self_two = Sum(SELF_REST, kinds[SELF_REST], here, r, r.grad_self.reshape(*shape))
    sums = (down, gate, up, cross, self_one, self_two)
    others = []

    ckeys, cvalues = r.dk.at[pl.ds(0, enc_count), :], r.dk.at[pl.ds(enc_count, enc_count), :]
    dck, dcv = r.dv.at[pl.ds(0, enc_count), :], r.dv.at[pl.ds(enc_count, enc_count), :]
    enc_all = r.token_part.at[pl.ds(0, enc_count), :]
    enc_part = r.token_part.at[pl.ds(enc_count, enc_count), :]
    token_sum = RowSum(TOKENS, here, r, r.token_part, 0)
    enc_sum = RowSum(ENCODED, here, r, enc_part, 1)
    act, d_gate, d_up = (r.token_part.at[pl.ds(n * rows, rows), pl.ds(0, band)] for n in range(3))

    def send(make):
        remote(*make()).start()
        others.append(make)

    def arrived(target, recv_sem):
        pltpu.make_async_copy(target, target, recv_sem).wait()

    def load(n, source, target):
        copy = pltpu.make_async_copy(source, target, r.load_sem.at[n])
        copy.start()
        return copy

    def ffn_copies(n):
        slot, part = n % 2, pl.ds(pl.multiple_of(n * band, band), band)
        return [
            pltpu.make_async_copy(r.w_gate.at[:, part], r.grad_self.at[slot, :, pl.ds(0, band)], r.f_sem.at[0, slot]),
            pltpu.make_async_copy(r.w_up.at[:, part], r.grad_self.at[2 + slot, :, pl.ds(0, band)], r.f_sem.at[1, slot]),
            pltpu.make_async_copy(r.w_down.at[part, :], r.grad_cross.at[slot, pl.ds(0, band), :], r.f_sem.at[2, slot]),
        ]

    def start_ffn(n):
        for copy in ffn_copies(n):
            copy.start()

    cotangent_load = load(0, r.cotangent, r.grad_mixed)
    normed_three_load = load(6, r.normed_three_in, r.normed)
    start_ffn(0)
    start_ffn(1)
    hidden_two_load = load(11, r.hidden_two_in, r.hidden)
    mixed_load = load(2, r.mixed_cross_in, r.mixed)
    cqueries_load = load(3, r.cqueries_in, r.queries)
    ckeys_load = load(4, r.ckeys_in, ckeys)
    cvalues_load = load(5, r.cvalues_in, cvalues)
    here.meet()

    def grad_result(part, step):
        slots = place * rows + part.start + iota((step, 1), 0)
        return jnp.where(slots < length, r.grad_mixed[part, :].astype(f32), 0.0)

    cotangent_load.wait()

    @row_steps(rows, 64)
    def _(part):
        r.branch[part, :] = grad_result(part, 64).astype(bf16)

    normed_three_load.wait()

    @pl.loop(0, 4)
    def _(n):
        slot = n % 2
        for copy in ffn_copies(n):
            copy.wait()
        normed = r.normed[...]
        branch = r.branch[...]
        w_gate = r.grad_self[slot, :, 0:band]
        w_up = r.grad_self[2 + slot, :, 0:band]
        w_down = r.grad_cross[slot, 0:band, :]
        gate_band = product(normed, w_gate)
        up_band = product(normed, w_up)
        inner = jnp.tanh(GELU_SCALE * (gate_band + GELU_CUBE * (gate_band * gate_band * gate_band)))
        lifted = 0.5 * (1.0 + inner)
        gelu = gate_band * lifted
        slope = lifted + (0.5 * GELU_SCALE) * gate_band * (1.0 - inner * inner) * (
            1.0 + (3.0 * GELU_CUBE) * (gate_band * gate_band)
        )
        act[...] = (gelu * up_band).astype(bf16)
        grad_act = outer_rows(branch, w_down)
        d_gate[...] = (grad_act * up_band * slope).astype(bf16)
        d_up[...] = (grad_act * gelu).astype(bf16)
        first = pl.ds(pl.multiple_of(n * band, band), band)
        r.rows_both[first, :] = inner_rows(act[...], branch).astype(bf16)
        r.grad_gate[n] = inner_rows(normed, d_gate[...]).astype(bf16)
        r.grad_up[n] = inner_rows(normed, d_up[...]).astype(bf16)
        down.start_pair(n)
        gate.start_pair(n)
        up.start_pair(n)
        out = product(act[...], w_down)
        gy = outer_rows(d_gate[...], w_gate) + outer_rows(d_up[...], w_up)

        @pl.when(n == 0)
        def _():
            r.grad_two[...] = out
            r.gy[...] = gy

        @pl.when(n > 0)
        def _():
            r.grad_two[...] += out
            r.gy[...] += gy

        @pl.when(n < 2)
        def _():
            start_ffn(n + 2)

    w_cout_load = load(1, r.w_two.at[3], r.grad_self.at[3])
    w_two_loads = [load(8 + m, r.w_two.at[m], r.grad_self.at[m]) for m in range(3)]
    encoded_load = load(7, r.enc_in, enc_all)
    hidden_two_load.wait()
    r.small[...] = jnp.zeros_like(r.small)

    @row_steps(rows, 64)
    def _(part):
        hidden = r.hidden[part, :]
        slots = place * rows + part.start + iota((64, 1), 0)
        r.dq[part, :] = jnp.where(slots < length, hidden + r.grad_two[part, :], 0.0).astype(bf16)
        grad, gain = norm_back_rows(hidden, r.gain_three[...], r.gy[part, :])
        total = grad_result(part, 64) + grad
        r.grad_two[part, :] = total
        r.branch[part, :] = total.astype(bf16)
        r.small[2:3, :] += gain

    result_copy = load(13, r.dq, r.layer_out)
    normed_two_load = load(6, r.normed_two_in, r.normed)
    hidden_load = load(11, r.hidden_one_in, r.hidden)
    fill_pads(r.pads, count)
    fill_fixed_bias(r.bias)
    down.pair_sum()
    down.start_planes()
    w_cout_load.wait()
    r.grad_mixed[...] = outer_rows(r.branch[...], r.grad_self[3]).astype(bf16)
    w_sout_load = load(12, r.w_one.at[3], r.grad_self.at[3])
    mixed_load.wait()
    weight_grad_turned(r.grad_cross.at[3], r.mixed, r.branch)
    gate.pair_sum()
    gate.sides()
    up.pair_sum()
    up.sides()
    for copy in (cqueries_load, ckeys_load, cvalues_load):
        copy.wait()
    result_copy.wait()
    down.pair_sent()
    keys_load = load(13, r.keys_in, keys)
    values_load = load(14, r.values_in, values)

    def stepped(table, pair):
        for when, steps in table.items():

            @pl.when(pair == when)
            def _(steps=steps):
                for step in steps:
                    step()

    @pl.loop(0, PAIRS)
    def _(pair):
        part = columns(pair)
        backward_pair(
            None, None, r.queries.at[:, part], ckeys.at[:, part], cvalues.at[:, part],
            r.grad_mixed.at[:, part], r.mixed.at[part, :], r.log_cross.at[pair],
            r.dq.at[:, part], dck.at[:, part], dcv.at[:, part], None, None, r.pads, None, r.kt_buf, None,
        )

    fill_pads(r.pads, length)
    mixed_self_load = load(15, r.mixed_self_in, r.mixed)
    queries_load = load(16, r.queries_in, r.queries)
    w_two_loads[0].wait()
    r.gy[...] = outer_rows(r.dq[...], r.grad_self[0])
    normed_two_load.wait()
    weight_grad(r.grad_cross.at[0], r.normed, r.dq)
    gate.first_side()
    encoded_load.wait()
    weight_grad(r.grad_cross.at[1], enc_all, dck)
    weight_grad(r.grad_cross.at[2], enc_all, dcv)
    for n in range(4):
        cross.start_pair(n)
    w_two_loads[1].wait()
    w_two_loads[2].wait()
    enc_part[...] = (outer_rows(dck[...], r.grad_self[1]) + outer_rows(dcv[...], r.grad_self[2])).astype(bf16)
    quarters = ((here.along_x, here.to_x), (here.along_y, here.to_y), (here.corner, here.to_corner))

    def own_rows(ref, size, part, step):
        return ref[pl.ds(pl.multiple_of(place * size + part.start, step), step), :].astype(f32)

    enc_sum.sides()
    hidden_load.wait()

    @row_steps(rows, 64)
    def _(part):
        grad, gain = norm_back_rows(r.hidden[part, :], r.gain_two[...], r.gy[part, :])
        total = r.grad_two[part, :] + grad
        r.grad_two[part, :] = total
        r.branch[part, :] = total.astype(bf16)
        r.small[1:2, :] += gain

    w_sout_load.wait()
    r.grad_mixed[...] = outer_rows(r.branch[...], r.grad_self[3]).astype(bf16)
    mixed_self_load.wait()
    weight_grad_turned(r.grad_self.at[3], r.mixed, r.branch)
    for copy in (queries_load, keys_load, values_load):
        copy.wait()

    def keep_enc(part, total):
        r.enc_total[part, :] = total

    def enc_done():
        enc_sum.total(keep_enc)
        pltpu.make_async_copy(r.enc_total, r.enc_sum, r.load_sem.at[20]).start()

    def cross_sides():
        cross.pair_sum()
        cross.sides()

    def load_normed():
        enc_sum.sent()
        pltpu.make_async_copy(r.normed_all_in, r.token_part, r.load_sem.at[21]).start()

    def w_one_copies():
        return [
            pltpu.make_async_copy(r.w_one.at[m], r.grad_cross.at[m], r.load_sem.at[17 + m]) for m in range(3)
        ]

    def load_w_one():
        cross.pair_sent()
        for copy in w_one_copies():
            copy.start()

    self_steps = {
        0: [up.first_side, cross_sides],
        1: [enc_sum.first_side, gate.second_side],
        2: [down.along_planes, up.second_side],
        3: [enc_done, load_normed],
        4: [down.first_side, load_w_one],
        5: [cross.first_side],
    }

    @pl.loop(0, PAIRS)
    def _(pair):
        part = columns(pair)
        backward_pair(
            place, r.profile.at[pair], r.queries.at[:, part], keys.at[:, part],
            values.at[:, part], r.grad_mixed.at[:, part], r.mixed.at[part, :],
            r.log_self.at[pair], r.dq.at[:, part], r.dk.at[:, part], r.dv.at[:, part],
            r.near.at[pair], r.far.at[pair], r.pads, r.bias, r.kt_buf, r.grad_buf,
        )
        stepped(self_steps, pair)

    tokens_load = load(22, r.tokens_all_in, keys)
    pltpu.make_async_copy(r.normed_all_in, r.token_part, r.load_sem.at[21]).wait()
    own = pl.ds(pl.multiple_of(place * rows, BLOCK), rows)
    weight_grad(r.grad_self.at[0], r.token_part.at[own, :], r.dq)
    weight_grad(r.grad_self.at[1], r.token_part, r.dk)
    weight_grad(r.grad_self.at[2], r.token_part, r.dv)
    for n in range(4):
        self_one.start_pair(n)
    for n in range(4):
        self_two.start_pair(n)
    for copy in w_one_copies():
        copy.wait()

    @row_steps(count, 512)
    def _(part):
        total = outer_rows(r.dk[part, :], r.grad_cross[1]) + outer_rows(r.dv[part, :], r.grad_cross[2])
        r.token_part[part, :] = total.astype(bf16)

    self_one.pair_sum()
    self_one.sides()
    self_two.pair_sum()
    self_two.sides()
    gate.along_planes()
    down.second_side()
    cross.second_side()
    token_sum.sides()
    r.gy[...] = outer_rows(r.dq[...], r.grad_cross[0])
    up.along_planes()
    tokens_load.wait()

    @row_steps(count, 64)
    def _(part):
        values = keys[part, :].astype(f32)
        scale = lax.rsqrt(jnp.mean(values * values, axis=-1, keepdims=True) + EPSILON)
        grad = r.token_part[part, :].astype(f32)
        r.small[0:1, :] += jnp.sum(grad * values * scale, axis=0, keepdims=True)

    @row_steps(rows, 64)
    def _(part):
        values = own_rows(keys, rows, part, 64)
        scale = lax.rsqrt(jnp.mean(values * values, axis=-1, keepdims=True) + EPSILON)
        r.small[0:1, :] += jnp.sum(r.gy[part, :] * values * scale, axis=0, keepdims=True)

    for pair in range(PAIRS):
        table = jnp.dot(
            r.near[pair], r.one_hot[...], precision=lax.Precision.HIGHEST, preferred_element_type=f32
        )
        last_bucket = iota(table.shape, 1) == BUCKETS - 1
        table = table + jnp.where(last_bucket, jnp.sum(r.far[pair], axis=1, keepdims=True), 0.0)
        r.small[8 + 2 * pair : 10 + 2 * pair, 0 : table.shape[1]] = table

    small, small_core, small_seq, small_plane = r.small, r.small_core, r.small_seq, r.small_plane
    send(lambda: (small, small_core, r.s_send.at[0], r.s_recv.at[0], here.partner))
    down.spread()
    gate.spread()
    self_one.first_side()
    arrived(small_core, r.s_recv.at[0])
    small_seq[place] = small[...] + small_core[...]
    for k, (_, device) in enumerate(quarters):
        send(
            lambda k=k, device=device: (
                small_seq.at[place], small_seq.at[place], r.s_send.at[1 + k], r.s_recv.at[1 + k], device
            )
        )
    down.finish()
    self_two.first_side()
    token_sum.first_side()
    cross.along_planes()
    up.spread()
    self_one.second_side()
    for k, (quarter, _) in enumerate(quarters):
        arrived(small_seq.at[quarter], r.s_recv.at[1 + k])
    small_plane[here.plane] = (small_seq[0] + small_seq[1]) + (small_seq[2] + small_seq[3])
    for k in range(1, planes):
        send(
            lambda k=k: (
                small_plane.at[here.plane], small_plane.at[here.plane],
                r.s_send.at[3 + k], r.s_recv.at[3 + k], here.at_plane(here.ahead(k)),
            )
        )
    gate.finish()
    self_two.second_side()
    cross.spread()
    up.finish()
    self_one.along_planes()
    cross.finish()

    def keep_tokens(part, total):
        values = own_rows(keys, rows, part, 64)
        grad, _ = norm_back_rows(values, r.gain_one[...], r.gy[part, :] + total)
        r.hidden[part, :] = r.grad_two[part, :] + grad

    token_sum.total(keep_tokens)
    token_copy = pltpu.make_async_copy(r.hidden, r.grad_tokens, r.load_sem.at[23])
    token_copy.start()
    for k in range(1, planes):
        arrived(small_plane.at[here.ahead(planes - k)], r.s_recv.at[3 + k])
    total = small_plane[0]
    for k in range(1, planes):
        total = total + small_plane[k]
    r.small_out[...] = total
    self_two.along_planes()
    self_one.spread()
    self_one.finish()
    self_two.spread()
    self_two.finish()
    token_copy.wait()
    pltpu.make_async_copy(r.enc_total, r.enc_sum, r.load_sem.at[20]).wait()
    for group in sums:
        group.end()
    token_sum.sent()
    for make in others:
        remote(*make()).wait_send()


def backward_fused(shards, length, small, large):
    stack, _, band, _, tall = make_kinds(shards)
    planes = lax.axis_size("fsdp") // 2
    lower = planes // 2
    first_rows = stack.rows // 2
    parts = [StackRows(n * first_rows, first_rows, stack.cols) for n in range(2)]
    kinds = [tall, band, band, stack, *parts]
    f32, low = jnp.float32, jnp.bfloat16
    rows, width = large["cotangent"].shape
    count, enc_count = large["keys_in"].shape[0], large["ckeys_in"].shape[0]
    in_vmem = pl.BlockSpec(memory_space=pltpu.VMEM)
    in_layout, operands = flatten(dict(length=length), small, large)
    in_specs = [SCALARS] + [in_vmem] * len(small)
    in_specs += [ANYWHERE] * (len(operands) - len(in_specs))
    small_shape = (24, width)

    def chunk(kind, *lead):
        return pltpu.VMEM(lead + (kind.rows, kind.cols), low)

    results = dict(
        out=[
            shaped((kind.rows, 4 * kind.cols) if isinstance(kind, Wide) else (4, kind.rows, kind.cols), low)
            for kind in (tall, band, band, stack, stack)
        ],
        layer_out=shaped((rows, width), low),
        grad_tokens=shaped((rows, width), f32),
        enc_sum=shaped((enc_count // 4, width), f32),
        small_out=shaped(small_shape, f32),
    )
    out_layout, out_shapes = flatten(results)
    square = (width, width)
    all_rows = pltpu.VMEM((count, width), low)
    some_rows = pltpu.VMEM((rows, width), low)
    wide_rows = pltpu.VMEM((rows, width), f32)
    half_tall = pltpu.VMEM((2, tall.rows, tall.cols // 2), low)
    later = kinds[1:]
    sides = [half_tall] + [chunk(kind, 2, lower) for kind in later]
    row_sides = [pltpu.VMEM((2, size, width // 2), low) for size in (rows, enc_count // 4)]
    buffers = backward_scratch(count)
    scratch = dict(
        sums=[chunk(kind, 4, planes) for kind in kinds],
        side_x=sides, side_y=sides, last=sides,
        from_z=[chunk(tall, planes - 1, 4)] + [chunk(kind, planes - 1) for kind in later],
        final=[chunk(kind, 4) for kind in kinds],
        grad_gate=pltpu.VMEM((4, width, band.cols), low),
        grad_up=pltpu.VMEM((4, width, band.cols), low),
        grad_cross=pltpu.VMEM((4,) + square, low),
        grad_self=pltpu.VMEM((4,) + square, low),
        rows_both=pltpu.VMEM((2 * count, width), low),
        dk=all_rows, dv=all_rows, token_part=all_rows,
        queries=some_rows, normed=some_rows, branch=some_rows, grad_mixed=some_rows, dq=some_rows,
        grad_two=wide_rows, hidden=wide_rows, gy=wide_rows,
        mixed=pltpu.VMEM((width, rows), f32),
        enc_total=pltpu.VMEM((enc_count // 4, width), f32),
        row_x=row_sides, row_y=row_sides, row_last=row_sides,
        pads=buffers[0], bias=buffers[1], kt_buf=buffers[2], grad_buf=buffers[3],
        near=pltpu.VMEM((PAIRS, 2, BLOCK), f32),
        far=pltpu.VMEM((PAIRS, 2, rows), f32),
        small=pltpu.VMEM(small_shape, f32),
        small_core=pltpu.VMEM(small_shape, f32),
        small_seq=pltpu.VMEM((4,) + small_shape, f32),
        small_plane=pltpu.VMEM((planes,) + small_shape, f32),
        f_sem=DMA((3, 2)),
        c_send=DMA((GROUPS, 4)), c_recv=DMA((GROUPS, 4)),
        a_send=DMA((GROUPS + 2, 4)), a_recv=DMA((GROUPS + 2, 4)),
        b_send=DMA((GROUPS + 2, 2)), b_recv=DMA((GROUPS + 2, 2)),
        z_send=DMA((GROUPS, planes - 1)), z_recv=DMA((GROUPS, planes - 1)),
        g_send=DMA((GROUPS, 4)), g_recv=DMA((GROUPS, 4)),
        s_send=DMA((3 + planes,)), s_recv=DMA((3 + planes,)),
        out_sem=DMA((GROUPS, 4)), load_sem=DMA((24,)),
    )
    scratch_layout, scratch_shapes = flatten(scratch)
    outs = pl.pallas_call(
        functools.partial(backward_kernel, kinds, planes, in_layout | out_layout | scratch_layout),
        in_specs=in_specs,
        out_specs=[ANYWHERE] * (len(out_shapes) - 1) + [in_vmem],
        out_shape=out_shapes,
        scratch_shapes=scratch_shapes,
        compiler_params=pltpu.CompilerParams(
            collective_id=1, has_side_effects=True, vmem_limit_bytes=67_000_000
        ),
        name="backward_fused",
    )(*operands)
    got = Space(out_layout, outs)
    grads = [got.out[SELF][m] for m in range(4)] + [got.out[CROSS][m] for m in range(4)]
    grads += [got.out[GATE], got.out[UP], got.out[DOWN].reshape(-1, width)]
    return got.layer_out, [grad.astype(f32) for grad in grads], got.grad_tokens, got.enc_sum, got.small_out


ONE, TWO, GATE_IN, UP_IN, DOWN_IN = range(5)


class Gathering:
    def __init__(self, kinds, here, r):
        self.kinds, self.here, self.r = kinds, here, r
        self.planes = here.planes
        shape = (4, here.planes, 2, kinds[ONE].rows, kinds[ONE].cols)
        self.full = [r.weights_one.reshape(*shape), r.weights_two.reshape(*shape), *r.ffn_full]
        self.shards = [r.shards[0:4], r.shards[4:8], r.shards[8], r.shards[9], r.shards[10]]
        self.started = []

    def send(self, make):
        remote(*make()).start()
        self.started.append(make)

    def arrived(self, target, recv_sem):
        pltpu.make_async_copy(target, target, recv_sem).wait()

    def plane_copy(self, g, k, source):
        here, r = self.here, self.r
        return remote(
            source, self.kinds[g].part(self.full[g], here.seq, here.plane, here.core),
            r.z_send.at[g, k - 1], r.z_recv.at[g, k - 1], here.at_plane(here.ahead(k)),
        )

    def start_planes(self, g):
        for k in range(1, self.planes):
            if g <= TWO:
                for m in range(4):

                    @pl.when(self.here.seq == m)
                    def _(m=m, k=k):
                        self.plane_copy(g, k, self.shards[g][m]).start()

            else:
                self.plane_copy(g, k, self.kinds[g].own(self.shards[g], self.here.seq)).start()

    def own_copies(self, g):
        here, r, full = self.here, self.r, self.full[g]
        if g <= TWO:
            return [
                pltpu.make_async_copy(
                    self.shards[g][m], full.at[m, here.plane, here.core], r.own_sem.at[g, m]
                )
                for m in range(4)
            ]
        return [
            pltpu.make_async_copy(
                self.shards[g], self.kinds[g].whole(full, here.plane, here.core), r.own_sem.at[g, 0]
            )
        ]

    def start_own(self, g):
        here, r, full = self.here, self.r, self.full[g]
        for copy in self.own_copies(g):
            copy.start()
        if g <= TWO:
            for m in range(4):
                self.send(
                    lambda m=m: (
                        self.shards[g][m], full.at[m, here.plane, here.core],
                        r.p_send.at[g, m], r.p_recv.at[g, m], here.partner,
                    )
                )
        else:
            self.send(
                lambda: (
                    self.shards[g], self.kinds[g].whole(full, here.plane, here.core),
                    r.p_send.at[g, 0], r.p_recv.at[g, 0], here.partner,
                )
            )

    def chunk(self, g, quarter, k, first=0, count=None):
        here = self.here
        return self.kinds[g].part(self.full[g], quarter, here.ahead(self.planes - k), here.core, first, count)

    def from_plane(self, g):
        here, r = self.here, self.r
        for k in range(1, self.planes):
            self.arrived(self.chunk(g, here.seq, k), r.z_recv.at[g, k - 1])
            for n, device in enumerate((here.to_x, here.to_y)):

                def make(k=k, n=n, device=device):
                    chunk = self.chunk(g, here.seq, k)
                    return chunk, chunk, r.x_send.at[n, g, k - 1], r.x_recv.at[n, g, k - 1], device

                self.send(make)

    def from_sides(self, g):
        here, r = self.here, self.r
        half = self.kinds[g].rows // 2
        turns = ((here.along_x, 0, here.to_y), (here.along_y, half, here.to_x))
        for k in range(1, self.planes):
            for n, (quarter, first, device) in enumerate(turns):
                self.arrived(self.chunk(g, quarter, k), r.x_recv.at[n, g, k - 1])

                def make(k=k, n=n, quarter=quarter, first=first, device=device):
                    chunk = self.chunk(g, quarter, k, first, half)
                    return chunk, chunk, r.d_send.at[n, g, k - 1], r.d_recv.at[n, g, k - 1], device

                self.send(make)

    def from_corner(self, g):
        here, r = self.here, self.r
        half = self.kinds[g].rows // 2
        for k in range(1, self.planes):
            self.arrived(self.chunk(g, here.corner, k, 0, half), r.d_recv.at[0, g, k - 1])
            self.arrived(self.chunk(g, here.corner, k, half, half), r.d_recv.at[1, g, k - 1])

            def make(k=k):
                whole = self.kinds[g].whole(self.full[g], here.ahead(self.planes - k), here.core)
                return whole, whole, r.c_send.at[g, k - 1], r.c_recv.at[g, k - 1], here.partner

            self.send(make)

    def complete(self, g):
        here, r, full = self.here, self.r, self.full[g]
        for copy in self.own_copies(g):
            copy.wait()
        if g <= TWO:
            for m in range(4):
                self.arrived(full.at[m, here.plane, 1 - here.core], r.p_recv.at[g, m])
        else:
            self.arrived(self.kinds[g].whole(full, here.plane, 1 - here.core), r.p_recv.at[g, 0])
        for k in range(1, self.planes):
            behind = here.ahead(self.planes - k)
            self.arrived(self.kinds[g].whole(full, behind, 1 - here.core), r.c_recv.at[g, k - 1])

    def end(self):
        for g in range(5):
            for k in range(1, self.planes):
                source = self.shards[g][0] if g <= TWO else self.kinds[g].own(self.shards[g], self.here.seq)
                self.plane_copy(g, k, source).wait_send()
        for make in self.started:
            remote(*make()).wait_send()


def forward_kernel(kinds, planes, layout, *refs):
    r = Space(layout, refs)
    bf16, f32 = jnp.bfloat16, jnp.float32
    here = Peers(planes)
    place, length = here.seq, r.length[0]
    gather = Gathering(kinds, here, r)
    rows, width = r.tokens.shape
    count, enc_count = r.normed.shape[0], r.encoded_rows.shape[0]
    row_ins = (r.tokens, r.encoded)
    row_alls = (r.source_rows, r.encoded_rows)
    stores = []

    def store(n, source, target):
        stores.append((n, source, target))
        pltpu.make_async_copy(source, target, r.store_sem.at[n]).start()

    def block_of(item, quarter, first=0, size=None):
        size_here = row_ins[item].shape[0]
        return row_alls[item].at[pl.ds(quarter * size_here + first, size or size_here), :]

    def rows_start(item):
        for n, device in enumerate((here.to_x, here.to_y)):
            gather.send(
                lambda n=n, device=device: (
                    row_ins[item], block_of(item, place), r.r_send.at[item, n], r.r_recv.at[item, n], device
                )
            )
        pltpu.make_async_copy(row_ins[item], block_of(item, place), r.r_own.at[item]).start()

    def rows_turn(item):
        half = row_ins[item].shape[0] // 2
        turns = ((here.along_x, 0, here.to_y), (here.along_y, half, here.to_x))
        for n, (quarter, first, device) in enumerate(turns):
            gather.arrived(block_of(item, quarter), r.r_recv.at[item, n])

            def make(n=n, quarter=quarter, first=first, device=device):
                chunk = block_of(item, quarter, first, half)
                return chunk, chunk, r.r_send.at[item, 2 + n], r.r_recv.at[item, 2 + n], device

            gather.send(make)

    def rows_done(item):
        half = row_ins[item].shape[0] // 2
        gather.arrived(block_of(item, here.corner, 0, half), r.r_recv.at[item, 2])
        gather.arrived(block_of(item, here.corner, half, half), r.r_recv.at[item, 3])
        pltpu.make_async_copy(row_ins[item], block_of(item, place), r.r_own.at[item]).wait()

    def norm_rows(values, gain):
        scale = lax.rsqrt(jnp.mean(values * values, axis=-1, keepdims=True) + EPSILON)
        return (values * scale * gain[...]).astype(bf16)

    def project(out, left, weight):
        step = min(left.shape[0], 512)

        @row_steps(left.shape[0], step)
        def _(part):
            out[part, :] = product(left[part, :], weight[...]).astype(out.dtype)

    here.meet()
    rows_start(0)
    gather.start_planes(ONE)
    rows_start(1)
    for g in (TWO, GATE_IN, UP_IN, DOWN_IN):
        gather.start_planes(g)
    for g in range(5):
        gather.start_own(g)
    fill_pads(r.pads, length)
    fill_fixed_bias(r.bias)
    rows_turn(0)
    gather.from_plane(ONE)
    rows_turn(1)
    rows_done(0)

    @row_steps(count, 128)
    def _(part):
        r.normed[part, :] = norm_rows(r.source_rows[part, :].astype(f32), r.gain_one)

    store(0, r.source_rows, r.tokens_all)
    store(1, r.normed, r.normed_all)
    gather.from_sides(ONE)
    gather.from_plane(TWO)
    gather.from_corner(ONE)
    rows_done(1)
    store(2, r.encoded_rows, r.enc_all)
    gather.complete(ONE)
    store(3, r.weights_one, r.w_one)
    own = pl.ds(pl.multiple_of(place * rows, BLOCK), rows)
    project(r.query_rows, r.normed.at[own, :], r.weights_one.at[0])
    project(r.key_rows, r.normed, r.weights_one.at[1])
    project(r.value_rows, r.normed, r.weights_one.at[2])
    store(4, r.query_rows, r.queries)
    store(5, r.key_rows, r.keys)
    store(6, r.value_rows, r.values)
    gather.from_plane(GATE_IN)
    gather.from_sides(TWO)
    self_steps = {2: [lambda: gather.from_plane(UP_IN)], 4: [lambda: gather.from_corner(TWO)]}

    def stepped(table, pair):
        for when, steps in table.items():

            @pl.when(pair == when)
            def _(steps=steps):
                for step in steps:
                    step()

    @pl.loop(0, PAIRS)
    def _(pair):
        part = columns(pair)
        self_forward_pair(
            place, r.profile.at[pair], r.query_rows.at[:, part], r.key_rows.at[:, part],
            r.value_rows.at[:, part], r.mixed.at[:, part], r.turned_one.at[part, :], r.log_self.at[pair],
            r.pads, r.bias, r.s_buf, r.vt_buf,
        )
        stepped(self_steps, pair)

    store(7, r.turned_one, r.mixed_self_turned)
    project(r.hidden, r.mixed, r.weights_one.at[3])

    @row_steps(rows, 64)
    def _(part):
        start = pl.multiple_of(place * rows + part.start, 64)
        total = r.hidden[part, :] + r.source_rows[pl.ds(start, 64), :].astype(f32)
        r.hidden[part, :] = total
        r.normed_rows[part, :] = norm_rows(total, r.gain_two)

    store(8, r.hidden, r.hidden_one)
    store(9, r.normed_rows, r.normed_two)
    gather.from_plane(DOWN_IN)
    gather.from_sides(GATE_IN)
    gather.complete(TWO)
    store(10, r.weights_two, r.w_two)
    project(r.cquery_rows, r.normed_rows, r.weights_two.at[0])
    project(r.ckey_rows, r.encoded_rows, r.weights_two.at[1])
    project(r.cvalue_rows, r.encoded_rows, r.weights_two.at[2])
    store(11, r.cquery_rows, r.cqueries)
    store(12, r.ckey_rows, r.ckeys)
    store(13, r.cvalue_rows, r.cvalues)
    cross_steps = {
        1: [lambda: gather.from_corner(GATE_IN)],
        3: [lambda: gather.from_sides(UP_IN)],
    }

    @pl.loop(0, PAIRS)
    def _(pair):
        part = columns(pair)
        cross_forward_pair(
            r.cquery_rows.at[:, part], r.ckey_rows.at[:, part], r.cvalue_rows.at[:, part],
            r.cmixed.at[:, part], r.turned_two.at[part, :], r.log_cross.at[pair],
        )
        stepped(cross_steps, pair)

    store(14, r.turned_two, r.mixed_cross_turned)
    gather.from_sides(DOWN_IN)
    project(r.hidden_last, r.cmixed, r.weights_two.at[3])

    @row_steps(rows, 64)
    def _(part):
        total = r.hidden_last[part, :] + r.hidden[part, :]
        r.hidden_last[part, :] = total
        r.normed_last[part, :] = norm_rows(total, r.gain_three)

    store(15, r.hidden_last, r.hidden_two)
    store(16, r.normed_last, r.normed_three)
    gather.from_corner(UP_IN)
    gather.from_corner(DOWN_IN)
    for g in (GATE_IN, UP_IN, DOWN_IN):
        gather.complete(g)
    gather.end()
    for n, source, target in stores:
        pltpu.make_async_copy(source, target, r.store_sem.at[n]).wait()


def forward_fused(shards, length, tokens, encoded, small):
    kinds = make_kinds(shards)
    planes = lax.axis_size("fsdp") // 2
    f32, low = jnp.float32, jnp.bfloat16
    rows, width = tokens.shape
    enc_rows = encoded.shape[0]
    count, enc_count = 4 * rows, 4 * enc_rows
    square = (4, width, width)
    in_vmem = pl.BlockSpec(memory_space=pltpu.VMEM)
    in_layout, operands = flatten(
        dict(length=length), small, dict(tokens=tokens, encoded=encoded, shards=list(shards))
    )
    in_specs = [SCALARS] + [in_vmem] * len(small)
    in_specs += [ANYWHERE] * (len(operands) - len(in_specs))
    shapes = full_shapes(kinds, planes)
    large_outs = dict(
        w_one=shaped(square, low), w_two=shaped(square, low),
        ffn_full=[shaped(shape, low) for shape in shapes[2:]],
        tokens_all=shaped((count, width), low), normed_all=shaped((count, width), low),
        enc_all=shaped((enc_count, width), low),
        queries=shaped((rows, width), low), keys=shaped((count, width), low),
        values=shaped((count, width), low), mixed_self_turned=shaped((width, rows), f32),
        hidden_one=shaped((rows, width), f32), normed_two=shaped((rows, width), low),
        cqueries=shaped((rows, width), low), ckeys=shaped((enc_count, width), low),
        cvalues=shaped((enc_count, width), low), mixed_cross_turned=shaped((width, rows), f32),
        hidden_two=shaped((rows, width), f32), normed_three=shaped((rows, width), low),
    )
    small_outs = dict(
        log_self=shaped((PAIRS, 2, rows), f32), log_cross=shaped((PAIRS, 2, rows), f32)
    )
    out_layout, out_shapes = flatten(large_outs, small_outs)
    all_rows = pltpu.VMEM((count, width), low)
    enc_all = pltpu.VMEM((enc_count, width), low)
    some_rows = pltpu.VMEM((rows, width), low)
    wide_rows = pltpu.VMEM((rows, width), f32)
    turned = pltpu.VMEM((width, rows), f32)
    buffers = forward_scratch(count, rows)
    steps = planes - 1
    scratch = dict(
        weights_one=pltpu.VMEM(square, low), weights_two=pltpu.VMEM(square, low),
        source_rows=all_rows, normed=all_rows, key_rows=all_rows, value_rows=all_rows,
        encoded_rows=enc_all, ckey_rows=enc_all, cvalue_rows=enc_all,
        query_rows=some_rows, cquery_rows=some_rows, mixed=some_rows, cmixed=some_rows,
        normed_rows=some_rows, normed_last=some_rows,
        hidden=wide_rows, hidden_last=wide_rows, turned_one=turned, turned_two=turned,
        pads=buffers[0], bias=buffers[1], s_buf=buffers[2], vt_buf=buffers[3],
        z_send=DMA((5, steps)), z_recv=DMA((5, steps)),
        own_sem=DMA((5, 4)), p_send=DMA((5, 4)), p_recv=DMA((5, 4)),
        x_send=DMA((2, 5, steps)), x_recv=DMA((2, 5, steps)),
        d_send=DMA((2, 5, steps)), d_recv=DMA((2, 5, steps)),
        c_send=DMA((5, steps)), c_recv=DMA((5, steps)),
        r_send=DMA((2, 4)), r_recv=DMA((2, 4)), r_own=DMA((2,)), store_sem=DMA((17,)),
    )
    scratch_layout, scratch_shapes = flatten(scratch)
    outs = pl.pallas_call(
        functools.partial(forward_kernel, kinds, planes, in_layout | out_layout | scratch_layout),
        in_specs=in_specs,
        out_specs=[ANYWHERE] * (len(out_shapes) - 2) + [in_vmem] * 2,
        out_shape=out_shapes,
        scratch_shapes=scratch_shapes,
        compiler_params=pltpu.CompilerParams(
            collective_id=0, has_side_effects=True, vmem_limit_bytes=66_000_000
        ),
        name="forward_fused",
    )(*operands)
    return Space(out_layout, outs)


def local(
    tokens, encoded, lengths, cotangent, gain_self, gain_cross, gain_ff, bucket_table,
    self_query, self_key, self_value, self_out, cross_query, cross_key, cross_value, cross_out,
    ff_gate, ff_up, ff_down,
):
    rows_here = tokens.shape[1]
    seq_place = lax.axis_index("seq")
    length = lengths[0]
    bf16, f32 = jnp.bfloat16, jnp.float32
    gain_one = gain_self.astype(f32)
    gain_two = gain_cross.astype(f32)
    gain_three = gain_ff.astype(f32)
    shards = (
        self_query, self_key, self_value, self_out, cross_query, cross_key, cross_value, cross_out,
        ff_gate, ff_up, ff_down,
    )
    one_hot = (
        bucket_ids(BLOCK)[:, None] == jnp.arange(BUCKETS, dtype=jnp.int32)[None, :]
    ).astype(bf16)
    profile = inner_rows(bucket_table, one_hot.T).reshape(PAIRS, 2, BLOCK)
    place = jnp.stack([seq_place.astype(jnp.int32), length])

    source = tokens[0].astype(f32)
    if kernels_fit(shards):
        forward = forward_fused(
            shards, lengths, tokens[0], encoded[0],
            dict(
                profile=profile, gain_one=gain_one[None], gain_two=gain_two[None], gain_three=gain_three[None]
            ),
        )
        one_hot_wide = jnp.pad(one_hot.astype(f32), ((0, 0), (0, PAIR - BUCKETS)))
        width = source.shape[1]
        w_gate, w_up, w_down = (full.reshape(-1, full.shape[-1]) for full in forward.ffn_full)
        layer_out, grads, grad_tokens, enc_sum, small = backward_fused(
            shards, lengths,
            dict(
                profile=profile, log_cross=forward.log_cross, log_self=forward.log_self,
                gain_one=gain_one[None], gain_two=gain_two[None], gain_three=gain_three[None],
                one_hot=one_hot_wide,
            ),
            dict(
                cotangent=cotangent[0], w_gate=w_gate, w_up=w_up, w_down=w_down,
                normed_three_in=forward.normed_three, hidden_two_in=forward.hidden_two,
                w_one=forward.w_one, w_two=forward.w_two, mixed_cross_in=forward.mixed_cross_turned,
                cqueries_in=forward.cqueries, ckeys_in=forward.ckeys, cvalues_in=forward.cvalues,
                normed_two_in=forward.normed_two, enc_in=forward.enc_all, hidden_one_in=forward.hidden_one,
                mixed_self_in=forward.mixed_self_turned, queries_in=forward.queries, keys_in=forward.keys,
                values_in=forward.values, normed_all_in=forward.normed_all,
                tokens_all_in=forward.tokens_all,
            ),
        )
        table_sum = small[8 : 8 + HEADS, :BUCKETS].T
        return (
            layer_out[None], grad_tokens[None], enc_sum[None], small[0], small[1], small[2], table_sum, *grads
        )
    weights, tokens_all, enc_all = gather_plain(shards, tokens[0], encoded[0])
    (w_query, w_key, w_value, w_sout, w_cquery, w_ckey, w_cvalue, w_cout, w_gate, w_up, w_down) = weights
    normed_all = rms_scale(tokens_all.astype(f32), gain_one).astype(bf16)
    normed_one = rms_scale(source, gain_one).astype(bf16)
    queries = product(normed_one, w_query).astype(bf16)
    keys = product(normed_all, w_key).astype(bf16)
    values = product(normed_all, w_value).astype(bf16)
    mixed_self, mixed_self_turned, log_self = self_forward(place, profile, queries, keys, values)
    hidden_one = source + product(mixed_self, w_sout)
    normed_two = rms_scale(hidden_one, gain_two).astype(bf16)
    cqueries = product(normed_two, w_cquery).astype(bf16)
    ckeys = product(enc_all, w_ckey).astype(bf16)
    cvalues = product(enc_all, w_cvalue).astype(bf16)
    mixed_cross, mixed_cross_turned, log_cross = cross_forward(cqueries, ckeys, cvalues)
    hidden_two = hidden_one + product(mixed_cross, w_cout)
    normed_three = rms_scale(hidden_two, gain_three).astype(bf16)
    gate = product(normed_three, w_gate)
    up = product(normed_three, w_up)

    def gated(gate_rows, up_rows):
        return jax.nn.gelu(gate_rows, approximate=True) * up_rows

    activated_f, pull_gate = jax.vjp(gated, gate, up)
    activated = activated_f.astype(bf16)
    slot_ids = seq_place * rows_here + jnp.arange(rows_here, dtype=jnp.int32)
    valid = (slot_ids < length).astype(f32)[:, None]
    result = (valid * (hidden_two + product(activated, w_down))).astype(bf16)

    grad_result = valid * cotangent[0].astype(f32)
    branch_ff = grad_result.astype(bf16)
    grad_gate_f, grad_up_f = pull_gate(outer_rows(branch_ff, w_down))
    grad_gate = grad_gate_f.astype(bf16)
    grad_up = grad_up_f.astype(bf16)
    g_down = inner_rows(activated, branch_ff).astype(bf16)
    g_gate = inner_rows(normed_three, grad_gate).astype(bf16)
    g_up = inner_rows(normed_three, grad_up).astype(bf16)
    grad_three, grad_gain_three = norm_back(
        hidden_two, gain_three, outer_rows(grad_gate, w_gate) + outer_rows(grad_up, w_up)
    )
    grad_two = grad_result + grad_three
    branch_cross = grad_two.astype(bf16)
    g_cout = inner_rows(mixed_cross, branch_cross).astype(bf16)
    grad_mixed_cross = outer_rows(branch_cross, w_cout).astype(bf16)
    grad_cq, grad_ck, grad_cv = cross_backward(
        cqueries, ckeys, cvalues, grad_mixed_cross, mixed_cross_turned, log_cross
    )
    g_cquery = inner_rows(normed_two, grad_cq).astype(bf16)
    g_ckey = inner_rows(enc_all, grad_ck).astype(bf16)
    g_cvalue = inner_rows(enc_all, grad_cv).astype(bf16)
    enc_part = (outer_rows(grad_ck, w_ckey) + outer_rows(grad_cv, w_cvalue)).astype(bf16)
    grad_two_back, grad_gain_two = norm_back(hidden_one, gain_two, outer_rows(grad_cq, w_cquery))
    grad_one = grad_two + grad_two_back
    branch_self = grad_one.astype(bf16)
    g_sout = inner_rows(mixed_self, branch_self).astype(bf16)
    grad_mixed_self = outer_rows(branch_self, w_sout).astype(bf16)
    grad_q, grad_k, grad_v, near_part, far_part = self_backward(
        place, profile, queries, keys, values, grad_mixed_self, mixed_self_turned, log_self
    )
    g_query = inner_rows(normed_one, grad_q).astype(bf16)
    g_key = inner_rows(normed_all, grad_k).astype(bf16)
    g_value = inner_rows(normed_all, grad_v).astype(bf16)
    token_part = (outer_rows(grad_k, w_key) + outer_rows(grad_v, w_value)).astype(bf16)
    query_part = outer_rows(grad_q, w_query)

    near_rows = near_part.reshape(HEADS, BLOCK)
    far_rows = jnp.sum(far_part, axis=-1).reshape(HEADS)
    table_part = lax.dot_general(
        one_hot.astype(f32), near_rows, (((0,), (1,)), ((), ())),
        precision=lax.Precision.HIGHEST, preferred_element_type=f32,
    )
    table_part = table_part.at[BUCKETS - 1].add(far_rows)

    hat_all = rms_scale(tokens_all.astype(f32), jnp.ones_like(gain_one))
    hat_one = rms_scale(source, jnp.ones_like(gain_one))
    grad_gain_one = jnp.sum(token_part.astype(f32) * hat_all, axis=0) + jnp.sum(
        query_part * hat_one, axis=0
    )
    table_row = jnp.zeros((gain_one.shape[0],), f32).at[: BUCKETS * HEADS].set(table_part.reshape(-1))
    small = jnp.stack([grad_gain_one, grad_gain_two, grad_gain_three, table_row] + [jnp.zeros_like(gain_one)] * 4)
    reduced, token_sum, enc_sum, small = reduce_plain(
        (g_query, g_key, g_value, g_sout, g_cquery, g_ckey, g_cvalue, g_cout, g_gate, g_up, g_down),
        token_part, enc_part, small,
    )
    grad_zero, _ = norm_back(source, gain_one, query_part + token_sum)
    grad_tokens = grad_one + grad_zero
    table_sum = small[3, : BUCKETS * HEADS].reshape(BUCKETS, HEADS)
    small = (small[0], small[1], small[2], table_sum)
    return (result[None], grad_tokens[None], enc_sum[None], *small, *reduced)


def solution(mesh):
    rows3 = P("fsdp", "seq", None)
    rows2 = P("fsdp", None)
    return jax.shard_map(
        local,
        mesh=mesh,
        in_specs=(rows3, rows3, P("fsdp"), rows3, P(), P(), P(), P(), *([rows2] * 11)),
        out_specs=(rows3, rows3, rows3, P(), P(), P(), P(), *([rows2] * 11)),
        check_vma=False,
    )
```

```python
import functools
import math

import jax
import jax.numpy as jnp
from jax import lax
from jax.experimental import pallas as pl
from jax.experimental.pallas import tpu as pltpu
from jax.sharding import PartitionSpec as P

HEADS = 12
HEAD = 64
BUCKETS = 32
MAX_DISTANCE = 128
EPSILON = 1e-06
NEGATIVE = -1e30
BLOCK = 256
PAIR = 2 * HEAD
MESH = pl.DeviceIdType.MESH


def thresholds():
    exact_limit = BUCKETS // 2
    return [
        int(math.ceil(exact_limit * (MAX_DISTANCE / exact_limit) ** (number / exact_limit)))
        for number in range(1, exact_limit)
    ]


def bucket_ids(key_count):
    exact_limit = BUCKETS // 2
    offsets = jnp.arange(key_count, dtype=jnp.int32)
    passed = jnp.zeros((key_count,), jnp.int32)
    for border in thresholds():
        passed = passed + (offsets >= border).astype(jnp.int32)
    return jnp.where(offsets < exact_limit, offsets, exact_limit + passed)


def rms_scale(values, gain):
    return values * lax.rsqrt(jnp.mean(values * values, axis=-1, keepdims=True) + EPSILON) * gain


def norm_back(values, gain, grad_normed):
    _, pullback = jax.vjp(rms_scale, values, gain)
    return pullback(grad_normed)


def product(left, right):
    return jnp.dot(left, right, preferred_element_type=jnp.float32)


def inner_rows(left, right):
    return lax.dot_general(
        left, right, (((0,), (0,)), ((), ())), preferred_element_type=jnp.float32
    )


def outer_rows(left, right):
    return lax.dot_general(
        left, right, (((1,), (1,)), ((), ())), preferred_element_type=jnp.float32
    )


def iota(shape, axis):
    return lax.broadcasted_iota(jnp.int32, shape, axis)


def head_rows(value, head):
    place = iota(value.shape, 0) // HEAD
    return jnp.where(place == head, value, jnp.zeros_like(value))


def head_cols(value, head):
    place = iota(value.shape, 1) // HEAD
    return jnp.where(place == head, value, jnp.zeros_like(value))


def skew(profile_row):
    wide = jnp.broadcast_to(profile_row, (BLOCK, BLOCK))
    return pltpu.roll(wide, 0, 1, stride=1, stride_axis=0)


def unskew(tile):
    rows = iota(tile.shape, 0)
    bit = 1
    while bit < BLOCK:
        tile = jnp.where((rows // bit) % 2 == 1, pltpu.roll(tile, BLOCK - bit, 1), tile)
        bit *= 2
    return tile


def fill_pads(pads, length):
    rows = pads.shape[1]
    lanes = iota((BLOCK, PAIR), 1)

    @pl.loop(0, rows // BLOCK)
    def _(n):
        start = pl.multiple_of(n * BLOCK, BLOCK)
        beyond = iota((BLOCK, PAIR), 0) >= length - start
        for head in range(2):
            first = (1 - head) * HEAD
            ones = jnp.where((lanes > first) & (lanes <= first + 3), 1.0, 0.0)
            pads[head, pl.ds(start, BLOCK), :] = jnp.where(
                (lanes == first) & beyond, NEGATIVE, ones
            ).astype(jnp.bfloat16)


def padded(value, pads, head, start):
    own = iota(value.shape, 1) // HEAD == head
    return jnp.where(own, value, pads[head, start : start + value.shape[0], :])


def split_low(value):
    first = value.astype(jnp.bfloat16).astype(jnp.float32)
    rest = value - first
    second = rest.astype(jnp.bfloat16).astype(jnp.float32)
    return first, second, rest - second


def with_terms(turned, head, mask_term, terms):
    place = iota(turned.shape, 0)
    first = (1 - head) * HEAD
    value = jnp.where(place // HEAD == head, turned.astype(jnp.float32), 0.0)
    value = jnp.where(place == first, mask_term, value)
    for n, term in enumerate(terms):
        value = jnp.where(place == first + 1 + n, term, value)
    return value.astype(jnp.bfloat16)


HIDDEN, DIAGONAL, NEAR, FAR = range(4)


def fill_fixed_bias(bias):
    for head in range(2):
        bias[head, HIDDEN] = jnp.full((BLOCK, BLOCK), NEGATIVE, jnp.float32)
        bias[head, FAR] = jnp.zeros((BLOCK, BLOCK), jnp.float32)


def fill_near_bias(bias, profile_ref):
    later = iota((BLOCK, BLOCK), 1) >= iota((BLOCK, BLOCK), 0)
    for head in range(2):
        profile = profile_ref[head : head + 1, :]
        near = skew(profile - profile[:, BLOCK - 1 :])
        bias[head, DIAGONAL] = jnp.where(later, near, NEGATIVE)
        bias[head, NEAR] = jnp.where(later, 0.0, near)


def bias_kind(place, block):
    return jnp.clip(place - block, -1, 2) + 1


def self_forward_pair(place, profile_ref, q_ref, k_ref, v_ref, o_ref, ot_ref, log_ref, pads, bias, s_buf, vt_buf):
    qt = q_ref[...].T
    vt_buf[...] = v_ref[...].T
    fill_near_bias(bias, profile_ref)
    blocks = k_ref.shape[0] // BLOCK
    tops = []
    for head in range(2):
        far = profile_ref[head : head + 1, BLOCK - 1 :]
        queries = with_terms(qt, head, 1.0, (far,))
        top = None
        for block in range(blocks):
            start = block * BLOCK
            keys = padded(k_ref[start : start + BLOCK, :], pads, head, start)
            scores = product(keys, queries) + bias[head, bias_kind(place, block)]
            s_buf[head, start : start + BLOCK, :] = scores
            most = jnp.max(scores, axis=0, keepdims=True)
            top = most if top is None else jnp.maximum(top, most)
        tops.append(top)
    totals = []
    for head in range(2):
        total = None
        for block in range(blocks):
            part = slice(block * BLOCK, (block + 1) * BLOCK)
            raised = jnp.exp(s_buf[head, part, :] - tops[head])
            s_buf[head, part, :] = raised
            amount = jnp.sum(raised, axis=0, keepdims=True)
            total = amount if total is None else total + amount
        totals.append(total)
    for head in range(2):
        rows = slice(head * HEAD, (head + 1) * HEAD)
        scale, mixed = 1.0 / totals[head], None
        for block in range(blocks):
            part = slice(block * BLOCK, (block + 1) * BLOCK)
            soft = (s_buf[head, part, :] * scale).astype(jnp.bfloat16)
            share = product(vt_buf[rows, part], soft)
            mixed = share if mixed is None else mixed + share
        ot_ref[rows, :] = mixed
        log_ref[head : head + 1, :] = tops[head] + jnp.log(totals[head])
    o_ref[...] = ot_ref[...].T.astype(jnp.bfloat16)


def self_forward_kernel(place_ref, profile_ref, q_ref, k_ref, v_ref, o_ref, ot_ref, log_ref, pads, bias, s_buf, vt_buf):
    @pl.when(pl.program_id(0) == 0)
    def _():
        fill_pads(pads, place_ref[1])
        fill_fixed_bias(bias)

    self_forward_pair(
        place_ref[0], profile_ref.at[0], q_ref, k_ref, v_ref, o_ref, ot_ref, log_ref.at[0],
        pads, bias, s_buf, vt_buf,
    )


def cross_forward_pair(q_ref, k_ref, v_ref, o_ref, ot_ref, log_ref):
    qt = q_ref[...].T
    vt = v_ref[...].T
    all_scores = [product(k_ref[...], head_rows(qt, head)) for head in range(2)]
    for head, scores in enumerate(all_scores):
        top = jnp.max(scores, axis=0, keepdims=True)
        raised = jnp.exp(scores - top)
        total = jnp.sum(raised, axis=0, keepdims=True)
        soft = (raised * (1.0 / total)).astype(jnp.bfloat16)
        ot_ref[head * HEAD : (head + 1) * HEAD, :] = product(vt[head * HEAD : (head + 1) * HEAD, :], soft)
        log_ref[head : head + 1, :] = top + jnp.log(total)
    o_ref[...] = ot_ref[...].T.astype(jnp.bfloat16)


def cross_forward_kernel(q_ref, k_ref, v_ref, o_ref, ot_ref, log_ref):
    cross_forward_pair(q_ref, k_ref, v_ref, o_ref, ot_ref, log_ref.at[0])


EXTRA = 16


def backward_pair(
    place, profile_ref, q_ref, k_ref, v_ref, g_ref, ot_ref, log_ref, dq_ref, dk_ref, dv_ref,
    near_ref, far_ref, pads, bias, kt_buf, grad_buf,
):
    q_value = q_ref[...]
    g_value = g_ref[...]
    qt = q_value.T
    gt = g_value.T
    kt = k_ref[...].T
    keys_count = k_ref.shape[0]
    ones = jnp.ones((EXTRA, keys_count), jnp.bfloat16)
    for head in range(2):
        kt_buf[head, 0:HEAD, 0:keys_count] = kt[head * HEAD : (head + 1) * HEAD, :]
        kt_buf[head, HEAD : HEAD + EXTRA, 0:keys_count] = ones
    both_q = jnp.concatenate([head_cols(q_value, 0), head_cols(q_value, 1)], axis=0)
    both_g = jnp.concatenate([head_cols(g_value, 0), head_cols(g_value, 1)], axis=0)
    weighted = gt.astype(jnp.float32) * ot_ref[...]
    if profile_ref is not None:
        fill_near_bias(bias, profile_ref)
    queries, grads_out = [], []
    for head in range(2):
        rows = slice(head * HEAD, (head + 1) * HEAD)
        delta = jnp.sum(weighted[rows, :], axis=0, keepdims=True)
        constant = -log_ref[head : head + 1, :]
        if profile_ref is not None:
            constant = constant + profile_ref[head : head + 1, BLOCK - 1 :]
        queries.append(with_terms(qt, head, 1.0, split_low(constant)))
        grads_out.append(with_terms(gt, head, 0.0, split_low(-delta)))
    sums = [None, None]
    for start in range(0, keys_count, BLOCK):
        k_block = k_ref[start : start + BLOCK, :]
        v_block = v_ref[start : start + BLOCK, :]
        softs, grads = [], []
        for head in range(2):
            scores = product(padded(k_block, pads, head, start), queries[head])
            if profile_ref is not None:
                scores = scores + bias[head, bias_kind(place, start // BLOCK)]
            soft = jnp.exp(scores)
            change = product(padded(v_block, pads, head, start), grads_out[head])
            grad = (soft * change).astype(jnp.bfloat16)
            softs.append(soft.astype(jnp.bfloat16))
            grads.append(grad)
            if profile_ref is not None:
                grad_buf[head, start // BLOCK] = grad
            share = product(kt_buf[head, :, start : start + BLOCK], grad)
            sums[head] = share if sums[head] is None else sums[head] + share
        dv_ref[start : start + BLOCK, :] = product(jnp.concatenate(softs, axis=1), both_g).astype(
            jnp.bfloat16
        )
        dk_ref[start : start + BLOCK, :] = product(jnp.concatenate(grads, axis=1), both_q).astype(
            jnp.bfloat16
        )
    turned = jnp.concatenate([sums[0][0:HEAD, :], sums[1][0:HEAD, :]], axis=0)
    dq_ref[...] = turned.T.astype(jnp.bfloat16)
    if profile_ref is not None:
        later = iota((BLOCK, BLOCK), 1) >= iota((BLOCK, BLOCK), 0)
        for head in range(2):
            diagonal = grad_buf[head, place].astype(jnp.float32)
            before = grad_buf[head, jnp.maximum(place - 1, 0)].astype(jnp.float32)
            before = jnp.where(place >= 1, before, 0.0)
            near = jnp.sum(unskew(jnp.where(later, diagonal, before)), axis=0, keepdims=True)
            near_ref[head : head + 1, :] = near
            far_ref[head : head + 1, :] = sums[head][HEAD : HEAD + 1, :] - near


def self_backward_kernel(
    place_ref, profile_ref, q_ref, k_ref, v_ref, g_ref, ot_ref, log_ref,
    dq_ref, dk_ref, dv_ref, near_ref, far_ref, pads, bias, kt_buf, grad_buf,
):
    @pl.when(pl.program_id(0) == 0)
    def _():
        fill_pads(pads, place_ref[1])
        fill_fixed_bias(bias)

    backward_pair(
        place_ref[0], profile_ref.at[0], q_ref, k_ref, v_ref, g_ref, ot_ref, log_ref.at[0],
        dq_ref, dk_ref, dv_ref, near_ref.at[0], far_ref.at[0], pads, bias, kt_buf, grad_buf,
    )


def cross_backward_kernel(q_ref, k_ref, v_ref, g_ref, ot_ref, log_ref, dq_ref, dk_ref, dv_ref, pads, kt_buf):
    @pl.when(pl.program_id(0) == 0)
    def _():
        fill_pads(pads, pads.shape[1])

    backward_pair(
        None, None, q_ref, k_ref, v_ref, g_ref, ot_ref, log_ref.at[0], dq_ref, dk_ref, dv_ref,
        None, None, pads, None, kt_buf, None,
    )


def forward_scratch(count, rows):
    return [
        pltpu.VMEM((2, count, PAIR), jnp.bfloat16),
        pltpu.VMEM((2, 4, BLOCK, BLOCK), jnp.float32),
        pltpu.VMEM((2, count, rows), jnp.float32),
        pltpu.VMEM((PAIR, count), jnp.bfloat16),
    ]


def backward_scratch(count):
    return [
        pltpu.VMEM((2, count, PAIR), jnp.bfloat16),
        pltpu.VMEM((2, 4, BLOCK, BLOCK), jnp.float32),
        pltpu.VMEM((2, HEAD + EXTRA, count), jnp.bfloat16),
        pltpu.VMEM((2, count // BLOCK, BLOCK, BLOCK), jnp.bfloat16),
    ]


def pair_block(rows):
    return pl.BlockSpec((rows, PAIR), lambda pair: (0, pair))


def turned_block(rows):
    return pl.BlockSpec((PAIR, rows), lambda pair: (pair, 0))


def head_block(width):
    return pl.BlockSpec((1, 2, width), lambda pair: (pair, 0, 0))


SCALARS = pl.BlockSpec(memory_space=pltpu.SMEM)
PAIRS = HEADS // 2


def shaped(shape, dtype):
    return jax.ShapeDtypeStruct(shape, dtype)


def self_forward(place, profile, queries, keys, values):
    rows, width = queries.shape
    count = keys.shape[0]
    return pl.pallas_call(
        self_forward_kernel,
        grid=(PAIRS,),
        in_specs=[SCALARS, head_block(BLOCK), pair_block(rows), pair_block(count), pair_block(count)],
        out_specs=[pair_block(rows), turned_block(rows), head_block(rows)],
        out_shape=[
            shaped((rows, width), jnp.bfloat16),
            shaped((width, rows), jnp.float32),
            shaped((PAIRS, 2, rows), jnp.float32),
        ],
        scratch_shapes=forward_scratch(count, rows),
        name="self_forward",
    )(place, profile, queries, keys, values)


def cross_forward(queries, keys, values):
    rows, width = queries.shape
    count = keys.shape[0]
    return pl.pallas_call(
        cross_forward_kernel,
        grid=(PAIRS,),
        in_specs=[pair_block(rows), pair_block(count), pair_block(count)],
        out_specs=[pair_block(rows), turned_block(rows), head_block(rows)],
        out_shape=[
            shaped((rows, width), jnp.bfloat16),
            shaped((width, rows), jnp.float32),
            shaped((PAIRS, 2, rows), jnp.float32),
        ],
        name="cross_forward",
    )(queries, keys, values)


def self_backward(place, profile, queries, keys, values, grad_mixed, mixed_turned, log_totals):
    rows, width = queries.shape
    count = keys.shape[0]
    return pl.pallas_call(
        self_backward_kernel,
        grid=(PAIRS,),
        in_specs=[
            SCALARS, head_block(BLOCK), pair_block(rows), pair_block(count), pair_block(count),
            pair_block(rows), turned_block(rows), head_block(rows),
        ],
        out_specs=[
            pair_block(rows), pair_block(count), pair_block(count), head_block(BLOCK), head_block(rows),
        ],
        out_shape=[
            shaped((rows, width), jnp.bfloat16),
            shaped((count, width), jnp.bfloat16),
            shaped((count, width), jnp.bfloat16),
            shaped((PAIRS, 2, BLOCK), jnp.float32),
            shaped((PAIRS, 2, rows), jnp.float32),
        ],
        scratch_shapes=backward_scratch(count),
        name="self_backward",
    )(place, profile, queries, keys, values, grad_mixed, mixed_turned, log_totals)


def cross_backward(queries, keys, values, grad_mixed, mixed_turned, log_totals):
    rows, width = queries.shape
    count = keys.shape[0]
    return pl.pallas_call(
        cross_backward_kernel,
        grid=(PAIRS,),
        in_specs=[
            pair_block(rows), pair_block(count), pair_block(count),
            pair_block(rows), turned_block(rows), head_block(rows),
        ],
        out_specs=[pair_block(rows), pair_block(count), pair_block(count)],
        out_shape=[
            shaped((rows, width), jnp.bfloat16),
            shaped((count, width), jnp.bfloat16),
            shaped((count, width), jnp.bfloat16),
        ],
        scratch_shapes=[
            pltpu.VMEM((2, count, PAIR), jnp.bfloat16),
            pltpu.VMEM((2, HEAD + EXTRA, count), jnp.bfloat16),
        ],
        name="cross_backward",
    )(queries, keys, values, grad_mixed, mixed_turned, log_totals)


class Peers:
    def __init__(self, planes):
        self.seq = lax.axis_index("seq")
        fsdp = lax.axis_index("fsdp")
        self.planes = planes
        self.plane = fsdp // 2
        self.core = fsdp % 2
        self.fsdp = fsdp
        self.along_x = self.seq + 1 - 2 * (self.seq % 2)
        self.along_y = (self.seq + 2) % 4
        self.corner = (self.along_x + 2) % 4
        self.partner = (self.seq, fsdp + 1 - 2 * self.core)
        self.to_x = (self.along_x, fsdp)
        self.to_y = (self.along_y, fsdp)
        self.to_corner = (self.corner, fsdp)

    def ahead(self, steps):
        return (self.plane + steps) % self.planes

    def at_plane(self, plane):
        return (self.seq, 2 * plane + self.core)

    def everyone(self):
        return [self.partner, self.to_x, self.to_y, self.to_corner] + [
            self.at_plane(self.ahead(k)) for k in range(1, self.planes)
        ]

    def greet(self):
        barrier = pltpu.get_barrier_semaphore()
        for other in self.everyone():
            pl.semaphore_signal(barrier, inc=1, device_id=other, device_id_type=MESH)

    def meet(self):
        pl.semaphore_wait(pltpu.get_barrier_semaphore(), len(self.everyone()))


def remote(source, target, send_sem, recv_sem, device):
    return pltpu.make_async_remote_copy(
        src_ref=source, dst_ref=target, send_sem=send_sem, recv_sem=recv_sem,
        device_id=device, device_id_type=MESH,
    )


class Stack:
    def __init__(self, rows, cols):
        self.rows, self.cols = rows, cols

    def own(self, ref, quarter, first=0, count=None):
        return ref.at[quarter, pl.ds(first, count or self.rows), :]

    def part(self, ref, quarter, plane, core, first=0, count=None):
        return ref.at[quarter, plane, core, pl.ds(first, count or self.rows), :]

    def planes(self, ref, quarter, core):
        return ref.at[quarter, :, core]

    def whole(self, ref, plane, core):
        return ref.at[:, plane, core]


class Wide:
    def __init__(self, rows, cols):
        self.rows, self.cols = rows, cols

    def own(self, ref, quarter, first=0, count=None):
        return ref.at[pl.ds(first, count or self.rows), pl.ds(quarter * self.cols, self.cols)]

    def part(self, ref, quarter, plane, core, first=0, count=None):
        return ref.at[
            plane, core, pl.ds(first, count or self.rows), pl.ds(quarter * self.cols, self.cols)
        ]

    def planes(self, ref, quarter, core):
        return ref.at[:, core, :, pl.ds(quarter * self.cols, self.cols)]

    def whole(self, ref, plane, core):
        return ref.at[plane, core]


class Tall:
    def __init__(self, rows, cols):
        self.rows, self.cols = rows, cols

    def own(self, ref, quarter, first=0, count=None):
        return ref.at[pl.ds(quarter * self.rows + first, count or self.rows), :]

    def part(self, ref, quarter, plane, core, first=0, count=None):
        return ref.at[plane, core, pl.ds(quarter * self.rows + first, count or self.rows), :]

    def planes(self, ref, quarter, core):
        return ref.at[:, core, pl.ds(quarter * self.rows, self.rows), :]

    def whole(self, ref, plane, core):
        return ref.at[plane, core]


def full_shapes(kinds, planes, cores=2):
    shapes = []
    for kind in kinds:
        if isinstance(kind, Stack):
            shapes.append((4, planes, cores, kind.rows, kind.cols))
        elif isinstance(kind, Wide):
            shapes.append((planes, cores, kind.rows, 4 * kind.cols))
        else:
            shapes.append((planes, cores, 4 * kind.rows, kind.cols))
    return shapes


ANYWHERE = pl.BlockSpec(memory_space=pl.ANY)
DMA = pltpu.SemaphoreType.DMA


def make_kinds(shards):
    square, wide, down = shards[0], shards[8], shards[10]
    stack = Stack(*square.shape)
    band = Wide(wide.shape[0], wide.shape[1] // 4)
    tall = Tall(down.shape[0] // 4, down.shape[1])
    return [stack, stack, band, band, tall]


def kernels_fit(shards):
    kinds = make_kinds(shards)
    return (
        lax.axis_size("seq") == 4
        and lax.axis_size("fsdp") == 8
        and all(kind.rows % 32 == 0 and kind.cols % 128 == 0 for kind in kinds)
    )


def gather_plain(shards, tokens, encoded):
    full = [lax.all_gather(shard, "fsdp", axis=0, tiled=True) for shard in shards]
    return (
        full,
        lax.all_gather(tokens, "seq", axis=0, tiled=True),
        lax.all_gather(encoded, "seq", axis=0, tiled=True),
    )


def add_low(target, *terms):
    total = target[...]
    for term in terms:
        total = total + term[...]
    target[...] = total


def reduce_plain(grads, token_part, enc_part, small):
    def sums(value):
        return lax.psum_scatter(value.astype(jnp.float32), "seq", scatter_dimension=0, tiled=True)

    reduced = [
        lax.psum(
            lax.psum_scatter(grad.astype(jnp.float32), "fsdp", scatter_dimension=0, tiled=True), "seq"
        )
        for grad in grads
    ]
    return reduced, sums(token_part), sums(enc_part), lax.psum(small, ("seq", "fsdp"))


def columns(pair):
    return pl.ds(pl.multiple_of(pair * PAIR, PAIR), PAIR)


def row_steps(count, step):
    def run(body):
        @pl.loop(0, count // step)
        def _(n):
            body(pl.ds(pl.multiple_of(n * step, step), step))

    return run


def weight_grad(out, left, right):
    @row_steps(out.shape[0], 384)
    def _(part):
        out[part, :] = inner_rows(left[:, part], right[...]).astype(jnp.bfloat16)


def weight_grad_turned(out, turned, right):
    @row_steps(out.shape[0], 384)
    def _(part):
        out[part, :] = product(turned[part, :].astype(jnp.bfloat16), right[...]).astype(jnp.bfloat16)


def norm_back_rows(values, gain, grad_normed):
    scale = lax.rsqrt(jnp.mean(values * values, axis=-1, keepdims=True) + EPSILON)
    scaled = grad_normed * gain
    along = jnp.mean(values * scaled, axis=-1, keepdims=True)
    grad_values = scale * scaled - values * (scale * scale * scale) * along
    return grad_values, jnp.sum(grad_normed * values * scale, axis=0, keepdims=True)


class Space:
    def __init__(self, layout, refs):
        refs = list(refs)
        for name, count in layout.items():
            value = refs.pop(0) if count is None else [refs.pop(0) for _ in range(count)]
            setattr(self, name, value)


def flatten(*tables):
    layout, flat = {}, []
    for table in tables:
        for name, value in table.items():
            many = isinstance(value, list)
            layout[name] = len(value) if many else None
            flat += value if many else [value]
    return layout, flat


class StackRows(Stack):
    def __init__(self, first, rows, cols):
        super().__init__(rows, cols)
        self.first = first

    def planes(self, ref, quarter, core):
        return ref.at[quarter, :, core, pl.ds(self.first, self.rows), :]


DOWN, GATE, UP, CROSS, SELF, SELF_REST = range(6)
GROUPS = 6


class Sum:
    planes_first = False

    def __init__(self, g, kind, here, r, part):
        self.g, self.kind, self.here, self.r = g, kind, here, r
        self.part = part
        self.planes = here.planes
        self.sums, self.final = r.sums[g], r.final[g]
        self.side_x, self.side_y, self.last, self.from_z = r.side_x[g], r.side_y[g], r.last[g], r.from_z[g]
        self.started = []

    def send(self, make):
        remote(*make()).start()
        self.started.append(make)

    def arrived(self, target, recv_sem):
        pltpu.make_async_copy(target, target, recv_sem).wait()

    def pair_source(self, n, core):
        return self.kind.planes(self.part, n, core), self.sums.at[n]

    def start_pair(self, n):
        r, g = self.r, self.g
        source, target = self.pair_source(n, 1 - self.here.core)
        remote(source, target, r.c_send.at[g, n], r.c_recv.at[g, n], self.here.partner).start()

    def pair_part(self, n):
        source, target = self.pair_source(n, self.here.core)
        self.arrived(target, self.r.c_recv.at[self.g, n])

        @pl.loop(0, 4)
        def _(m):
            add_low(target.at[m], source.at[m])

        self.send_part(n)

    def pair_sum(self):
        @pl.loop(0, 4)
        def _(n):
            self.pair_part(n)

        self.sent_parts()

    def parts_sends(self):
        r, g, here = self.r, self.g, self.here
        for n, quarter in enumerate((here.along_x, here.corner)):
            yield quarter, lambda n=n, quarter=quarter: (
                self.half(quarter, 0), self.side_x.at[n], r.a_send.at[g, n], r.a_recv.at[g, n], here.to_x
            )
        for n, quarter in enumerate((here.along_y, here.corner)):
            yield quarter, lambda n=n, quarter=quarter: (
                self.half(quarter, 1), self.side_y.at[n], r.a_send.at[g, 2 + n], r.a_recv.at[g, 2 + n], here.to_y
            )

    def send_part(self, n):
        for part, make in self.parts_sends():

            @pl.when(n == part)
            def _(make=make):
                remote(*make()).start()

    def sent_parts(self):
        self.started += [make for _, make in self.parts_sends()]

    def pair_sent(self):
        for n in range(4):
            source, target = self.pair_source(n, 1 - self.here.core)
            remote(
                source, target, self.r.c_send.at[self.g, n], self.r.c_recv.at[self.g, n], self.here.partner
            ).wait_send()

    def half(self, quarter, second):
        size = self.planes // 2
        return self.sums.at[quarter, pl.ds(second * size, size)]

    def sides(self):
        for _, make in Sum.parts_sends(self):
            self.send(make)

    def add_half(self, quarter, second, terms, out=None):
        size = self.planes // 2

        @pl.loop(0, size)
        def _(z):
            add_low(self.sums.at[quarter, second * size + z], *[term.at[z] for term in terms])

    def first_side(self):
        r, g, here = self.r, self.g, self.here
        for n in range(2):
            self.arrived(self.side_x.at[n], r.a_recv.at[g, n])
            self.arrived(self.side_y.at[n], r.a_recv.at[g, 2 + n])
        self.add_half(here.along_y, 0, [self.side_x.at[1]])
        self.add_half(here.along_x, 1, [self.side_y.at[1]])
        for n, (quarter, device) in enumerate(((here.along_y, here.to_y), (here.along_x, here.to_x))):
            self.send(
                lambda n=n, quarter=quarter, device=device: (
                    self.half(quarter, n), self.last.at[n], r.b_send.at[g, n], r.b_recv.at[g, n], device
                )
            )

    def second_side(self):
        r, g, here = self.r, self.g, self.here
        for n in range(2):
            self.arrived(self.last.at[n], r.b_recv.at[g, n])
        self.add_half(here.seq, 0, [self.side_x.at[0], self.last.at[0]])
        self.add_half(here.seq, 1, [self.side_y.at[0], self.last.at[1]])
        self.after_square()

    def after_square(self):
        self.start_planes()

    def plane_share(self, plane):
        return self.sums.at[self.here.seq, plane]

    def plane_sends(self):
        r, g, here = self.r, self.g, self.here
        for k in range(1, self.planes):
            yield here.ahead(k), lambda k=k: (
                self.plane_share(here.ahead(k)), self.from_z.at[k - 1],
                r.z_send.at[g, k - 1], r.z_recv.at[g, k - 1], here.at_plane(here.ahead(k)),
            )

    def start_planes(self):
        for _, make in self.plane_sends():
            self.send(make)

    def along_planes(self):
        r, g, here = self.r, self.g, self.here
        for k in range(1, self.planes):
            self.arrived(self.from_z.at[k - 1], r.z_recv.at[g, k - 1])
        step = 16

        @pl.loop(0, self.kind.rows // step)
        def _(n):
            rows = pl.ds(pl.multiple_of(n * step, step), step)
            total = self.sums[here.seq, here.plane, rows, :].astype(jnp.float32)
            for k in range(1, self.planes):
                total = total + self.from_z[k - 1, rows, :].astype(jnp.float32)
            self.final[here.seq, rows, :] = total.astype(jnp.bfloat16)

        self.start_spread()

    def start_spread(self):
        r, g, here = self.r, self.g, self.here
        for n, device in enumerate((here.to_x, here.to_y)):
            self.send(
                lambda n=n, device=device: (
                    self.final.at[here.seq], self.final.at[here.seq], r.g_send.at[g, n], r.g_recv.at[g, n], device
                )
            )

    def across(self, quarter, second):
        size = self.kind.cols // 2
        return self.final.at[quarter, :, pl.ds(second * size, size)]

    def spread(self):
        r, g, here = self.r, self.g, self.here
        for n, (quarter, device) in enumerate(((here.along_x, here.to_y), (here.along_y, here.to_x))):
            self.arrived(self.final.at[quarter], r.g_recv.at[g, n])
            self.send(
                lambda n=n, quarter=quarter, device=device: (
                    self.across(quarter, n), self.across(quarter, n),
                    r.g_send.at[g, 2 + n], r.g_recv.at[g, 2 + n], device,
                )
            )

    def out_copies(self):
        r, g, kind = self.r, self.g, self.kind
        if isinstance(kind, Wide):
            return [
                pltpu.make_async_copy(
                    self.final.at[q], r.out[g].at[:, pl.ds(q * kind.cols, kind.cols)], r.out_sem.at[g, q]
                )
                for q in range(4)
            ]
        out = r.out[min(g, SELF)]
        if isinstance(kind, StackRows):
            out = out.at[:, pl.ds(kind.first, kind.rows), :]
        return [pltpu.make_async_copy(self.final, out, r.out_sem.at[g, 0])]

    def finish(self):
        r, g, here = self.r, self.g, self.here
        for n in range(2):
            self.arrived(self.across(here.corner, n), r.g_recv.at[g, 2 + n])
        for copy in self.out_copies():
            copy.start()

    def end(self):
        for copy in self.out_copies():
            copy.wait()
        if self.g not in (DOWN, CROSS):
            self.pair_sent()
        for make in self.started:
            remote(*make()).wait_send()


class PlanesFirst(Sum):
    planes_first = True

    def pair_source(self, n, core):
        return self.part.at[n, core], self.sums.at[:, n]

    def half(self, quarter, second):
        size = self.kind.cols // 2
        return self.sums.at[quarter, self.here.plane, :, pl.ds(second * size, size)]

    def plane_share(self, plane):
        return self.sums.at[:, plane]

    def parts_sends(self):
        return self.plane_sends()

    def along_planes(self):
        r, g, here = self.r, self.g, self.here
        for k in range(1, self.planes):
            self.arrived(self.from_z.at[k - 1], r.z_recv.at[g, k - 1])

        @pl.loop(0, 4)
        def _(q):
            add_low(self.sums.at[q, here.plane], *[self.from_z.at[k - 1, q] for k in range(1, self.planes)])

        self.sides()

    def add_half(self, quarter, second, terms, out=None):
        size = self.kind.cols // 2
        add_low(self.half(quarter, second), *terms)

    def after_square(self):
        self.final[self.here.seq] = self.sums[self.here.seq, self.here.plane]
        self.start_spread()


class BandSum(Sum):
    def pair_source(self, n, core):
        return self.part.at[n, :, core], self.sums.at[n]


class RowSum(Sum):
    def __init__(self, g, here, r, source, n):
        self.g, self.here, self.r, self.source = g, here, r, source
        self.size, self.cols = source.shape[0] // 4, source.shape[1] // 2
        self.side_x, self.side_y, self.last = r.row_x[n], r.row_y[n], r.row_last[n]
        self.started = []

    def half(self, quarter, second):
        return self.source.at[pl.ds(quarter * self.size, self.size), pl.ds(second * self.cols, self.cols)]

    def add_half(self, quarter, second, terms):
        @row_steps(self.size, 64)
        def _(part):
            add_low(self.half(quarter, second).at[part, :], *[term.at[part, :] for term in terms])

    def total(self, keep):
        r, g, here = self.r, self.g, self.here
        for n in range(2):
            self.arrived(self.last.at[n], r.b_recv.at[g, n])
        step = 64

        @row_steps(self.size, step)
        def _(part):
            halves = []
            for second, side in enumerate((self.side_x, self.side_y)):
                value = self.half(here.seq, second)[part, :].astype(jnp.float32)
                halves.append(
                    value + side[0, part, :].astype(jnp.float32) + self.last[second, part, :].astype(jnp.float32)
                )
            keep(part, jnp.concatenate(halves, axis=1))

    def sent(self):
        for make in self.started:
            remote(*make()).wait_send()


GELU_SCALE = math.sqrt(2.0 / math.pi)
GELU_CUBE = 0.044715
TOKENS, ENCODED = GROUPS, GROUPS + 1


def backward_kernel(kinds, planes, layout, *refs):
    r = Space(layout, refs)
    bf16, f32 = jnp.bfloat16, jnp.float32
    here = Peers(planes)
    place, length = here.seq, r.length[0]
    rows, width = r.grad_two.shape
    count, enc_count = r.rows_both.shape[0] // 2, r.ckeys_in.shape[0]
    owner_rows = width // (2 * planes)
    shape = (4, planes, 2, owner_rows, width)
    band = kinds[GATE].cols
    band_shape = (4, planes, 2, owner_rows, band)
    tall_shape = (planes, 2, 4, kinds[DOWN].rows, width)
    keys, values = r.rows_both.at[pl.ds(0, count), :], r.rows_both.at[pl.ds(count, count), :]
    down = PlanesFirst(DOWN, kinds[DOWN], here, r, r.rows_both.reshape(*tall_shape))
    gate = BandSum(GATE, kinds[GATE], here, r, r.grad_gate.reshape(*band_shape))
    up = BandSum(UP, kinds[UP], here, r, r.grad_up.reshape(*band_shape))
    cross = Sum(CROSS, kinds[CROSS], here, r, r.grad_cross.reshape(*shape))
    self_one = Sum(SELF, kinds[SELF], here, r, r.grad_self.reshape(*shape))
    self_two = Sum(SELF_REST, kinds[SELF_REST], here, r, r.grad_self.reshape(*shape))
    sums = (down, gate, up, cross, self_one, self_two)
    others = []

    ckeys, cvalues = r.dk.at[pl.ds(0, enc_count), :], r.dk.at[pl.ds(enc_count, enc_count), :]
    dck, dcv = r.dv.at[pl.ds(0, enc_count), :], r.dv.at[pl.ds(enc_count, enc_count), :]
    enc_all = r.token_part.at[pl.ds(0, enc_count), :]
    enc_part = r.token_part.at[pl.ds(enc_count, enc_count), :]
    token_sum = RowSum(TOKENS, here, r, r.token_part, 0)
    enc_sum = RowSum(ENCODED, here, r, enc_part, 1)
    act, d_gate, d_up = (r.token_part.at[pl.ds(n * rows, rows), pl.ds(0, band)] for n in range(3))

    def send(make):
        remote(*make()).start()
        others.append(make)

    def arrived(target, recv_sem):
        pltpu.make_async_copy(target, target, recv_sem).wait()

    def load(n, source, target):
        copy = pltpu.make_async_copy(source, target, r.load_sem.at[n])
        copy.start()
        return copy

    def ffn_copies(n):
        slot, part = n % 2, pl.ds(pl.multiple_of(n * band, band), band)
        return [
            pltpu.make_async_copy(r.w_gate.at[:, part], r.grad_self.at[slot, :, pl.ds(0, band)], r.f_sem.at[0, slot]),
            pltpu.make_async_copy(r.w_up.at[:, part], r.grad_self.at[2 + slot, :, pl.ds(0, band)], r.f_sem.at[1, slot]),
            pltpu.make_async_copy(r.w_down.at[part, :], r.grad_cross.at[slot, pl.ds(0, band), :], r.f_sem.at[2, slot]),
        ]

    def start_ffn(n):
        for copy in ffn_copies(n):
            copy.start()

    here.greet()
    cotangent_load = load(0, r.cotangent, r.grad_mixed)
    normed_three_load = load(6, r.normed_three_in, r.normed)
    start_ffn(0)
    start_ffn(1)
    hidden_two_load = load(11, r.hidden_two_in, r.hidden)
    mixed_load = load(2, r.mixed_cross_in, r.mixed)
    cqueries_load = load(3, r.cqueries_in, r.queries)
    ckeys_load = load(4, r.ckeys_in, ckeys)
    cvalues_load = load(5, r.cvalues_in, cvalues)

    def grad_result(part, step):
        slots = place * rows + part.start + iota((step, 1), 0)
        return jnp.where(slots < length, r.grad_mixed[part, :].astype(f32), 0.0)

    cotangent_load.wait()

    @row_steps(rows, 64)
    def _(part):
        r.branch[part, :] = grad_result(part, 64).astype(bf16)

    normed_three_load.wait()

    @pl.loop(0, 4)
    def _(n):
        slot = n % 2
        for copy in ffn_copies(n):
            copy.wait()
        normed = r.normed[...]
        branch = r.branch[...]
        w_gate = r.grad_self[slot, :, 0:band]
        w_up = r.grad_self[2 + slot, :, 0:band]
        w_down = r.grad_cross[slot, 0:band, :]
        gate_band = product(normed, w_gate)
        up_band = product(normed, w_up)
        inner = jnp.tanh(GELU_SCALE * (gate_band + GELU_CUBE * (gate_band * gate_band * gate_band)))
        lifted = 0.5 * (1.0 + inner)
        gelu = gate_band * lifted
        slope = lifted + (0.5 * GELU_SCALE) * gate_band * (1.0 - inner * inner) * (
            1.0 + (3.0 * GELU_CUBE) * (gate_band * gate_band)
        )
        act[...] = (gelu * up_band).astype(bf16)
        grad_act = outer_rows(branch, w_down)
        d_gate[...] = (grad_act * up_band * slope).astype(bf16)
        d_up[...] = (grad_act * gelu).astype(bf16)
        first = pl.ds(pl.multiple_of(n * band, band), band)
        r.rows_both[first, :] = inner_rows(act[...], branch).astype(bf16)
        r.grad_gate[n] = inner_rows(normed, d_gate[...]).astype(bf16)
        r.grad_up[n] = inner_rows(normed, d_up[...]).astype(bf16)

        @pl.when(n == 0)
        def _():
            here.meet()

        down.start_pair(n)
        gate.start_pair(n)
        up.start_pair(n)
        out = product(act[...], w_down)
        gy = outer_rows(d_gate[...], w_gate) + outer_rows(d_up[...], w_up)

        @pl.when(n == 0)
        def _():
            r.grad_two[...] = out
            r.gy[...] = gy

        @pl.when(n > 0)
        def _():
            r.grad_two[...] += out
            r.gy[...] += gy

        @pl.when(n < 2)
        def _():
            start_ffn(n + 2)

        @pl.when(n > 0)
        def _():
            for group in (down, gate, up):
                group.pair_part(n - 1)

    w_cout_load = load(1, r.w_two.at[3], r.grad_self.at[3])
    w_two_loads = [load(8 + m, r.w_two.at[m], r.grad_self.at[m]) for m in range(3)]
    encoded_load = load(7, r.enc_in, enc_all)
    hidden_two_load.wait()
    r.small[...] = jnp.zeros_like(r.small)

    @row_steps(rows, 64)
    def _(part):
        hidden = r.hidden[part, :]
        slots = place * rows + part.start + iota((64, 1), 0)
        r.dq[part, :] = jnp.where(slots < length, hidden + r.grad_two[part, :], 0.0).astype(bf16)
        grad, gain = norm_back_rows(hidden, r.gains[2:3, :], r.gy[part, :])
        total = grad_result(part, 64) + grad
        r.grad_two[part, :] = total
        r.branch[part, :] = total.astype(bf16)
        r.small[2:3, :] += gain

    result_copy = load(13, r.dq, r.layer_out)
    normed_two_load = load(6, r.normed_two_in, r.normed)
    hidden_load = load(11, r.hidden_one_in, r.hidden)
    fill_pads(r.pads, count)
    fill_fixed_bias(r.bias)
    for group in (down, gate, up):
        group.pair_part(3)
        group.sent_parts()
    w_cout_load.wait()
    r.grad_mixed[...] = outer_rows(r.branch[...], r.grad_self[3]).astype(bf16)
    w_sout_load = load(12, r.w_one.at[3], r.grad_self.at[3])
    mixed_load.wait()
    weight_grad_turned(r.grad_cross.at[3], r.mixed, r.branch)
    for copy in (cqueries_load, ckeys_load, cvalues_load):
        copy.wait()
    result_copy.wait()
    down.pair_sent()
    keys_load = load(13, r.keys_in, keys)
    values_load = load(14, r.values_in, values)

    def stepped(table, pair):
        for when, steps in table.items():

            @pl.when(pair == when)
            def _(steps=steps):
                for step in steps:
                    step()

    @pl.loop(0, PAIRS)
    def _(pair):
        part = columns(pair)
        backward_pair(
            None, None, r.queries.at[:, part], ckeys.at[:, part], cvalues.at[:, part],
            r.grad_mixed.at[:, part], r.mixed.at[part, :], r.log_cross.at[pair],
            r.dq.at[:, part], dck.at[:, part], dcv.at[:, part], None, None, r.pads, None, r.kt_buf, None,
        )

    fill_pads(r.pads, length)
    mixed_self_load = load(15, r.mixed_self_in, r.mixed)
    queries_load = load(16, r.queries_in, r.queries)
    w_two_loads[0].wait()
    r.gy[...] = outer_rows(r.dq[...], r.grad_self[0])
    normed_two_load.wait()
    weight_grad(r.grad_cross.at[0], r.normed, r.dq)
    gate.first_side()
    encoded_load.wait()
    weight_grad(r.grad_cross.at[1], enc_all, dck)
    weight_grad(r.grad_cross.at[2], enc_all, dcv)
    for n in range(4):
        cross.start_pair(n)
    w_two_loads[1].wait()
    w_two_loads[2].wait()
    enc_part[...] = (outer_rows(dck[...], r.grad_self[1]) + outer_rows(dcv[...], r.grad_self[2])).astype(bf16)
    quarters = ((here.along_x, here.to_x), (here.along_y, here.to_y), (here.corner, here.to_corner))

    def own_rows(ref, size, part, step):
        return ref[pl.ds(pl.multiple_of(place * size + part.start, step), step), :].astype(f32)

    enc_sum.sides()
    hidden_load.wait()

    @row_steps(rows, 64)
    def _(part):
        grad, gain = norm_back_rows(r.hidden[part, :], r.gains[1:2, :], r.gy[part, :])
        total = r.grad_two[part, :] + grad
        r.grad_two[part, :] = total
        r.branch[part, :] = total.astype(bf16)
        r.small[1:2, :] += gain

    w_sout_load.wait()
    r.grad_mixed[...] = outer_rows(r.branch[...], r.grad_self[3]).astype(bf16)
    mixed_self_load.wait()
    weight_grad_turned(r.grad_self.at[3], r.mixed, r.branch)
    for copy in (queries_load, keys_load, values_load):
        copy.wait()

    def keep_enc(part, total):
        r.enc_total[part, :] = total

    def enc_done():
        enc_sum.total(keep_enc)
        pltpu.make_async_copy(r.enc_total, r.enc_sum, r.load_sem.at[20]).start()

    def cross_sides():
        cross.pair_sum()

    def load_normed():
        enc_sum.sent()
        pltpu.make_async_copy(r.normed_all_in, r.token_part, r.load_sem.at[21]).start()

    def w_one_copies():
        return [
            pltpu.make_async_copy(r.w_one.at[m], r.grad_cross.at[m], r.load_sem.at[17 + m]) for m in range(3)
        ]

    def load_w_one():
        cross.pair_sent()
        for copy in w_one_copies():
            copy.start()

    self_steps = {
        0: [up.first_side, cross_sides],
        1: [enc_sum.first_side, gate.second_side],
        2: [down.along_planes, up.second_side],
        3: [enc_done, load_normed],
        4: [down.first_side, load_w_one],
        5: [cross.first_side],
    }

    @pl.loop(0, PAIRS)
    def _(pair):
        part = columns(pair)
        backward_pair(
            place, r.profile.at[pair], r.queries.at[:, part], keys.at[:, part],
            values.at[:, part], r.grad_mixed.at[:, part], r.mixed.at[part, :],
            r.log_self.at[pair], r.dq.at[:, part], r.dk.at[:, part], r.dv.at[:, part],
            r.near.at[pair], r.far.at[pair], r.pads, r.bias, r.kt_buf, r.grad_buf,
        )
        stepped(self_steps, pair)

    tokens_load = load(22, r.tokens_all_in, keys)
    pltpu.make_async_copy(r.normed_all_in, r.token_part, r.load_sem.at[21]).wait()
    own = pl.ds(pl.multiple_of(place * rows, BLOCK), rows)
    weight_grad(r.grad_self.at[0], r.token_part.at[own, :], r.dq)
    weight_grad(r.grad_self.at[1], r.token_part, r.dk)
    weight_grad(r.grad_self.at[2], r.token_part, r.dv)
    for n in range(4):
        self_one.start_pair(n)
    for n in range(4):
        self_two.start_pair(n)
    for copy in w_one_copies():
        copy.wait()

    @row_steps(count, 512)
    def _(part):
        total = outer_rows(r.dk[part, :], r.grad_cross[1]) + outer_rows(r.dv[part, :], r.grad_cross[2])
        r.token_part[part, :] = total.astype(bf16)

    self_one.pair_sum()
    self_two.pair_sum()
    gate.along_planes()
    down.second_side()
    cross.second_side()
    token_sum.sides()
    r.gy[...] = outer_rows(r.dq[...], r.grad_cross[0])
    up.along_planes()
    tokens_load.wait()

    @row_steps(count, 64)
    def _(part):
        values = keys[part, :].astype(f32)
        scale = lax.rsqrt(jnp.mean(values * values, axis=-1, keepdims=True) + EPSILON)
        grad = r.token_part[part, :].astype(f32)
        r.small[0:1, :] += jnp.sum(grad * values * scale, axis=0, keepdims=True)

    @row_steps(rows, 64)
    def _(part):
        values = own_rows(keys, rows, part, 64)
        scale = lax.rsqrt(jnp.mean(values * values, axis=-1, keepdims=True) + EPSILON)
        r.small[0:1, :] += jnp.sum(r.gy[part, :] * values * scale, axis=0, keepdims=True)

    for pair in range(PAIRS):
        table = jnp.dot(
            r.near[pair], r.one_hot[...], precision=lax.Precision.HIGHEST, preferred_element_type=f32
        )
        last_bucket = iota(table.shape, 1) == BUCKETS - 1
        table = table + jnp.where(last_bucket, jnp.sum(r.far[pair], axis=1, keepdims=True), 0.0)
        r.small[8 + 2 * pair : 10 + 2 * pair, 0 : table.shape[1]] = table

    small, small_core, small_seq, small_plane = r.small, r.small_core, r.small_seq, r.small_plane
    send(lambda: (small, small_core, r.s_send.at[0], r.s_recv.at[0], here.partner))
    down.spread()
    gate.spread()
    self_one.first_side()
    arrived(small_core, r.s_recv.at[0])
    small_seq[place] = small[...] + small_core[...]
    for k, (_, device) in enumerate(quarters):
        send(
            lambda k=k, device=device: (
                small_seq.at[place], small_seq.at[place], r.s_send.at[1 + k], r.s_recv.at[1 + k], device
            )
        )
    down.finish()
    self_two.first_side()
    token_sum.first_side()
    cross.along_planes()
    up.spread()
    self_one.second_side()
    for k, (quarter, _) in enumerate(quarters):
        arrived(small_seq.at[quarter], r.s_recv.at[1 + k])
    small_plane[here.plane] = (small_seq[0] + small_seq[1]) + (small_seq[2] + small_seq[3])
    for k in range(1, planes):
        send(
            lambda k=k: (
                small_plane.at[here.plane], small_plane.at[here.plane],
                r.s_send.at[3 + k], r.s_recv.at[3 + k], here.at_plane(here.ahead(k)),
            )
        )
    gate.finish()
    self_two.second_side()
    cross.spread()
    up.finish()
    self_one.along_planes()
    cross.finish()

    def keep_tokens(part, total):
        values = own_rows(keys, rows, part, 64)
        grad, _ = norm_back_rows(values, r.gains[0:1, :], r.gy[part, :] + total)
        r.hidden[part, :] = r.grad_two[part, :] + grad

    token_sum.total(keep_tokens)
    token_copy = pltpu.make_async_copy(r.hidden, r.grad_tokens, r.load_sem.at[23])
    token_copy.start()
    for k in range(1, planes):
        arrived(small_plane.at[here.ahead(planes - k)], r.s_recv.at[3 + k])
    total = small_plane[0]
    for k in range(1, planes):
        total = total + small_plane[k]
    r.small_out[...] = total
    self_two.along_planes()
    self_one.spread()
    self_one.finish()
    self_two.spread()
    self_two.finish()
    token_copy.wait()
    pltpu.make_async_copy(r.enc_total, r.enc_sum, r.load_sem.at[20]).wait()
    for group in sums:
        group.end()
    token_sum.sent()
    for make in others:
        remote(*make()).wait_send()


def backward_fused(shards, length, small, large):
    stack, _, band, _, tall = make_kinds(shards)
    planes = lax.axis_size("fsdp") // 2
    lower = planes // 2
    first_rows = stack.rows // 2
    parts = [StackRows(n * first_rows, first_rows, stack.cols) for n in range(2)]
    kinds = [tall, band, band, stack, *parts]
    f32, low = jnp.float32, jnp.bfloat16
    rows, width = large["cotangent"].shape
    count, enc_count = large["keys_in"].shape[0], large["ckeys_in"].shape[0]
    in_vmem = pl.BlockSpec(memory_space=pltpu.VMEM)
    in_layout, operands = flatten(dict(length=length), small, large)
    in_specs = [SCALARS] + [in_vmem] * len(small)
    in_specs += [ANYWHERE] * (len(operands) - len(in_specs))
    small_shape = (24, width)

    def chunk(kind, *lead):
        return pltpu.VMEM(lead + (kind.rows, kind.cols), low)

    results = dict(
        out=[
            shaped((kind.rows, 4 * kind.cols) if isinstance(kind, Wide) else (4, kind.rows, kind.cols), low)
            for kind in (tall, band, band, stack, stack)
        ],
        layer_out=shaped((rows, width), low),
        grad_tokens=shaped((rows, width), f32),
        enc_sum=shaped((enc_count // 4, width), f32),
        small_out=shaped(small_shape, f32),
    )
    out_layout, out_shapes = flatten(results)
    square = (width, width)
    all_rows = pltpu.VMEM((count, width), low)
    some_rows = pltpu.VMEM((rows, width), low)
    wide_rows = pltpu.VMEM((rows, width), f32)
    half_tall = pltpu.VMEM((2, tall.rows, tall.cols // 2), low)
    later = kinds[1:]
    sides = [half_tall] + [chunk(kind, 2, lower) for kind in later]
    row_sides = [pltpu.VMEM((2, size, width // 2), low) for size in (rows, enc_count // 4)]
    buffers = backward_scratch(count)
    scratch = dict(
        sums=[chunk(kind, 4, planes) for kind in kinds],
        side_x=sides, side_y=sides, last=sides,
        from_z=[chunk(tall, planes - 1, 4)] + [chunk(kind, planes - 1) for kind in later],
        final=[chunk(kind, 4) for kind in kinds],
        grad_gate=pltpu.VMEM((4, width, band.cols), low),
        grad_up=pltpu.VMEM((4, width, band.cols), low),
        grad_cross=pltpu.VMEM((4,) + square, low),
        grad_self=pltpu.VMEM((4,) + square, low),
        rows_both=pltpu.VMEM((2 * count, width), low),
        dk=all_rows, dv=all_rows, token_part=all_rows,
        queries=some_rows, normed=some_rows, branch=some_rows, grad_mixed=some_rows, dq=some_rows,
        grad_two=wide_rows, hidden=wide_rows, gy=wide_rows,
        mixed=pltpu.VMEM((width, rows), f32),
        enc_total=pltpu.VMEM((enc_count // 4, width), f32),
        row_x=row_sides, row_y=row_sides, row_last=row_sides,
        pads=buffers[0], bias=buffers[1], kt_buf=buffers[2], grad_buf=buffers[3],
        near=pltpu.VMEM((PAIRS, 2, BLOCK), f32),
        far=pltpu.VMEM((PAIRS, 2, rows), f32),
        small=pltpu.VMEM(small_shape, f32),
        small_core=pltpu.VMEM(small_shape, f32),
        small_seq=pltpu.VMEM((4,) + small_shape, f32),
        small_plane=pltpu.VMEM((planes,) + small_shape, f32),
        f_sem=DMA((3, 2)),
        c_send=DMA((GROUPS, 4)), c_recv=DMA((GROUPS, 4)),
        a_send=DMA((GROUPS + 2, 4)), a_recv=DMA((GROUPS + 2, 4)),
        b_send=DMA((GROUPS + 2, 2)), b_recv=DMA((GROUPS + 2, 2)),
        z_send=DMA((GROUPS, planes - 1)), z_recv=DMA((GROUPS, planes - 1)),
        g_send=DMA((GROUPS, 4)), g_recv=DMA((GROUPS, 4)),
        s_send=DMA((3 + planes,)), s_recv=DMA((3 + planes,)),
        out_sem=DMA((GROUPS, 4)), load_sem=DMA((24,)),
    )
    scratch_layout, scratch_shapes = flatten(scratch)
    outs = pl.pallas_call(
        functools.partial(backward_kernel, kinds, planes, in_layout | out_layout | scratch_layout),
        in_specs=in_specs,
        out_specs=[ANYWHERE] * (len(out_shapes) - 1) + [in_vmem],
        out_shape=out_shapes,
        scratch_shapes=scratch_shapes,
        compiler_params=pltpu.CompilerParams(
            collective_id=1, has_side_effects=True, vmem_limit_bytes=67_000_000
        ),
        name="backward_fused",
    )(*operands)
    got = Space(out_layout, outs)
    grads = [got.out[SELF][m] for m in range(4)] + [got.out[CROSS][m] for m in range(4)]
    grads += [got.out[GATE], got.out[UP], got.out[DOWN].reshape(-1, width)]
    return got.layer_out, [grad.astype(f32) for grad in grads], got.grad_tokens, got.enc_sum, got.small_out


ONE, TWO, GATE_IN, UP_IN, DOWN_IN = range(5)


class Gathering:
    def __init__(self, kinds, here, r):
        self.kinds, self.here, self.r = kinds, here, r
        self.planes = here.planes
        shape = (4, here.planes, 2, kinds[ONE].rows, kinds[ONE].cols)
        self.full = [r.weights_one.reshape(*shape), r.weights_two.reshape(*shape), *r.ffn_full]
        self.shards = [r.shards[0:4], r.shards[4:8], r.shards[8], r.shards[9], r.shards[10]]
        self.started = []

    def send(self, make):
        remote(*make()).start()
        self.started.append(make)

    def arrived(self, target, recv_sem):
        pltpu.make_async_copy(target, target, recv_sem).wait()

    def plane_copy(self, g, k, source):
        here, r = self.here, self.r
        return remote(
            source, self.kinds[g].part(self.full[g], here.seq, here.plane, here.core),
            r.z_send.at[g, k - 1], r.z_recv.at[g, k - 1], here.at_plane(here.ahead(k)),
        )

    def start_planes(self, g):
        for k in range(1, self.planes):
            if g <= TWO:
                for m in range(4):

                    @pl.when(self.here.seq == m)
                    def _(m=m, k=k):
                        self.plane_copy(g, k, self.shards[g][m]).start()

            else:
                self.plane_copy(g, k, self.kinds[g].own(self.shards[g], self.here.seq)).start()

    def own_copies(self, g):
        here, r, full = self.here, self.r, self.full[g]
        if g <= TWO:
            return [
                pltpu.make_async_copy(
                    self.shards[g][m], full.at[m, here.plane, here.core], r.own_sem.at[g, m]
                )
                for m in range(4)
            ]
        return [
            pltpu.make_async_copy(
                self.shards[g], self.kinds[g].whole(full, here.plane, here.core), r.own_sem.at[g, 0]
            )
        ]

    def start_own(self, g):
        here, r, full = self.here, self.r, self.full[g]
        for copy in self.own_copies(g):
            copy.start()
        if g <= TWO:
            for m in range(4):
                self.send(
                    lambda m=m: (
                        self.shards[g][m], full.at[m, here.plane, here.core],
                        r.p_send.at[g, m], r.p_recv.at[g, m], here.partner,
                    )
                )
        else:
            self.send(
                lambda: (
                    self.shards[g], self.kinds[g].whole(full, here.plane, here.core),
                    r.p_send.at[g, 0], r.p_recv.at[g, 0], here.partner,
                )
            )

    def chunk(self, g, quarter, k, first=0, count=None):
        here = self.here
        return self.kinds[g].part(self.full[g], quarter, here.ahead(self.planes - k), here.core, first, count)

    def from_plane(self, g):
        here, r = self.here, self.r
        for k in range(1, self.planes):
            self.arrived(self.chunk(g, here.seq, k), r.z_recv.at[g, k - 1])
            for n, device in enumerate((here.to_x, here.to_y)):

                def make(k=k, n=n, device=device):
                    chunk = self.chunk(g, here.seq, k)
                    return chunk, chunk, r.x_send.at[n, g, k - 1], r.x_recv.at[n, g, k - 1], device

                self.send(make)

    def from_sides(self, g):
        here, r = self.here, self.r
        half = self.kinds[g].rows // 2
        turns = ((here.along_x, 0, here.to_y), (here.along_y, half, here.to_x))
        for k in range(1, self.planes):
            for n, (quarter, first, device) in enumerate(turns):
                self.arrived(self.chunk(g, quarter, k), r.x_recv.at[n, g, k - 1])

                def make(k=k, n=n, quarter=quarter, first=first, device=device):
                    chunk = self.chunk(g, quarter, k, first, half)
                    return chunk, chunk, r.d_send.at[n, g, k - 1], r.d_recv.at[n, g, k - 1], device

                self.send(make)

    def from_corner(self, g):
        here, r = self.here, self.r
        half = self.kinds[g].rows // 2
        for k in range(1, self.planes):
            self.arrived(self.chunk(g, here.corner, k, 0, half), r.d_recv.at[0, g, k - 1])
            self.arrived(self.chunk(g, here.corner, k, half, half), r.d_recv.at[1, g, k - 1])

            def make(k=k):
                whole = self.kinds[g].whole(self.full[g], here.ahead(self.planes - k), here.core)
                return whole, whole, r.c_send.at[g, k - 1], r.c_recv.at[g, k - 1], here.partner

            self.send(make)

    def complete(self, g):
        here, r, full = self.here, self.r, self.full[g]
        for copy in self.own_copies(g):
            copy.wait()
        if g <= TWO:
            for m in range(4):
                self.arrived(full.at[m, here.plane, 1 - here.core], r.p_recv.at[g, m])
        else:
            self.arrived(self.kinds[g].whole(full, here.plane, 1 - here.core), r.p_recv.at[g, 0])
        for k in range(1, self.planes):
            behind = here.ahead(self.planes - k)
            self.arrived(self.kinds[g].whole(full, behind, 1 - here.core), r.c_recv.at[g, k - 1])

    def end(self):
        for g in range(5):
            for k in range(1, self.planes):
                source = self.shards[g][0] if g <= TWO else self.kinds[g].own(self.shards[g], self.here.seq)
                self.plane_copy(g, k, source).wait_send()
        for make in self.started:
            remote(*make()).wait_send()


def forward_kernel(kinds, planes, layout, *refs):
    r = Space(layout, refs)
    bf16, f32 = jnp.bfloat16, jnp.float32
    here = Peers(planes)
    place, length = here.seq, r.length[0]
    gather = Gathering(kinds, here, r)
    rows, width = r.tokens.shape
    count, enc_count = r.normed.shape[0], r.encoded_rows.shape[0]
    row_ins = (r.tokens, r.encoded)
    row_alls = (r.source_rows, r.encoded_rows)
    stores = []

    def store(n, source, target):
        stores.append((n, source, target))
        pltpu.make_async_copy(source, target, r.store_sem.at[n]).start()

    def block_of(item, quarter, first=0, size=None):
        size_here = row_ins[item].shape[0]
        return row_alls[item].at[pl.ds(quarter * size_here + first, size or size_here), :]

    def rows_start(item):
        for n, device in enumerate((here.to_x, here.to_y)):
            gather.send(
                lambda n=n, device=device: (
                    row_ins[item], block_of(item, place), r.r_send.at[item, n], r.r_recv.at[item, n], device
                )
            )
        pltpu.make_async_copy(row_ins[item], block_of(item, place), r.r_own.at[item]).start()

    def rows_turn(item):
        half = row_ins[item].shape[0] // 2
        turns = ((here.along_x, 0, here.to_y), (here.along_y, half, here.to_x))
        for n, (quarter, first, device) in enumerate(turns):
            gather.arrived(block_of(item, quarter), r.r_recv.at[item, n])

            def make(n=n, quarter=quarter, first=first, device=device):
                chunk = block_of(item, quarter, first, half)
                return chunk, chunk, r.r_send.at[item, 2 + n], r.r_recv.at[item, 2 + n], device

            gather.send(make)

    def rows_done(item):
        half = row_ins[item].shape[0] // 2
        gather.arrived(block_of(item, here.corner, 0, half), r.r_recv.at[item, 2])
        gather.arrived(block_of(item, here.corner, half, half), r.r_recv.at[item, 3])
        pltpu.make_async_copy(row_ins[item], block_of(item, place), r.r_own.at[item]).wait()

    def norm_rows(values, gain):
        scale = lax.rsqrt(jnp.mean(values * values, axis=-1, keepdims=True) + EPSILON)
        return (values * scale * gain).astype(bf16)

    def project(out, left, weight):
        step = min(left.shape[0], 512)

        @row_steps(left.shape[0], step)
        def _(part):
            out[part, :] = product(left[part, :], weight[...]).astype(out.dtype)

    here.greet()
    here.meet()
    rows_start(0)
    gather.start_planes(ONE)
    rows_start(1)
    for g in (TWO, GATE_IN, UP_IN, DOWN_IN):
        gather.start_planes(g)
    for g in range(5):
        gather.start_own(g)
    fill_pads(r.pads, length)
    fill_fixed_bias(r.bias)
    rows_turn(0)
    gather.from_plane(ONE)
    rows_turn(1)
    rows_done(0)

    @row_steps(count, 128)
    def _(part):
        r.normed[part, :] = norm_rows(r.source_rows[part, :].astype(f32), r.gains[0:1, :])

    store(0, r.source_rows, r.tokens_all)
    store(1, r.normed, r.normed_all)
    gather.from_sides(ONE)
    gather.from_plane(TWO)
    gather.from_corner(ONE)
    rows_done(1)
    store(2, r.encoded_rows, r.enc_all)
    gather.complete(ONE)
    store(3, r.weights_one, r.w_one)
    own = pl.ds(pl.multiple_of(place * rows, BLOCK), rows)
    project(r.query_rows, r.normed.at[own, :], r.weights_one.at[0])
    project(r.key_rows, r.normed, r.weights_one.at[1])
    project(r.value_rows, r.normed, r.weights_one.at[2])
    store(4, r.query_rows, r.queries)
    store(5, r.key_rows, r.keys)
    store(6, r.value_rows, r.values)
    gather.from_plane(GATE_IN)
    gather.from_sides(TWO)
    self_steps = {2: [lambda: gather.from_plane(UP_IN)], 4: [lambda: gather.from_corner(TWO)]}

    def stepped(table, pair):
        for when, steps in table.items():

            @pl.when(pair == when)
            def _(steps=steps):
                for step in steps:
                    step()

    @pl.loop(0, PAIRS)
    def _(pair):
        part = columns(pair)
        self_forward_pair(
            place, r.profile.at[pair], r.query_rows.at[:, part], r.key_rows.at[:, part],
            r.value_rows.at[:, part], r.mixed.at[:, part], r.turned_one.at[part, :], r.log_self.at[pair],
            r.pads, r.bias, r.s_buf, r.vt_buf,
        )
        stepped(self_steps, pair)

    store(7, r.turned_one, r.mixed_self_turned)
    project(r.hidden, r.mixed, r.weights_one.at[3])

    @row_steps(rows, 64)
    def _(part):
        start = pl.multiple_of(place * rows + part.start, 64)
        total = r.hidden[part, :] + r.source_rows[pl.ds(start, 64), :].astype(f32)
        r.hidden[part, :] = total
        r.normed_rows[part, :] = norm_rows(total, r.gains[1:2, :])

    store(8, r.hidden, r.hidden_one)
    store(9, r.normed_rows, r.normed_two)
    gather.from_plane(DOWN_IN)
    gather.from_sides(GATE_IN)
    gather.complete(TWO)
    store(10, r.weights_two, r.w_two)
    project(r.cquery_rows, r.normed_rows, r.weights_two.at[0])
    project(r.ckey_rows, r.encoded_rows, r.weights_two.at[1])
    project(r.cvalue_rows, r.encoded_rows, r.weights_two.at[2])
    store(11, r.cquery_rows, r.cqueries)
    store(12, r.ckey_rows, r.ckeys)
    store(13, r.cvalue_rows, r.cvalues)
    cross_steps = {
        1: [lambda: gather.from_corner(GATE_IN)],
        3: [lambda: gather.from_sides(UP_IN)],
    }

    @pl.loop(0, PAIRS)
    def _(pair):
        part = columns(pair)
        cross_forward_pair(
            r.cquery_rows.at[:, part], r.ckey_rows.at[:, part], r.cvalue_rows.at[:, part],
            r.cmixed.at[:, part], r.turned_two.at[part, :], r.log_cross.at[pair],
        )
        stepped(cross_steps, pair)

    store(14, r.turned_two, r.mixed_cross_turned)
    gather.from_sides(DOWN_IN)
    project(r.hidden_last, r.cmixed, r.weights_two.at[3])

    @row_steps(rows, 64)
    def _(part):
        total = r.hidden_last[part, :] + r.hidden[part, :]
        r.hidden_last[part, :] = total
        r.normed_last[part, :] = norm_rows(total, r.gains[2:3, :])

    store(15, r.hidden_last, r.hidden_two)
    store(16, r.normed_last, r.normed_three)
    gather.from_corner(UP_IN)
    gather.from_corner(DOWN_IN)
    for g in (GATE_IN, UP_IN, DOWN_IN):
        gather.complete(g)
    gather.end()
    for n, source, target in stores:
        pltpu.make_async_copy(source, target, r.store_sem.at[n]).wait()


def forward_fused(shards, length, tokens, encoded, small):
    kinds = make_kinds(shards)
    planes = lax.axis_size("fsdp") // 2
    f32, low = jnp.float32, jnp.bfloat16
    rows, width = tokens.shape
    enc_rows = encoded.shape[0]
    count, enc_count = 4 * rows, 4 * enc_rows
    square = (4, width, width)
    in_vmem = pl.BlockSpec(memory_space=pltpu.VMEM)
    in_layout, operands = flatten(
        dict(length=length), small, dict(tokens=tokens, encoded=encoded, shards=list(shards))
    )
    in_specs = [SCALARS] + [in_vmem] * len(small)
    in_specs += [ANYWHERE] * (len(operands) - len(in_specs))
    shapes = full_shapes(kinds, planes)
    large_outs = dict(
        w_one=shaped(square, low), w_two=shaped(square, low),
        ffn_full=[shaped(shape, low) for shape in shapes[2:]],
        tokens_all=shaped((count, width), low), normed_all=shaped((count, width), low),
        enc_all=shaped((enc_count, width), low),
        queries=shaped((rows, width), low), keys=shaped((count, width), low),
        values=shaped((count, width), low), mixed_self_turned=shaped((width, rows), f32),
        hidden_one=shaped((rows, width), f32), normed_two=shaped((rows, width), low),
        cqueries=shaped((rows, width), low), ckeys=shaped((enc_count, width), low),
        cvalues=shaped((enc_count, width), low), mixed_cross_turned=shaped((width, rows), f32),
        hidden_two=shaped((rows, width), f32), normed_three=shaped((rows, width), low),
    )
    small_outs = dict(
        log_self=shaped((PAIRS, 2, rows), f32), log_cross=shaped((PAIRS, 2, rows), f32)
    )
    out_layout, out_shapes = flatten(large_outs, small_outs)
    all_rows = pltpu.VMEM((count, width), low)
    enc_all = pltpu.VMEM((enc_count, width), low)
    some_rows = pltpu.VMEM((rows, width), low)
    wide_rows = pltpu.VMEM((rows, width), f32)
    turned = pltpu.VMEM((width, rows), f32)
    buffers = forward_scratch(count, rows)
    steps = planes - 1
    scratch = dict(
        weights_one=pltpu.VMEM(square, low), weights_two=pltpu.VMEM(square, low),
        source_rows=all_rows, normed=all_rows, key_rows=all_rows, value_rows=all_rows,
        encoded_rows=enc_all, ckey_rows=enc_all, cvalue_rows=enc_all,
        query_rows=some_rows, cquery_rows=some_rows, mixed=some_rows, cmixed=some_rows,
        normed_rows=some_rows, normed_last=some_rows,
        hidden=wide_rows, hidden_last=wide_rows, turned_one=turned, turned_two=turned,
        pads=buffers[0], bias=buffers[1], s_buf=buffers[2], vt_buf=buffers[3],
        z_send=DMA((5, steps)), z_recv=DMA((5, steps)),
        own_sem=DMA((5, 4)), p_send=DMA((5, 4)), p_recv=DMA((5, 4)),
        x_send=DMA((2, 5, steps)), x_recv=DMA((2, 5, steps)),
        d_send=DMA((2, 5, steps)), d_recv=DMA((2, 5, steps)),
        c_send=DMA((5, steps)), c_recv=DMA((5, steps)),
        r_send=DMA((2, 4)), r_recv=DMA((2, 4)), r_own=DMA((2,)), store_sem=DMA((17,)),
    )
    scratch_layout, scratch_shapes = flatten(scratch)
    outs = pl.pallas_call(
        functools.partial(forward_kernel, kinds, planes, in_layout | out_layout | scratch_layout),
        in_specs=in_specs,
        out_specs=[ANYWHERE] * (len(out_shapes) - 2) + [in_vmem] * 2,
        out_shape=out_shapes,
        scratch_shapes=scratch_shapes,
        compiler_params=pltpu.CompilerParams(
            collective_id=0, has_side_effects=True, vmem_limit_bytes=66_000_000
        ),
        name="forward_fused",
    )(*operands)
    return Space(out_layout, outs)


def local(
    tokens, encoded, lengths, cotangent, gain_self, gain_cross, gain_ff, bucket_table,
    self_query, self_key, self_value, self_out, cross_query, cross_key, cross_value, cross_out,
    ff_gate, ff_up, ff_down,
):
    rows_here = tokens.shape[1]
    seq_place = lax.axis_index("seq")
    length = lengths[0]
    bf16, f32 = jnp.bfloat16, jnp.float32
    gain_one = gain_self.astype(f32)
    gain_two = gain_cross.astype(f32)
    gain_three = gain_ff.astype(f32)
    shards = (
        self_query, self_key, self_value, self_out, cross_query, cross_key, cross_value, cross_out,
        ff_gate, ff_up, ff_down,
    )
    one_hot = (
        bucket_ids(BLOCK)[:, None] == jnp.arange(BUCKETS, dtype=jnp.int32)[None, :]
    ).astype(bf16)
    profile = inner_rows(bucket_table, one_hot.T).reshape(PAIRS, 2, BLOCK)
    place = jnp.stack([seq_place.astype(jnp.int32), length])

    source = tokens[0].astype(f32)
    if kernels_fit(shards):
        gains = jnp.stack([gain_one, gain_two, gain_three])
        forward = forward_fused(
            shards, lengths, tokens[0], encoded[0],
            dict(
                profile=profile, gains=gains
            ),
        )
        one_hot_wide = jnp.pad(one_hot.astype(f32), ((0, 0), (0, PAIR - BUCKETS)))
        width = source.shape[1]
        w_gate, w_up, w_down = (full.reshape(-1, full.shape[-1]) for full in forward.ffn_full)
        layer_out, grads, grad_tokens, enc_sum, small = backward_fused(
            shards, lengths,
            dict(
                profile=profile, log_cross=forward.log_cross, log_self=forward.log_self,
                gains=gains, one_hot=one_hot_wide,
            ),
            dict(
                cotangent=cotangent[0], w_gate=w_gate, w_up=w_up, w_down=w_down,
                normed_three_in=forward.normed_three, hidden_two_in=forward.hidden_two,
                w_one=forward.w_one, w_two=forward.w_two, mixed_cross_in=forward.mixed_cross_turned,
                cqueries_in=forward.cqueries, ckeys_in=forward.ckeys, cvalues_in=forward.cvalues,
                normed_two_in=forward.normed_two, enc_in=forward.enc_all, hidden_one_in=forward.hidden_one,
                mixed_self_in=forward.mixed_self_turned, queries_in=forward.queries, keys_in=forward.keys,
                values_in=forward.values, normed_all_in=forward.normed_all,
                tokens_all_in=forward.tokens_all,
            ),
        )
        table_sum = small[8 : 8 + HEADS, :BUCKETS].T
        return (
            layer_out[None], grad_tokens[None], enc_sum[None], small[0], small[1], small[2], table_sum, *grads
        )
    weights, tokens_all, enc_all = gather_plain(shards, tokens[0], encoded[0])
    (w_query, w_key, w_value, w_sout, w_cquery, w_ckey, w_cvalue, w_cout, w_gate, w_up, w_down) = weights
    normed_all = rms_scale(tokens_all.astype(f32), gain_one).astype(bf16)
    normed_one = rms_scale(source, gain_one).astype(bf16)
    queries = product(normed_one, w_query).astype(bf16)
    keys = product(normed_all, w_key).astype(bf16)
    values = product(normed_all, w_value).astype(bf16)
    mixed_self, mixed_self_turned, log_self = self_forward(place, profile, queries, keys, values)
    hidden_one = source + product(mixed_self, w_sout)
    normed_two = rms_scale(hidden_one, gain_two).astype(bf16)
    cqueries = product(normed_two, w_cquery).astype(bf16)
    ckeys = product(enc_all, w_ckey).astype(bf16)
    cvalues = product(enc_all, w_cvalue).astype(bf16)
    mixed_cross, mixed_cross_turned, log_cross = cross_forward(cqueries, ckeys, cvalues)
    hidden_two = hidden_one + product(mixed_cross, w_cout)
    normed_three = rms_scale(hidden_two, gain_three).astype(bf16)
    gate = product(normed_three, w_gate)
    up = product(normed_three, w_up)

    def gated(gate_rows, up_rows):
        return jax.nn.gelu(gate_rows, approximate=True) * up_rows

    activated_f, pull_gate = jax.vjp(gated, gate, up)
    activated = activated_f.astype(bf16)
    slot_ids = seq_place * rows_here + jnp.arange(rows_here, dtype=jnp.int32)
    valid = (slot_ids < length).astype(f32)[:, None]
    result = (valid * (hidden_two + product(activated, w_down))).astype(bf16)

    grad_result = valid * cotangent[0].astype(f32)
    branch_ff = grad_result.astype(bf16)
    grad_gate_f, grad_up_f = pull_gate(outer_rows(branch_ff, w_down))
    grad_gate = grad_gate_f.astype(bf16)
    grad_up = grad_up_f.astype(bf16)
    g_down = inner_rows(activated, branch_ff).astype(bf16)
    g_gate = inner_rows(normed_three, grad_gate).astype(bf16)
    g_up = inner_rows(normed_three, grad_up).astype(bf16)
    grad_three, grad_gain_three = norm_back(
        hidden_two, gain_three, outer_rows(grad_gate, w_gate) + outer_rows(grad_up, w_up)
    )
    grad_two = grad_result + grad_three
    branch_cross = grad_two.astype(bf16)
    g_cout = inner_rows(mixed_cross, branch_cross).astype(bf16)
    grad_mixed_cross = outer_rows(branch_cross, w_cout).astype(bf16)
    grad_cq, grad_ck, grad_cv = cross_backward(
        cqueries, ckeys, cvalues, grad_mixed_cross, mixed_cross_turned, log_cross
    )
    g_cquery = inner_rows(normed_two, grad_cq).astype(bf16)
    g_ckey = inner_rows(enc_all, grad_ck).astype(bf16)
    g_cvalue = inner_rows(enc_all, grad_cv).astype(bf16)
    enc_part = (outer_rows(grad_ck, w_ckey) + outer_rows(grad_cv, w_cvalue)).astype(bf16)
    grad_two_back, grad_gain_two = norm_back(hidden_one, gain_two, outer_rows(grad_cq, w_cquery))
    grad_one = grad_two + grad_two_back
    branch_self = grad_one.astype(bf16)
    g_sout = inner_rows(mixed_self, branch_self).astype(bf16)
    grad_mixed_self = outer_rows(branch_self, w_sout).astype(bf16)
    grad_q, grad_k, grad_v, near_part, far_part = self_backward(
        place, profile, queries, keys, values, grad_mixed_self, mixed_self_turned, log_self
    )
    g_query = inner_rows(normed_one, grad_q).astype(bf16)
    g_key = inner_rows(normed_all, grad_k).astype(bf16)
    g_value = inner_rows(normed_all, grad_v).astype(bf16)
    token_part = (outer_rows(grad_k, w_key) + outer_rows(grad_v, w_value)).astype(bf16)
    query_part = outer_rows(grad_q, w_query)

    near_rows = near_part.reshape(HEADS, BLOCK)
    far_rows = jnp.sum(far_part, axis=-1).reshape(HEADS)
    table_part = lax.dot_general(
        one_hot.astype(f32), near_rows, (((0,), (1,)), ((), ())),
        precision=lax.Precision.HIGHEST, preferred_element_type=f32,
    )
    table_part = table_part.at[BUCKETS - 1].add(far_rows)

    hat_all = rms_scale(tokens_all.astype(f32), jnp.ones_like(gain_one))
    hat_one = rms_scale(source, jnp.ones_like(gain_one))
    grad_gain_one = jnp.sum(token_part.astype(f32) * hat_all, axis=0) + jnp.sum(
        query_part * hat_one, axis=0
    )
    table_row = jnp.zeros((gain_one.shape[0],), f32).at[: BUCKETS * HEADS].set(table_part.reshape(-1))
    small = jnp.stack([grad_gain_one, grad_gain_two, grad_gain_three, table_row] + [jnp.zeros_like(gain_one)] * 4)
    reduced, token_sum, enc_sum, small = reduce_plain(
        (g_query, g_key, g_value, g_sout, g_cquery, g_ckey, g_cvalue, g_cout, g_gate, g_up, g_down),
        token_part, enc_part, small,
    )
    grad_zero, _ = norm_back(source, gain_one, query_part + token_sum)
    grad_tokens = grad_one + grad_zero
    table_sum = small[3, : BUCKETS * HEADS].reshape(BUCKETS, HEADS)
    small = (small[0], small[1], small[2], table_sum)
    return (result[None], grad_tokens[None], enc_sum[None], *small, *reduced)


def solution(mesh):
    rows3 = P("fsdp", "seq", None)
    rows2 = P("fsdp", None)
    return jax.shard_map(
        local,
        mesh=mesh,
        in_specs=(rows3, rows3, P("fsdp"), rows3, P(), P(), P(), P(), *([rows2] * 11)),
        out_specs=(rows3, rows3, rows3, P(), P(), P(), P(), *([rows2] * 11)),
        check_vma=False,
    )
```

```python
import functools
import math

import jax
import jax.numpy as jnp
from jax import lax
from jax.experimental import pallas as pl
from jax.experimental.pallas import tpu as pltpu
from jax.sharding import PartitionSpec as P

HEADS = 12
HEAD = 64
BUCKETS = 32
MAX_DISTANCE = 128
EPSILON = 1e-06
NEGATIVE = -1e30
BLOCK = 256
PAIR = 2 * HEAD
MESH = pl.DeviceIdType.MESH


def thresholds():
    exact_limit = BUCKETS // 2
    return [
        int(math.ceil(exact_limit * (MAX_DISTANCE / exact_limit) ** (number / exact_limit)))
        for number in range(1, exact_limit)
    ]


def bucket_ids(key_count):
    exact_limit = BUCKETS // 2
    offsets = jnp.arange(key_count, dtype=jnp.int32)
    passed = jnp.zeros((key_count,), jnp.int32)
    for border in thresholds():
        passed = passed + (offsets >= border).astype(jnp.int32)
    return jnp.where(offsets < exact_limit, offsets, exact_limit + passed)


def rms_scale(values, gain):
    return values * lax.rsqrt(jnp.mean(values * values, axis=-1, keepdims=True) + EPSILON) * gain


def norm_back(values, gain, grad_normed):
    _, pullback = jax.vjp(rms_scale, values, gain)
    return pullback(grad_normed)


def product(left, right):
    return jnp.dot(left, right, preferred_element_type=jnp.float32)


def inner_rows(left, right):
    return lax.dot_general(
        left, right, (((0,), (0,)), ((), ())), preferred_element_type=jnp.float32
    )


def outer_rows(left, right):
    return lax.dot_general(
        left, right, (((1,), (1,)), ((), ())), preferred_element_type=jnp.float32
    )


def iota(shape, axis):
    return lax.broadcasted_iota(jnp.int32, shape, axis)


def head_rows(value, head):
    place = iota(value.shape, 0) // HEAD
    return jnp.where(place == head, value, jnp.zeros_like(value))


def head_cols(value, head):
    place = iota(value.shape, 1) // HEAD
    return jnp.where(place == head, value, jnp.zeros_like(value))


def skew(profile_row):
    wide = jnp.broadcast_to(profile_row, (BLOCK, BLOCK))
    return pltpu.roll(wide, 0, 1, stride=1, stride_axis=0)


def unskew(tile):
    rows = iota(tile.shape, 0)
    bit = 1
    while bit < BLOCK:
        tile = jnp.where((rows // bit) % 2 == 1, pltpu.roll(tile, BLOCK - bit, 1), tile)
        bit *= 2
    return tile


def fill_pads(pads, length):
    rows = pads.shape[1]
    lanes = iota((BLOCK, PAIR), 1)

    @pl.loop(0, rows // BLOCK)
    def _(n):
        start = pl.multiple_of(n * BLOCK, BLOCK)
        beyond = iota((BLOCK, PAIR), 0) >= length - start
        for head in range(2):
            first = (1 - head) * HEAD
            ones = jnp.where((lanes > first) & (lanes <= first + 3), 1.0, 0.0)
            pads[head, pl.ds(start, BLOCK), :] = jnp.where(
                (lanes == first) & beyond, NEGATIVE, ones
            ).astype(jnp.bfloat16)


def padded(value, pads, head, start):
    own = iota(value.shape, 1) // HEAD == head
    return jnp.where(own, value, pads[head, start : start + value.shape[0], :])


def split_low(value):
    first = value.astype(jnp.bfloat16).astype(jnp.float32)
    rest = value - first
    second = rest.astype(jnp.bfloat16).astype(jnp.float32)
    return first, second, rest - second


def with_terms(turned, head, mask_term, terms):
    place = iota(turned.shape, 0)
    first = (1 - head) * HEAD
    value = jnp.where(place // HEAD == head, turned.astype(jnp.float32), 0.0)
    value = jnp.where(place == first, mask_term, value)
    for n, term in enumerate(terms):
        value = jnp.where(place == first + 1 + n, term, value)
    return value.astype(jnp.bfloat16)


HIDDEN, DIAGONAL, NEAR, FAR = range(4)


def fill_fixed_bias(bias):
    for head in range(2):
        bias[head, HIDDEN] = jnp.full((BLOCK, BLOCK), NEGATIVE, jnp.float32)
        bias[head, FAR] = jnp.zeros((BLOCK, BLOCK), jnp.float32)


def fill_near_bias(bias, profile_ref):
    later = iota((BLOCK, BLOCK), 1) >= iota((BLOCK, BLOCK), 0)
    for head in range(2):
        profile = profile_ref[head : head + 1, :]
        near = skew(profile - profile[:, BLOCK - 1 :])
        bias[head, DIAGONAL] = jnp.where(later, near, NEGATIVE)
        bias[head, NEAR] = jnp.where(later, 0.0, near)


def bias_kind(place, block):
    return jnp.clip(place - block, -1, 2) + 1


def self_forward_pair(place, profile_ref, q_ref, k_ref, v_ref, o_ref, ot_ref, log_ref, pads, bias, s_buf, vt_buf):
    qt = q_ref[...].T
    vt_buf[...] = v_ref[...].T
    fill_near_bias(bias, profile_ref)
    blocks = k_ref.shape[0] // BLOCK
    tops = []
    for head in range(2):
        far = profile_ref[head : head + 1, BLOCK - 1 :]
        queries = with_terms(qt, head, 1.0, (far,))
        top = None
        for block in range(blocks):
            start = block * BLOCK
            keys = padded(k_ref[start : start + BLOCK, :], pads, head, start)
            scores = product(keys, queries) + bias[head, bias_kind(place, block)]
            s_buf[head, start : start + BLOCK, :] = scores
            most = jnp.max(scores, axis=0, keepdims=True)
            top = most if top is None else jnp.maximum(top, most)
        tops.append(top)
    totals = []
    for head in range(2):
        total = None
        for block in range(blocks):
            part = slice(block * BLOCK, (block + 1) * BLOCK)
            raised = jnp.exp(s_buf[head, part, :] - tops[head])
            s_buf[head, part, :] = raised
            amount = jnp.sum(raised, axis=0, keepdims=True)
            total = amount if total is None else total + amount
        totals.append(total)
    for head in range(2):
        rows = slice(head * HEAD, (head + 1) * HEAD)
        scale, mixed = 1.0 / totals[head], None
        for block in range(blocks):
            part = slice(block * BLOCK, (block + 1) * BLOCK)
            soft = (s_buf[head, part, :] * scale).astype(jnp.bfloat16)
            share = product(vt_buf[rows, part], soft)
            mixed = share if mixed is None else mixed + share
        ot_ref[rows, :] = mixed
        log_ref[head : head + 1, :] = tops[head] + jnp.log(totals[head])
    o_ref[...] = ot_ref[...].T.astype(jnp.bfloat16)


def self_forward_kernel(place_ref, profile_ref, q_ref, k_ref, v_ref, o_ref, ot_ref, log_ref, pads, bias, s_buf, vt_buf):
    @pl.when(pl.program_id(0) == 0)
    def _():
        fill_pads(pads, place_ref[1])
        fill_fixed_bias(bias)

    self_forward_pair(
        place_ref[0], profile_ref.at[0], q_ref, k_ref, v_ref, o_ref, ot_ref, log_ref.at[0],
        pads, bias, s_buf, vt_buf,
    )


def cross_forward_pair(q_ref, k_ref, v_ref, o_ref, ot_ref, log_ref):
    qt = q_ref[...].T
    vt = v_ref[...].T
    all_scores = [product(k_ref[...], head_rows(qt, head)) for head in range(2)]
    for head, scores in enumerate(all_scores):
        top = jnp.max(scores, axis=0, keepdims=True)
        raised = jnp.exp(scores - top)
        total = jnp.sum(raised, axis=0, keepdims=True)
        soft = (raised * (1.0 / total)).astype(jnp.bfloat16)
        ot_ref[head * HEAD : (head + 1) * HEAD, :] = product(vt[head * HEAD : (head + 1) * HEAD, :], soft)
        log_ref[head : head + 1, :] = top + jnp.log(total)
    o_ref[...] = ot_ref[...].T.astype(jnp.bfloat16)


def cross_forward_kernel(q_ref, k_ref, v_ref, o_ref, ot_ref, log_ref):
    cross_forward_pair(q_ref, k_ref, v_ref, o_ref, ot_ref, log_ref.at[0])


EXTRA = 16


def backward_pair(
    place, profile_ref, q_ref, k_ref, v_ref, g_ref, ot_ref, log_ref, dq_ref, dk_ref, dv_ref,
    near_ref, far_ref, pads, bias, kt_buf, grad_buf,
):
    q_value = q_ref[...]
    g_value = g_ref[...]
    qt = q_value.T
    gt = g_value.T
    kt = k_ref[...].T
    keys_count = k_ref.shape[0]
    ones = jnp.ones((EXTRA, keys_count), jnp.bfloat16)
    for head in range(2):
        kt_buf[head, 0:HEAD, 0:keys_count] = kt[head * HEAD : (head + 1) * HEAD, :]
        kt_buf[head, HEAD : HEAD + EXTRA, 0:keys_count] = ones
    both_q = jnp.concatenate([head_cols(q_value, 0), head_cols(q_value, 1)], axis=0)
    both_g = jnp.concatenate([head_cols(g_value, 0), head_cols(g_value, 1)], axis=0)
    weighted = gt.astype(jnp.float32) * ot_ref[...]
    if profile_ref is not None:
        fill_near_bias(bias, profile_ref)
    queries, grads_out = [], []
    for head in range(2):
        rows = slice(head * HEAD, (head + 1) * HEAD)
        delta = jnp.sum(weighted[rows, :], axis=0, keepdims=True)
        constant = -log_ref[head : head + 1, :]
        if profile_ref is not None:
            constant = constant + profile_ref[head : head + 1, BLOCK - 1 :]
        queries.append(with_terms(qt, head, 1.0, split_low(constant)))
        grads_out.append(with_terms(gt, head, 0.0, split_low(-delta)))
    sums = [None, None]
    for start in range(0, keys_count, BLOCK):
        k_block = k_ref[start : start + BLOCK, :]
        v_block = v_ref[start : start + BLOCK, :]
        softs, grads = [], []
        for head in range(2):
            scores = product(padded(k_block, pads, head, start), queries[head])
            if profile_ref is not None:
                scores = scores + bias[head, bias_kind(place, start // BLOCK)]
            soft = jnp.exp(scores)
            change = product(padded(v_block, pads, head, start), grads_out[head])
            grad = (soft * change).astype(jnp.bfloat16)
            softs.append(soft.astype(jnp.bfloat16))
            grads.append(grad)
            if profile_ref is not None:
                grad_buf[head, start // BLOCK] = grad
            share = product(kt_buf[head, :, start : start + BLOCK], grad)
            sums[head] = share if sums[head] is None else sums[head] + share
        dv_ref[start : start + BLOCK, :] = product(jnp.concatenate(softs, axis=1), both_g).astype(
            jnp.bfloat16
        )
        dk_ref[start : start + BLOCK, :] = product(jnp.concatenate(grads, axis=1), both_q).astype(
            jnp.bfloat16
        )
    turned = jnp.concatenate([sums[0][0:HEAD, :], sums[1][0:HEAD, :]], axis=0)
    dq_ref[...] = turned.T.astype(jnp.bfloat16)
    if profile_ref is not None:
        later = iota((BLOCK, BLOCK), 1) >= iota((BLOCK, BLOCK), 0)
        for head in range(2):
            diagonal = grad_buf[head, place].astype(jnp.float32)
            before = grad_buf[head, jnp.maximum(place - 1, 0)].astype(jnp.float32)
            before = jnp.where(place >= 1, before, 0.0)
            near = jnp.sum(unskew(jnp.where(later, diagonal, before)), axis=0, keepdims=True)
            near_ref[head : head + 1, :] = near
            far_ref[head : head + 1, :] = sums[head][HEAD : HEAD + 1, :] - near


def self_backward_kernel(
    place_ref, profile_ref, q_ref, k_ref, v_ref, g_ref, ot_ref, log_ref,
    dq_ref, dk_ref, dv_ref, near_ref, far_ref, pads, bias, kt_buf, grad_buf,
):
    @pl.when(pl.program_id(0) == 0)
    def _():
        fill_pads(pads, place_ref[1])
        fill_fixed_bias(bias)

    backward_pair(
        place_ref[0], profile_ref.at[0], q_ref, k_ref, v_ref, g_ref, ot_ref, log_ref.at[0],
        dq_ref, dk_ref, dv_ref, near_ref.at[0], far_ref.at[0], pads, bias, kt_buf, grad_buf,
    )


def cross_backward_kernel(q_ref, k_ref, v_ref, g_ref, ot_ref, log_ref, dq_ref, dk_ref, dv_ref, pads, kt_buf):
    @pl.when(pl.program_id(0) == 0)
    def _():
        fill_pads(pads, pads.shape[1])

    backward_pair(
        None, None, q_ref, k_ref, v_ref, g_ref, ot_ref, log_ref.at[0], dq_ref, dk_ref, dv_ref,
        None, None, pads, None, kt_buf, None,
    )


def forward_scratch(count, rows):
    return [
        pltpu.VMEM((2, count, PAIR), jnp.bfloat16),
        pltpu.VMEM((2, 4, BLOCK, BLOCK), jnp.float32),
        pltpu.VMEM((2, count, rows), jnp.float32),
        pltpu.VMEM((PAIR, count), jnp.bfloat16),
    ]


def backward_scratch(count):
    return [
        pltpu.VMEM((2, count, PAIR), jnp.bfloat16),
        pltpu.VMEM((2, 4, BLOCK, BLOCK), jnp.float32),
        pltpu.VMEM((2, HEAD + EXTRA, count), jnp.bfloat16),
        pltpu.VMEM((2, count // BLOCK, BLOCK, BLOCK), jnp.bfloat16),
    ]


def pair_block(rows):
    return pl.BlockSpec((rows, PAIR), lambda pair: (0, pair))


def turned_block(rows):
    return pl.BlockSpec((PAIR, rows), lambda pair: (pair, 0))


def head_block(width):
    return pl.BlockSpec((1, 2, width), lambda pair: (pair, 0, 0))


SCALARS = pl.BlockSpec(memory_space=pltpu.SMEM)
PAIRS = HEADS // 2


def shaped(shape, dtype):
    return jax.ShapeDtypeStruct(shape, dtype)


def self_forward(place, profile, queries, keys, values):
    rows, width = queries.shape
    count = keys.shape[0]
    return pl.pallas_call(
        self_forward_kernel,
        grid=(PAIRS,),
        in_specs=[SCALARS, head_block(BLOCK), pair_block(rows), pair_block(count), pair_block(count)],
        out_specs=[pair_block(rows), turned_block(rows), head_block(rows)],
        out_shape=[
            shaped((rows, width), jnp.bfloat16),
            shaped((width, rows), jnp.float32),
            shaped((PAIRS, 2, rows), jnp.float32),
        ],
        scratch_shapes=forward_scratch(count, rows),
        name="self_forward",
    )(place, profile, queries, keys, values)


def cross_forward(queries, keys, values):
    rows, width = queries.shape
    count = keys.shape[0]
    return pl.pallas_call(
        cross_forward_kernel,
        grid=(PAIRS,),
        in_specs=[pair_block(rows), pair_block(count), pair_block(count)],
        out_specs=[pair_block(rows), turned_block(rows), head_block(rows)],
        out_shape=[
            shaped((rows, width), jnp.bfloat16),
            shaped((width, rows), jnp.float32),
            shaped((PAIRS, 2, rows), jnp.float32),
        ],
        name="cross_forward",
    )(queries, keys, values)


def self_backward(place, profile, queries, keys, values, grad_mixed, mixed_turned, log_totals):
    rows, width = queries.shape
    count = keys.shape[0]
    return pl.pallas_call(
        self_backward_kernel,
        grid=(PAIRS,),
        in_specs=[
            SCALARS, head_block(BLOCK), pair_block(rows), pair_block(count), pair_block(count),
            pair_block(rows), turned_block(rows), head_block(rows),
        ],
        out_specs=[
            pair_block(rows), pair_block(count), pair_block(count), head_block(BLOCK), head_block(rows),
        ],
        out_shape=[
            shaped((rows, width), jnp.bfloat16),
            shaped((count, width), jnp.bfloat16),
            shaped((count, width), jnp.bfloat16),
            shaped((PAIRS, 2, BLOCK), jnp.float32),
            shaped((PAIRS, 2, rows), jnp.float32),
        ],
        scratch_shapes=backward_scratch(count),
        name="self_backward",
    )(place, profile, queries, keys, values, grad_mixed, mixed_turned, log_totals)


def cross_backward(queries, keys, values, grad_mixed, mixed_turned, log_totals):
    rows, width = queries.shape
    count = keys.shape[0]
    return pl.pallas_call(
        cross_backward_kernel,
        grid=(PAIRS,),
        in_specs=[
            pair_block(rows), pair_block(count), pair_block(count),
            pair_block(rows), turned_block(rows), head_block(rows),
        ],
        out_specs=[pair_block(rows), pair_block(count), pair_block(count)],
        out_shape=[
            shaped((rows, width), jnp.bfloat16),
            shaped((count, width), jnp.bfloat16),
            shaped((count, width), jnp.bfloat16),
        ],
        scratch_shapes=[
            pltpu.VMEM((2, count, PAIR), jnp.bfloat16),
            pltpu.VMEM((2, HEAD + EXTRA, count), jnp.bfloat16),
        ],
        name="cross_backward",
    )(queries, keys, values, grad_mixed, mixed_turned, log_totals)


class Peers:
    def __init__(self, planes):
        self.seq = lax.axis_index("seq")
        fsdp = lax.axis_index("fsdp")
        self.planes = planes
        self.plane = fsdp // 2
        self.core = fsdp % 2
        self.fsdp = fsdp
        self.along_x = self.seq + 1 - 2 * (self.seq % 2)
        self.along_y = (self.seq + 2) % 4
        self.corner = (self.along_x + 2) % 4
        self.partner = (self.seq, fsdp + 1 - 2 * self.core)
        self.to_x = (self.along_x, fsdp)
        self.to_y = (self.along_y, fsdp)
        self.to_corner = (self.corner, fsdp)

    def ahead(self, steps):
        return (self.plane + steps) % self.planes

    def at_plane(self, plane):
        return (self.seq, 2 * plane + self.core)

    def everyone(self):
        return [self.partner, self.to_x, self.to_y, self.to_corner] + [
            self.at_plane(self.ahead(k)) for k in range(1, self.planes)
        ]

    def greet(self):
        barrier = pltpu.get_barrier_semaphore()
        for other in self.everyone():
            pl.semaphore_signal(barrier, inc=1, device_id=other, device_id_type=MESH)

    def meet(self):
        pl.semaphore_wait(pltpu.get_barrier_semaphore(), len(self.everyone()))


def remote(source, target, send_sem, recv_sem, device):
    return pltpu.make_async_remote_copy(
        src_ref=source, dst_ref=target, send_sem=send_sem, recv_sem=recv_sem,
        device_id=device, device_id_type=MESH,
    )


class Stack:
    def __init__(self, rows, cols):
        self.rows, self.cols = rows, cols

    def own(self, ref, quarter, first=0, count=None):
        return ref.at[quarter, pl.ds(first, count or self.rows), :]

    def part(self, ref, quarter, plane, core, first=0, count=None):
        return ref.at[quarter, plane, core, pl.ds(first, count or self.rows), :]

    def planes(self, ref, quarter, core):
        return ref.at[quarter, :, core]

    def whole(self, ref, plane, core):
        return ref.at[:, plane, core]


class Wide:
    def __init__(self, rows, cols):
        self.rows, self.cols = rows, cols

    def own(self, ref, quarter, first=0, count=None):
        return ref.at[pl.ds(first, count or self.rows), pl.ds(quarter * self.cols, self.cols)]

    def part(self, ref, quarter, plane, core, first=0, count=None):
        return ref.at[
            plane, core, pl.ds(first, count or self.rows), pl.ds(quarter * self.cols, self.cols)
        ]

    def planes(self, ref, quarter, core):
        return ref.at[:, core, :, pl.ds(quarter * self.cols, self.cols)]

    def whole(self, ref, plane, core):
        return ref.at[plane, core]


class Tall:
    def __init__(self, rows, cols):
        self.rows, self.cols = rows, cols

    def own(self, ref, quarter, first=0, count=None):
        return ref.at[pl.ds(quarter * self.rows + first, count or self.rows), :]

    def part(self, ref, quarter, plane, core, first=0, count=None):
        return ref.at[plane, core, pl.ds(quarter * self.rows + first, count or self.rows), :]

    def planes(self, ref, quarter, core):
        return ref.at[:, core, pl.ds(quarter * self.rows, self.rows), :]

    def whole(self, ref, plane, core):
        return ref.at[plane, core]


def full_shapes(kinds, planes, cores=2):
    shapes = []
    for kind in kinds:
        if isinstance(kind, Stack):
            shapes.append((4, planes, cores, kind.rows, kind.cols))
        elif isinstance(kind, Wide):
            shapes.append((planes, cores, kind.rows, 4 * kind.cols))
        else:
            shapes.append((planes, cores, 4 * kind.rows, kind.cols))
    return shapes


ANYWHERE = pl.BlockSpec(memory_space=pl.ANY)
DMA = pltpu.SemaphoreType.DMA


def make_kinds(shards):
    square, wide, down = shards[0], shards[8], shards[10]
    stack = Stack(*square.shape)
    band = Wide(wide.shape[0], wide.shape[1] // 4)
    tall = Tall(down.shape[0] // 4, down.shape[1])
    return [stack, stack, band, band, tall]


def kernels_fit(shards):
    kinds = make_kinds(shards)
    return (
        lax.axis_size("seq") == 4
        and lax.axis_size("fsdp") == 8
        and all(kind.rows % 32 == 0 and kind.cols % 128 == 0 for kind in kinds)
    )


def gather_plain(shards, tokens, encoded):
    full = [lax.all_gather(shard, "fsdp", axis=0, tiled=True) for shard in shards]
    return (
        full,
        lax.all_gather(tokens, "seq", axis=0, tiled=True),
        lax.all_gather(encoded, "seq", axis=0, tiled=True),
    )


def add_low(target, *terms):
    total = target[...]
    for term in terms:
        total = total + term[...]
    target[...] = total


def reduce_plain(grads, token_part, enc_part, small):
    def sums(value):
        return lax.psum_scatter(value.astype(jnp.float32), "seq", scatter_dimension=0, tiled=True)

    reduced = [
        lax.psum(
            lax.psum_scatter(grad.astype(jnp.float32), "fsdp", scatter_dimension=0, tiled=True), "seq"
        )
        for grad in grads
    ]
    return reduced, sums(token_part), sums(enc_part), lax.psum(small, ("seq", "fsdp"))


def columns(pair):
    return pl.ds(pl.multiple_of(pair * PAIR, PAIR), PAIR)


def row_steps(count, step):
    def run(body):
        @pl.loop(0, count // step)
        def _(n):
            body(pl.ds(pl.multiple_of(n * step, step), step))

    return run


def weight_grad(out, left, right):
    @row_steps(out.shape[0], 384)
    def _(part):
        out[part, :] = inner_rows(left[:, part], right[...]).astype(jnp.bfloat16)


def weight_grad_turned(out, turned, right):
    @row_steps(out.shape[0], 384)
    def _(part):
        out[part, :] = product(turned[part, :].astype(jnp.bfloat16), right[...]).astype(jnp.bfloat16)


def norm_back_rows(values, gain, grad_normed):
    scale = lax.rsqrt(jnp.mean(values * values, axis=-1, keepdims=True) + EPSILON)
    scaled = grad_normed * gain
    along = jnp.mean(values * scaled, axis=-1, keepdims=True)
    grad_values = scale * scaled - values * (scale * scale * scale) * along
    return grad_values, jnp.sum(grad_normed * values * scale, axis=0, keepdims=True)


class Space:
    def __init__(self, layout, refs):
        refs = list(refs)
        for name, count in layout.items():
            value = refs.pop(0) if count is None else [refs.pop(0) for _ in range(count)]
            setattr(self, name, value)


def flatten(*tables):
    layout, flat = {}, []
    for table in tables:
        for name, value in table.items():
            many = isinstance(value, list)
            layout[name] = len(value) if many else None
            flat += value if many else [value]
    return layout, flat


class StackRows(Stack):
    def __init__(self, first, rows, cols):
        super().__init__(rows, cols)
        self.first = first

    def planes(self, ref, quarter, core):
        return ref.at[quarter, :, core, pl.ds(self.first, self.rows), :]


DOWN, GATE, UP, CROSS, SELF, SELF_REST = range(6)
GROUPS = 6


class Sum:
    planes_first = False

    def __init__(self, g, kind, here, r, part):
        self.g, self.kind, self.here, self.r = g, kind, here, r
        self.part = part
        self.planes = here.planes
        self.sums, self.final = r.sums[g], r.final[g]
        self.side_x, self.side_y, self.last, self.from_z = r.side_x[g], r.side_y[g], r.last[g], r.from_z[g]
        self.started = []

    def send(self, make):
        remote(*make()).start()
        self.started.append(make)

    def arrived(self, target, recv_sem):
        pltpu.make_async_copy(target, target, recv_sem).wait()

    def pair_source(self, n, core):
        return self.kind.planes(self.part, n, core), self.sums.at[n]

    def start_pair(self, n):
        r, g = self.r, self.g
        source, target = self.pair_source(n, 1 - self.here.core)
        remote(source, target, r.c_send.at[g, n], r.c_recv.at[g, n], self.here.partner).start()

    def pair_part(self, n):
        source, target = self.pair_source(n, self.here.core)
        self.arrived(target, self.r.c_recv.at[self.g, n])

        @pl.loop(0, 4)
        def _(m):
            add_low(target.at[m], source.at[m])

        self.send_part(n)

    def pair_sum(self):
        @pl.loop(0, 4)
        def _(n):
            self.pair_part(n)

        self.sent_parts()

    def parts_sends(self):
        r, g, here = self.r, self.g, self.here
        for n, quarter in enumerate((here.along_x, here.corner)):
            yield quarter, lambda n=n, quarter=quarter: (
                self.half(quarter, 0), self.side_x.at[n], r.a_send.at[g, n], r.a_recv.at[g, n], here.to_x
            )
        for n, quarter in enumerate((here.along_y, here.corner)):
            yield quarter, lambda n=n, quarter=quarter: (
                self.half(quarter, 1), self.side_y.at[n], r.a_send.at[g, 2 + n], r.a_recv.at[g, 2 + n], here.to_y
            )

    def send_part(self, n):
        for part, make in self.parts_sends():

            @pl.when(n == part)
            def _(make=make):
                remote(*make()).start()

    def sent_parts(self):
        self.started += [make for _, make in self.parts_sends()]

    def pair_sent(self):
        for n in range(4):
            source, target = self.pair_source(n, 1 - self.here.core)
            remote(
                source, target, self.r.c_send.at[self.g, n], self.r.c_recv.at[self.g, n], self.here.partner
            ).wait_send()

    def half(self, quarter, second):
        size = self.planes // 2
        return self.sums.at[quarter, pl.ds(second * size, size)]

    def sides(self):
        for _, make in Sum.parts_sends(self):
            self.send(make)

    def add_half(self, quarter, second, terms, out=None):
        size = self.planes // 2

        @pl.loop(0, size)
        def _(z):
            add_low(self.sums.at[quarter, second * size + z], *[term.at[z] for term in terms])

    def first_side(self):
        r, g, here = self.r, self.g, self.here
        for n in range(2):
            self.arrived(self.side_x.at[n], r.a_recv.at[g, n])
            self.arrived(self.side_y.at[n], r.a_recv.at[g, 2 + n])
        self.add_half(here.along_y, 0, [self.side_x.at[1]])
        self.add_half(here.along_x, 1, [self.side_y.at[1]])
        for n, (quarter, device) in enumerate(((here.along_y, here.to_y), (here.along_x, here.to_x))):
            self.send(
                lambda n=n, quarter=quarter, device=device: (
                    self.half(quarter, n), self.last.at[n], r.b_send.at[g, n], r.b_recv.at[g, n], device
                )
            )

    def second_side(self):
        r, g, here = self.r, self.g, self.here
        for n in range(2):
            self.arrived(self.last.at[n], r.b_recv.at[g, n])
        self.add_half(here.seq, 0, [self.side_x.at[0], self.last.at[0]])
        self.add_half(here.seq, 1, [self.side_y.at[0], self.last.at[1]])
        self.after_square()

    def after_square(self):
        self.start_planes()

    def plane_share(self, plane):
        return self.sums.at[self.here.seq, plane]

    def plane_sends(self):
        r, g, here = self.r, self.g, self.here
        for k in range(1, self.planes):
            yield here.ahead(k), lambda k=k: (
                self.plane_share(here.ahead(k)), self.from_z.at[k - 1],
                r.z_send.at[g, k - 1], r.z_recv.at[g, k - 1], here.at_plane(here.ahead(k)),
            )

    def start_planes(self):
        for _, make in self.plane_sends():
            self.send(make)

    def along_planes(self):
        r, g, here = self.r, self.g, self.here
        for k in range(1, self.planes):
            self.arrived(self.from_z.at[k - 1], r.z_recv.at[g, k - 1])
        step = 16

        @pl.loop(0, self.kind.rows // step)
        def _(n):
            rows = pl.ds(pl.multiple_of(n * step, step), step)
            total = self.sums[here.seq, here.plane, rows, :].astype(jnp.float32)
            for k in range(1, self.planes):
                total = total + self.from_z[k - 1, rows, :].astype(jnp.float32)
            self.final[here.seq, rows, :] = total.astype(jnp.bfloat16)

        self.start_spread()

    def start_spread(self):
        r, g, here = self.r, self.g, self.here
        for n, device in enumerate((here.to_x, here.to_y)):
            self.send(
                lambda n=n, device=device: (
                    self.final.at[here.seq], self.final.at[here.seq], r.g_send.at[g, n], r.g_recv.at[g, n], device
                )
            )

    def across(self, quarter, second):
        size = self.kind.cols // 2
        return self.final.at[quarter, :, pl.ds(second * size, size)]

    def spread(self):
        r, g, here = self.r, self.g, self.here
        for n, (quarter, device) in enumerate(((here.along_x, here.to_y), (here.along_y, here.to_x))):
            self.arrived(self.final.at[quarter], r.g_recv.at[g, n])
            self.send(
                lambda n=n, quarter=quarter, device=device: (
                    self.across(quarter, n), self.across(quarter, n),
                    r.g_send.at[g, 2 + n], r.g_recv.at[g, 2 + n], device,
                )
            )

    def out_copies(self):
        r, g, kind = self.r, self.g, self.kind
        if isinstance(kind, Wide):
            return [
                pltpu.make_async_copy(
                    self.final.at[q], r.out[g].at[:, pl.ds(q * kind.cols, kind.cols)], r.out_sem.at[g, q]
                )
                for q in range(4)
            ]
        out = r.out[min(g, SELF)]
        if isinstance(kind, StackRows):
            out = out.at[:, pl.ds(kind.first, kind.rows), :]
        return [pltpu.make_async_copy(self.final, out, r.out_sem.at[g, 0])]

    def finish(self):
        r, g, here = self.r, self.g, self.here
        for n in range(2):
            self.arrived(self.across(here.corner, n), r.g_recv.at[g, 2 + n])
        for copy in self.out_copies():
            copy.start()

    def end(self):
        for copy in self.out_copies():
            copy.wait()
        if self.g not in (DOWN, CROSS):
            self.pair_sent()
        for make in self.started:
            remote(*make()).wait_send()


class PlanesFirst(Sum):
    planes_first = True

    def pair_source(self, n, core):
        return self.part.at[n, core], self.sums.at[:, n]

    def half(self, quarter, second):
        size = self.kind.cols // 2
        return self.sums.at[quarter, self.here.plane, :, pl.ds(second * size, size)]

    def plane_share(self, plane):
        return self.sums.at[:, plane]

    def parts_sends(self):
        return self.plane_sends()

    def along_planes(self):
        r, g, here = self.r, self.g, self.here
        for k in range(1, self.planes):
            self.arrived(self.from_z.at[k - 1], r.z_recv.at[g, k - 1])

        @pl.loop(0, 4)
        def _(q):
            add_low(self.sums.at[q, here.plane], *[self.from_z.at[k - 1, q] for k in range(1, self.planes)])

        self.sides()

    def add_half(self, quarter, second, terms, out=None):
        size = self.kind.cols // 2
        add_low(self.half(quarter, second), *terms)

    def after_square(self):
        self.final[self.here.seq] = self.sums[self.here.seq, self.here.plane]
        self.start_spread()


class BandSum(Sum):
    def pair_source(self, n, core):
        return self.part.at[n, :, core], self.sums.at[n]


class RowSum(Sum):
    def __init__(self, g, here, r, source, n):
        self.g, self.here, self.r, self.source = g, here, r, source
        self.size, self.cols = source.shape[0] // 4, source.shape[1] // 2
        self.side_x, self.side_y, self.last = r.row_x[n], r.row_y[n], r.row_last[n]
        self.started = []

    def half(self, quarter, second):
        return self.source.at[pl.ds(quarter * self.size, self.size), pl.ds(second * self.cols, self.cols)]

    def add_half(self, quarter, second, terms):
        @row_steps(self.size, 64)
        def _(part):
            add_low(self.half(quarter, second).at[part, :], *[term.at[part, :] for term in terms])

    def total(self, keep):
        r, g, here = self.r, self.g, self.here
        for n in range(2):
            self.arrived(self.last.at[n], r.b_recv.at[g, n])
        step = 64

        @row_steps(self.size, step)
        def _(part):
            halves = []
            for second, side in enumerate((self.side_x, self.side_y)):
                value = self.half(here.seq, second)[part, :].astype(jnp.float32)
                halves.append(
                    value + side[0, part, :].astype(jnp.float32) + self.last[second, part, :].astype(jnp.float32)
                )
            keep(part, jnp.concatenate(halves, axis=1))

    def sent(self):
        for make in self.started:
            remote(*make()).wait_send()


GELU_SCALE = math.sqrt(2.0 / math.pi)
GELU_CUBE = 0.044715
TOKENS, ENCODED = GROUPS, GROUPS + 1


def backward_kernel(kinds, planes, layout, *refs):
    r = Space(layout, refs)
    bf16, f32 = jnp.bfloat16, jnp.float32
    here = Peers(planes)
    place, length = here.seq, r.length[0]
    rows, width = r.grad_two.shape
    count, enc_count = r.rows_both.shape[0] // 2, r.ckeys_in.shape[0]
    owner_rows = width // (2 * planes)
    shape = (4, planes, 2, owner_rows, width)
    band = kinds[GATE].cols
    band_shape = (4, planes, 2, owner_rows, band)
    tall_shape = (planes, 2, 4, kinds[DOWN].rows, width)
    keys, values = r.rows_both.at[pl.ds(0, count), :], r.rows_both.at[pl.ds(count, count), :]
    down = PlanesFirst(DOWN, kinds[DOWN], here, r, r.rows_both.reshape(*tall_shape))
    gate = BandSum(GATE, kinds[GATE], here, r, r.grad_gate.reshape(*band_shape))
    up = BandSum(UP, kinds[UP], here, r, r.grad_up.reshape(*band_shape))
    cross = Sum(CROSS, kinds[CROSS], here, r, r.grad_cross.reshape(*shape))
    self_one = Sum(SELF, kinds[SELF], here, r, r.grad_self.reshape(*shape))
    self_two = Sum(SELF_REST, kinds[SELF_REST], here, r, r.grad_self.reshape(*shape))
    sums = (down, gate, up, cross, self_one, self_two)
    others = []

    ckeys, cvalues = r.dk.at[pl.ds(0, enc_count), :], r.dk.at[pl.ds(enc_count, enc_count), :]
    dck, dcv = r.dv.at[pl.ds(0, enc_count), :], r.dv.at[pl.ds(enc_count, enc_count), :]
    enc_all = r.token_part.at[pl.ds(0, enc_count), :]
    enc_part = r.token_part.at[pl.ds(enc_count, enc_count), :]
    token_sum = RowSum(TOKENS, here, r, r.token_part, 0)
    enc_sum = RowSum(ENCODED, here, r, enc_part, 1)
    act, d_gate, d_up = (r.token_part.at[pl.ds(n * rows, rows), pl.ds(0, band)] for n in range(3))

    def send(make):
        remote(*make()).start()
        others.append(make)

    def arrived(target, recv_sem):
        pltpu.make_async_copy(target, target, recv_sem).wait()

    def load(n, source, target):
        copy = pltpu.make_async_copy(source, target, r.load_sem.at[n])
        copy.start()
        return copy

    def ffn_copies(n):
        slot, part = n % 2, pl.ds(pl.multiple_of(n * band, band), band)
        return [
            pltpu.make_async_copy(r.w_gate.at[:, part], r.grad_self.at[slot, :, pl.ds(0, band)], r.f_sem.at[0, slot]),
            pltpu.make_async_copy(r.w_up.at[:, part], r.grad_self.at[2 + slot, :, pl.ds(0, band)], r.f_sem.at[1, slot]),
            pltpu.make_async_copy(r.w_down.at[part, :], r.grad_cross.at[slot, pl.ds(0, band), :], r.f_sem.at[2, slot]),
        ]

    def start_ffn(n):
        for copy in ffn_copies(n):
            copy.start()

    here.greet()
    cotangent_load = load(0, r.cotangent, r.grad_mixed)
    normed_three_load = load(6, r.normed_three_in, r.normed)
    start_ffn(0)
    start_ffn(1)
    hidden_two_load = load(11, r.hidden_two_in, r.hidden)
    mixed_load = load(2, r.mixed_cross_in, r.mixed)
    cqueries_load = load(3, r.cqueries_in, r.queries)
    ckeys_load = load(4, r.ckeys_in, ckeys)
    cvalues_load = load(5, r.cvalues_in, cvalues)

    def grad_result(part, step):
        slots = place * rows + part.start + iota((step, 1), 0)
        return jnp.where(slots < length, r.grad_mixed[part, :].astype(f32), 0.0)

    cotangent_load.wait()

    @row_steps(rows, 64)
    def _(part):
        r.branch[part, :] = grad_result(part, 64).astype(bf16)

    normed_three_load.wait()

    @pl.loop(0, 4)
    def _(n):
        slot = n % 2
        for copy in ffn_copies(n):
            copy.wait()
        normed = r.normed[...]
        branch = r.branch[...]
        w_gate = r.grad_self[slot, :, 0:band]
        w_up = r.grad_self[2 + slot, :, 0:band]
        w_down = r.grad_cross[slot, 0:band, :]
        gate_band = product(normed, w_gate)
        up_band = product(normed, w_up)
        inner = jnp.tanh(GELU_SCALE * (gate_band + GELU_CUBE * (gate_band * gate_band * gate_band)))
        lifted = 0.5 * (1.0 + inner)
        gelu = gate_band * lifted
        slope = lifted + (0.5 * GELU_SCALE) * gate_band * (1.0 - inner * inner) * (
            1.0 + (3.0 * GELU_CUBE) * (gate_band * gate_band)
        )
        act[...] = (gelu * up_band).astype(bf16)
        grad_act = outer_rows(branch, w_down)
        d_gate[...] = (grad_act * up_band * slope).astype(bf16)
        d_up[...] = (grad_act * gelu).astype(bf16)
        first = pl.ds(pl.multiple_of(n * band, band), band)
        r.rows_both[first, :] = inner_rows(act[...], branch).astype(bf16)
        r.grad_gate[n] = inner_rows(normed, d_gate[...]).astype(bf16)
        r.grad_up[n] = inner_rows(normed, d_up[...]).astype(bf16)

        @pl.when(n == 0)
        def _():
            here.meet()

        down.start_pair(n)
        gate.start_pair(n)
        up.start_pair(n)
        out = product(act[...], w_down)
        gy = outer_rows(d_gate[...], w_gate) + outer_rows(d_up[...], w_up)

        @pl.when(n == 0)
        def _():
            r.grad_two[...] = out
            r.gy[...] = gy

        @pl.when(n > 0)
        def _():
            r.grad_two[...] += out
            r.gy[...] += gy

        @pl.when(n < 2)
        def _():
            start_ffn(n + 2)

        @pl.when(n > 0)
        def _():
            for group in (down, gate, up):
                group.pair_part(n - 1)

    w_cout_load = load(1, r.w_two.at[3], r.grad_self.at[3])
    w_two_loads = [load(8 + m, r.w_two.at[m], r.grad_self.at[m]) for m in range(3)]
    encoded_load = load(7, r.enc_in, enc_all)
    hidden_two_load.wait()
    r.small[...] = jnp.zeros_like(r.small)

    @row_steps(rows, 64)
    def _(part):
        hidden = r.hidden[part, :]
        slots = place * rows + part.start + iota((64, 1), 0)
        r.dq[part, :] = jnp.where(slots < length, hidden + r.grad_two[part, :], 0.0).astype(bf16)
        grad, gain = norm_back_rows(hidden, r.gains[2:3, :], r.gy[part, :])
        total = grad_result(part, 64) + grad
        r.grad_two[part, :] = total
        r.branch[part, :] = total.astype(bf16)
        r.small[2:3, :] += gain

    result_copy = load(13, r.dq, r.layer_out)
    normed_two_load = load(6, r.normed_two_in, r.normed)
    hidden_load = load(11, r.hidden_one_in, r.hidden)
    fill_pads(r.pads, count)
    fill_fixed_bias(r.bias)
    for group in (down, gate, up):
        group.pair_part(3)
        group.sent_parts()
    w_cout_load.wait()
    r.grad_mixed[...] = outer_rows(r.branch[...], r.grad_self[3]).astype(bf16)
    w_sout_load = load(12, r.w_one.at[3], r.grad_self.at[3])
    mixed_load.wait()
    weight_grad_turned(r.grad_cross.at[3], r.mixed, r.branch)
    for copy in (cqueries_load, ckeys_load, cvalues_load):
        copy.wait()
    result_copy.wait()
    down.pair_sent()
    keys_load = load(13, r.keys_in, keys)
    values_load = load(14, r.values_in, values)

    def stepped(table, pair):
        for when, steps in table.items():

            @pl.when(pair == when)
            def _(steps=steps):
                for step in steps:
                    step()

    @pl.loop(0, PAIRS)
    def _(pair):
        part = columns(pair)
        backward_pair(
            None, None, r.queries.at[:, part], ckeys.at[:, part], cvalues.at[:, part],
            r.grad_mixed.at[:, part], r.mixed.at[part, :], r.log_cross.at[pair],
            r.dq.at[:, part], dck.at[:, part], dcv.at[:, part], None, None, r.pads, None, r.kt_buf, None,
        )

    fill_pads(r.pads, length)
    mixed_self_load = load(15, r.mixed_self_in, r.mixed)
    queries_load = load(16, r.queries_in, r.queries)
    w_two_loads[0].wait()
    r.gy[...] = outer_rows(r.dq[...], r.grad_self[0])
    normed_two_load.wait()
    weight_grad(r.grad_cross.at[0], r.normed, r.dq)
    gate.first_side()
    encoded_load.wait()
    weight_grad(r.grad_cross.at[1], enc_all, dck)
    weight_grad(r.grad_cross.at[2], enc_all, dcv)
    for n in range(4):
        cross.start_pair(n)
    w_two_loads[1].wait()
    w_two_loads[2].wait()
    enc_part[...] = (outer_rows(dck[...], r.grad_self[1]) + outer_rows(dcv[...], r.grad_self[2])).astype(bf16)
    quarters = ((here.along_x, here.to_x), (here.along_y, here.to_y), (here.corner, here.to_corner))

    def own_rows(ref, size, part, step):
        return ref[pl.ds(pl.multiple_of(place * size + part.start, step), step), :].astype(f32)

    enc_sum.sides()
    hidden_load.wait()

    @row_steps(rows, 64)
    def _(part):
        grad, gain = norm_back_rows(r.hidden[part, :], r.gains[1:2, :], r.gy[part, :])
        total = r.grad_two[part, :] + grad
        r.grad_two[part, :] = total
        r.branch[part, :] = total.astype(bf16)
        r.small[1:2, :] += gain

    w_sout_load.wait()
    r.grad_mixed[...] = outer_rows(r.branch[...], r.grad_self[3]).astype(bf16)
    mixed_self_load.wait()
    weight_grad_turned(r.grad_self.at[3], r.mixed, r.branch)
    for copy in (queries_load, keys_load, values_load):
        copy.wait()

    def keep_enc(part, total):
        r.enc_total[part, :] = total

    def enc_done():
        enc_sum.total(keep_enc)
        pltpu.make_async_copy(r.enc_total, r.enc_sum, r.load_sem.at[20]).start()

    def cross_sides():
        cross.pair_sum()

    def load_normed():
        enc_sum.sent()
        pltpu.make_async_copy(r.normed_all_in, r.token_part, r.load_sem.at[21]).start()

    def w_one_copies():
        return [
            pltpu.make_async_copy(r.w_one.at[m], r.grad_cross.at[m], r.load_sem.at[17 + m]) for m in range(3)
        ]

    def load_w_one():
        cross.pair_sent()
        for copy in w_one_copies():
            copy.start()

    self_steps = {
        0: [up.first_side, cross_sides],
        1: [enc_sum.first_side],
        2: [gate.second_side],
        3: [enc_done, load_normed, down.along_planes, up.second_side],
        4: [down.first_side, load_w_one],
        5: [cross.first_side],
    }

    @pl.loop(0, PAIRS)
    def _(pair):
        part = columns(pair)
        backward_pair(
            place, r.profile.at[pair], r.queries.at[:, part], keys.at[:, part],
            values.at[:, part], r.grad_mixed.at[:, part], r.mixed.at[part, :],
            r.log_self.at[pair], r.dq.at[:, part], r.dk.at[:, part], r.dv.at[:, part],
            r.near.at[pair], r.far.at[pair], r.pads, r.bias, r.kt_buf, r.grad_buf,
        )
        stepped(self_steps, pair)

    tokens_load = load(22, r.tokens_all_in, keys)
    pltpu.make_async_copy(r.normed_all_in, r.token_part, r.load_sem.at[21]).wait()
    own = pl.ds(pl.multiple_of(place * rows, BLOCK), rows)
    weight_grad(r.grad_self.at[0], r.token_part.at[own, :], r.dq)
    weight_grad(r.grad_self.at[1], r.token_part, r.dk)
    weight_grad(r.grad_self.at[2], r.token_part, r.dv)
    for n in range(4):
        self_one.start_pair(n)
    for n in range(4):
        self_two.start_pair(n)
    for copy in w_one_copies():
        copy.wait()

    @row_steps(count, 512)
    def _(part):
        total = outer_rows(r.dk[part, :], r.grad_cross[1]) + outer_rows(r.dv[part, :], r.grad_cross[2])
        r.token_part[part, :] = total.astype(bf16)

    self_one.pair_sum()
    self_two.pair_sum()
    gate.along_planes()
    down.second_side()
    cross.second_side()
    r.gy[...] = outer_rows(r.dq[...], r.grad_cross[0])
    up.along_planes()
    tokens_load.wait()

    @row_steps(count, 64)
    def _(part):
        values = keys[part, :].astype(f32)
        scale = lax.rsqrt(jnp.mean(values * values, axis=-1, keepdims=True) + EPSILON)
        grad = r.token_part[part, :].astype(f32)
        r.small[0:1, :] += jnp.sum(grad * values * scale, axis=0, keepdims=True)

    @row_steps(rows, 64)
    def _(part):
        values = own_rows(keys, rows, part, 64)
        scale = lax.rsqrt(jnp.mean(values * values, axis=-1, keepdims=True) + EPSILON)
        r.small[0:1, :] += jnp.sum(r.gy[part, :] * values * scale, axis=0, keepdims=True)

    for pair in range(PAIRS):
        table = jnp.dot(
            r.near[pair], r.one_hot[...], precision=lax.Precision.HIGHEST, preferred_element_type=f32
        )
        last_bucket = iota(table.shape, 1) == BUCKETS - 1
        table = table + jnp.where(last_bucket, jnp.sum(r.far[pair], axis=1, keepdims=True), 0.0)
        r.small[8 + 2 * pair : 10 + 2 * pair, 0 : table.shape[1]] = table

    small, small_core, small_seq, small_plane = r.small, r.small_core, r.small_seq, r.small_plane
    send(lambda: (small, small_core, r.s_send.at[0], r.s_recv.at[0], here.partner))
    down.spread()
    gate.spread()
    self_one.first_side()
    arrived(small_core, r.s_recv.at[0])
    small_seq[place] = small[...] + small_core[...]
    for k, (_, device) in enumerate(quarters):
        send(
            lambda k=k, device=device: (
                small_seq.at[place], small_seq.at[place], r.s_send.at[1 + k], r.s_recv.at[1 + k], device
            )
        )
    down.finish()
    self_two.first_side()
    token_sum.sides()
    cross.along_planes()
    up.spread()
    self_one.second_side()
    for k, (quarter, _) in enumerate(quarters):
        arrived(small_seq.at[quarter], r.s_recv.at[1 + k])
    small_plane[here.plane] = (small_seq[0] + small_seq[1]) + (small_seq[2] + small_seq[3])
    for k in range(1, planes):
        send(
            lambda k=k: (
                small_plane.at[here.plane], small_plane.at[here.plane],
                r.s_send.at[3 + k], r.s_recv.at[3 + k], here.at_plane(here.ahead(k)),
            )
        )
    gate.finish()
    self_two.second_side()
    token_sum.first_side()
    cross.spread()
    up.finish()
    self_one.along_planes()
    cross.finish()

    def keep_tokens(part, total):
        values = own_rows(keys, rows, part, 64)
        grad, _ = norm_back_rows(values, r.gains[0:1, :], r.gy[part, :] + total)
        r.hidden[part, :] = r.grad_two[part, :] + grad

    token_sum.total(keep_tokens)
    token_copy = pltpu.make_async_copy(r.hidden, r.grad_tokens, r.load_sem.at[23])
    token_copy.start()
    for k in range(1, planes):
        arrived(small_plane.at[here.ahead(planes - k)], r.s_recv.at[3 + k])
    total = small_plane[0]
    for k in range(1, planes):
        total = total + small_plane[k]
    r.small_out[...] = total
    self_two.along_planes()
    self_one.spread()
    self_one.finish()
    self_two.spread()
    self_two.finish()
    token_copy.wait()
    pltpu.make_async_copy(r.enc_total, r.enc_sum, r.load_sem.at[20]).wait()
    for group in sums:
        group.end()
    token_sum.sent()
    for make in others:
        remote(*make()).wait_send()


def backward_fused(shards, length, small, large):
    stack, _, band, _, tall = make_kinds(shards)
    planes = lax.axis_size("fsdp") // 2
    lower = planes // 2
    first_rows = stack.rows // 2
    parts = [StackRows(n * first_rows, first_rows, stack.cols) for n in range(2)]
    kinds = [tall, band, band, stack, *parts]
    f32, low = jnp.float32, jnp.bfloat16
    rows, width = large["cotangent"].shape
    count, enc_count = large["keys_in"].shape[0], large["ckeys_in"].shape[0]
    in_vmem = pl.BlockSpec(memory_space=pltpu.VMEM)
    in_layout, operands = flatten(dict(length=length), small, large)
    in_specs = [SCALARS] + [in_vmem] * len(small)
    in_specs += [ANYWHERE] * (len(operands) - len(in_specs))
    small_shape = (24, width)

    def chunk(kind, *lead):
        return pltpu.VMEM(lead + (kind.rows, kind.cols), low)

    results = dict(
        out=[
            shaped((kind.rows, 4 * kind.cols) if isinstance(kind, Wide) else (4, kind.rows, kind.cols), low)
            for kind in (tall, band, band, stack, stack)
        ],
        layer_out=shaped((rows, width), low),
        grad_tokens=shaped((rows, width), f32),
        enc_sum=shaped((enc_count // 4, width), f32),
        small_out=shaped(small_shape, f32),
    )
    out_layout, out_shapes = flatten(results)
    square = (width, width)
    all_rows = pltpu.VMEM((count, width), low)
    some_rows = pltpu.VMEM((rows, width), low)
    wide_rows = pltpu.VMEM((rows, width), f32)
    half_tall = pltpu.VMEM((2, tall.rows, tall.cols // 2), low)
    later = kinds[1:]
    sides = [half_tall] + [chunk(kind, 2, lower) for kind in later]
    row_sides = [pltpu.VMEM((2, size, width // 2), low) for size in (rows, enc_count // 4)]
    buffers = backward_scratch(count)
    scratch = dict(
        sums=[chunk(kind, 4, planes) for kind in kinds],
        side_x=sides, side_y=sides, last=sides,
        from_z=[chunk(tall, planes - 1, 4)] + [chunk(kind, planes - 1) for kind in later],
        final=[chunk(kind, 4) for kind in kinds],
        grad_gate=pltpu.VMEM((4, width, band.cols), low),
        grad_up=pltpu.VMEM((4, width, band.cols), low),
        grad_cross=pltpu.VMEM((4,) + square, low),
        grad_self=pltpu.VMEM((4,) + square, low),
        rows_both=pltpu.VMEM((2 * count, width), low),
        dk=all_rows, dv=all_rows, token_part=all_rows,
        queries=some_rows, normed=some_rows, branch=some_rows, grad_mixed=some_rows, dq=some_rows,
        grad_two=wide_rows, hidden=wide_rows, gy=wide_rows,
        mixed=pltpu.VMEM((width, rows), f32),
        enc_total=pltpu.VMEM((enc_count // 4, width), f32),
        row_x=row_sides, row_y=row_sides, row_last=row_sides,
        pads=buffers[0], bias=buffers[1], kt_buf=buffers[2], grad_buf=buffers[3],
        near=pltpu.VMEM((PAIRS, 2, BLOCK), f32),
        far=pltpu.VMEM((PAIRS, 2, rows), f32),
        small=pltpu.VMEM(small_shape, f32),
        small_core=pltpu.VMEM(small_shape, f32),
        small_seq=pltpu.VMEM((4,) + small_shape, f32),
        small_plane=pltpu.VMEM((planes,) + small_shape, f32),
        f_sem=DMA((3, 2)),
        c_send=DMA((GROUPS, 4)), c_recv=DMA((GROUPS, 4)),
        a_send=DMA((GROUPS + 2, 4)), a_recv=DMA((GROUPS + 2, 4)),
        b_send=DMA((GROUPS + 2, 2)), b_recv=DMA((GROUPS + 2, 2)),
        z_send=DMA((GROUPS, planes - 1)), z_recv=DMA((GROUPS, planes - 1)),
        g_send=DMA((GROUPS, 4)), g_recv=DMA((GROUPS, 4)),
        s_send=DMA((3 + planes,)), s_recv=DMA((3 + planes,)),
        out_sem=DMA((GROUPS, 4)), load_sem=DMA((24,)),
    )
    scratch_layout, scratch_shapes = flatten(scratch)
    outs = pl.pallas_call(
        functools.partial(backward_kernel, kinds, planes, in_layout | out_layout | scratch_layout),
        in_specs=in_specs,
        out_specs=[ANYWHERE] * (len(out_shapes) - 1) + [in_vmem],
        out_shape=out_shapes,
        scratch_shapes=scratch_shapes,
        compiler_params=pltpu.CompilerParams(
            collective_id=1, has_side_effects=True, vmem_limit_bytes=67_000_000
        ),
        name="backward_fused",
    )(*operands)
    got = Space(out_layout, outs)
    grads = [got.out[SELF][m] for m in range(4)] + [got.out[CROSS][m] for m in range(4)]
    grads += [got.out[GATE], got.out[UP], got.out[DOWN].reshape(-1, width)]
    return got.layer_out, [grad.astype(f32) for grad in grads], got.grad_tokens, got.enc_sum, got.small_out


ONE, TWO, GATE_IN, UP_IN, DOWN_IN = range(5)


class Gathering:
    def __init__(self, kinds, here, r):
        self.kinds, self.here, self.r = kinds, here, r
        self.planes = here.planes
        shape = (4, here.planes, 2, kinds[ONE].rows, kinds[ONE].cols)
        self.full = [r.weights_one.reshape(*shape), r.weights_two.reshape(*shape), *r.ffn_full]
        self.shards = [r.shards[0:4], r.shards[4:8], r.shards[8], r.shards[9], r.shards[10]]
        self.started = []

    def send(self, make):
        remote(*make()).start()
        self.started.append(make)

    def arrived(self, target, recv_sem):
        pltpu.make_async_copy(target, target, recv_sem).wait()

    def plane_copy(self, g, k, source):
        here, r = self.here, self.r
        return remote(
            source, self.kinds[g].part(self.full[g], here.seq, here.plane, here.core),
            r.z_send.at[g, k - 1], r.z_recv.at[g, k - 1], here.at_plane(here.ahead(k)),
        )

    def start_planes(self, g):
        for k in range(1, self.planes):
            if g <= TWO:
                for m in range(4):

                    @pl.when(self.here.seq == m)
                    def _(m=m, k=k):
                        self.plane_copy(g, k, self.shards[g][m]).start()

            else:
                self.plane_copy(g, k, self.kinds[g].own(self.shards[g], self.here.seq)).start()

    def own_copies(self, g):
        here, r, full = self.here, self.r, self.full[g]
        if g <= TWO:
            return [
                pltpu.make_async_copy(
                    self.shards[g][m], full.at[m, here.plane, here.core], r.own_sem.at[g, m]
                )
                for m in range(4)
            ]
        return [
            pltpu.make_async_copy(
                self.shards[g], self.kinds[g].whole(full, here.plane, here.core), r.own_sem.at[g, 0]
            )
        ]

    def start_own(self, g):
        here, r, full = self.here, self.r, self.full[g]
        for copy in self.own_copies(g):
            copy.start()
        if g <= TWO:
            for m in range(4):
                self.send(
                    lambda m=m: (
                        self.shards[g][m], full.at[m, here.plane, here.core],
                        r.p_send.at[g, m], r.p_recv.at[g, m], here.partner,
                    )
                )
        else:
            self.send(
                lambda: (
                    self.shards[g], self.kinds[g].whole(full, here.plane, here.core),
                    r.p_send.at[g, 0], r.p_recv.at[g, 0], here.partner,
                )
            )

    def chunk(self, g, quarter, k, first=0, count=None):
        here = self.here
        return self.kinds[g].part(self.full[g], quarter, here.ahead(self.planes - k), here.core, first, count)

    def from_plane(self, g):
        here, r = self.here, self.r
        for k in range(1, self.planes):
            self.arrived(self.chunk(g, here.seq, k), r.z_recv.at[g, k - 1])
            for n, device in enumerate((here.to_x, here.to_y)):

                def make(k=k, n=n, device=device):
                    chunk = self.chunk(g, here.seq, k)
                    return chunk, chunk, r.x_send.at[n, g, k - 1], r.x_recv.at[n, g, k - 1], device

                self.send(make)

    def from_sides(self, g):
        here, r = self.here, self.r
        half = self.kinds[g].rows // 2
        turns = ((here.along_x, 0, here.to_y), (here.along_y, half, here.to_x))
        for k in range(1, self.planes):
            for n, (quarter, first, device) in enumerate(turns):
                self.arrived(self.chunk(g, quarter, k), r.x_recv.at[n, g, k - 1])

                def make(k=k, n=n, quarter=quarter, first=first, device=device):
                    chunk = self.chunk(g, quarter, k, first, half)
                    return chunk, chunk, r.d_send.at[n, g, k - 1], r.d_recv.at[n, g, k - 1], device

                self.send(make)

    def from_corner(self, g):
        here, r = self.here, self.r
        half = self.kinds[g].rows // 2
        for k in range(1, self.planes):
            self.arrived(self.chunk(g, here.corner, k, 0, half), r.d_recv.at[0, g, k - 1])
            self.arrived(self.chunk(g, here.corner, k, half, half), r.d_recv.at[1, g, k - 1])

            def make(k=k):
                whole = self.kinds[g].whole(self.full[g], here.ahead(self.planes - k), here.core)
                return whole, whole, r.c_send.at[g, k - 1], r.c_recv.at[g, k - 1], here.partner

            self.send(make)

    def complete(self, g):
        here, r, full = self.here, self.r, self.full[g]
        for copy in self.own_copies(g):
            copy.wait()
        if g <= TWO:
            for m in range(4):
                self.arrived(full.at[m, here.plane, 1 - here.core], r.p_recv.at[g, m])
        else:
            self.arrived(self.kinds[g].whole(full, here.plane, 1 - here.core), r.p_recv.at[g, 0])
        for k in range(1, self.planes):
            behind = here.ahead(self.planes - k)
            self.arrived(self.kinds[g].whole(full, behind, 1 - here.core), r.c_recv.at[g, k - 1])

    def end(self):
        for g in range(5):
            for k in range(1, self.planes):
                source = self.shards[g][0] if g <= TWO else self.kinds[g].own(self.shards[g], self.here.seq)
                self.plane_copy(g, k, source).wait_send()
        for make in self.started:
            remote(*make()).wait_send()


def forward_kernel(kinds, planes, layout, *refs):
    r = Space(layout, refs)
    bf16, f32 = jnp.bfloat16, jnp.float32
    here = Peers(planes)
    place, length = here.seq, r.length[0]
    gather = Gathering(kinds, here, r)
    rows, width = r.tokens.shape
    count, enc_count = r.normed.shape[0], r.encoded_rows.shape[0]
    row_ins = (r.tokens, r.encoded)
    row_alls = (r.source_rows, r.encoded_rows)
    stores = []

    def store(n, source, target):
        stores.append((n, source, target))
        pltpu.make_async_copy(source, target, r.store_sem.at[n]).start()

    def block_of(item, quarter, first=0, size=None):
        size_here = row_ins[item].shape[0]
        return row_alls[item].at[pl.ds(quarter * size_here + first, size or size_here), :]

    def rows_start(item):
        for n, device in enumerate((here.to_x, here.to_y)):
            gather.send(
                lambda n=n, device=device: (
                    row_ins[item], block_of(item, place), r.r_send.at[item, n], r.r_recv.at[item, n], device
                )
            )
        pltpu.make_async_copy(row_ins[item], block_of(item, place), r.r_own.at[item]).start()

    def rows_turn(item):
        half = row_ins[item].shape[0] // 2
        turns = ((here.along_x, 0, here.to_y), (here.along_y, half, here.to_x))
        for n, (quarter, first, device) in enumerate(turns):
            gather.arrived(block_of(item, quarter), r.r_recv.at[item, n])

            def make(n=n, quarter=quarter, first=first, device=device):
                chunk = block_of(item, quarter, first, half)
                return chunk, chunk, r.r_send.at[item, 2 + n], r.r_recv.at[item, 2 + n], device

            gather.send(make)

    def rows_done(item):
        half = row_ins[item].shape[0] // 2
        gather.arrived(block_of(item, here.corner, 0, half), r.r_recv.at[item, 2])
        gather.arrived(block_of(item, here.corner, half, half), r.r_recv.at[item, 3])
        pltpu.make_async_copy(row_ins[item], block_of(item, place), r.r_own.at[item]).wait()

    def norm_rows(values, gain):
        scale = lax.rsqrt(jnp.mean(values * values, axis=-1, keepdims=True) + EPSILON)
        return (values * scale * gain).astype(bf16)

    def project(out, left, weight):
        step = min(left.shape[0], 512)

        @row_steps(left.shape[0], step)
        def _(part):
            out[part, :] = product(left[part, :], weight[...]).astype(out.dtype)

    here.greet()
    here.meet()
    rows_start(0)
    gather.start_planes(ONE)
    rows_start(1)
    for g in (TWO, GATE_IN, UP_IN, DOWN_IN):
        gather.start_planes(g)
    for g in range(5):
        gather.start_own(g)
    fill_pads(r.pads, length)
    fill_fixed_bias(r.bias)
    rows_turn(0)
    gather.from_plane(ONE)
    rows_turn(1)
    rows_done(0)

    @row_steps(count, 128)
    def _(part):
        r.normed[part, :] = norm_rows(r.source_rows[part, :].astype(f32), r.gains[0:1, :])

    store(0, r.source_rows, r.tokens_all)
    store(1, r.normed, r.normed_all)
    gather.from_sides(ONE)
    gather.from_plane(TWO)
    gather.from_corner(ONE)
    rows_done(1)
    store(2, r.encoded_rows, r.enc_all)
    gather.complete(ONE)
    store(3, r.weights_one, r.w_one)
    own = pl.ds(pl.multiple_of(place * rows, BLOCK), rows)
    project(r.query_rows, r.normed.at[own, :], r.weights_one.at[0])
    project(r.key_rows, r.normed, r.weights_one.at[1])
    project(r.value_rows, r.normed, r.weights_one.at[2])
    store(4, r.query_rows, r.queries)
    store(5, r.key_rows, r.keys)
    store(6, r.value_rows, r.values)
    gather.from_plane(GATE_IN)
    gather.from_sides(TWO)
    self_steps = {2: [lambda: gather.from_plane(UP_IN)], 4: [lambda: gather.from_corner(TWO)]}

    def stepped(table, pair):
        for when, steps in table.items():

            @pl.when(pair == when)
            def _(steps=steps):
                for step in steps:
                    step()

    @pl.loop(0, PAIRS)
    def _(pair):
        part = columns(pair)
        self_forward_pair(
            place, r.profile.at[pair], r.query_rows.at[:, part], r.key_rows.at[:, part],
            r.value_rows.at[:, part], r.mixed.at[:, part], r.turned_one.at[part, :], r.log_self.at[pair],
            r.pads, r.bias, r.s_buf, r.vt_buf,
        )
        stepped(self_steps, pair)

    store(7, r.turned_one, r.mixed_self_turned)
    project(r.hidden, r.mixed, r.weights_one.at[3])

    @row_steps(rows, 64)
    def _(part):
        start = pl.multiple_of(place * rows + part.start, 64)
        total = r.hidden[part, :] + r.source_rows[pl.ds(start, 64), :].astype(f32)
        r.hidden[part, :] = total
        r.normed_rows[part, :] = norm_rows(total, r.gains[1:2, :])

    store(8, r.hidden, r.hidden_one)
    store(9, r.normed_rows, r.normed_two)
    gather.from_plane(DOWN_IN)
    gather.from_sides(GATE_IN)
    gather.complete(TWO)
    store(10, r.weights_two, r.w_two)
    project(r.cquery_rows, r.normed_rows, r.weights_two.at[0])
    project(r.ckey_rows, r.encoded_rows, r.weights_two.at[1])
    project(r.cvalue_rows, r.encoded_rows, r.weights_two.at[2])
    store(11, r.cquery_rows, r.cqueries)
    store(12, r.ckey_rows, r.ckeys)
    store(13, r.cvalue_rows, r.cvalues)
    cross_steps = {
        1: [lambda: gather.from_corner(GATE_IN)],
        3: [lambda: gather.from_sides(UP_IN)],
    }

    @pl.loop(0, PAIRS)
    def _(pair):
        part = columns(pair)
        cross_forward_pair(
            r.cquery_rows.at[:, part], r.ckey_rows.at[:, part], r.cvalue_rows.at[:, part],
            r.cmixed.at[:, part], r.turned_two.at[part, :], r.log_cross.at[pair],
        )
        stepped(cross_steps, pair)

    store(14, r.turned_two, r.mixed_cross_turned)
    gather.from_sides(DOWN_IN)
    project(r.hidden_last, r.cmixed, r.weights_two.at[3])

    @row_steps(rows, 64)
    def _(part):
        total = r.hidden_last[part, :] + r.hidden[part, :]
        r.hidden_last[part, :] = total
        r.normed_last[part, :] = norm_rows(total, r.gains[2:3, :])

    store(15, r.hidden_last, r.hidden_two)
    store(16, r.normed_last, r.normed_three)
    gather.from_corner(UP_IN)
    gather.from_corner(DOWN_IN)
    for g in (GATE_IN, UP_IN, DOWN_IN):
        gather.complete(g)
    gather.end()
    for n, source, target in stores:
        pltpu.make_async_copy(source, target, r.store_sem.at[n]).wait()


def forward_fused(shards, length, tokens, encoded, small):
    kinds = make_kinds(shards)
    planes = lax.axis_size("fsdp") // 2
    f32, low = jnp.float32, jnp.bfloat16
    rows, width = tokens.shape
    enc_rows = encoded.shape[0]
    count, enc_count = 4 * rows, 4 * enc_rows
    square = (4, width, width)
    in_vmem = pl.BlockSpec(memory_space=pltpu.VMEM)
    in_layout, operands = flatten(
        dict(length=length), small, dict(tokens=tokens, encoded=encoded, shards=list(shards))
    )
    in_specs = [SCALARS] + [in_vmem] * len(small)
    in_specs += [ANYWHERE] * (len(operands) - len(in_specs))
    shapes = full_shapes(kinds, planes)
    large_outs = dict(
        w_one=shaped(square, low), w_two=shaped(square, low),
        ffn_full=[shaped(shape, low) for shape in shapes[2:]],
        tokens_all=shaped((count, width), low), normed_all=shaped((count, width), low),
        enc_all=shaped((enc_count, width), low),
        queries=shaped((rows, width), low), keys=shaped((count, width), low),
        values=shaped((count, width), low), mixed_self_turned=shaped((width, rows), f32),
        hidden_one=shaped((rows, width), f32), normed_two=shaped((rows, width), low),
        cqueries=shaped((rows, width), low), ckeys=shaped((enc_count, width), low),
        cvalues=shaped((enc_count, width), low), mixed_cross_turned=shaped((width, rows), f32),
        hidden_two=shaped((rows, width), f32), normed_three=shaped((rows, width), low),
    )
    small_outs = dict(
        log_self=shaped((PAIRS, 2, rows), f32), log_cross=shaped((PAIRS, 2, rows), f32)
    )
    out_layout, out_shapes = flatten(large_outs, small_outs)
    all_rows = pltpu.VMEM((count, width), low)
    enc_all = pltpu.VMEM((enc_count, width), low)
    some_rows = pltpu.VMEM((rows, width), low)
    wide_rows = pltpu.VMEM((rows, width), f32)
    turned = pltpu.VMEM((width, rows), f32)
    buffers = forward_scratch(count, rows)
    steps = planes - 1
    scratch = dict(
        weights_one=pltpu.VMEM(square, low), weights_two=pltpu.VMEM(square, low),
        source_rows=all_rows, normed=all_rows, key_rows=all_rows, value_rows=all_rows,
        encoded_rows=enc_all, ckey_rows=enc_all, cvalue_rows=enc_all,
        query_rows=some_rows, cquery_rows=some_rows, mixed=some_rows, cmixed=some_rows,
        normed_rows=some_rows, normed_last=some_rows,
        hidden=wide_rows, hidden_last=wide_rows, turned_one=turned, turned_two=turned,
        pads=buffers[0], bias=buffers[1], s_buf=buffers[2], vt_buf=buffers[3],
        z_send=DMA((5, steps)), z_recv=DMA((5, steps)),
        own_sem=DMA((5, 4)), p_send=DMA((5, 4)), p_recv=DMA((5, 4)),
        x_send=DMA((2, 5, steps)), x_recv=DMA((2, 5, steps)),
        d_send=DMA((2, 5, steps)), d_recv=DMA((2, 5, steps)),
        c_send=DMA((5, steps)), c_recv=DMA((5, steps)),
        r_send=DMA((2, 4)), r_recv=DMA((2, 4)), r_own=DMA((2,)), store_sem=DMA((17,)),
    )
    scratch_layout, scratch_shapes = flatten(scratch)
    outs = pl.pallas_call(
        functools.partial(forward_kernel, kinds, planes, in_layout | out_layout | scratch_layout),
        in_specs=in_specs,
        out_specs=[ANYWHERE] * (len(out_shapes) - 2) + [in_vmem] * 2,
        out_shape=out_shapes,
        scratch_shapes=scratch_shapes,
        compiler_params=pltpu.CompilerParams(
            collective_id=0, has_side_effects=True, vmem_limit_bytes=66_000_000
        ),
        name="forward_fused",
    )(*operands)
    return Space(out_layout, outs)


def local(
    tokens, encoded, lengths, cotangent, gain_self, gain_cross, gain_ff, bucket_table,
    self_query, self_key, self_value, self_out, cross_query, cross_key, cross_value, cross_out,
    ff_gate, ff_up, ff_down,
):
    rows_here = tokens.shape[1]
    seq_place = lax.axis_index("seq")
    length = lengths[0]
    bf16, f32 = jnp.bfloat16, jnp.float32
    gain_one = gain_self.astype(f32)
    gain_two = gain_cross.astype(f32)
    gain_three = gain_ff.astype(f32)
    shards = (
        self_query, self_key, self_value, self_out, cross_query, cross_key, cross_value, cross_out,
        ff_gate, ff_up, ff_down,
    )
    one_hot = (
        bucket_ids(BLOCK)[:, None] == jnp.arange(BUCKETS, dtype=jnp.int32)[None, :]
    ).astype(bf16)
    profile = inner_rows(bucket_table, one_hot.T).reshape(PAIRS, 2, BLOCK)
    place = jnp.stack([seq_place.astype(jnp.int32), length])

    source = tokens[0].astype(f32)
    if kernels_fit(shards):
        gains = jnp.stack([gain_one, gain_two, gain_three])
        forward = forward_fused(
            shards, lengths, tokens[0], encoded[0],
            dict(
                profile=profile, gains=gains
            ),
        )
        one_hot_wide = jnp.pad(one_hot.astype(f32), ((0, 0), (0, PAIR - BUCKETS)))
        width = source.shape[1]
        w_gate, w_up, w_down = (full.reshape(-1, full.shape[-1]) for full in forward.ffn_full)
        layer_out, grads, grad_tokens, enc_sum, small = backward_fused(
            shards, lengths,
            dict(
                profile=profile, log_cross=forward.log_cross, log_self=forward.log_self,
                gains=gains, one_hot=one_hot_wide,
            ),
            dict(
                cotangent=cotangent[0], w_gate=w_gate, w_up=w_up, w_down=w_down,
                normed_three_in=forward.normed_three, hidden_two_in=forward.hidden_two,
                w_one=forward.w_one, w_two=forward.w_two, mixed_cross_in=forward.mixed_cross_turned,
                cqueries_in=forward.cqueries, ckeys_in=forward.ckeys, cvalues_in=forward.cvalues,
                normed_two_in=forward.normed_two, enc_in=forward.enc_all, hidden_one_in=forward.hidden_one,
                mixed_self_in=forward.mixed_self_turned, queries_in=forward.queries, keys_in=forward.keys,
                values_in=forward.values, normed_all_in=forward.normed_all,
                tokens_all_in=forward.tokens_all,
            ),
        )
        table_sum = small[8 : 8 + HEADS, :BUCKETS].T
        return (
            layer_out[None], grad_tokens[None], enc_sum[None], small[0], small[1], small[2], table_sum, *grads
        )
    weights, tokens_all, enc_all = gather_plain(shards, tokens[0], encoded[0])
    (w_query, w_key, w_value, w_sout, w_cquery, w_ckey, w_cvalue, w_cout, w_gate, w_up, w_down) = weights
    normed_all = rms_scale(tokens_all.astype(f32), gain_one).astype(bf16)
    normed_one = rms_scale(source, gain_one).astype(bf16)
    queries = product(normed_one, w_query).astype(bf16)
    keys = product(normed_all, w_key).astype(bf16)
    values = product(normed_all, w_value).astype(bf16)
    mixed_self, mixed_self_turned, log_self = self_forward(place, profile, queries, keys, values)
    hidden_one = source + product(mixed_self, w_sout)
    normed_two = rms_scale(hidden_one, gain_two).astype(bf16)
    cqueries = product(normed_two, w_cquery).astype(bf16)
    ckeys = product(enc_all, w_ckey).astype(bf16)
    cvalues = product(enc_all, w_cvalue).astype(bf16)
    mixed_cross, mixed_cross_turned, log_cross = cross_forward(cqueries, ckeys, cvalues)
    hidden_two = hidden_one + product(mixed_cross, w_cout)
    normed_three = rms_scale(hidden_two, gain_three).astype(bf16)
    gate = product(normed_three, w_gate)
    up = product(normed_three, w_up)

    def gated(gate_rows, up_rows):
        return jax.nn.gelu(gate_rows, approximate=True) * up_rows

    activated_f, pull_gate = jax.vjp(gated, gate, up)
    activated = activated_f.astype(bf16)
    slot_ids = seq_place * rows_here + jnp.arange(rows_here, dtype=jnp.int32)
    valid = (slot_ids < length).astype(f32)[:, None]
    result = (valid * (hidden_two + product(activated, w_down))).astype(bf16)

    grad_result = valid * cotangent[0].astype(f32)
    branch_ff = grad_result.astype(bf16)
    grad_gate_f, grad_up_f = pull_gate(outer_rows(branch_ff, w_down))
    grad_gate = grad_gate_f.astype(bf16)
    grad_up = grad_up_f.astype(bf16)
    g_down = inner_rows(activated, branch_ff).astype(bf16)
    g_gate = inner_rows(normed_three, grad_gate).astype(bf16)
    g_up = inner_rows(normed_three, grad_up).astype(bf16)
    grad_three, grad_gain_three = norm_back(
        hidden_two, gain_three, outer_rows(grad_gate, w_gate) + outer_rows(grad_up, w_up)
    )
    grad_two = grad_result + grad_three
    branch_cross = grad_two.astype(bf16)
    g_cout = inner_rows(mixed_cross, branch_cross).astype(bf16)
    grad_mixed_cross = outer_rows(branch_cross, w_cout).astype(bf16)
    grad_cq, grad_ck, grad_cv = cross_backward(
        cqueries, ckeys, cvalues, grad_mixed_cross, mixed_cross_turned, log_cross
    )
    g_cquery = inner_rows(normed_two, grad_cq).astype(bf16)
    g_ckey = inner_rows(enc_all, grad_ck).astype(bf16)
    g_cvalue = inner_rows(enc_all, grad_cv).astype(bf16)
    enc_part = (outer_rows(grad_ck, w_ckey) + outer_rows(grad_cv, w_cvalue)).astype(bf16)
    grad_two_back, grad_gain_two = norm_back(hidden_one, gain_two, outer_rows(grad_cq, w_cquery))
    grad_one = grad_two + grad_two_back
    branch_self = grad_one.astype(bf16)
    g_sout = inner_rows(mixed_self, branch_self).astype(bf16)
    grad_mixed_self = outer_rows(branch_self, w_sout).astype(bf16)
    grad_q, grad_k, grad_v, near_part, far_part = self_backward(
        place, profile, queries, keys, values, grad_mixed_self, mixed_self_turned, log_self
    )
    g_query = inner_rows(normed_one, grad_q).astype(bf16)
    g_key = inner_rows(normed_all, grad_k).astype(bf16)
    g_value = inner_rows(normed_all, grad_v).astype(bf16)
    token_part = (outer_rows(grad_k, w_key) + outer_rows(grad_v, w_value)).astype(bf16)
    query_part = outer_rows(grad_q, w_query)

    near_rows = near_part.reshape(HEADS, BLOCK)
    far_rows = jnp.sum(far_part, axis=-1).reshape(HEADS)
    table_part = lax.dot_general(
        one_hot.astype(f32), near_rows, (((0,), (1,)), ((), ())),
        precision=lax.Precision.HIGHEST, preferred_element_type=f32,
    )
    table_part = table_part.at[BUCKETS - 1].add(far_rows)

    hat_all = rms_scale(tokens_all.astype(f32), jnp.ones_like(gain_one))
    hat_one = rms_scale(source, jnp.ones_like(gain_one))
    grad_gain_one = jnp.sum(token_part.astype(f32) * hat_all, axis=0) + jnp.sum(
        query_part * hat_one, axis=0
    )
    table_row = jnp.zeros((gain_one.shape[0],), f32).at[: BUCKETS * HEADS].set(table_part.reshape(-1))
    small = jnp.stack([grad_gain_one, grad_gain_two, grad_gain_three, table_row] + [jnp.zeros_like(gain_one)] * 4)
    reduced, token_sum, enc_sum, small = reduce_plain(
        (g_query, g_key, g_value, g_sout, g_cquery, g_ckey, g_cvalue, g_cout, g_gate, g_up, g_down),
        token_part, enc_part, small,
    )
    grad_zero, _ = norm_back(source, gain_one, query_part + token_sum)
    grad_tokens = grad_one + grad_zero
    table_sum = small[3, : BUCKETS * HEADS].reshape(BUCKETS, HEADS)
    small = (small[0], small[1], small[2], table_sum)
    return (result[None], grad_tokens[None], enc_sum[None], *small, *reduced)


def solution(mesh):
    rows3 = P("fsdp", "seq", None)
    rows2 = P("fsdp", None)
    return jax.shard_map(
        local,
        mesh=mesh,
        in_specs=(rows3, rows3, P("fsdp"), rows3, P(), P(), P(), P(), *([rows2] * 11)),
        out_specs=(rows3, rows3, rows3, P(), P(), P(), P(), *([rows2] * 11)),
        check_vma=False,
    )
```

```python
import functools
import math

import jax
import jax.numpy as jnp
from jax import lax
from jax.experimental import pallas as pl
from jax.experimental.pallas import tpu as pltpu
from jax.sharding import PartitionSpec as P

HEADS = 12
HEAD = 64
BUCKETS = 32
MAX_DISTANCE = 128
EPSILON = 1e-06
NEGATIVE = -1e30
BLOCK = 256
PAIR = 2 * HEAD
MESH = pl.DeviceIdType.MESH


def thresholds():
    exact_limit = BUCKETS // 2
    return [
        int(math.ceil(exact_limit * (MAX_DISTANCE / exact_limit) ** (number / exact_limit)))
        for number in range(1, exact_limit)
    ]


def bucket_ids(key_count):
    exact_limit = BUCKETS // 2
    offsets = jnp.arange(key_count, dtype=jnp.int32)
    passed = jnp.zeros((key_count,), jnp.int32)
    for border in thresholds():
        passed = passed + (offsets >= border).astype(jnp.int32)
    return jnp.where(offsets < exact_limit, offsets, exact_limit + passed)


def rms_scale(values, gain):
    return values * lax.rsqrt(jnp.mean(values * values, axis=-1, keepdims=True) + EPSILON) * gain


def norm_back(values, gain, grad_normed):
    _, pullback = jax.vjp(rms_scale, values, gain)
    return pullback(grad_normed)


def product(left, right):
    return jnp.dot(left, right, preferred_element_type=jnp.float32)


def inner_rows(left, right):
    return lax.dot_general(
        left, right, (((0,), (0,)), ((), ())), preferred_element_type=jnp.float32
    )


def outer_rows(left, right):
    return lax.dot_general(
        left, right, (((1,), (1,)), ((), ())), preferred_element_type=jnp.float32
    )


def iota(shape, axis):
    return lax.broadcasted_iota(jnp.int32, shape, axis)


def head_rows(value, head):
    place = iota(value.shape, 0) // HEAD
    return jnp.where(place == head, value, jnp.zeros_like(value))


def head_cols(value, head):
    place = iota(value.shape, 1) // HEAD
    return jnp.where(place == head, value, jnp.zeros_like(value))


def skew(profile_row):
    wide = jnp.broadcast_to(profile_row, (BLOCK, BLOCK))
    return pltpu.roll(wide, 0, 1, stride=1, stride_axis=0)


def unskew(tile):
    rows = iota(tile.shape, 0)
    bit = 1
    while bit < BLOCK:
        tile = jnp.where((rows // bit) % 2 == 1, pltpu.roll(tile, BLOCK - bit, 1), tile)
        bit *= 2
    return tile


def fill_pads(pads, length):
    rows = pads.shape[1]
    lanes = iota((BLOCK, PAIR), 1)

    @pl.loop(0, rows // BLOCK)
    def _(n):
        start = pl.multiple_of(n * BLOCK, BLOCK)
        beyond = iota((BLOCK, PAIR), 0) >= length - start
        for head in range(2):
            first = (1 - head) * HEAD
            ones = jnp.where((lanes > first) & (lanes <= first + 3), 1.0, 0.0)
            pads[head, pl.ds(start, BLOCK), :] = jnp.where(
                (lanes == first) & beyond, NEGATIVE, ones
            ).astype(jnp.bfloat16)


def padded(value, pads, head, start):
    own = iota(value.shape, 1) // HEAD == head
    return jnp.where(own, value, pads[head, start : start + value.shape[0], :])


def split_low(value):
    first = value.astype(jnp.bfloat16).astype(jnp.float32)
    rest = value - first
    second = rest.astype(jnp.bfloat16).astype(jnp.float32)
    return first, second, rest - second


def with_terms(turned, head, mask_term, terms):
    place = iota(turned.shape, 0)
    first = (1 - head) * HEAD
    value = jnp.where(place // HEAD == head, turned.astype(jnp.float32), 0.0)
    value = jnp.where(place == first, mask_term, value)
    for n, term in enumerate(terms):
        value = jnp.where(place == first + 1 + n, term, value)
    return value.astype(jnp.bfloat16)


HIDDEN, DIAGONAL, NEAR, FAR = range(4)


def fill_fixed_bias(bias):
    for head in range(2):
        bias[head, HIDDEN] = jnp.full((BLOCK, BLOCK), NEGATIVE, jnp.float32)
        bias[head, FAR] = jnp.zeros((BLOCK, BLOCK), jnp.float32)


def fill_near_bias(bias, profile_ref):
    later = iota((BLOCK, BLOCK), 1) >= iota((BLOCK, BLOCK), 0)
    for head in range(2):
        profile = profile_ref[head : head + 1, :]
        near = skew(profile - profile[:, BLOCK - 1 :])
        bias[head, DIAGONAL] = jnp.where(later, near, NEGATIVE)
        bias[head, NEAR] = jnp.where(later, 0.0, near)


def bias_kind(place, block):
    return jnp.clip(place - block, -1, 2) + 1


def self_forward_pair(place, profile_ref, q_ref, k_ref, v_ref, o_ref, ot_ref, log_ref, pads, bias, s_buf, vt_buf):
    qt = q_ref[...].T
    vt_buf[...] = v_ref[...].T
    fill_near_bias(bias, profile_ref)
    blocks = k_ref.shape[0] // BLOCK
    tops = []
    for head in range(2):
        far = profile_ref[head : head + 1, BLOCK - 1 :]
        queries = with_terms(qt, head, 1.0, (far,))
        top = None
        for block in range(blocks):
            start = block * BLOCK
            keys = padded(k_ref[start : start + BLOCK, :], pads, head, start)
            scores = product(keys, queries) + bias[head, bias_kind(place, block)]
            s_buf[head, start : start + BLOCK, :] = scores
            most = jnp.max(scores, axis=0, keepdims=True)
            top = most if top is None else jnp.maximum(top, most)
        tops.append(top)
    totals = []
    for head in range(2):
        total = None
        for block in range(blocks):
            part = slice(block * BLOCK, (block + 1) * BLOCK)
            raised = jnp.exp(s_buf[head, part, :] - tops[head])
            s_buf[head, part, :] = raised
            amount = jnp.sum(raised, axis=0, keepdims=True)
            total = amount if total is None else total + amount
        totals.append(total)
    for head in range(2):
        rows = slice(head * HEAD, (head + 1) * HEAD)
        scale, mixed = 1.0 / totals[head], None
        for block in range(blocks):
            part = slice(block * BLOCK, (block + 1) * BLOCK)
            soft = (s_buf[head, part, :] * scale).astype(jnp.bfloat16)
            share = product(vt_buf[rows, part], soft)
            mixed = share if mixed is None else mixed + share
        ot_ref[rows, :] = mixed
        log_ref[head : head + 1, :] = tops[head] + jnp.log(totals[head])
    o_ref[...] = ot_ref[...].T.astype(jnp.bfloat16)


def self_forward_kernel(place_ref, profile_ref, q_ref, k_ref, v_ref, o_ref, ot_ref, log_ref, pads, bias, s_buf, vt_buf):
    @pl.when(pl.program_id(0) == 0)
    def _():
        fill_pads(pads, place_ref[1])
        fill_fixed_bias(bias)

    self_forward_pair(
        place_ref[0], profile_ref.at[0], q_ref, k_ref, v_ref, o_ref, ot_ref, log_ref.at[0],
        pads, bias, s_buf, vt_buf,
    )


def cross_forward_pair(q_ref, k_ref, v_ref, o_ref, ot_ref, log_ref):
    qt = q_ref[...].T
    vt = v_ref[...].T
    all_scores = [product(k_ref[...], head_rows(qt, head)) for head in range(2)]
    for head, scores in enumerate(all_scores):
        top = jnp.max(scores, axis=0, keepdims=True)
        raised = jnp.exp(scores - top)
        total = jnp.sum(raised, axis=0, keepdims=True)
        soft = (raised * (1.0 / total)).astype(jnp.bfloat16)
        ot_ref[head * HEAD : (head + 1) * HEAD, :] = product(vt[head * HEAD : (head + 1) * HEAD, :], soft)
        log_ref[head : head + 1, :] = top + jnp.log(total)
    o_ref[...] = ot_ref[...].T.astype(jnp.bfloat16)


def cross_forward_kernel(q_ref, k_ref, v_ref, o_ref, ot_ref, log_ref):
    cross_forward_pair(q_ref, k_ref, v_ref, o_ref, ot_ref, log_ref.at[0])


EXTRA = 16


def backward_pair(
    place, profile_ref, q_ref, k_ref, v_ref, g_ref, ot_ref, log_ref, dq_ref, dk_ref, dv_ref,
    near_ref, far_ref, pads, bias, kt_buf, grad_buf,
):
    q_value = q_ref[...]
    g_value = g_ref[...]
    qt = q_value.T
    gt = g_value.T
    kt = k_ref[...].T
    keys_count = k_ref.shape[0]
    ones = jnp.ones((EXTRA, keys_count), jnp.bfloat16)
    for head in range(2):
        kt_buf[head, 0:HEAD, 0:keys_count] = kt[head * HEAD : (head + 1) * HEAD, :]
        kt_buf[head, HEAD : HEAD + EXTRA, 0:keys_count] = ones
    both_q = jnp.concatenate([head_cols(q_value, 0), head_cols(q_value, 1)], axis=0)
    both_g = jnp.concatenate([head_cols(g_value, 0), head_cols(g_value, 1)], axis=0)
    weighted = gt.astype(jnp.float32) * ot_ref[...]
    if profile_ref is not None:
        fill_near_bias(bias, profile_ref)
    queries, grads_out = [], []
    for head in range(2):
        rows = slice(head * HEAD, (head + 1) * HEAD)
        delta = jnp.sum(weighted[rows, :], axis=0, keepdims=True)
        constant = -log_ref[head : head + 1, :]
        if profile_ref is not None:
            constant = constant + profile_ref[head : head + 1, BLOCK - 1 :]
        queries.append(with_terms(qt, head, 1.0, split_low(constant)))
        grads_out.append(with_terms(gt, head, 0.0, split_low(-delta)))
    sums = [None, None]
    for start in range(0, keys_count, BLOCK):
        k_block = k_ref[start : start + BLOCK, :]
        v_block = v_ref[start : start + BLOCK, :]
        softs, grads = [], []
        for head in range(2):
            scores = product(padded(k_block, pads, head, start), queries[head])
            if profile_ref is not None:
                scores = scores + bias[head, bias_kind(place, start // BLOCK)]
            soft = jnp.exp(scores)
            change = product(padded(v_block, pads, head, start), grads_out[head])
            grad = (soft * change).astype(jnp.bfloat16)
            softs.append(soft.astype(jnp.bfloat16))
            grads.append(grad)
            if profile_ref is not None:
                grad_buf[head, start // BLOCK] = grad
            share = product(kt_buf[head, :, start : start + BLOCK], grad)
            sums[head] = share if sums[head] is None else sums[head] + share
        dv_ref[start : start + BLOCK, :] = product(jnp.concatenate(softs, axis=1), both_g).astype(
            jnp.bfloat16
        )
        dk_ref[start : start + BLOCK, :] = product(jnp.concatenate(grads, axis=1), both_q).astype(
            jnp.bfloat16
        )
    turned = jnp.concatenate([sums[0][0:HEAD, :], sums[1][0:HEAD, :]], axis=0)
    dq_ref[...] = turned.T.astype(jnp.bfloat16)
    if profile_ref is not None:
        later = iota((BLOCK, BLOCK), 1) >= iota((BLOCK, BLOCK), 0)
        for head in range(2):
            diagonal = grad_buf[head, place].astype(jnp.float32)
            before = grad_buf[head, jnp.maximum(place - 1, 0)].astype(jnp.float32)
            before = jnp.where(place >= 1, before, 0.0)
            near = jnp.sum(unskew(jnp.where(later, diagonal, before)), axis=0, keepdims=True)
            near_ref[head : head + 1, :] = near
            far_ref[head : head + 1, :] = sums[head][HEAD : HEAD + 1, :] - near


def self_backward_kernel(
    place_ref, profile_ref, q_ref, k_ref, v_ref, g_ref, ot_ref, log_ref,
    dq_ref, dk_ref, dv_ref, near_ref, far_ref, pads, bias, kt_buf, grad_buf,
):
    @pl.when(pl.program_id(0) == 0)
    def _():
        fill_pads(pads, place_ref[1])
        fill_fixed_bias(bias)

    backward_pair(
        place_ref[0], profile_ref.at[0], q_ref, k_ref, v_ref, g_ref, ot_ref, log_ref.at[0],
        dq_ref, dk_ref, dv_ref, near_ref.at[0], far_ref.at[0], pads, bias, kt_buf, grad_buf,
    )


def cross_backward_kernel(q_ref, k_ref, v_ref, g_ref, ot_ref, log_ref, dq_ref, dk_ref, dv_ref, pads, kt_buf):
    @pl.when(pl.program_id(0) == 0)
    def _():
        fill_pads(pads, pads.shape[1])

    backward_pair(
        None, None, q_ref, k_ref, v_ref, g_ref, ot_ref, log_ref.at[0], dq_ref, dk_ref, dv_ref,
        None, None, pads, None, kt_buf, None,
    )


def forward_scratch(count, rows):
    return [
        pltpu.VMEM((2, count, PAIR), jnp.bfloat16),
        pltpu.VMEM((2, 4, BLOCK, BLOCK), jnp.float32),
        pltpu.VMEM((2, count, rows), jnp.float32),
        pltpu.VMEM((PAIR, count), jnp.bfloat16),
    ]


def backward_scratch(count):
    return [
        pltpu.VMEM((2, count, PAIR), jnp.bfloat16),
        pltpu.VMEM((2, 4, BLOCK, BLOCK), jnp.float32),
        pltpu.VMEM((2, HEAD + EXTRA, count), jnp.bfloat16),
        pltpu.VMEM((2, count // BLOCK, BLOCK, BLOCK), jnp.bfloat16),
    ]


def pair_block(rows):
    return pl.BlockSpec((rows, PAIR), lambda pair: (0, pair))


def turned_block(rows):
    return pl.BlockSpec((PAIR, rows), lambda pair: (pair, 0))


def head_block(width):
    return pl.BlockSpec((1, 2, width), lambda pair: (pair, 0, 0))


SCALARS = pl.BlockSpec(memory_space=pltpu.SMEM)
PAIRS = HEADS // 2


def shaped(shape, dtype):
    return jax.ShapeDtypeStruct(shape, dtype)


def self_forward(place, profile, queries, keys, values):
    rows, width = queries.shape
    count = keys.shape[0]
    return pl.pallas_call(
        self_forward_kernel,
        grid=(PAIRS,),
        in_specs=[SCALARS, head_block(BLOCK), pair_block(rows), pair_block(count), pair_block(count)],
        out_specs=[pair_block(rows), turned_block(rows), head_block(rows)],
        out_shape=[
            shaped((rows, width), jnp.bfloat16),
            shaped((width, rows), jnp.float32),
            shaped((PAIRS, 2, rows), jnp.float32),
        ],
        scratch_shapes=forward_scratch(count, rows),
        name="self_forward",
    )(place, profile, queries, keys, values)


def cross_forward(queries, keys, values):
    rows, width = queries.shape
    count = keys.shape[0]
    return pl.pallas_call(
        cross_forward_kernel,
        grid=(PAIRS,),
        in_specs=[pair_block(rows), pair_block(count), pair_block(count)],
        out_specs=[pair_block(rows), turned_block(rows), head_block(rows)],
        out_shape=[
            shaped((rows, width), jnp.bfloat16),
            shaped((width, rows), jnp.float32),
            shaped((PAIRS, 2, rows), jnp.float32),
        ],
        name="cross_forward",
    )(queries, keys, values)


def self_backward(place, profile, queries, keys, values, grad_mixed, mixed_turned, log_totals):
    rows, width = queries.shape
    count = keys.shape[0]
    return pl.pallas_call(
        self_backward_kernel,
        grid=(PAIRS,),
        in_specs=[
            SCALARS, head_block(BLOCK), pair_block(rows), pair_block(count), pair_block(count),
            pair_block(rows), turned_block(rows), head_block(rows),
        ],
        out_specs=[
            pair_block(rows), pair_block(count), pair_block(count), head_block(BLOCK), head_block(rows),
        ],
        out_shape=[
            shaped((rows, width), jnp.bfloat16),
            shaped((count, width), jnp.bfloat16),
            shaped((count, width), jnp.bfloat16),
            shaped((PAIRS, 2, BLOCK), jnp.float32),
            shaped((PAIRS, 2, rows), jnp.float32),
        ],
        scratch_shapes=backward_scratch(count),
        name="self_backward",
    )(place, profile, queries, keys, values, grad_mixed, mixed_turned, log_totals)


def cross_backward(queries, keys, values, grad_mixed, mixed_turned, log_totals):
    rows, width = queries.shape
    count = keys.shape[0]
    return pl.pallas_call(
        cross_backward_kernel,
        grid=(PAIRS,),
        in_specs=[
            pair_block(rows), pair_block(count), pair_block(count),
            pair_block(rows), turned_block(rows), head_block(rows),
        ],
        out_specs=[pair_block(rows), pair_block(count), pair_block(count)],
        out_shape=[
            shaped((rows, width), jnp.bfloat16),
            shaped((count, width), jnp.bfloat16),
            shaped((count, width), jnp.bfloat16),
        ],
        scratch_shapes=[
            pltpu.VMEM((2, count, PAIR), jnp.bfloat16),
            pltpu.VMEM((2, HEAD + EXTRA, count), jnp.bfloat16),
        ],
        name="cross_backward",
    )(queries, keys, values, grad_mixed, mixed_turned, log_totals)


class Peers:
    def __init__(self, planes):
        self.seq = lax.axis_index("seq")
        fsdp = lax.axis_index("fsdp")
        self.planes = planes
        self.plane = fsdp // 2
        self.core = fsdp % 2
        self.fsdp = fsdp
        self.along_x = self.seq + 1 - 2 * (self.seq % 2)
        self.along_y = (self.seq + 2) % 4
        self.corner = (self.along_x + 2) % 4
        self.partner = (self.seq, fsdp + 1 - 2 * self.core)
        self.to_x = (self.along_x, fsdp)
        self.to_y = (self.along_y, fsdp)
        self.to_corner = (self.corner, fsdp)

    def ahead(self, steps):
        return (self.plane + steps) % self.planes

    def at_plane(self, plane):
        return (self.seq, 2 * plane + self.core)

    def everyone(self):
        return [self.partner, self.to_x, self.to_y, self.to_corner] + [
            self.at_plane(self.ahead(k)) for k in range(1, self.planes)
        ]

    def greet(self):
        barrier = pltpu.get_barrier_semaphore()
        for other in self.everyone():
            pl.semaphore_signal(barrier, inc=1, device_id=other, device_id_type=MESH)

    def meet(self):
        pl.semaphore_wait(pltpu.get_barrier_semaphore(), len(self.everyone()))


def remote(source, target, send_sem, recv_sem, device):
    return pltpu.make_async_remote_copy(
        src_ref=source, dst_ref=target, send_sem=send_sem, recv_sem=recv_sem,
        device_id=device, device_id_type=MESH,
    )


class Stack:
    def __init__(self, rows, cols):
        self.rows, self.cols = rows, cols

    def own(self, ref, quarter, first=0, count=None):
        return ref.at[quarter, pl.ds(first, count or self.rows), :]

    def part(self, ref, quarter, plane, core, first=0, count=None):
        return ref.at[quarter, plane, core, pl.ds(first, count or self.rows), :]

    def planes(self, ref, quarter, core):
        return ref.at[quarter, :, core]

    def whole(self, ref, plane, core):
        return ref.at[:, plane, core]


class Wide:
    def __init__(self, rows, cols):
        self.rows, self.cols = rows, cols

    def own(self, ref, quarter, first=0, count=None):
        return ref.at[pl.ds(first, count or self.rows), pl.ds(quarter * self.cols, self.cols)]

    def part(self, ref, quarter, plane, core, first=0, count=None):
        return ref.at[
            plane, core, pl.ds(first, count or self.rows), pl.ds(quarter * self.cols, self.cols)
        ]

    def planes(self, ref, quarter, core):
        return ref.at[:, core, :, pl.ds(quarter * self.cols, self.cols)]

    def whole(self, ref, plane, core):
        return ref.at[plane, core]


class Tall:
    def __init__(self, rows, cols):
        self.rows, self.cols = rows, cols

    def own(self, ref, quarter, first=0, count=None):
        return ref.at[pl.ds(quarter * self.rows + first, count or self.rows), :]

    def part(self, ref, quarter, plane, core, first=0, count=None):
        return ref.at[plane, core, pl.ds(quarter * self.rows + first, count or self.rows), :]

    def planes(self, ref, quarter, core):
        return ref.at[:, core, pl.ds(quarter * self.rows, self.rows), :]

    def whole(self, ref, plane, core):
        return ref.at[plane, core]


def full_shapes(kinds, planes, cores=2):
    shapes = []
    for kind in kinds:
        if isinstance(kind, Stack):
            shapes.append((4, planes, cores, kind.rows, kind.cols))
        elif isinstance(kind, Wide):
            shapes.append((planes, cores, kind.rows, 4 * kind.cols))
        else:
            shapes.append((planes, cores, 4 * kind.rows, kind.cols))
    return shapes


ANYWHERE = pl.BlockSpec(memory_space=pl.ANY)
DMA = pltpu.SemaphoreType.DMA


def make_kinds(shards):
    square, wide, down = shards[0], shards[8], shards[10]
    stack = Stack(*square.shape)
    band = Wide(wide.shape[0], wide.shape[1] // 4)
    tall = Tall(down.shape[0] // 4, down.shape[1])
    return [stack, stack, band, band, tall]


def kernels_fit(shards):
    kinds = make_kinds(shards)
    return (
        lax.axis_size("seq") == 4
        and lax.axis_size("fsdp") == 8
        and all(kind.rows % 32 == 0 and kind.cols % 128 == 0 for kind in kinds)
    )


def gather_plain(shards, tokens, encoded):
    full = [lax.all_gather(shard, "fsdp", axis=0, tiled=True) for shard in shards]
    return (
        full,
        lax.all_gather(tokens, "seq", axis=0, tiled=True),
        lax.all_gather(encoded, "seq", axis=0, tiled=True),
    )


def add_low(target, *terms):
    total = target[...]
    for term in terms:
        total = total + term[...]
    target[...] = total


def reduce_plain(grads, token_part, enc_part, small):
    def sums(value):
        return lax.psum_scatter(value.astype(jnp.float32), "seq", scatter_dimension=0, tiled=True)

    reduced = [
        lax.psum(
            lax.psum_scatter(grad.astype(jnp.float32), "fsdp", scatter_dimension=0, tiled=True), "seq"
        )
        for grad in grads
    ]
    return reduced, sums(token_part), sums(enc_part), lax.psum(small, ("seq", "fsdp"))


def columns(pair):
    return pl.ds(pl.multiple_of(pair * PAIR, PAIR), PAIR)


def row_steps(count, step):
    def run(body):
        @pl.loop(0, count // step)
        def _(n):
            body(pl.ds(pl.multiple_of(n * step, step), step))

    return run


def weight_grad(out, left, right):
    @row_steps(out.shape[0], 384)
    def _(part):
        out[part, :] = inner_rows(left[:, part], right[...]).astype(jnp.bfloat16)


def weight_grad_turned(out, turned, right):
    @row_steps(out.shape[0], 384)
    def _(part):
        out[part, :] = product(turned[part, :].astype(jnp.bfloat16), right[...]).astype(jnp.bfloat16)


def norm_back_rows(values, gain, grad_normed):
    scale = lax.rsqrt(jnp.mean(values * values, axis=-1, keepdims=True) + EPSILON)
    scaled = grad_normed * gain
    along = jnp.mean(values * scaled, axis=-1, keepdims=True)
    grad_values = scale * scaled - values * (scale * scale * scale) * along
    return grad_values, jnp.sum(grad_normed * values * scale, axis=0, keepdims=True)


class Space:
    def __init__(self, layout, refs):
        refs = list(refs)
        for name, count in layout.items():
            value = refs.pop(0) if count is None else [refs.pop(0) for _ in range(count)]
            setattr(self, name, value)


def flatten(*tables):
    layout, flat = {}, []
    for table in tables:
        for name, value in table.items():
            many = isinstance(value, list)
            layout[name] = len(value) if many else None
            flat += value if many else [value]
    return layout, flat


class StackRows(Stack):
    def __init__(self, first, rows, cols):
        super().__init__(rows, cols)
        self.first = first

    def planes(self, ref, quarter, core):
        return ref.at[quarter, :, core, pl.ds(self.first, self.rows), :]


DOWN, GATE, UP, CROSS, SELF, SELF_REST = range(6)
GROUPS = 6


class Sum:
    planes_first = False

    def __init__(self, g, kind, here, r, part):
        self.g, self.kind, self.here, self.r = g, kind, here, r
        self.part = part
        self.planes = here.planes
        self.sums, self.final = r.sums[g], r.final[g]
        self.side_x, self.side_y, self.last, self.from_z = r.side_x[g], r.side_y[g], r.last[g], r.from_z[g]
        self.started = []

    def send(self, make):
        remote(*make()).start()
        self.started.append(make)

    def arrived(self, target, recv_sem):
        pltpu.make_async_copy(target, target, recv_sem).wait()

    def pair_source(self, n, core):
        return self.kind.planes(self.part, n, core), self.sums.at[n]

    def start_pair(self, n):
        r, g = self.r, self.g
        source, target = self.pair_source(n, 1 - self.here.core)
        remote(source, target, r.c_send.at[g, n], r.c_recv.at[g, n], self.here.partner).start()

    def pair_part(self, n):
        source, target = self.pair_source(n, self.here.core)
        self.arrived(target, self.r.c_recv.at[self.g, n])

        @pl.loop(0, 4)
        def _(m):
            add_low(target.at[m], source.at[m])

        self.send_part(n)

    def pair_sum(self):
        @pl.loop(0, 4)
        def _(n):
            self.pair_part(n)

        self.sent_parts()

    def parts_sends(self):
        r, g, here = self.r, self.g, self.here
        for n, quarter in enumerate((here.along_x, here.corner)):
            yield quarter, lambda n=n, quarter=quarter: (
                self.half(quarter, 0), self.side_x.at[n], r.a_send.at[g, n], r.a_recv.at[g, n], here.to_x
            )
        for n, quarter in enumerate((here.along_y, here.corner)):
            yield quarter, lambda n=n, quarter=quarter: (
                self.half(quarter, 1), self.side_y.at[n], r.a_send.at[g, 2 + n], r.a_recv.at[g, 2 + n], here.to_y
            )

    def send_part(self, n):
        for part, make in self.parts_sends():

            @pl.when(n == part)
            def _(make=make):
                remote(*make()).start()

    def sent_parts(self):
        self.started += [make for _, make in self.parts_sends()]

    def pair_sent(self):
        for n in range(4):
            source, target = self.pair_source(n, 1 - self.here.core)
            remote(
                source, target, self.r.c_send.at[self.g, n], self.r.c_recv.at[self.g, n], self.here.partner
            ).wait_send()

    def half(self, quarter, second):
        size = self.planes // 2
        return self.sums.at[quarter, pl.ds(second * size, size)]

    def sides(self):
        for _, make in Sum.parts_sends(self):
            self.send(make)

    def add_half(self, quarter, second, terms, out=None):
        size = self.planes // 2

        @pl.loop(0, size)
        def _(z):
            add_low(self.sums.at[quarter, second * size + z], *[term.at[z] for term in terms])

    def first_side(self):
        r, g, here = self.r, self.g, self.here
        for n in range(2):
            self.arrived(self.side_x.at[n], r.a_recv.at[g, n])
            self.arrived(self.side_y.at[n], r.a_recv.at[g, 2 + n])
        self.add_half(here.along_y, 0, [self.side_x.at[1]])
        self.add_half(here.along_x, 1, [self.side_y.at[1]])
        for n, (quarter, device) in enumerate(((here.along_y, here.to_y), (here.along_x, here.to_x))):
            self.send(
                lambda n=n, quarter=quarter, device=device: (
                    self.half(quarter, n), self.last.at[n], r.b_send.at[g, n], r.b_recv.at[g, n], device
                )
            )

    def second_side(self):
        r, g, here = self.r, self.g, self.here
        for n in range(2):
            self.arrived(self.last.at[n], r.b_recv.at[g, n])
        self.add_half(here.seq, 0, [self.side_x.at[0], self.last.at[0]])
        self.add_half(here.seq, 1, [self.side_y.at[0], self.last.at[1]])
        self.after_square()

    def after_square(self):
        self.start_planes()

    def plane_share(self, plane):
        return self.sums.at[self.here.seq, plane]

    def plane_sends(self):
        r, g, here = self.r, self.g, self.here
        for k in range(1, self.planes):
            yield here.ahead(k), lambda k=k: (
                self.plane_share(here.ahead(k)), self.from_z.at[k - 1],
                r.z_send.at[g, k - 1], r.z_recv.at[g, k - 1], here.at_plane(here.ahead(k)),
            )

    def start_planes(self):
        for _, make in self.plane_sends():
            self.send(make)

    def along_planes(self):
        r, g, here = self.r, self.g, self.here
        for k in range(1, self.planes):
            self.arrived(self.from_z.at[k - 1], r.z_recv.at[g, k - 1])
        step = 16

        @pl.loop(0, self.kind.rows // step)
        def _(n):
            rows = pl.ds(pl.multiple_of(n * step, step), step)
            total = self.sums[here.seq, here.plane, rows, :].astype(jnp.float32)
            for k in range(1, self.planes):
                total = total + self.from_z[k - 1, rows, :].astype(jnp.float32)
            self.final[here.seq, rows, :] = total.astype(jnp.bfloat16)

        self.start_spread()

    def start_spread(self):
        r, g, here = self.r, self.g, self.here
        for n, device in enumerate((here.to_x, here.to_y)):
            self.send(
                lambda n=n, device=device: (
                    self.final.at[here.seq], self.final.at[here.seq], r.g_send.at[g, n], r.g_recv.at[g, n], device
                )
            )

    def across(self, quarter, second):
        size = self.kind.cols // 2
        return self.final.at[quarter, :, pl.ds(second * size, size)]

    def spread(self):
        r, g, here = self.r, self.g, self.here
        for n, (quarter, device) in enumerate(((here.along_x, here.to_y), (here.along_y, here.to_x))):
            self.arrived(self.final.at[quarter], r.g_recv.at[g, n])
            self.send(
                lambda n=n, quarter=quarter, device=device: (
                    self.across(quarter, n), self.across(quarter, n),
                    r.g_send.at[g, 2 + n], r.g_recv.at[g, 2 + n], device,
                )
            )

    def out_copies(self):
        r, g, kind = self.r, self.g, self.kind
        if isinstance(kind, Wide):
            return [
                pltpu.make_async_copy(
                    self.final.at[q], r.out[g].at[:, pl.ds(q * kind.cols, kind.cols)], r.out_sem.at[g, q]
                )
                for q in range(4)
            ]
        out = r.out[min(g, SELF)]
        if isinstance(kind, StackRows):
            out = out.at[:, pl.ds(kind.first, kind.rows), :]
        return [pltpu.make_async_copy(self.final, out, r.out_sem.at[g, 0])]

    def finish(self):
        r, g, here = self.r, self.g, self.here
        for n in range(2):
            self.arrived(self.across(here.corner, n), r.g_recv.at[g, 2 + n])
        for copy in self.out_copies():
            copy.start()

    def end(self):
        for copy in self.out_copies():
            copy.wait()
        if self.g not in (DOWN, CROSS):
            self.pair_sent()
        for make in self.started:
            remote(*make()).wait_send()


class PlanesFirst(Sum):
    planes_first = True

    def pair_source(self, n, core):
        return self.part.at[n, core], self.sums.at[:, n]

    def half(self, quarter, second):
        size = self.kind.cols // 2
        return self.sums.at[quarter, self.here.plane, :, pl.ds(second * size, size)]

    def plane_share(self, plane):
        return self.sums.at[:, plane]

    def parts_sends(self):
        return self.plane_sends()

    def along_planes(self):
        r, g, here = self.r, self.g, self.here
        for k in range(1, self.planes):
            self.arrived(self.from_z.at[k - 1], r.z_recv.at[g, k - 1])

        @pl.loop(0, 4)
        def _(q):
            add_low(self.sums.at[q, here.plane], *[self.from_z.at[k - 1, q] for k in range(1, self.planes)])

        self.sides()

    def add_half(self, quarter, second, terms, out=None):
        size = self.kind.cols // 2
        add_low(self.half(quarter, second), *terms)

    def after_square(self):
        self.final[self.here.seq] = self.sums[self.here.seq, self.here.plane]
        self.start_spread()


class BandSum(Sum):
    def pair_source(self, n, core):
        return self.part.at[n, :, core], self.sums.at[n]


class RowSum(Sum):
    def __init__(self, g, here, r, source, n):
        self.g, self.here, self.r, self.source = g, here, r, source
        self.size, self.cols = source.shape[0] // 4, source.shape[1] // 2
        self.side_x, self.side_y, self.last = r.row_x[n], r.row_y[n], r.row_last[n]
        self.started = []

    def half(self, quarter, second):
        return self.source.at[pl.ds(quarter * self.size, self.size), pl.ds(second * self.cols, self.cols)]

    def add_half(self, quarter, second, terms):
        @row_steps(self.size, 64)
        def _(part):
            add_low(self.half(quarter, second).at[part, :], *[term.at[part, :] for term in terms])

    def total(self, keep):
        r, g, here = self.r, self.g, self.here
        for n in range(2):
            self.arrived(self.last.at[n], r.b_recv.at[g, n])
        step = 64

        @row_steps(self.size, step)
        def _(part):
            halves = []
            for second, side in enumerate((self.side_x, self.side_y)):
                value = self.half(here.seq, second)[part, :].astype(jnp.float32)
                halves.append(
                    value + side[0, part, :].astype(jnp.float32) + self.last[second, part, :].astype(jnp.float32)
                )
            keep(part, jnp.concatenate(halves, axis=1))

    def sent(self):
        for make in self.started:
            remote(*make()).wait_send()


GELU_SCALE = math.sqrt(2.0 / math.pi)
GELU_CUBE = 0.044715
TOKENS, ENCODED = GROUPS, GROUPS + 1


def backward_kernel(kinds, planes, layout, *refs):
    r = Space(layout, refs)
    bf16, f32 = jnp.bfloat16, jnp.float32
    here = Peers(planes)
    place, length = here.seq, r.length[0]
    rows, width = r.grad_two.shape
    count, enc_count = r.rows_both.shape[0] // 2, r.ckeys_in.shape[0]
    owner_rows = width // (2 * planes)
    shape = (4, planes, 2, owner_rows, width)
    band = kinds[GATE].cols
    band_shape = (4, planes, 2, owner_rows, band)
    tall_shape = (planes, 2, 4, kinds[DOWN].rows, width)
    keys, values = r.rows_both.at[pl.ds(0, count), :], r.rows_both.at[pl.ds(count, count), :]
    down = PlanesFirst(DOWN, kinds[DOWN], here, r, r.rows_both.reshape(*tall_shape))
    gate = BandSum(GATE, kinds[GATE], here, r, r.grad_gate.reshape(*band_shape))
    up = BandSum(UP, kinds[UP], here, r, r.grad_up.reshape(*band_shape))
    cross = Sum(CROSS, kinds[CROSS], here, r, r.grad_cross.reshape(*shape))
    self_one = Sum(SELF, kinds[SELF], here, r, r.grad_self.reshape(*shape))
    self_two = Sum(SELF_REST, kinds[SELF_REST], here, r, r.grad_self.reshape(*shape))
    sums = (down, gate, up, cross, self_one, self_two)
    others = []

    ckeys, cvalues = r.dk.at[pl.ds(0, enc_count), :], r.dk.at[pl.ds(enc_count, enc_count), :]
    dck, dcv = r.dv.at[pl.ds(0, enc_count), :], r.dv.at[pl.ds(enc_count, enc_count), :]
    enc_all = r.token_part.at[pl.ds(0, enc_count), :]
    enc_part = r.token_part.at[pl.ds(enc_count, enc_count), :]
    token_sum = RowSum(TOKENS, here, r, r.token_part, 0)
    enc_sum = RowSum(ENCODED, here, r, enc_part, 1)
    act, d_gate, d_up = (r.token_part.at[pl.ds(n * rows, rows), pl.ds(0, band)] for n in range(3))

    def send(make):
        remote(*make()).start()
        others.append(make)

    def arrived(target, recv_sem):
        pltpu.make_async_copy(target, target, recv_sem).wait()

    def load(n, source, target):
        copy = pltpu.make_async_copy(source, target, r.load_sem.at[n])
        copy.start()
        return copy

    def ffn_copies(n):
        slot, part = n % 2, pl.ds(pl.multiple_of(n * band, band), band)
        return [
            pltpu.make_async_copy(r.w_gate.at[:, part], r.grad_self.at[slot, :, pl.ds(0, band)], r.f_sem.at[0, slot]),
            pltpu.make_async_copy(r.w_up.at[:, part], r.grad_self.at[2 + slot, :, pl.ds(0, band)], r.f_sem.at[1, slot]),
            pltpu.make_async_copy(r.w_down.at[part, :], r.grad_cross.at[slot, pl.ds(0, band), :], r.f_sem.at[2, slot]),
        ]

    def start_ffn(n):
        for copy in ffn_copies(n):
            copy.start()

    here.greet()
    cotangent_load = load(0, r.cotangent, r.grad_mixed)
    normed_three_load = load(6, r.normed_three_in, r.normed)
    start_ffn(0)
    start_ffn(1)
    hidden_two_load = load(11, r.hidden_two_in, r.hidden)
    mixed_load = load(2, r.mixed_cross_in, r.mixed)
    cqueries_load = load(3, r.cqueries_in, r.queries)
    ckeys_load = load(4, r.ckeys_in, ckeys)
    cvalues_load = load(5, r.cvalues_in, cvalues)

    def grad_result(part, step):
        slots = place * rows + part.start + iota((step, 1), 0)
        return jnp.where(slots < length, r.grad_mixed[part, :].astype(f32), 0.0)

    cotangent_load.wait()

    @row_steps(rows, 64)
    def _(part):
        r.branch[part, :] = grad_result(part, 64).astype(bf16)

    normed_three_load.wait()

    @pl.loop(0, 4)
    def _(n):
        slot = n % 2
        for copy in ffn_copies(n):
            copy.wait()
        normed = r.normed[...]
        branch = r.branch[...]
        w_gate = r.grad_self[slot, :, 0:band]
        w_up = r.grad_self[2 + slot, :, 0:band]
        w_down = r.grad_cross[slot, 0:band, :]
        gate_band = product(normed, w_gate)
        up_band = product(normed, w_up)
        inner = jnp.tanh(GELU_SCALE * (gate_band + GELU_CUBE * (gate_band * gate_band * gate_band)))
        lifted = 0.5 * (1.0 + inner)
        gelu = gate_band * lifted
        slope = lifted + (0.5 * GELU_SCALE) * gate_band * (1.0 - inner * inner) * (
            1.0 + (3.0 * GELU_CUBE) * (gate_band * gate_band)
        )
        act[...] = (gelu * up_band).astype(bf16)
        grad_act = outer_rows(branch, w_down)
        d_gate[...] = (grad_act * up_band * slope).astype(bf16)
        d_up[...] = (grad_act * gelu).astype(bf16)
        first = pl.ds(pl.multiple_of(n * band, band), band)
        r.rows_both[first, :] = inner_rows(act[...], branch).astype(bf16)
        r.grad_gate[n] = inner_rows(normed, d_gate[...]).astype(bf16)
        r.grad_up[n] = inner_rows(normed, d_up[...]).astype(bf16)

        @pl.when(n == 0)
        def _():
            here.meet()

        down.start_pair(n)
        gate.start_pair(n)
        up.start_pair(n)
        out = product(act[...], w_down)
        gy = outer_rows(d_gate[...], w_gate) + outer_rows(d_up[...], w_up)

        @pl.when(n == 0)
        def _():
            r.grad_two[...] = out
            r.gy[...] = gy

        @pl.when(n > 0)
        def _():
            r.grad_two[...] += out
            r.gy[...] += gy

        @pl.when(n < 2)
        def _():
            start_ffn(n + 2)

        @pl.when(n > 0)
        def _():
            for group in (down, gate, up):
                group.pair_part(n - 1)

    w_cout_load = load(1, r.w_two.at[3], r.grad_self.at[3])
    w_two_loads = [load(8 + m, r.w_two.at[m], r.grad_self.at[m]) for m in range(3)]
    encoded_load = load(7, r.enc_in, enc_all)
    hidden_two_load.wait()
    r.small[...] = jnp.zeros_like(r.small)

    @row_steps(rows, 64)
    def _(part):
        hidden = r.hidden[part, :]
        slots = place * rows + part.start + iota((64, 1), 0)
        r.dq[part, :] = jnp.where(slots < length, hidden + r.grad_two[part, :], 0.0).astype(bf16)
        grad, gain = norm_back_rows(hidden, r.gains[:, 2 * width : 3 * width], r.gy[part, :])
        total = grad_result(part, 64) + grad
        r.grad_two[part, :] = total
        r.branch[part, :] = total.astype(bf16)
        r.small[2:3, :] += gain

    result_copy = load(13, r.dq, r.layer_out)
    normed_two_load = load(6, r.normed_two_in, r.normed)
    hidden_load = load(11, r.hidden_one_in, r.hidden)
    fill_pads(r.pads, count)
    fill_fixed_bias(r.bias)
    for group in (down, gate, up):
        group.pair_part(3)
        group.sent_parts()
    w_cout_load.wait()
    r.grad_mixed[...] = outer_rows(r.branch[...], r.grad_self[3]).astype(bf16)
    w_sout_load = load(12, r.w_one.at[3], r.grad_self.at[3])
    mixed_load.wait()
    weight_grad_turned(r.grad_cross.at[3], r.mixed, r.branch)
    for copy in (cqueries_load, ckeys_load, cvalues_load):
        copy.wait()
    result_copy.wait()
    down.pair_sent()
    keys_load = load(13, r.keys_in, keys)
    values_load = load(14, r.values_in, values)

    def stepped(table, pair):
        for when, steps in table.items():

            @pl.when(pair == when)
            def _(steps=steps):
                for step in steps:
                    step()

    @pl.loop(0, PAIRS)
    def _(pair):
        part = columns(pair)
        backward_pair(
            None, None, r.queries.at[:, part], ckeys.at[:, part], cvalues.at[:, part],
            r.grad_mixed.at[:, part], r.mixed.at[part, :], r.log_cross.at[pair],
            r.dq.at[:, part], dck.at[:, part], dcv.at[:, part], None, None, r.pads, None, r.kt_buf, None,
        )

    fill_pads(r.pads, length)
    mixed_self_load = load(15, r.mixed_self_in, r.mixed)
    queries_load = load(16, r.queries_in, r.queries)
    w_two_loads[0].wait()
    r.gy[...] = outer_rows(r.dq[...], r.grad_self[0])
    normed_two_load.wait()
    weight_grad(r.grad_cross.at[0], r.normed, r.dq)
    gate.first_side()
    encoded_load.wait()
    weight_grad(r.grad_cross.at[1], enc_all, dck)
    weight_grad(r.grad_cross.at[2], enc_all, dcv)
    for n in range(4):
        cross.start_pair(n)
    w_two_loads[1].wait()
    w_two_loads[2].wait()
    enc_part[...] = (outer_rows(dck[...], r.grad_self[1]) + outer_rows(dcv[...], r.grad_self[2])).astype(bf16)
    quarters = ((here.along_x, here.to_x), (here.along_y, here.to_y), (here.corner, here.to_corner))

    def own_rows(ref, size, part, step):
        return ref[pl.ds(pl.multiple_of(place * size + part.start, step), step), :].astype(f32)

    enc_sum.sides()
    hidden_load.wait()

    @row_steps(rows, 64)
    def _(part):
        grad, gain = norm_back_rows(r.hidden[part, :], r.gains[:, 1 * width : 2 * width], r.gy[part, :])
        total = r.grad_two[part, :] + grad
        r.grad_two[part, :] = total
        r.branch[part, :] = total.astype(bf16)
        r.small[1:2, :] += gain

    w_sout_load.wait()
    r.grad_mixed[...] = outer_rows(r.branch[...], r.grad_self[3]).astype(bf16)
    mixed_self_load.wait()
    weight_grad_turned(r.grad_self.at[3], r.mixed, r.branch)
    for copy in (queries_load, keys_load, values_load):
        copy.wait()

    def keep_enc(part, total):
        r.enc_total[part, :] = total

    def enc_done():
        enc_sum.total(keep_enc)
        pltpu.make_async_copy(r.enc_total, r.enc_sum, r.load_sem.at[20]).start()

    def cross_sides():
        cross.pair_sum()

    def load_normed():
        enc_sum.sent()
        pltpu.make_async_copy(r.normed_all_in, r.token_part, r.load_sem.at[21]).start()

    def w_one_copies():
        return [
            pltpu.make_async_copy(r.w_one.at[m], r.grad_cross.at[m], r.load_sem.at[17 + m]) for m in range(3)
        ]

    def load_w_one():
        cross.pair_sent()
        for copy in w_one_copies():
            copy.start()

    self_steps = {
        0: [up.first_side, cross_sides],
        1: [enc_sum.first_side],
        2: [gate.second_side],
        3: [enc_done, load_normed, down.along_planes, up.second_side],
        4: [down.first_side, load_w_one],
        5: [cross.first_side],
    }

    @pl.loop(0, PAIRS)
    def _(pair):
        part = columns(pair)
        backward_pair(
            place, r.profile.at[pair], r.queries.at[:, part], keys.at[:, part],
            values.at[:, part], r.grad_mixed.at[:, part], r.mixed.at[part, :],
            r.log_self.at[pair], r.dq.at[:, part], r.dk.at[:, part], r.dv.at[:, part],
            r.near.at[pair], r.far.at[pair], r.pads, r.bias, r.kt_buf, r.grad_buf,
        )
        stepped(self_steps, pair)

    tokens_load = load(22, r.tokens_all_in, keys)
    pltpu.make_async_copy(r.normed_all_in, r.token_part, r.load_sem.at[21]).wait()
    own = pl.ds(pl.multiple_of(place * rows, BLOCK), rows)
    weight_grad(r.grad_self.at[0], r.token_part.at[own, :], r.dq)
    weight_grad(r.grad_self.at[1], r.token_part, r.dk)
    weight_grad(r.grad_self.at[2], r.token_part, r.dv)
    for n in range(4):
        self_one.start_pair(n)
    for n in range(4):
        self_two.start_pair(n)
    for copy in w_one_copies():
        copy.wait()

    @row_steps(count, 512)
    def _(part):
        total = outer_rows(r.dk[part, :], r.grad_cross[1]) + outer_rows(r.dv[part, :], r.grad_cross[2])
        r.token_part[part, :] = total.astype(bf16)

    self_one.pair_sum()
    self_two.pair_sum()
    gate.along_planes()
    down.second_side()
    cross.second_side()
    r.gy[...] = outer_rows(r.dq[...], r.grad_cross[0])
    up.along_planes()
    tokens_load.wait()

    @row_steps(count, 64)
    def _(part):
        values = keys[part, :].astype(f32)
        scale = lax.rsqrt(jnp.mean(values * values, axis=-1, keepdims=True) + EPSILON)
        grad = r.token_part[part, :].astype(f32)
        r.small[0:1, :] += jnp.sum(grad * values * scale, axis=0, keepdims=True)

    @row_steps(rows, 64)
    def _(part):
        values = own_rows(keys, rows, part, 64)
        scale = lax.rsqrt(jnp.mean(values * values, axis=-1, keepdims=True) + EPSILON)
        r.small[0:1, :] += jnp.sum(r.gy[part, :] * values * scale, axis=0, keepdims=True)

    for pair in range(PAIRS):
        table = jnp.dot(
            r.near[pair], r.one_hot[...], precision=lax.Precision.HIGHEST, preferred_element_type=f32
        )
        last_bucket = iota(table.shape, 1) == BUCKETS - 1
        table = table + jnp.where(last_bucket, jnp.sum(r.far[pair], axis=1, keepdims=True), 0.0)
        r.small[8 + 2 * pair : 10 + 2 * pair, 0 : table.shape[1]] = table

    small, small_core, small_seq, small_plane = r.small, r.small_core, r.small_seq, r.small_plane
    send(lambda: (small, small_core, r.s_send.at[0], r.s_recv.at[0], here.partner))
    down.spread()
    gate.spread()
    self_one.first_side()
    arrived(small_core, r.s_recv.at[0])
    small_seq[place] = small[...] + small_core[...]
    for k, (_, device) in enumerate(quarters):
        send(
            lambda k=k, device=device: (
                small_seq.at[place], small_seq.at[place], r.s_send.at[1 + k], r.s_recv.at[1 + k], device
            )
        )
    down.finish()
    self_two.first_side()
    token_sum.sides()
    cross.along_planes()
    up.spread()
    self_one.second_side()
    for k, (quarter, _) in enumerate(quarters):
        arrived(small_seq.at[quarter], r.s_recv.at[1 + k])
    small_plane[here.plane] = (small_seq[0] + small_seq[1]) + (small_seq[2] + small_seq[3])
    for k in range(1, planes):
        send(
            lambda k=k: (
                small_plane.at[here.plane], small_plane.at[here.plane],
                r.s_send.at[3 + k], r.s_recv.at[3 + k], here.at_plane(here.ahead(k)),
            )
        )
    gate.finish()
    self_two.second_side()
    token_sum.first_side()
    cross.spread()
    up.finish()
    self_one.along_planes()
    cross.finish()

    def keep_tokens(part, total):
        values = own_rows(keys, rows, part, 64)
        grad, _ = norm_back_rows(values, r.gains[:, 0 * width : 1 * width], r.gy[part, :] + total)
        r.hidden[part, :] = r.grad_two[part, :] + grad

    token_sum.total(keep_tokens)
    token_copy = pltpu.make_async_copy(r.hidden, r.grad_tokens, r.load_sem.at[23])
    token_copy.start()
    for k in range(1, planes):
        arrived(small_plane.at[here.ahead(planes - k)], r.s_recv.at[3 + k])
    total = small_plane[0]
    for k in range(1, planes):
        total = total + small_plane[k]
    r.small_out[...] = total
    self_two.along_planes()
    self_one.spread()
    self_one.finish()
    self_two.spread()
    self_two.finish()
    token_copy.wait()
    pltpu.make_async_copy(r.enc_total, r.enc_sum, r.load_sem.at[20]).wait()
    for group in sums:
        group.end()
    token_sum.sent()
    for make in others:
        remote(*make()).wait_send()


def backward_fused(shards, length, small, large):
    stack, _, band, _, tall = make_kinds(shards)
    planes = lax.axis_size("fsdp") // 2
    lower = planes // 2
    first_rows = stack.rows // 2
    parts = [StackRows(n * first_rows, first_rows, stack.cols) for n in range(2)]
    kinds = [tall, band, band, stack, *parts]
    f32, low = jnp.float32, jnp.bfloat16
    rows, width = large["cotangent"].shape
    count, enc_count = large["keys_in"].shape[0], large["ckeys_in"].shape[0]
    in_vmem = pl.BlockSpec(memory_space=pltpu.VMEM)
    in_layout, operands = flatten(dict(length=length), small, large)
    in_specs = [SCALARS] + [in_vmem] * len(small)
    in_specs += [ANYWHERE] * (len(operands) - len(in_specs))
    small_shape = (24, width)

    def chunk(kind, *lead):
        return pltpu.VMEM(lead + (kind.rows, kind.cols), low)

    results = dict(
        out=[
            shaped((kind.rows, 4 * kind.cols) if isinstance(kind, Wide) else (4, kind.rows, kind.cols), low)
            for kind in (tall, band, band, stack, stack)
        ],
        layer_out=shaped((rows, width), low),
        grad_tokens=shaped((rows, width), f32),
        enc_sum=shaped((enc_count // 4, width), f32),
        small_out=shaped(small_shape, f32),
    )
    out_layout, out_shapes = flatten(results)
    square = (width, width)
    all_rows = pltpu.VMEM((count, width), low)
    some_rows = pltpu.VMEM((rows, width), low)
    wide_rows = pltpu.VMEM((rows, width), f32)
    half_tall = pltpu.VMEM((2, tall.rows, tall.cols // 2), low)
    later = kinds[1:]
    sides = [half_tall] + [chunk(kind, 2, lower) for kind in later]
    row_sides = [pltpu.VMEM((2, size, width // 2), low) for size in (rows, enc_count // 4)]
    buffers = backward_scratch(count)
    scratch = dict(
        sums=[chunk(kind, 4, planes) for kind in kinds],
        side_x=sides, side_y=sides, last=sides,
        from_z=[chunk(tall, planes - 1, 4)] + [chunk(kind, planes - 1) for kind in later],
        final=[chunk(kind, 4) for kind in kinds],
        grad_gate=pltpu.VMEM((4, width, band.cols), low),
        grad_up=pltpu.VMEM((4, width, band.cols), low),
        grad_cross=pltpu.VMEM((4,) + square, low),
        grad_self=pltpu.VMEM((4,) + square, low),
        rows_both=pltpu.VMEM((2 * count, width), low),
        dk=all_rows, dv=all_rows, token_part=all_rows,
        queries=some_rows, normed=some_rows, branch=some_rows, grad_mixed=some_rows, dq=some_rows,
        grad_two=wide_rows, hidden=wide_rows, gy=wide_rows,
        mixed=pltpu.VMEM((width, rows), f32),
        enc_total=pltpu.VMEM((enc_count // 4, width), f32),
        row_x=row_sides, row_y=row_sides, row_last=row_sides,
        pads=buffers[0], bias=buffers[1], kt_buf=buffers[2], grad_buf=buffers[3],
        near=pltpu.VMEM((PAIRS, 2, BLOCK), f32),
        far=pltpu.VMEM((PAIRS, 2, rows), f32),
        small=pltpu.VMEM(small_shape, f32),
        small_core=pltpu.VMEM(small_shape, f32),
        small_seq=pltpu.VMEM((4,) + small_shape, f32),
        small_plane=pltpu.VMEM((planes,) + small_shape, f32),
        f_sem=DMA((3, 2)),
        c_send=DMA((GROUPS, 4)), c_recv=DMA((GROUPS, 4)),
        a_send=DMA((GROUPS + 2, 4)), a_recv=DMA((GROUPS + 2, 4)),
        b_send=DMA((GROUPS + 2, 2)), b_recv=DMA((GROUPS + 2, 2)),
        z_send=DMA((GROUPS, planes - 1)), z_recv=DMA((GROUPS, planes - 1)),
        g_send=DMA((GROUPS, 4)), g_recv=DMA((GROUPS, 4)),
        s_send=DMA((3 + planes,)), s_recv=DMA((3 + planes,)),
        out_sem=DMA((GROUPS, 4)), load_sem=DMA((24,)),
    )
    scratch_layout, scratch_shapes = flatten(scratch)
    outs = pl.pallas_call(
        functools.partial(backward_kernel, kinds, planes, in_layout | out_layout | scratch_layout),
        in_specs=in_specs,
        out_specs=[ANYWHERE] * (len(out_shapes) - 1) + [in_vmem],
        out_shape=out_shapes,
        scratch_shapes=scratch_shapes,
        compiler_params=pltpu.CompilerParams(
            collective_id=1, has_side_effects=True, vmem_limit_bytes=67_000_000
        ),
        name="backward_fused",
    )(*operands)
    got = Space(out_layout, outs)
    grads = [got.out[SELF][m] for m in range(4)] + [got.out[CROSS][m] for m in range(4)]
    grads += [got.out[GATE], got.out[UP], got.out[DOWN].reshape(-1, width)]
    return got.layer_out, [grad.astype(f32) for grad in grads], got.grad_tokens, got.enc_sum, got.small_out


ONE, TWO, GATE_IN, UP_IN, DOWN_IN = range(5)


class Gathering:
    def __init__(self, kinds, here, r):
        self.kinds, self.here, self.r = kinds, here, r
        self.planes = here.planes
        shape = (4, here.planes, 2, kinds[ONE].rows, kinds[ONE].cols)
        self.full = [r.weights_one.reshape(*shape), r.weights_two.reshape(*shape), *r.ffn_full]
        self.shards = [r.shards[0:4], r.shards[4:8], r.shards[8], r.shards[9], r.shards[10]]
        self.started = []

    def send(self, make):
        remote(*make()).start()
        self.started.append(make)

    def arrived(self, target, recv_sem):
        pltpu.make_async_copy(target, target, recv_sem).wait()

    def plane_copy(self, g, k, source):
        here, r = self.here, self.r
        return remote(
            source, self.kinds[g].part(self.full[g], here.seq, here.plane, here.core),
            r.z_send.at[g, k - 1], r.z_recv.at[g, k - 1], here.at_plane(here.ahead(k)),
        )

    def start_planes(self, g):
        for k in range(1, self.planes):
            if g <= TWO:
                for m in range(4):

                    @pl.when(self.here.seq == m)
                    def _(m=m, k=k):
                        self.plane_copy(g, k, self.shards[g][m]).start()

            else:
                self.plane_copy(g, k, self.kinds[g].own(self.shards[g], self.here.seq)).start()

    def own_copies(self, g):
        here, r, full = self.here, self.r, self.full[g]
        if g <= TWO:
            return [
                pltpu.make_async_copy(
                    self.shards[g][m], full.at[m, here.plane, here.core], r.own_sem.at[g, m]
                )
                for m in range(4)
            ]
        return [
            pltpu.make_async_copy(
                self.shards[g], self.kinds[g].whole(full, here.plane, here.core), r.own_sem.at[g, 0]
            )
        ]

    def start_own(self, g):
        here, r, full = self.here, self.r, self.full[g]
        for copy in self.own_copies(g):
            copy.start()
        if g <= TWO:
            for m in range(4):
                self.send(
                    lambda m=m: (
                        self.shards[g][m], full.at[m, here.plane, here.core],
                        r.p_send.at[g, m], r.p_recv.at[g, m], here.partner,
                    )
                )
        else:
            self.send(
                lambda: (
                    self.shards[g], self.kinds[g].whole(full, here.plane, here.core),
                    r.p_send.at[g, 0], r.p_recv.at[g, 0], here.partner,
                )
            )

    def chunk(self, g, quarter, k, first=0, count=None):
        here = self.here
        return self.kinds[g].part(self.full[g], quarter, here.ahead(self.planes - k), here.core, first, count)

    def from_plane(self, g):
        here, r = self.here, self.r
        for k in range(1, self.planes):
            self.arrived(self.chunk(g, here.seq, k), r.z_recv.at[g, k - 1])
            for n, device in enumerate((here.to_x, here.to_y)):

                def make(k=k, n=n, device=device):
                    chunk = self.chunk(g, here.seq, k)
                    return chunk, chunk, r.x_send.at[n, g, k - 1], r.x_recv.at[n, g, k - 1], device

                self.send(make)

    def from_sides(self, g):
        here, r = self.here, self.r
        half = self.kinds[g].rows // 2
        turns = ((here.along_x, 0, here.to_y), (here.along_y, half, here.to_x))
        for k in range(1, self.planes):
            for n, (quarter, first, device) in enumerate(turns):
                self.arrived(self.chunk(g, quarter, k), r.x_recv.at[n, g, k - 1])

                def make(k=k, n=n, quarter=quarter, first=first, device=device):
                    chunk = self.chunk(g, quarter, k, first, half)
                    return chunk, chunk, r.d_send.at[n, g, k - 1], r.d_recv.at[n, g, k - 1], device

                self.send(make)

    def from_corner(self, g):
        here, r = self.here, self.r
        half = self.kinds[g].rows // 2
        for k in range(1, self.planes):
            self.arrived(self.chunk(g, here.corner, k, 0, half), r.d_recv.at[0, g, k - 1])
            self.arrived(self.chunk(g, here.corner, k, half, half), r.d_recv.at[1, g, k - 1])

            def make(k=k):
                whole = self.kinds[g].whole(self.full[g], here.ahead(self.planes - k), here.core)
                return whole, whole, r.c_send.at[g, k - 1], r.c_recv.at[g, k - 1], here.partner

            self.send(make)

    def complete(self, g):
        here, r, full = self.here, self.r, self.full[g]
        for copy in self.own_copies(g):
            copy.wait()
        if g <= TWO:
            for m in range(4):
                self.arrived(full.at[m, here.plane, 1 - here.core], r.p_recv.at[g, m])
        else:
            self.arrived(self.kinds[g].whole(full, here.plane, 1 - here.core), r.p_recv.at[g, 0])
        for k in range(1, self.planes):
            behind = here.ahead(self.planes - k)
            self.arrived(self.kinds[g].whole(full, behind, 1 - here.core), r.c_recv.at[g, k - 1])

    def end(self):
        for g in range(5):
            for k in range(1, self.planes):
                source = self.shards[g][0] if g <= TWO else self.kinds[g].own(self.shards[g], self.here.seq)
                self.plane_copy(g, k, source).wait_send()
        for make in self.started:
            remote(*make()).wait_send()


def forward_kernel(kinds, planes, layout, *refs):
    r = Space(layout, refs)
    bf16, f32 = jnp.bfloat16, jnp.float32
    here = Peers(planes)
    place, length = here.seq, r.length[0]
    gather = Gathering(kinds, here, r)
    rows, width = r.tokens.shape
    count, enc_count = r.normed.shape[0], r.encoded_rows.shape[0]
    row_ins = (r.tokens, r.encoded)
    row_alls = (r.source_rows, r.encoded_rows)
    stores = []

    def store(n, source, target):
        stores.append((n, source, target))
        pltpu.make_async_copy(source, target, r.store_sem.at[n]).start()

    def block_of(item, quarter, first=0, size=None):
        size_here = row_ins[item].shape[0]
        return row_alls[item].at[pl.ds(quarter * size_here + first, size or size_here), :]

    def rows_start(item):
        for n, device in enumerate((here.to_x, here.to_y)):
            gather.send(
                lambda n=n, device=device: (
                    row_ins[item], block_of(item, place), r.r_send.at[item, n], r.r_recv.at[item, n], device
                )
            )
        pltpu.make_async_copy(row_ins[item], block_of(item, place), r.r_own.at[item]).start()

    def rows_turn(item):
        half = row_ins[item].shape[0] // 2
        turns = ((here.along_x, 0, here.to_y), (here.along_y, half, here.to_x))
        for n, (quarter, first, device) in enumerate(turns):
            gather.arrived(block_of(item, quarter), r.r_recv.at[item, n])

            def make(n=n, quarter=quarter, first=first, device=device):
                chunk = block_of(item, quarter, first, half)
                return chunk, chunk, r.r_send.at[item, 2 + n], r.r_recv.at[item, 2 + n], device

            gather.send(make)

    def rows_done(item):
        half = row_ins[item].shape[0] // 2
        gather.arrived(block_of(item, here.corner, 0, half), r.r_recv.at[item, 2])
        gather.arrived(block_of(item, here.corner, half, half), r.r_recv.at[item, 3])
        pltpu.make_async_copy(row_ins[item], block_of(item, place), r.r_own.at[item]).wait()

    def norm_rows(values, gain):
        scale = lax.rsqrt(jnp.mean(values * values, axis=-1, keepdims=True) + EPSILON)
        return (values * scale * gain).astype(bf16)

    def project(out, left, weight):
        step = min(left.shape[0], 512)

        @row_steps(left.shape[0], step)
        def _(part):
            out[part, :] = product(left[part, :], weight[...]).astype(out.dtype)

    here.greet()
    here.meet()
    rows_start(0)
    gather.start_planes(ONE)
    rows_start(1)
    for g in (TWO, GATE_IN, UP_IN, DOWN_IN):
        gather.start_planes(g)
    for g in range(5):
        gather.start_own(g)
    fill_pads(r.pads, length)
    fill_fixed_bias(r.bias)
    rows_turn(0)
    gather.from_plane(ONE)
    rows_turn(1)
    rows_done(0)

    @row_steps(count, 128)
    def _(part):
        r.normed[part, :] = norm_rows(r.source_rows[part, :].astype(f32), r.gains[:, 0 * width : 1 * width])

    store(0, r.source_rows, r.tokens_all)
    store(1, r.normed, r.normed_all)
    gather.from_sides(ONE)
    gather.from_plane(TWO)
    gather.from_corner(ONE)
    rows_done(1)
    store(2, r.encoded_rows, r.enc_all)
    gather.complete(ONE)
    store(3, r.weights_one, r.w_one)
    own = pl.ds(pl.multiple_of(place * rows, BLOCK), rows)
    project(r.query_rows, r.normed.at[own, :], r.weights_one.at[0])
    project(r.key_rows, r.normed, r.weights_one.at[1])
    project(r.value_rows, r.normed, r.weights_one.at[2])
    store(4, r.query_rows, r.queries)
    store(5, r.key_rows, r.keys)
    store(6, r.value_rows, r.values)
    gather.from_plane(GATE_IN)
    gather.from_sides(TWO)
    self_steps = {2: [lambda: gather.from_plane(UP_IN)], 4: [lambda: gather.from_corner(TWO)]}

    def stepped(table, pair):
        for when, steps in table.items():

            @pl.when(pair == when)
            def _(steps=steps):
                for step in steps:
                    step()

    @pl.loop(0, PAIRS)
    def _(pair):
        part = columns(pair)
        self_forward_pair(
            place, r.profile.at[pair], r.query_rows.at[:, part], r.key_rows.at[:, part],
            r.value_rows.at[:, part], r.mixed.at[:, part], r.turned_one.at[part, :], r.log_self.at[pair],
            r.pads, r.bias, r.s_buf, r.vt_buf,
        )
        stepped(self_steps, pair)

    store(7, r.turned_one, r.mixed_self_turned)
    project(r.hidden, r.mixed, r.weights_one.at[3])

    @row_steps(rows, 64)
    def _(part):
        start = pl.multiple_of(place * rows + part.start, 64)
        total = r.hidden[part, :] + r.source_rows[pl.ds(start, 64), :].astype(f32)
        r.hidden[part, :] = total
        r.normed_rows[part, :] = norm_rows(total, r.gains[:, 1 * width : 2 * width])

    store(8, r.hidden, r.hidden_one)
    store(9, r.normed_rows, r.normed_two)
    gather.from_plane(DOWN_IN)
    gather.from_sides(GATE_IN)
    gather.complete(TWO)
    store(10, r.weights_two, r.w_two)
    project(r.cquery_rows, r.normed_rows, r.weights_two.at[0])
    project(r.ckey_rows, r.encoded_rows, r.weights_two.at[1])
    project(r.cvalue_rows, r.encoded_rows, r.weights_two.at[2])
    store(11, r.cquery_rows, r.cqueries)
    store(12, r.ckey_rows, r.ckeys)
    store(13, r.cvalue_rows, r.cvalues)
    cross_steps = {
        1: [lambda: gather.from_corner(GATE_IN)],
        3: [lambda: gather.from_sides(UP_IN)],
    }

    @pl.loop(0, PAIRS)
    def _(pair):
        part = columns(pair)
        cross_forward_pair(
            r.cquery_rows.at[:, part], r.ckey_rows.at[:, part], r.cvalue_rows.at[:, part],
            r.cmixed.at[:, part], r.turned_two.at[part, :], r.log_cross.at[pair],
        )
        stepped(cross_steps, pair)

    store(14, r.turned_two, r.mixed_cross_turned)
    gather.from_sides(DOWN_IN)
    project(r.hidden_last, r.cmixed, r.weights_two.at[3])

    @row_steps(rows, 64)
    def _(part):
        total = r.hidden_last[part, :] + r.hidden[part, :]
        r.hidden_last[part, :] = total
        r.normed_last[part, :] = norm_rows(total, r.gains[:, 2 * width : 3 * width])

    store(15, r.hidden_last, r.hidden_two)
    store(16, r.normed_last, r.normed_three)
    gather.from_corner(UP_IN)
    gather.from_corner(DOWN_IN)
    for g in (GATE_IN, UP_IN, DOWN_IN):
        gather.complete(g)
    gather.end()
    for n, source, target in stores:
        pltpu.make_async_copy(source, target, r.store_sem.at[n]).wait()


def forward_fused(shards, length, tokens, encoded, small):
    kinds = make_kinds(shards)
    planes = lax.axis_size("fsdp") // 2
    f32, low = jnp.float32, jnp.bfloat16
    rows, width = tokens.shape
    enc_rows = encoded.shape[0]
    count, enc_count = 4 * rows, 4 * enc_rows
    square = (4, width, width)
    in_vmem = pl.BlockSpec(memory_space=pltpu.VMEM)
    in_layout, operands = flatten(
        dict(length=length), small, dict(tokens=tokens, encoded=encoded, shards=list(shards))
    )
    in_specs = [SCALARS] + [in_vmem] * len(small)
    in_specs += [ANYWHERE] * (len(operands) - len(in_specs))
    shapes = full_shapes(kinds, planes)
    large_outs = dict(
        w_one=shaped(square, low), w_two=shaped(square, low),
        ffn_full=[shaped(shape, low) for shape in shapes[2:]],
        tokens_all=shaped((count, width), low), normed_all=shaped((count, width), low),
        enc_all=shaped((enc_count, width), low),
        queries=shaped((rows, width), low), keys=shaped((count, width), low),
        values=shaped((count, width), low), mixed_self_turned=shaped((width, rows), f32),
        hidden_one=shaped((rows, width), f32), normed_two=shaped((rows, width), low),
        cqueries=shaped((rows, width), low), ckeys=shaped((enc_count, width), low),
        cvalues=shaped((enc_count, width), low), mixed_cross_turned=shaped((width, rows), f32),
        hidden_two=shaped((rows, width), f32), normed_three=shaped((rows, width), low),
    )
    small_outs = dict(
        log_self=shaped((PAIRS, 2, rows), f32), log_cross=shaped((PAIRS, 2, rows), f32)
    )
    out_layout, out_shapes = flatten(large_outs, small_outs)
    all_rows = pltpu.VMEM((count, width), low)
    enc_all = pltpu.VMEM((enc_count, width), low)
    some_rows = pltpu.VMEM((rows, width), low)
    wide_rows = pltpu.VMEM((rows, width), f32)
    turned = pltpu.VMEM((width, rows), f32)
    buffers = forward_scratch(count, rows)
    steps = planes - 1
    scratch = dict(
        weights_one=pltpu.VMEM(square, low), weights_two=pltpu.VMEM(square, low),
        source_rows=all_rows, normed=all_rows, key_rows=all_rows, value_rows=all_rows,
        encoded_rows=enc_all, ckey_rows=enc_all, cvalue_rows=enc_all,
        query_rows=some_rows, cquery_rows=some_rows, mixed=some_rows, cmixed=some_rows,
        normed_rows=some_rows, normed_last=some_rows,
        hidden=wide_rows, hidden_last=wide_rows, turned_one=turned, turned_two=turned,
        pads=buffers[0], bias=buffers[1], s_buf=buffers[2], vt_buf=buffers[3],
        z_send=DMA((5, steps)), z_recv=DMA((5, steps)),
        own_sem=DMA((5, 4)), p_send=DMA((5, 4)), p_recv=DMA((5, 4)),
        x_send=DMA((2, 5, steps)), x_recv=DMA((2, 5, steps)),
        d_send=DMA((2, 5, steps)), d_recv=DMA((2, 5, steps)),
        c_send=DMA((5, steps)), c_recv=DMA((5, steps)),
        r_send=DMA((2, 4)), r_recv=DMA((2, 4)), r_own=DMA((2,)), store_sem=DMA((17,)),
    )
    scratch_layout, scratch_shapes = flatten(scratch)
    outs = pl.pallas_call(
        functools.partial(forward_kernel, kinds, planes, in_layout | out_layout | scratch_layout),
        in_specs=in_specs,
        out_specs=[ANYWHERE] * (len(out_shapes) - 2) + [in_vmem] * 2,
        out_shape=out_shapes,
        scratch_shapes=scratch_shapes,
        compiler_params=pltpu.CompilerParams(
            collective_id=0, has_side_effects=True, vmem_limit_bytes=66_000_000
        ),
        name="forward_fused",
    )(*operands)
    return Space(out_layout, outs)


def local(
    tokens, encoded, lengths, cotangent, gain_self, gain_cross, gain_ff, bucket_table,
    self_query, self_key, self_value, self_out, cross_query, cross_key, cross_value, cross_out,
    ff_gate, ff_up, ff_down,
):
    rows_here = tokens.shape[1]
    seq_place = lax.axis_index("seq")
    length = lengths[0]
    bf16, f32 = jnp.bfloat16, jnp.float32
    gain_one = gain_self.astype(f32)
    gain_two = gain_cross.astype(f32)
    gain_three = gain_ff.astype(f32)
    shards = (
        self_query, self_key, self_value, self_out, cross_query, cross_key, cross_value, cross_out,
        ff_gate, ff_up, ff_down,
    )
    one_hot = (
        bucket_ids(BLOCK)[:, None] == jnp.arange(BUCKETS, dtype=jnp.int32)[None, :]
    ).astype(bf16)
    profile = inner_rows(bucket_table, one_hot.T).reshape(PAIRS, 2, BLOCK)
    place = jnp.stack([seq_place.astype(jnp.int32), length])

    source = tokens[0].astype(f32)
    if kernels_fit(shards):
        gains = jnp.concatenate([gain_one, gain_two, gain_three])[None]
        forward = forward_fused(
            shards, lengths, tokens[0], encoded[0],
            dict(
                profile=profile, gains=gains
            ),
        )
        one_hot_wide = jnp.pad(one_hot.astype(f32), ((0, 0), (0, PAIR - BUCKETS)))
        width = source.shape[1]
        w_gate, w_up, w_down = (full.reshape(-1, full.shape[-1]) for full in forward.ffn_full)
        layer_out, grads, grad_tokens, enc_sum, small = backward_fused(
            shards, lengths,
            dict(
                profile=profile, log_cross=forward.log_cross, log_self=forward.log_self,
                gains=gains, one_hot=one_hot_wide,
            ),
            dict(
                cotangent=cotangent[0], w_gate=w_gate, w_up=w_up, w_down=w_down,
                normed_three_in=forward.normed_three, hidden_two_in=forward.hidden_two,
                w_one=forward.w_one, w_two=forward.w_two, mixed_cross_in=forward.mixed_cross_turned,
                cqueries_in=forward.cqueries, ckeys_in=forward.ckeys, cvalues_in=forward.cvalues,
                normed_two_in=forward.normed_two, enc_in=forward.enc_all, hidden_one_in=forward.hidden_one,
                mixed_self_in=forward.mixed_self_turned, queries_in=forward.queries, keys_in=forward.keys,
                values_in=forward.values, normed_all_in=forward.normed_all,
                tokens_all_in=forward.tokens_all,
            ),
        )
        table_sum = small[8 : 8 + HEADS, :BUCKETS].T
        return (
            layer_out[None], grad_tokens[None], enc_sum[None], small[0], small[1], small[2], table_sum, *grads
        )
    weights, tokens_all, enc_all = gather_plain(shards, tokens[0], encoded[0])
    (w_query, w_key, w_value, w_sout, w_cquery, w_ckey, w_cvalue, w_cout, w_gate, w_up, w_down) = weights
    normed_all = rms_scale(tokens_all.astype(f32), gain_one).astype(bf16)
    normed_one = rms_scale(source, gain_one).astype(bf16)
    queries = product(normed_one, w_query).astype(bf16)
    keys = product(normed_all, w_key).astype(bf16)
    values = product(normed_all, w_value).astype(bf16)
    mixed_self, mixed_self_turned, log_self = self_forward(place, profile, queries, keys, values)
    hidden_one = source + product(mixed_self, w_sout)
    normed_two = rms_scale(hidden_one, gain_two).astype(bf16)
    cqueries = product(normed_two, w_cquery).astype(bf16)
    ckeys = product(enc_all, w_ckey).astype(bf16)
    cvalues = product(enc_all, w_cvalue).astype(bf16)
    mixed_cross, mixed_cross_turned, log_cross = cross_forward(cqueries, ckeys, cvalues)
    hidden_two = hidden_one + product(mixed_cross, w_cout)
    normed_three = rms_scale(hidden_two, gain_three).astype(bf16)
    gate = product(normed_three, w_gate)
    up = product(normed_three, w_up)

    def gated(gate_rows, up_rows):
        return jax.nn.gelu(gate_rows, approximate=True) * up_rows

    activated_f, pull_gate = jax.vjp(gated, gate, up)
    activated = activated_f.astype(bf16)
    slot_ids = seq_place * rows_here + jnp.arange(rows_here, dtype=jnp.int32)
    valid = (slot_ids < length).astype(f32)[:, None]
    result = (valid * (hidden_two + product(activated, w_down))).astype(bf16)

    grad_result = valid * cotangent[0].astype(f32)
    branch_ff = grad_result.astype(bf16)
    grad_gate_f, grad_up_f = pull_gate(outer_rows(branch_ff, w_down))
    grad_gate = grad_gate_f.astype(bf16)
    grad_up = grad_up_f.astype(bf16)
    g_down = inner_rows(activated, branch_ff).astype(bf16)
    g_gate = inner_rows(normed_three, grad_gate).astype(bf16)
    g_up = inner_rows(normed_three, grad_up).astype(bf16)
    grad_three, grad_gain_three = norm_back(
        hidden_two, gain_three, outer_rows(grad_gate, w_gate) + outer_rows(grad_up, w_up)
    )
    grad_two = grad_result + grad_three
    branch_cross = grad_two.astype(bf16)
    g_cout = inner_rows(mixed_cross, branch_cross).astype(bf16)
    grad_mixed_cross = outer_rows(branch_cross, w_cout).astype(bf16)
    grad_cq, grad_ck, grad_cv = cross_backward(
        cqueries, ckeys, cvalues, grad_mixed_cross, mixed_cross_turned, log_cross
    )
    g_cquery = inner_rows(normed_two, grad_cq).astype(bf16)
    g_ckey = inner_rows(enc_all, grad_ck).astype(bf16)
    g_cvalue = inner_rows(enc_all, grad_cv).astype(bf16)
    enc_part = (outer_rows(grad_ck, w_ckey) + outer_rows(grad_cv, w_cvalue)).astype(bf16)
    grad_two_back, grad_gain_two = norm_back(hidden_one, gain_two, outer_rows(grad_cq, w_cquery))
    grad_one = grad_two + grad_two_back
    branch_self = grad_one.astype(bf16)
    g_sout = inner_rows(mixed_self, branch_self).astype(bf16)
    grad_mixed_self = outer_rows(branch_self, w_sout).astype(bf16)
    grad_q, grad_k, grad_v, near_part, far_part = self_backward(
        place, profile, queries, keys, values, grad_mixed_self, mixed_self_turned, log_self
    )
    g_query = inner_rows(normed_one, grad_q).astype(bf16)
    g_key = inner_rows(normed_all, grad_k).astype(bf16)
    g_value = inner_rows(normed_all, grad_v).astype(bf16)
    token_part = (outer_rows(grad_k, w_key) + outer_rows(grad_v, w_value)).astype(bf16)
    query_part = outer_rows(grad_q, w_query)

    near_rows = near_part.reshape(HEADS, BLOCK)
    far_rows = jnp.sum(far_part, axis=-1).reshape(HEADS)
    table_part = lax.dot_general(
        one_hot.astype(f32), near_rows, (((0,), (1,)), ((), ())),
        precision=lax.Precision.HIGHEST, preferred_element_type=f32,
    )
    table_part = table_part.at[BUCKETS - 1].add(far_rows)

    hat_all = rms_scale(tokens_all.astype(f32), jnp.ones_like(gain_one))
    hat_one = rms_scale(source, jnp.ones_like(gain_one))
    grad_gain_one = jnp.sum(token_part.astype(f32) * hat_all, axis=0) + jnp.sum(
        query_part * hat_one, axis=0
    )
    table_row = jnp.zeros((gain_one.shape[0],), f32).at[: BUCKETS * HEADS].set(table_part.reshape(-1))
    small = jnp.stack([grad_gain_one, grad_gain_two, grad_gain_three, table_row] + [jnp.zeros_like(gain_one)] * 4)
    reduced, token_sum, enc_sum, small = reduce_plain(
        (g_query, g_key, g_value, g_sout, g_cquery, g_ckey, g_cvalue, g_cout, g_gate, g_up, g_down),
        token_part, enc_part, small,
    )
    grad_zero, _ = norm_back(source, gain_one, query_part + token_sum)
    grad_tokens = grad_one + grad_zero
    table_sum = small[3, : BUCKETS * HEADS].reshape(BUCKETS, HEADS)
    small = (small[0], small[1], small[2], table_sum)
    return (result[None], grad_tokens[None], enc_sum[None], *small, *reduced)


def solution(mesh):
    rows3 = P("fsdp", "seq", None)
    rows2 = P("fsdp", None)
    return jax.shard_map(
        local,
        mesh=mesh,
        in_specs=(rows3, rows3, P("fsdp"), rows3, P(), P(), P(), P(), *([rows2] * 11)),
        out_specs=(rows3, rows3, rows3, P(), P(), P(), P(), *([rows2] * 11)),
        check_vma=False,
    )
```
